32 devices in a mesh: groups: 2 (over x), mesh: 16 (over z, y, core).
Axes of the slice: x: 2, y: 2, z: 4, core: 2. Of those that a mesh axis runs over, the one named last changes fastest.
Arguments:
- water_depth: float32 [768, 10, 640], P(('groups', 'mesh')), parts along dimension 0, may hold values from 1 to 3
- momentum: float32 [768, 2, 10, 640], P(('groups', 'mesh')), parts along dimension 0, may hold values from -3 to 3
- metric: float32 [768, 4, 64], P(('groups', 'mesh')), parts along dimension 0, may hold values from -2 to 2
- face_scale: float32 [768, 192], P(('groups', 'mesh')), parts along dimension 0, may hold values from 0.5 to 2
- face_angle: float32 [768, 192], P(('groups', 'mesh')), parts along dimension 0, may hold values from -3.140625 to 3.140625
- face_map: int32 [768, 192], P(('groups', 'mesh')), parts along dimension 0, may hold values from 0 to 4735, as said below
- rim_faces: int32 [32, 128], P(('groups', 'mesh')), parts along dimension 0, may hold values from 0 to 4607, as said below
- wet_blocks: int32 [768], P(('groups', 'mesh')), parts along dimension 0, may hold values from 0 to 1, as said below
- breach: int32 [768, 10], P(('groups', 'mesh')), parts along dimension 0, may hold values from 0 to 3
- block_plan: int32 [768], P('groups'), parts along dimension 0, may hold values from 0 to 383, as said below
Outputs:
- depth_out: float32 [768, 10, 640], P(('groups', 'mesh')), parts along dimension 0
- momentum_out: float32 [768, 2, 10, 640], P(('groups', 'mesh')), parts along dimension 0
The draws below stay inside these ranges and needn't reach their ends.
There are 2 independent parts, one for each index of `groups`. The reference program is written for one: setup_inputs(seed, part) draws one part's arguments, and reference() takes and returns one part's arrays. A program takes and returns all parts, laid end to end along the dimension named above; each array names one. Nothing has to cross between parts.
Inputs may be any that keep to these rules, and one draw needn't show every extreme that they name: `face_map`: per mesh index d, the values of its rows name faces as in the reference program: a local face number, where the pairing of local faces is symmetric, or an entry of the neighbouring index's rim list. The rim entries pair in order: entry i of index d's second half of rim_faces with entry i of index d + 1's first half. No face of the first index names a previous index, none of the last a next one. `rim_faces`: each row holds 128 distinct local face numbers. `wet_blocks`: every block of mesh index 0 is 1; the chance of a 1 falls along the mesh axis. `block_plan`: A permutation of the block slots. Each mesh index hands exactly 8 of its blocks to other indices, each to a different index, and receives exactly 8, each from a different index, into the slots it vacates; the other blocks stay.
All inputs are finite; a program needn't handle non-finite values.
Results may differ from the reference program's by a relative error of at most 0.000059.
Values sent between devices are 32-bit elements; how exact they have to be, the bound alone decides.
No kernel may reach another device: no remote copies, remote signals or barrier semaphores. Data moves between devices by JAX's collectives and lax.ppermute only.
A program may use at most 192 MiB of HBM per device.

```python
import math
import jax
import jax.numpy as jnp
import numpy as np
from jax import lax

S = 10
NP = 10
BLK = 64
BLK_DEV = 24
MOVE_DEV = 8
RIM = 64
NBLK = 384
N_MESH = 16


def topology(key):
    parts_count = NBLK // BLK_DEV
    faces_dev = 3 * BLK * BLK_DEV

    def one_device(device):
        shuffled = jax.random.permutation(jax.random.fold_in(key, device), faces_dev).astype(jnp.int32)
        left_rim = shuffled[:RIM]
        right_rim = shuffled[RIM:2 * RIM]
        wall_faces = shuffled[2 * RIM:3 * RIM]
        remaining = shuffled[3 * RIM:]
        first_half = remaining[0::2]
        second_half = remaining[1::2]
        neighbours = jnp.zeros((faces_dev,), jnp.int32)
        neighbours = neighbours.at[first_half].set(second_half).at[second_half].set(first_half).at[wall_faces].set(wall_faces)
        positions = jnp.arange(RIM, dtype=jnp.int32)
        neighbours = neighbours.at[left_rim].set(jnp.where(device == 0, left_rim, faces_dev + positions))
        neighbours = neighbours.at[right_rim].set(jnp.where(device == parts_count - 1, right_rim, faces_dev + RIM + positions))
        return (neighbours, jnp.concatenate([left_rim, right_rim]))
    neighbours, rim_lists = jax.vmap(one_device)(jnp.arange(parts_count, dtype=jnp.int32))
    return (neighbours.reshape(NBLK, 3 * BLK), rim_lists)


def draw_face_map(key, part):
    return topology(jax.random.fold_in(key, 11))[0]


def draw_rim_faces(key, part):
    return topology(jax.random.fold_in(key, 11))[1]


def draw_wet_blocks(key, part):
    parts_count = NBLK // BLK_DEV
    levels = jax.random.randint(key, (NBLK,), 0, parts_count)
    owners = jnp.arange(NBLK, dtype=jnp.int32) // BLK_DEV
    return (levels >= owners).astype(jnp.int32)


def draw_block_plan(key, part):
    parts_count = NBLK // BLK_DEV
    base_key = jax.random.fold_in(key, 23)
    offsets = 1 + jax.random.permutation(jax.random.fold_in(base_key, 1), parts_count - 1)[:MOVE_DEV].astype(jnp.int32)
    labels = jax.random.permutation(jax.random.fold_in(base_key, 2), parts_count).astype(jnp.int32)
    devices = jnp.arange(parts_count, dtype=jnp.int32)
    inverse = jnp.zeros((parts_count,), jnp.int32).at[labels].set(devices)
    shuffles = jax.vmap(lambda device: jax.random.permutation(jax.random.fold_in(jax.random.fold_in(base_key, 3), device), BLK_DEV))(devices).astype(jnp.int32)
    arrivals = jax.vmap(lambda device: jax.random.permutation(jax.random.fold_in(jax.random.fold_in(base_key, 4), device), MOVE_DEV))(devices).astype(jnp.int32)
    targets = labels[(inverse[:, None] + offsets[None, :]) % parts_count]
    sources = devices[:, None] * BLK_DEV + shuffles[:, :MOVE_DEV]
    moving_index = jnp.arange(MOVE_DEV, dtype=jnp.int32)[None, :]
    dest_slot = shuffles[targets, arrivals[targets, moving_index]]
    destinations = targets * BLK_DEV + dest_slot
    return jnp.arange(NBLK, dtype=jnp.int32).at[sources.reshape(-1)].set(destinations.reshape(-1).astype(jnp.int32))


def with_ends(values, rng, low, top_value):
    dims = values.shape
    place = [jax.random.randint(jax.random.fold_in(rng, axis), (), 0, dims[axis]) for axis in range(len(dims))]
    values = values.at[tuple(place)].set(low)
    longest = dims.index(max(dims))
    place[longest] = (place[longest] + 1) % dims[longest]
    return values.at[tuple(place)].set(top_value)


def steps_of(key, shape, pieces, low, high):
    gain, own = 1.0, jax.random.fold_in(key, 6)
    for dim, blocks in pieces:
        draws = jnp.exp(jax.random.uniform(jax.random.fold_in(own, dim), (blocks,), jnp.float32, low / len(pieces), high / len(pieces)))
        gain = gain * jnp.repeat(draws, shape[dim] // blocks).reshape([-1 if axis == dim else 1 for axis in range(len(shape))])
    return gain


def centred(own_key, shape, width, bound, pieces=(), held_as=jnp.bfloat16):
    entries = jax.random.normal(own_key, shape, jnp.float32) * width
    if len(pieces) > 0:
        entries = steps_of(own_key, shape, pieces, -0.22, 0.18) * entries
    return jnp.clip(entries, min=-bound, max=bound).astype(held_as)


def setup_inputs(seed: int = 0, part: int = 0) -> dict:
    seeds = jax.random.split(jax.random.key(seed), 11)
    own_keys = jax.random.split(jax.random.fold_in(seeds[10], part), 11)
    return {
        "water_depth": jnp.clip(1.0 + 2.0 * jax.random.uniform(own_keys[0], (NBLK, S, NP * BLK), jnp.float32) ** steps_of(own_keys[0], (NBLK, S, NP * BLK), ((0, 16),), -0.2, 0.2), 1.0, 3.0),
        "momentum": centred(own_keys[1], (NBLK, 2, S, NP * BLK), 0.5, 3.0, ((0, 16),), jnp.float32),
        "metric": centred(own_keys[2], (NBLK, 4, BLK), 0.5, 2.0, ((0, 16),), jnp.float32),
        "face_scale": jnp.clip(jnp.exp(math.log(2.0) - 1.3862944 * jax.random.uniform(own_keys[3], (NBLK, 3 * BLK), jnp.float32) ** steps_of(own_keys[3], (NBLK, 3 * BLK), ((0, 16),), -0.2, 0.2)), 0.5, 2.0),
        "face_angle": jnp.clip(jax.random.uniform(own_keys[4], (NBLK, 3 * BLK), jnp.float32, -3.140625, 3.140625), -3.140625, 3.140625),
        "face_map": draw_face_map(jax.random.fold_in(jax.random.fold_in(seeds[10], part), 71), part),
        "rim_faces": draw_rim_faces(jax.random.fold_in(jax.random.fold_in(seeds[10], part), 71), part),
        "wet_blocks": draw_wet_blocks(jax.random.fold_in(jax.random.fold_in(seeds[10], part), 71), part),
        "breach": with_ends(jax.random.randint(own_keys[8], (NBLK, S), 0, 4), jax.random.fold_in(own_keys[8], 1), 0, 3).astype(jnp.int32),
        "block_plan": draw_block_plan(jax.random.fold_in(jax.random.fold_in(seeds[10], part), 71), part),
    }


time_step = 0.01
gravity = 1.0
breach_rate = 5.0

def gauss_solve(matrix, right):
    dimension = matrix.shape[0]
    augmented = np.concatenate([np.array(matrix) * 1.0, np.array(right) * 1.0], axis=1)
    for pivot_col in range(dimension):
        largest = pivot_col + int(np.argmax(np.abs(augmented[pivot_col:, pivot_col])))
        swapped = augmented[[largest, pivot_col]]
        augmented[[pivot_col, largest]] = swapped
        augmented[pivot_col] = augmented[pivot_col] / augmented[pivot_col, pivot_col]
        for row_id in range(dimension):
            if row_id != pivot_col:
                augmented[row_id] = augmented[row_id] - augmented[row_id, pivot_col] * augmented[pivot_col]
    return augmented[:, dimension:]

def node_tables():
    points = np.array([(across / 3.0, upward / 3.0) for upward in range(4) for across in range(4 - upward)])
    powers = [(power_r, power_s) for power_r in range(4) for power_s in range(4 - power_r)]
    vander = np.zeros((10, 10))
    grad_r = np.zeros((10, 10))
    grad_s = np.zeros((10, 10))
    mono_mass = np.zeros((10, 10))
    for column, (power_r, power_s) in enumerate(powers):
        vander[:, column] = points[:, 0] ** power_r * points[:, 1] ** power_s
        if power_r > 0:
            grad_r[:, column] = power_r * points[:, 0] ** (power_r - 1) * points[:, 1] ** power_s
        if power_s > 0:
            grad_s[:, column] = power_s * points[:, 0] ** power_r * points[:, 1] ** (power_s - 1)
        for second_column, (other_r, other_s) in enumerate(powers):
            mono_mass[column, second_column] = math.factorial(power_r + other_r) * math.factorial(power_s + other_s) / math.factorial(power_r + other_r + power_s + other_s + 2)
    inverse = gauss_solve(vander, np.eye(10))
    mass_matrix = inverse.T @ mono_mass @ inverse
    line_points = np.arange(4) / 3.0
    line_vander = line_points[:, None] ** np.arange(4)[None, :]
    hilbert = 1.0 / (np.arange(4)[:, None] + np.arange(4)[None, :] + 1.0)
    line_inverse = gauss_solve(line_vander, np.eye(4))
    edge_mass = line_inverse.T @ hilbert @ line_inverse
    face_nodes = np.array([[0, 1, 2, 3], [3, 6, 8, 9], [9, 7, 4, 0]])
    edge_embed = np.zeros((10, 12))
    for face_id in range(3):
        for node_id in range(4):
            edge_embed[face_nodes[face_id, node_id], 4 * face_id:4 * face_id + 4] += edge_mass[node_id]
    lifting = gauss_solve(mass_matrix, edge_embed).reshape(10, 3, 4)
    return (jnp.asarray(grad_r @ inverse, jnp.float32), jnp.asarray(grad_s @ inverse, jnp.float32), jnp.asarray(lifting, jnp.float32), face_nodes.reshape(-1))

def normal_flux(height, flow_x, flow_y, normal_x, normal_y):
    normal_speed = (flow_x * normal_x + flow_y * normal_y) / height
    pressure = 0.5 * gravity * height * height
    fluxes = jnp.stack([flow_x * normal_x + flow_y * normal_y, flow_x * normal_speed + pressure * normal_x, flow_y * normal_speed + pressure * normal_y])
    return (fluxes, jnp.abs(normal_speed) + jnp.sqrt(gravity * height))

def flux_jumps(interior, exterior, wall_faces, normal_x, normal_y, face_scale):
    normal_flow = interior[1] * normal_x + interior[2] * normal_y
    mirrored = jnp.stack([interior[0], interior[1] - 2.0 * normal_flow * normal_x, interior[2] - 2.0 * normal_flow * normal_y])
    exterior = jnp.where(wall_faces, mirrored, exterior)
    inner_flux, inner_speed = normal_flux(interior[0], interior[1], interior[2], normal_x, normal_y)
    outer_flux, outer_speed = normal_flux(exterior[0], exterior[1], exterior[2], normal_x, normal_y)
    wave_speed = jnp.maximum(inner_speed, outer_speed)
    return face_scale * (0.5 * (inner_flux - outer_flux) + 0.5 * wave_speed * (exterior - interior))

def face_traces(fields, face_order):
    blocks, components, members, node_count, elements = fields.shape
    picked = fields[:, :, :, face_order, :].reshape(blocks, components, members, 3, 4, elements)
    return picked.transpose(1, 2, 4, 0, 3, 5).reshape(components, members, 4, blocks * 3 * elements)

def apply_matrix(matrix, values):
    return jnp.einsum('nm,bvsme->bvsne', matrix, values, precision=lax.Precision.HIGHEST)

def advance(fields, face_jumps, metric, wet_blocks, breach, tables):
    deriv_r, deriv_s, lifting, face_order = tables
    blocks, components, members, node_count, elements = fields.shape
    shaped = face_jumps.reshape(components, members, 4, blocks, 3, elements)
    lifted = jnp.einsum('nfj,vsjbfe->bvsne', lifting, shaped, precision=lax.Precision.HIGHEST)
    height = fields[:, 0]
    flow_x = fields[:, 1]
    flow_y = fields[:, 2]
    pressure = 0.5 * gravity * height * height
    speed_x = flow_x / height
    speed_y = flow_y / height
    flux_f = jnp.stack([flow_x, flow_x * speed_x + pressure, flow_y * speed_x], axis=1)
    flux_g = jnp.stack([flow_y, flow_x * speed_y, flow_y * speed_y + pressure], axis=1)
    factors = metric[:, :, None, None, None, :]
    divergence = factors[:, 0] * apply_matrix(deriv_r, flux_f) + factors[:, 1] * apply_matrix(deriv_s, flux_f) + factors[:, 2] * apply_matrix(deriv_r, flux_g) + factors[:, 3] * apply_matrix(deriv_s, flux_g)
    inflow = breach_rate * breach.astype(jnp.float32)[:, None, :, None, None] * (jnp.arange(3) == 0).astype(jnp.float32)[None, :, None, None, None]
    tendency = lifted - divergence + inflow
    return fields + time_step * wet_blocks.astype(jnp.float32)[:, None, None, None, None] * tendency

def reference(water_depth, momentum, metric, face_scale, face_angle, face_map, rim_faces, wet_blocks, breach, block_plan):
    tables = node_tables()
    node_count = tables[0].shape[0]
    blocks, members, node_cells = water_depth.shape
    elements = node_cells // node_count
    fields = jnp.concatenate([water_depth[:, None], momentum], axis=1).reshape(blocks, 3, members, node_count, elements)
    traces = face_traces(fields, tables[3])
    faces_dev = 3 * elements * BLK_DEV
    face_links = face_map.reshape(N_MESH, faces_dev).astype(jnp.int32)
    device = jnp.arange(N_MESH, dtype=jnp.int32)[:, None]
    before_dev = jnp.clip(device - 1, 0, N_MESH - 1)
    after_dev = jnp.clip(device + 1, 0, N_MESH - 1)
    from_before = jnp.take_along_axis(rim_faces[before_dev[:, 0], RIM:], jnp.clip(face_links - faces_dev, 0, RIM - 1), axis=1)
    from_after = jnp.take_along_axis(rim_faces[after_dev[:, 0], :RIM], jnp.clip(face_links - faces_dev - RIM, 0, RIM - 1), axis=1)
    partner = jnp.where(face_links < faces_dev, device * faces_dev + face_links, jnp.where(face_links < faces_dev + RIM, before_dev * faces_dev + from_before, after_dev * faces_dev + from_after)).astype(jnp.int32)
    wall_faces = (face_links == jnp.arange(faces_dev, dtype=jnp.int32)[None, :]).reshape(-1)
    exterior = jnp.take(traces, partner.reshape(-1), axis=3)[:, :, ::-1]
    angles = face_angle.reshape(-1)
    face_jumps = flux_jumps(traces, exterior, wall_faces, jnp.cos(angles), jnp.sin(angles), face_scale.reshape(-1))
    advanced = advance(fields, face_jumps, metric, wet_blocks, breach, tables)
    new_depth = advanced[:, 0].reshape(blocks, members, node_cells)
    new_flow = advanced[:, 1:].reshape(blocks, 2, members, node_cells)
    return (jnp.zeros_like(new_depth).at[block_plan].set(new_depth), jnp.zeros_like(new_flow).at[block_plan].set(new_flow))
```

```python
import functools
import math

import jax
import jax.numpy as jnp
import numpy as np
from jax import lax
from jax.experimental import pallas as pl
from jax.experimental.pallas import tpu as pltpu
from jax.sharding import PartitionSpec as P

time_step = 0.01
gravity = 1.0
breach_rate = 5.0
LANES = 128


def gauss_solve(matrix, right):
    dimension = matrix.shape[0]
    augmented = np.concatenate([np.array(matrix) * 1.0, np.array(right) * 1.0], axis=1)
    for pivot_col in range(dimension):
        largest = pivot_col + int(np.argmax(np.abs(augmented[pivot_col:, pivot_col])))
        swapped = augmented[[largest, pivot_col]]
        augmented[[pivot_col, largest]] = swapped
        augmented[pivot_col] = augmented[pivot_col] / augmented[pivot_col, pivot_col]
        for row_id in range(dimension):
            if row_id != pivot_col:
                augmented[row_id] = (
                    augmented[row_id] - augmented[row_id, pivot_col] * augmented[pivot_col]
                )
    return augmented[:, dimension:]


def node_tables():
    points = np.array(
        [(across / 3.0, upward / 3.0) for upward in range(4) for across in range(4 - upward)]
    )
    powers = [(power_r, power_s) for power_r in range(4) for power_s in range(4 - power_r)]
    vander = np.zeros((10, 10))
    grad_r = np.zeros((10, 10))
    grad_s = np.zeros((10, 10))
    mono_mass = np.zeros((10, 10))
    for column, (power_r, power_s) in enumerate(powers):
        vander[:, column] = points[:, 0] ** power_r * points[:, 1] ** power_s
        if power_r > 0:
            grad_r[:, column] = power_r * points[:, 0] ** (power_r - 1) * points[:, 1] ** power_s
        if power_s > 0:
            grad_s[:, column] = power_s * points[:, 0] ** power_r * points[:, 1] ** (power_s - 1)
        for second_column, (other_r, other_s) in enumerate(powers):
            mono_mass[column, second_column] = (
                math.factorial(power_r + other_r)
                * math.factorial(power_s + other_s)
                / math.factorial(power_r + other_r + power_s + other_s + 2)
            )
    inverse = gauss_solve(vander, np.eye(10))
    mass_matrix = inverse.T @ mono_mass @ inverse
    line_points = np.arange(4) / 3.0
    line_vander = line_points[:, None] ** np.arange(4)[None, :]
    hilbert = 1.0 / (np.arange(4)[:, None] + np.arange(4)[None, :] + 1.0)
    line_inverse = gauss_solve(line_vander, np.eye(4))
    edge_mass = line_inverse.T @ hilbert @ line_inverse
    face_nodes = np.array([[0, 1, 2, 3], [3, 6, 8, 9], [9, 7, 4, 0]])
    edge_embed = np.zeros((10, 12))
    for face_id in range(3):
        for node_id in range(4):
            edge_embed[face_nodes[face_id, node_id], 4 * face_id : 4 * face_id + 4] += edge_mass[
                node_id
            ]
    lifting = gauss_solve(mass_matrix, edge_embed).reshape(10, 3, 4)
    return (
        np.asarray(grad_r @ inverse, np.float32),
        np.asarray(grad_s @ inverse, np.float32),
        np.asarray(lifting, np.float32),
        face_nodes.reshape(-1),
    )


def round_up(value, step):
    return (value + step - 1) // step * step


def static_tables(members, elements):
    deriv_r, deriv_s, lifting, face_order = node_tables()
    nodes = deriv_r.shape[0]
    pairs = nodes // 2
    used = members * pairs
    comp = round_up(used, 8)
    face_nodes = face_order.reshape(3, 4)
    wide = members * 4
    pool = np.zeros((2, 3 * comp, 3 * LANES), np.float32)
    own = np.zeros((2, comp, LANES), np.float32)
    flat = np.zeros((2, comp, LANES), np.float32)
    for s in range(members):
        for n in range(nodes):
            flat[n % 2, s * pairs + n // 2, s * nodes + n] = 1.0
        for f in range(3):
            for k in range(4):
                n = int(face_nodes[f, k])
                own[n % 2, s * pairs + n // 2, f * wide + s * 4 + k] = 1.0
                for c in range(3):
                    pool[n % 2, c * comp + s * pairs + n // 2, f * LANES + c * wide + s * 4 + 3 - k] = 1.0
    lift = np.zeros((2 * comp, LANES), np.float32)
    vol = np.zeros((2 * comp, 2 * LANES), np.float32)
    for s in range(members):
        for n in range(nodes):
            row = (n % 2) * comp + s * pairs + n // 2
            for f in range(3):
                for k in range(4):
                    lift[row, f * wide + s * 4 + k] = lifting[n, f, k]
            for m in range(nodes):
                vol[row, s * nodes + m] = -deriv_r[n, m]
                vol[row, LANES + s * nodes + m] = -deriv_s[n, m]
            vol[row, members * nodes + s] = breach_rate
    faces = np.zeros((12, 4 * LANES), np.float32)
    for q in range(4):
        for f in range(3):
            faces[3 * q + f, q * LANES + f * wide : q * LANES + (f + 1) * wide] = 1.0
    factors = np.zeros((4, 4 * LANES), np.float32)
    for q in range(4):
        factors[q, q * LANES : (q + 1) * LANES] = 1.0
    return dict(
        pool=pool, own=np.concatenate([own, flat], axis=2), lift=lift, vol=vol, faces=faces, factors=factors,
        comp=comp, pairs=pairs, used=used, wide=wide, nodes=nodes,
    )


def high_low(matrix):
    high = jnp.asarray(matrix, jnp.float32).astype(jnp.bfloat16)
    low = (jnp.asarray(matrix, jnp.float32) - high.astype(jnp.float32)).astype(jnp.bfloat16)
    return high, low


def mm(a, b, dims=((1,), (0,))):
    return lax.dot_general(a, b, (dims, ((), ())), preferred_element_type=jnp.float32)


def split2(x):
    high = x.astype(jnp.bfloat16)
    return high, (x - high.astype(jnp.float32)).astype(jnp.bfloat16)


def split3(x):
    high = x.astype(jnp.bfloat16)
    rest = x - high.astype(jnp.float32)
    mid = rest.astype(jnp.bfloat16)
    return high, mid, (rest - mid.astype(jnp.float32)).astype(jnp.bfloat16)


def select_mm(x, onehot):
    return sum(mm(part, onehot) for part in split3(x))


def weight_mm(w_high, w_low, z):
    dims = ((1,), (1,))
    z_high, z_low = split2(z)
    return mm(w_high, z_high, dims) + mm(w_high, z_low, dims) + mm(w_low, z_high, dims)


def to_rows(tall, comp):
    return jnp.concatenate([tall[:comp], tall[comp:]], axis=1)


def gather_kernel(rim, depth, flow, pool0, pool1, fields, pool, rim_rows, *, t, members, elements, blocks):
    comp, pairs, used = t["comp"], t["pairs"], t["used"]

    def one(b, carry):
        fields[b] = jnp.zeros((3 * comp, LANES), jnp.float32)
        tile, sub = b // 8, b % 8
        for s in range(members):
            start = (s * (blocks // 8) * pairs + tile * pairs) * 8 + sub
            fields[b, s * pairs : (s + 1) * pairs] = depth[pl.ds(start, pairs, stride=8), :]
            for j in range(pairs):
                two = flow[b, s, :, j * LANES : (j + 1) * LANES]
                row = s * pairs + j
                fields[b, comp + row : comp + row + 1] = two[0:1]
                fields[b, 2 * comp + row : 2 * comp + row + 1] = two[1:2]
        turned = fields[b].T
        rows = select_mm(turned[:elements], pool0[...]) + select_mm(turned[elements:], pool1[...])
        for f in range(3):
            pool[pl.ds((b * 3 + f) * elements, elements), :] = rows[:, f * LANES : (f + 1) * LANES]
        return carry

    lax.fori_loop(0, blocks, one, 0)

    def pick(i, carry):
        for u in range(8):
            rim_rows[pl.ds(i * 8 + u, 1), :] = pool[pl.ds(rim[i * 8 + u], 1), :]
        return carry

    lax.fori_loop(0, rim_rows.shape[0] // 8, pick, 0)


def volume_kernel(
    links, wet, fields, pool, metric, inflow, own0, own1, spread, vol_h, vol_l, base, traces, outer,
    *, t, elements, blocks
):
    comp = t["comp"]
    faces = blocks * 3 * elements

    def one(b, carry):
        factors = select_mm(metric[b].T, spread[...])
        rx, sx, ry, sy = (factors[:, q * LANES : (q + 1) * LANES] for q in range(4))
        turned = fields[b].T
        parts = []
        for c in range(3):
            piece = turned[:, c * comp : (c + 1) * comp]
            both = select_mm(piece[:elements], own0[...]) + select_mm(piece[elements:], own1[...])
            traces[b, c] = both[:, :LANES]
            parts.append(both[:, LANES:])
        lane = lax.broadcasted_iota(jnp.int32, (elements, LANES), 1)
        height = jnp.where(lane < t["members"] * t["nodes"], parts[0], 1.0)
        flow_x, flow_y = parts[1], parts[2]
        pressure = 0.5 * gravity * height * height
        inverse = 1.0 / height
        speed_x = flow_x * inverse
        speed_y = flow_y * inverse
        cross = flow_y * speed_x
        flux_f = (flow_x, flow_x * speed_x + pressure, cross)
        flux_g = (flow_y, cross, flow_y * speed_y + pressure)
        rate = time_step * wet[b].astype(jnp.float32)
        for c in range(3):
            along_r = rx * flux_f[c] + ry * flux_g[c]
            along_s = sx * flux_f[c] + sy * flux_g[c]
            if c == 0:
                along_r = jnp.where(lane < t["members"] * t["nodes"], along_r, inflow[pl.ds(b, 1), :])
            else:
                along_r = jnp.where(lane < t["members"] * t["nodes"], along_r, 0.0)
            tall = weight_mm(vol_h[...], vol_l[...], jnp.concatenate([along_r, along_s], axis=1))
            base[b, c * comp : (c + 1) * comp] = fields[b, c * comp : (c + 1) * comp] + rate * to_rows(tall, comp)
        return carry

    lax.fori_loop(0, blocks, one, 0)

    def pick(i, carry):
        for u in range(8):
            g = i * 8 + u
            v = links[g]
            v = jnp.where(v < faces, v, g)
            outer[pl.ds(g, 1), :] = pool[pl.ds(v, 1), :]
        return carry

    lax.fori_loop(0, faces // 8, pick, 0)


def flux_kernel(
    order, place, count, links, rim, wet, base, traces, outer, halo, coefs, spread, lift_h, lift_l, out, patched,
    *, t, elements, blocks, leaving
):
    comp, wide, used = t["comp"], t["wide"], t["used"]
    faces = blocks * 3 * elements
    patched[...] = outer[...]

    def patch(i, carry):
        for u in range(8):
            g = rim[i * 8 + u]
            v = links[g] - faces
            far = halo[pl.ds(jnp.maximum(v, 0), 1), :]
            near = patched[pl.ds(g, 1), :]
            patched[pl.ds(g, 1), :] = jnp.where(v >= 0, far, near)
        return carry

    lax.fori_loop(0, halo.shape[0] // 8, patch, 0)

    def one(i, carry):
        b = order[i]
        spreads = select_mm(coefs[b].T, spread[...])
        n_x, n_y, scale, wall = (spreads[:, q * LANES : (q + 1) * LANES] for q in range(4))
        lane = lax.broadcasted_iota(jnp.int32, (elements, LANES), 1)
        rows = [patched[pl.ds((b * 3 + f) * elements, elements), :] for f in range(3)]

        def aligned(c):
            turn = [pltpu.roll(rows[f], ((f - c) * wide) % LANES, 1) if f != c else rows[f] for f in range(3)]
            return jnp.where(lane < wide, turn[0], jnp.where(lane < 2 * wide, turn[1], turn[2]))

        live = lane < 3 * wide
        height = jnp.where(live, traces[b, 0], 1.0)
        flow_x, flow_y = traces[b, 1], traces[b, 2]
        is_wall = wall > 0.5
        through = flow_x * n_x + flow_y * n_y
        height_o = jnp.where(live, jnp.where(is_wall, height, aligned(0)), 1.0)
        flow_xo = jnp.where(is_wall, flow_x - 2.0 * through * n_x, aligned(1))
        flow_yo = jnp.where(is_wall, flow_y - 2.0 * through * n_y, aligned(2))
        through_o = flow_xo * n_x + flow_yo * n_y
        speed = through / height
        speed_o = through_o / height_o
        fast = jnp.maximum(
            jnp.abs(speed) + jnp.sqrt(gravity * height), jnp.abs(speed_o) + jnp.sqrt(gravity * height_o)
        )
        push = 0.5 * gravity * (height * height - height_o * height_o)
        half = 0.5 * scale
        jumps = (
            half * (through - through_o + fast * (height_o - height)),
            half * (flow_x * speed - flow_xo * speed_o + push * n_x + fast * (flow_xo - flow_x)),
            half * (flow_y * speed - flow_yo * speed_o + push * n_y + fast * (flow_yo - flow_y)),
        )
        rate = time_step * wet[b].astype(jnp.float32)
        slot = place[b] if leaving else b
        for c in range(3):
            tall = weight_mm(lift_h[...], lift_l[...], jnp.where(live, jumps[c], 0.0))
            done = base[b, c * comp : (c + 1) * comp] + rate * to_rows(tall, comp)
            out[slot, c * used : (c + 1) * used] = done[:used]
        return carry

    if leaving:
        lax.fori_loop(0, count[0], one, 0)
    else:
        lax.fori_loop(count[0], blocks, one, 0)


def store_kernel(source, arrives, kept, got, depth, flow, *, t, members, blocks):
    pairs, used = t["pairs"], t["used"]

    def write(b, rows):
        tile, sub = b // 8, b % 8
        for s in range(members):
            start = (s * (blocks // 8) * pairs + tile * pairs) * 8 + sub
            depth[pl.ds(start, pairs, stride=8), :] = rows[s * pairs : (s + 1) * pairs]
            for j in range(pairs):
                row = s * pairs + j
                flow[b, s, 0:1, j * LANES : (j + 1) * LANES] = rows[used + row : used + row + 1]
                flow[b, s, 1:2, j * LANES : (j + 1) * LANES] = rows[2 * used + row : 2 * used + row + 1]

    def one(b, carry):
        @pl.when(arrives[b] == 1)
        def _():
            write(b, got.at[source[b]])

        @pl.when(arrives[b] == 0)
        def _():
            write(b, kept.at[b])

        return carry

    lax.fori_loop(0, blocks, one, 0)


def call(kernel, out_shape, n_smem, n_args, scratch=(), **keys):
    smem = pl.BlockSpec(memory_space=pltpu.SMEM)
    vmem = pl.BlockSpec(memory_space=pltpu.VMEM)
    return pl.pallas_call(
        kernel,
        out_shape=out_shape,
        in_specs=[smem] * n_smem + [vmem] * n_args,
        out_specs=jax.tree.map(lambda _: vmem, out_shape),
        scratch_shapes=scratch,
        compiler_params=pltpu.CompilerParams(vmem_limit_bytes=48 << 20),
        **keys,
    )


def body(
    water_depth, momentum, metric, face_scale, face_angle, face_map, rim_faces, wet_blocks, breach, block_plan
):
    blocks, members, node_cells = water_depth.shape
    elements = metric.shape[2]
    t = static_tables(members, elements)
    t["members"] = members
    comp, pairs, used, nodes = t["comp"], t["pairs"], t["used"], t["nodes"]
    f32 = jnp.float32
    tiles = blocks // 8
    depth_rows = water_depth.reshape(tiles, 8, members, pairs, LANES).transpose(2, 0, 3, 1, 4).reshape(-1, LANES)
    flow_rows = momentum.transpose(0, 2, 1, 3)
    links = face_map.reshape(-1)
    faces_here = links.shape[0]
    rim_list = rim_faces.reshape(-1)
    rim_width = rim_list.shape[0] // 2

    pool_mats = jnp.asarray(t["pool"], jnp.bfloat16)
    fields, pool, rim_rows = call(
        functools.partial(gather_kernel, t=t, members=members, elements=elements, blocks=blocks),
        (
            jax.ShapeDtypeStruct((blocks, 3 * comp, LANES), f32),
            jax.ShapeDtypeStruct((faces_here, LANES), f32),
            jax.ShapeDtypeStruct((2 * rim_width, LANES), f32),
        ),
        1, 4,
    )(rim_list, depth_rows, flow_rows, pool_mats[0], pool_mats[1])

    count = lax.axis_size("mesh")
    from_before = lax.ppermute(rim_rows[rim_width:], "mesh", [(i, i + 1) for i in range(count - 1)])
    from_after = lax.ppermute(rim_rows[:rim_width], "mesh", [(i + 1, i) for i in range(count - 1)])
    halo = jnp.concatenate([from_before, from_after], axis=0)

    own_mats = jnp.asarray(t["own"], jnp.bfloat16)
    vol_h, vol_l = high_low(t["vol"])
    inflow = jnp.pad(breach.astype(f32), ((0, 0), (members * nodes, LANES - members * nodes - members)))
    base, traces, outer = call(
        functools.partial(volume_kernel, t=t, elements=elements, blocks=blocks),
        (
            jax.ShapeDtypeStruct((blocks, 3 * comp, LANES), f32),
            jax.ShapeDtypeStruct((blocks, 3, elements, LANES), f32),
            jax.ShapeDtypeStruct((faces_here, LANES), f32),
        ),
        2, 9,
    )(
        links, wet_blocks, fields, pool, metric, inflow, own_mats[0], own_mats[1],
        jnp.asarray(t["factors"], jnp.bfloat16), vol_h, vol_l,
    )

    own_index = lax.axis_index("mesh")
    all_slots = block_plan.shape[0]
    local_ids = jnp.arange(blocks, dtype=jnp.int32)
    slot_ids = own_index * blocks + local_ids
    targets = lax.dynamic_slice_in_dim(block_plan, own_index * blocks, blocks)
    target_dev = targets // blocks
    leaving = (target_dev != own_index).astype(jnp.int32)
    every_slot = jnp.arange(all_slots, dtype=jnp.int32)
    source = jnp.sum(jnp.where(block_plan[None, :] == slot_ids[:, None], every_slot[None, :], 0), axis=1)
    source_dev = source // blocks
    arrives = (source_dev != own_index).astype(jnp.int32)
    n_leaving = jnp.sum(leaving)
    earlier = local_ids[None, :] < local_ids[:, None]
    rank_leave = jnp.sum(jnp.where(earlier, leaving[None, :], 0), axis=1)
    rank = jnp.where(leaving == 1, rank_leave, n_leaving + local_ids - rank_leave)
    order = jnp.sum(jnp.where(rank[None, :] == local_ids[:, None], local_ids[None, :], 0), axis=1)

    walls = (links == jnp.arange(faces_here, dtype=jnp.int32)).astype(f32).reshape(blocks, 3, elements)
    angles = face_angle.reshape(blocks, 3, elements)
    coefs = jnp.concatenate(
        [jnp.cos(angles), jnp.sin(angles), face_scale.reshape(blocks, 3, elements), walls], axis=1
    )
    lift_h, lift_l = high_low(t["lift"])
    packed = round_up(3 * used, 8)

    def flux(is_leaving, slots):
        return call(
            functools.partial(flux_kernel, t=t, elements=elements, blocks=blocks, leaving=is_leaving),
            jax.ShapeDtypeStruct((slots, packed, LANES), f32),
            6, 8,
            scratch=[pltpu.VMEM((faces_here, LANES), f32)],
        )(
            order, target_dev, n_leaving.reshape(1), links, rim_list, wet_blocks, base, traces, outer, halo, coefs,
            jnp.asarray(t["faces"], jnp.bfloat16), lift_h, lift_l,
        )

    sent = flux(True, count)
    got = lax.all_to_all(sent, "mesh", split_axis=0, concat_axis=0, tiled=True)
    kept = flux(False, blocks)
    depth_new, flow_new = call(
        functools.partial(store_kernel, t=t, members=members, blocks=blocks),
        (jax.ShapeDtypeStruct(depth_rows.shape, f32), jax.ShapeDtypeStruct(flow_rows.shape, f32)),
        2, 2,
    )(source_dev, arrives, kept, got)
    depth_out = depth_new.reshape(members, tiles, pairs, 8, LANES).transpose(1, 3, 0, 2, 4).reshape(water_depth.shape)
    return depth_out, flow_new.transpose(0, 2, 1, 3)


def solution(mesh):
    in_specs = (
        P(("groups", "mesh"), None, None),
        P(("groups", "mesh"), None, None, None),
        P(("groups", "mesh"), None, None),
        P(("groups", "mesh"), None),
        P(("groups", "mesh"), None),
        P(("groups", "mesh"), None),
        P(("groups", "mesh"), None),
        P(("groups", "mesh")),
        P(("groups", "mesh"), None),
        P("groups"),
    )
    out_specs = (P(("groups", "mesh"), None, None), P(("groups", "mesh"), None, None, None))
    return jax.shard_map(body, mesh=mesh, in_specs=in_specs, out_specs=out_specs, check_vma=False)
```

```python
import functools
import math

import jax
import jax.numpy as jnp
import numpy as np
from jax import lax
from jax.experimental import pallas as pl
from jax.experimental.pallas import tpu as pltpu
from jax.sharding import PartitionSpec as P

time_step = 0.01
gravity = 1.0
breach_rate = 5.0
LANES = 128


def gauss_solve(matrix, right):
    dimension = matrix.shape[0]
    augmented = np.concatenate([np.array(matrix) * 1.0, np.array(right) * 1.0], axis=1)
    for pivot_col in range(dimension):
        largest = pivot_col + int(np.argmax(np.abs(augmented[pivot_col:, pivot_col])))
        swapped = augmented[[largest, pivot_col]]
        augmented[[pivot_col, largest]] = swapped
        augmented[pivot_col] = augmented[pivot_col] / augmented[pivot_col, pivot_col]
        for row_id in range(dimension):
            if row_id != pivot_col:
                augmented[row_id] = (
                    augmented[row_id] - augmented[row_id, pivot_col] * augmented[pivot_col]
                )
    return augmented[:, dimension:]


def node_tables():
    points = np.array(
        [(across / 3.0, upward / 3.0) for upward in range(4) for across in range(4 - upward)]
    )
    powers = [(power_r, power_s) for power_r in range(4) for power_s in range(4 - power_r)]
    vander = np.zeros((10, 10))
    grad_r = np.zeros((10, 10))
    grad_s = np.zeros((10, 10))
    mono_mass = np.zeros((10, 10))
    for column, (power_r, power_s) in enumerate(powers):
        vander[:, column] = points[:, 0] ** power_r * points[:, 1] ** power_s
        if power_r > 0:
            grad_r[:, column] = power_r * points[:, 0] ** (power_r - 1) * points[:, 1] ** power_s
        if power_s > 0:
            grad_s[:, column] = power_s * points[:, 0] ** power_r * points[:, 1] ** (power_s - 1)
        for second_column, (other_r, other_s) in enumerate(powers):
            mono_mass[column, second_column] = (
                math.factorial(power_r + other_r)
                * math.factorial(power_s + other_s)
                / math.factorial(power_r + other_r + power_s + other_s + 2)
            )
    inverse = gauss_solve(vander, np.eye(10))
    mass_matrix = inverse.T @ mono_mass @ inverse
    line_points = np.arange(4) / 3.0
    line_vander = line_points[:, None] ** np.arange(4)[None, :]
    hilbert = 1.0 / (np.arange(4)[:, None] + np.arange(4)[None, :] + 1.0)
    line_inverse = gauss_solve(line_vander, np.eye(4))
    edge_mass = line_inverse.T @ hilbert @ line_inverse
    face_nodes = np.array([[0, 1, 2, 3], [3, 6, 8, 9], [9, 7, 4, 0]])
    edge_embed = np.zeros((10, 12))
    for face_id in range(3):
        for node_id in range(4):
            edge_embed[face_nodes[face_id, node_id], 4 * face_id : 4 * face_id + 4] += edge_mass[
                node_id
            ]
    lifting = gauss_solve(mass_matrix, edge_embed).reshape(10, 3, 4)
    return (
        np.asarray(grad_r @ inverse, np.float32),
        np.asarray(grad_s @ inverse, np.float32),
        np.asarray(lifting, np.float32),
        face_nodes.reshape(-1),
    )


def round_up(value, step):
    return (value + step - 1) // step * step


def static_tables(members, elements):
    deriv_r, deriv_s, lifting, face_order = node_tables()
    nodes = deriv_r.shape[0]
    pairs = nodes // 2
    used = members * pairs
    comp = round_up(used, 8)
    face_nodes = face_order.reshape(3, 4)
    wide = members * 4

    def lane_of(s, n):
        return (n % 2) * comp + s * pairs + n // 2

    own = np.zeros((LANES, LANES), np.float32)
    back = np.zeros((LANES, LANES), np.float32)
    lift = np.zeros((2 * comp, LANES), np.float32)
    along = np.zeros((2, 2 * comp, LANES), np.float32)
    for s in range(members):
        for f in range(3):
            for k in range(4):
                n = int(face_nodes[f, k])
                own[lane_of(s, n), f * wide + s * 4 + k] = 1.0
                back[lane_of(s, n), f * wide + s * 4 + 3 - k] = 1.0
        for n in range(nodes):
            for f in range(3):
                for k in range(4):
                    lift[lane_of(s, n), f * wide + s * 4 + k] = lifting[n, f, k]
            for m in range(nodes):
                along[0, lane_of(s, n), lane_of(s, m)] = -deriv_r[n, m]
                along[1, lane_of(s, n), lane_of(s, m)] = -deriv_s[n, m]
            along[0, lane_of(s, n), 2 * comp + s] = breach_rate
    spread = np.zeros((16, 8 * LANES), np.float32)
    for q in range(4):
        for f in range(3):
            spread[3 * q + f, q * LANES + f * wide : q * LANES + (f + 1) * wide] = 1.0
        spread[12 + q, (4 + q) * LANES : (5 + q) * LANES] = 1.0
    return dict(
        own=own, back=back, lift=lift, along=along, spread=spread,
        comp=comp, pairs=pairs, used=used, wide=wide, nodes=nodes, members=members,
    )


def high_low(matrix):
    high = matrix.astype(jnp.bfloat16)
    low = (matrix - high.astype(np.float32)).astype(jnp.bfloat16)
    return high, low


def mm(a, b, dims=((1,), (0,))):
    return lax.dot_general(a, b, (dims, ((), ())), preferred_element_type=jnp.float32)


def split(x):
    high = x.astype(jnp.bfloat16)
    return high, (x - high.astype(jnp.float32)).astype(jnp.bfloat16)


def swap_halves(x):
    return pltpu.roll(x, LANES // 2, 1)


def turn_pair(fields, first, second, turned, halves, comp):
    lower = lax.broadcasted_iota(jnp.int32, (comp, LANES), 1) < LANES // 2
    for c in range(3):
        a = fields[first, c * comp : (c + 1) * comp]
        b = fields[second, c * comp : (c + 1) * comp]
        even = jnp.where(lower, a, swap_halves(b))
        odd = jnp.where(lower, swap_halves(a), b)
        fill = jnp.full((LANES - 2 * comp, LANES), 1.0 if c == 0 else 0.0, jnp.float32)
        flat = jnp.concatenate([even, odd, fill], axis=0).T
        if turned is not None:
            turned[c] = flat
        high, low = split(flat)
        halves[c * LANES : (c + 1) * LANES, :LANES] = high
        halves[c * LANES : (c + 1) * LANES, LANES:] = low


def place_face(pieces, c, wide, lane):
    moved = [pltpu.roll(p, ((i - c) * wide) % LANES, 1) if i != c else p for i, p in enumerate(pieces)]
    return jnp.where(lane < wide, moved[0], jnp.where(lane < 2 * wide, moved[1], moved[2]))


def start_all(copies):
    for copy in copies:
        copy.start()
    return copies


def wait_all(copies):
    for copy in copies:
        copy.wait()


def prepare_kernel(
    rim, depth_in, flow_in, back_in, fields_out, pool_out, head, tail,
    depth, flow, back, fields, pool, halves, sems, *, t, blocks, elements,
):
    comp, pairs, members, wide = t["comp"], t["pairs"], t["members"], t["wide"]
    tiles = blocks // 8
    group = 8 * 3 * elements
    first = start_all(
        [pltpu.make_async_copy(depth_in, depth, sems.at[0]), pltpu.make_async_copy(back_in, back, sems.at[1])]
    )
    flows = start_all(
        [
            pltpu.make_async_copy(flow_in.at[pl.ds(8 * i, 8)], flow.at[pl.ds(8 * i, 8)], sems.at[2 + i])
            for i in range(tiles)
        ]
    )
    wait_all(first)
    outs = []
    filled = members * pairs
    for tile in range(tiles):
        flows[tile].wait()

        def rows_of(sub, carry):
            b = tile * 8 + sub
            for c in range(3):
                end = comp * (c + 1)
                fields[b, end - 8 : end] = jnp.full((8, LANES), 1.0 if c == 0 else 0.0, jnp.float32)
            for s in range(members):
                start = (s * tiles + tile) * pairs * 8 + sub
                fields[b, s * pairs : (s + 1) * pairs] = depth[pl.ds(start, pairs, stride=8), :]
                for j in range(pairs):
                    two = flow[b, s, :, j * LANES : (j + 1) * LANES]
                    row = s * pairs + j
                    fields[b, comp + row : comp + row + 1] = two[0:1]
                    fields[b, 2 * comp + row : 2 * comp + row + 1] = two[1:2]
            return carry

        lax.fori_loop(0, 8, rows_of, 0)

        def faces_of(i, carry):
            b = tile * 8 + 2 * i
            turn_pair(fields, b, b + 1, None, halves, comp)
            rows = mm(halves[...], back[...])
            lane = lax.broadcasted_iota(jnp.int32, (LANES, LANES), 1)
            pieces = [rows[c * LANES : (c + 1) * LANES] for c in range(3)]
            for f in range(3):
                face = place_face(pieces, f, wide, lane)
                for u in range(2):
                    pool[pl.ds(((b + u) * 3 + f) * elements, elements), :] = face[u * elements : (u + 1) * elements]
            return carry

        lax.fori_loop(0, 4, faces_of, 0)
        outs += start_all(
            [
                pltpu.make_async_copy(
                    fields.at[pl.ds(8 * tile, 8)], fields_out.at[pl.ds(8 * tile, 8)], sems.at[2 + tiles + 2 * tile]
                ),
                pltpu.make_async_copy(
                    pool.at[pl.ds(group * tile, group)], pool_out.at[pl.ds(group * tile, group)],
                    sems.at[3 + tiles + 2 * tile],
                ),
            ]
        )
    width = head.shape[0]

    def pick(i, carry):
        for u in range(16):
            r = i * 16 + u
            head[pl.ds(r, 1), :] = pool[pl.ds(rim[r], 1), :]
            tail[pl.ds(r, 1), :] = pool[pl.ds(rim[width + r], 1), :]
        return carry

    lax.fori_loop(0, width // 16, pick, 0)
    wait_all(outs)


def finish_kernel(
    order, place, count, links, wet,
    fields_in, pool_in, before_in, after_in, coefs_in, inflow_in, own_in, spread_in, matrix_in, low_in,
    *rest, t, blocks, elements, leaving,
):
    outs, scratch = (rest[:1], rest[1:]) if leaving else (rest[:2], rest[2:])
    fields, pool, coefs, inflow, own, spread, matrix, low, turned, halves, traces, factors, outer, pieces, *scratch = scratch
    staged, sems = scratch[0], scratch[-1]
    comp, pairs, members, wide, used = t["comp"], t["pairs"], t["members"], t["wide"], t["used"]
    faces = blocks * 3 * elements
    width = before_in.shape[0]
    loads = [
        (fields_in, fields), (pool_in, pool.at[pl.ds(0, faces)]), (before_in, pool.at[pl.ds(faces, width)]),
        (after_in, pool.at[pl.ds(faces + width, width)]), (coefs_in, coefs), (inflow_in, inflow), (own_in, own),
        (spread_in, spread), (matrix_in, matrix), (low_in, low),
    ]
    wait_all(start_all([pltpu.make_async_copy(a, b, sems.at[i]) for i, (a, b) in enumerate(loads)]))
    n_loads = len(loads)
    begin = 0 if leaving else count[0]
    end = count[0] if leaving else blocks
    step = 32
    chunks = [slice(i * step, (i + 1) * step) for i in range(LANES // step)]

    def one(i, carry):
        at = (begin + 2 * i, jnp.minimum(begin + 2 * i + 1, end - 1))
        both = (order[at[0]], order[at[1]])

        for u in range(2):
            base = both[u] * (3 * elements)
            for f in range(3):

                def pick(r, carry):
                    for w in range(32):
                        e = r * 32 + w
                        v = links[base + f * elements + e]
                        outer[pl.ds(f * LANES + u * elements + e, 1), :] = pool[pl.ds(v, 1), :]
                    return carry

                lax.fori_loop(0, elements // 32, pick, 0)

        turn_pair(fields, both[0], both[1], turned, halves, comp)
        inner = mm(halves[...], own[...])
        for c in range(3):
            traces[c] = inner[c * LANES : (c + 1) * LANES]
        lower = lax.broadcasted_iota(jnp.int32, (16, LANES), 1) < elements
        values = jnp.where(lower, coefs[both[0]], coefs[both[1]])
        rough = values.astype(jnp.bfloat16).astype(jnp.float32)
        stacked = jnp.concatenate([rough, values - rough], axis=0).T.astype(jnp.bfloat16)
        factors[...] = mm(stacked, spread[...])

        lane = lax.broadcasted_iota(jnp.int32, (step, LANES), 1)
        for rows in chunks:
            n_x, n_y, scale, wall, rx, sx, ry, sy = (
                factors[rows, q * LANES : (q + 1) * LANES] for q in range(8)
            )
            height, flow_x, flow_y = (turned[c, rows] for c in range(3))
            pressure = 0.5 * gravity * height * height
            inverse = 1.0 / height
            speed_x = flow_x * inverse
            speed_y = flow_y * inverse
            cross = flow_y * speed_x
            flux_f = (flow_x, flow_x * speed_x + pressure, cross)
            flux_g = (flow_y, cross, flow_y * speed_y + pressure)
            add = inflow[pl.ds(both[0] if rows.start < elements else both[1], 1), :]
            for c in range(3):
                along_r = rx * flux_f[c] + ry * flux_g[c]
                along_s = sx * flux_f[c] + sy * flux_g[c]
                along_r = jnp.where(lane < 2 * comp, along_r, add if c == 0 else 0.0)
                pieces[c, rows, 0:LANES], pieces[c, rows, LANES : 2 * LANES] = split(along_r)
                pieces[c, rows, 2 * LANES : 3 * LANES], pieces[c, rows, 3 * LANES : 4 * LANES] = split(along_s)

            live = lane < 3 * wide
            theirs = [outer[f * LANES + rows.start : f * LANES + rows.stop] for f in range(3)]
            height = jnp.where(live, traces[0, rows], 1.0)
            flow_x, flow_y = traces[1, rows], traces[2, rows]
            is_wall = wall > 0.5
            through = flow_x * n_x + flow_y * n_y
            height_o = jnp.where(live, jnp.where(is_wall, height, place_face(theirs, 0, wide, lane)), 1.0)
            flow_xo = jnp.where(is_wall, flow_x - 2.0 * through * n_x, place_face(theirs, 1, wide, lane))
            flow_yo = jnp.where(is_wall, flow_y - 2.0 * through * n_y, place_face(theirs, 2, wide, lane))
            through_o = flow_xo * n_x + flow_yo * n_y
            speed = through / height
            speed_o = through_o / height_o
            fast = jnp.maximum(
                jnp.abs(speed) + jnp.sqrt(gravity * height), jnp.abs(speed_o) + jnp.sqrt(gravity * height_o)
            )
            push = 0.5 * gravity * (height * height - height_o * height_o)
            half = 0.5 * scale
            jumps = (
                half * (through - through_o + fast * (height_o - height)),
                half * (flow_x * speed - flow_xo * speed_o + push * n_x + fast * (flow_xo - flow_x)),
                half * (flow_y * speed - flow_yo * speed_o + push * n_y + fast * (flow_yo - flow_y)),
            )
            for c in range(3):
                jump = jnp.where(live, jumps[c], 0.0)
                pieces[c, rows, 4 * LANES : 5 * LANES], pieces[c, rows, 5 * LANES : 6 * LANES] = split(jump)

        rates = [time_step * wet[b].astype(jnp.float32) for b in both]
        last = ((1,), (1,))
        narrow = lax.broadcasted_iota(jnp.int32, (comp, LANES), 1) < elements
        for c in range(3):
            tall = mm(matrix[...], pieces[c], last) + mm(low[...], pieces[c, :, 4 * LANES : 5 * LANES], last)
            even, odd = tall[:comp], tall[comp:]
            gains = (jnp.where(narrow, even, swap_halves(odd)), jnp.where(narrow, swap_halves(even), odd))
            for u in range(2):
                done = fields[both[u], c * comp : (c + 1) * comp] + rates[u] * gains[u]
                if leaving:
                    staged[at[u], c * used : (c + 1) * used] = done[:used]
                else:
                    staged[u, c * comp : (c + 1) * comp] = done

        if leaving:
            for u in range(2):

                @pl.when(begin + 2 * i + u < end)
                def _():
                    pltpu.make_async_copy(
                        staged.at[at[u]], outs[0].at[place[both[u]]], sems.at[n_loads + at[u]]
                    ).start()
        else:
            for u in range(2):
                write_block(both[u], staged.at[u], comp, scratch[1], scratch[2], t, blocks)
        return carry

    lax.fori_loop(0, (end - begin + 1) // 2, one, 0)
    if leaving:

        def finish(i, carry):
            pltpu.make_async_copy(staged.at[i], outs[0].at[place[order[i]]], sems.at[n_loads + i]).wait()
            return carry

        lax.fori_loop(0, end, finish, 0)
    else:
        wait_all(
            start_all([pltpu.make_async_copy(scratch[1 + i], outs[i], sems.at[n_loads + i]) for i in range(2)])
        )


def write_block(b, rows, step, depth, flow, t, blocks):
    pairs, members = t["pairs"], t["members"]
    tile, sub = b // 8, b % 8
    for s in range(members):
        start = (s * (blocks // 8) + tile) * pairs * 8 + sub
        depth[pl.ds(start, pairs, stride=8), :] = rows[s * pairs : (s + 1) * pairs]
        for j in range(pairs):
            row = s * pairs + j
            flow[b, s, 0:1, j * LANES : (j + 1) * LANES] = rows[step + row : step + row + 1]
            flow[b, s, 1:2, j * LANES : (j + 1) * LANES] = rows[2 * step + row : 2 * step + row + 1]


def merge_kernel(source, arrives, got, depth_in, flow_in, depth_out, flow_out, depth, flow, came, sems, *, t, blocks):
    def arrival(b):
        return pltpu.make_async_copy(got.at[source[b]], came.at[b], sems.at[b])

    def leave(b):
        return pltpu.make_async_copy(flow.at[b], flow_out.at[b], sems.at[blocks + b])

    whole = pltpu.make_async_copy(depth_in, depth, sems.at[2 * blocks])
    whole.start()

    def each(act):
        def one(b, carry):
            @pl.when(arrives[b] == 1)
            def _():
                act(b)

            return carry

        lax.fori_loop(0, blocks, one, 0)

    each(lambda b: arrival(b).start())
    whole.wait()

    def put(b):
        arrival(b).wait()
        write_block(b, came.at[b], t["used"], depth, flow, t, blocks)
        leave(b).start()

    each(put)
    back = pltpu.make_async_copy(depth, depth_out, sems.at[2 * blocks])
    back.start()
    each(lambda b: leave(b).wait())
    back.wait()


SMEM = pl.BlockSpec(memory_space=pltpu.SMEM)
ANY = pl.BlockSpec(memory_space=pl.ANY)
VMEM = pl.BlockSpec(memory_space=pltpu.VMEM)


def call(kernel, out_shape, n_smem, n_args, scratch, out_specs, **keys):
    return pl.pallas_call(
        kernel,
        out_shape=out_shape,
        in_specs=[SMEM] * n_smem + [ANY] * n_args,
        out_specs=out_specs,
        scratch_shapes=scratch,
        compiler_params=pltpu.CompilerParams(vmem_limit_bytes=48 << 20),
        **keys,
    )


def body(
    water_depth, momentum, metric, face_scale, face_angle, face_map, rim_faces, wet_blocks, breach, block_plan
):
    blocks, members, node_cells = water_depth.shape
    elements = metric.shape[2]
    t = static_tables(members, elements)
    comp, pairs, used = t["comp"], t["pairs"], t["used"]
    f32, bf16 = jnp.float32, jnp.bfloat16
    tiles = blocks // 8
    depth_rows = water_depth.reshape(tiles, 8, members, pairs, LANES).transpose(2, 0, 3, 1, 4).reshape(-1, LANES)
    flow_rows = momentum.transpose(0, 2, 1, 3)
    links = face_map.reshape(-1)
    faces = links.shape[0]
    rim_list = rim_faces.reshape(-1)
    width = rim_list.shape[0] // 2
    dma = pltpu.SemaphoreType.DMA

    back = jnp.asarray(np.tile(t["back"], (2, 1)), bf16)
    fields, pool, head, tail = call(
        functools.partial(prepare_kernel, t=t, blocks=blocks, elements=elements),
        (
            jax.ShapeDtypeStruct((blocks, 3 * comp, LANES), f32),
            jax.ShapeDtypeStruct((faces, LANES), f32),
            jax.ShapeDtypeStruct((width, LANES), f32),
            jax.ShapeDtypeStruct((width, LANES), f32),
        ),
        1, 3,
        [
            pltpu.VMEM(depth_rows.shape, f32), pltpu.VMEM(flow_rows.shape, f32), pltpu.VMEM(back.shape, bf16),
            pltpu.VMEM((blocks, 3 * comp, LANES), f32), pltpu.VMEM((faces, LANES), f32),
            pltpu.VMEM((3 * LANES, 2 * LANES), bf16), dma((2 + 3 * tiles,)),
        ],
        (ANY, ANY, VMEM, VMEM),
    )(rim_list, depth_rows, flow_rows, back)

    count = lax.axis_size("mesh")
    before = lax.ppermute(tail, "mesh", [(i, i + 1) for i in range(count - 1)])
    after = lax.ppermute(head, "mesh", [(i + 1, i) for i in range(count - 1)])

    own_index = lax.axis_index("mesh")
    all_slots = block_plan.shape[0]
    local_ids = jnp.arange(blocks, dtype=jnp.int32)
    slot_ids = own_index * blocks + local_ids
    targets = lax.dynamic_slice_in_dim(block_plan, own_index * blocks, blocks)
    target_dev = targets // blocks
    leaves = (target_dev != own_index).astype(jnp.int32)
    every_slot = jnp.arange(all_slots, dtype=jnp.int32)
    source = jnp.sum(jnp.where(block_plan[None, :] == slot_ids[:, None], every_slot[None, :], 0), axis=1)
    source_dev = source // blocks
    arrives = (source_dev != own_index).astype(jnp.int32)
    n_leaving = jnp.sum(leaves)
    earlier = local_ids[None, :] < local_ids[:, None]
    rank_leave = jnp.sum(jnp.where(earlier, leaves[None, :], 0), axis=1)
    rank = jnp.where(leaves == 1, rank_leave, n_leaving + local_ids - rank_leave)
    order = jnp.sum(jnp.where(rank[None, :] == local_ids[:, None], local_ids[None, :], 0), axis=1)

    walls = (links == jnp.arange(faces, dtype=jnp.int32)).astype(f32).reshape(blocks, 3, elements)
    angles = face_angle.reshape(blocks, 3, elements)
    coefs = jnp.concatenate(
        [jnp.cos(angles), jnp.sin(angles), face_scale.reshape(blocks, 3, elements), walls, metric], axis=1
    )
    coefs = jnp.concatenate([coefs, coefs], axis=2)
    inflow = jnp.pad(breach.astype(f32), ((0, 0), (2 * comp, LANES - 2 * comp - members)))
    lift_h, lift_l = high_low(t["lift"])
    matrix = np.concatenate(
        [t["along"][0], t["along"][0], t["along"][1], t["along"][1], lift_h.astype(np.float32), lift_h.astype(np.float32)],
        axis=1,
    )
    mats = [
        jnp.asarray(np.tile(t["own"], (2, 1)), bf16), jnp.asarray(np.tile(t["spread"], (2, 1)), bf16),
        jnp.asarray(matrix, bf16), jnp.asarray(lift_l),
    ]
    packed = round_up(3 * used, 8)

    def finish(leaving, out_shape, extra, n_sems):
        return call(
            functools.partial(finish_kernel, t=t, blocks=blocks, elements=elements, leaving=leaving),
            out_shape,
            5, 10,
            [
                pltpu.VMEM((blocks, 3 * comp, LANES), f32), pltpu.VMEM((faces + 2 * width, LANES), f32),
                pltpu.VMEM(coefs.shape, f32), pltpu.VMEM(inflow.shape, f32),
                *[pltpu.VMEM(m.shape, bf16) for m in mats],
                pltpu.VMEM((3, LANES, LANES), f32), pltpu.VMEM((3 * LANES, 2 * LANES), bf16),
                pltpu.VMEM((3, LANES, LANES), f32), pltpu.VMEM((LANES, 8 * LANES), f32),
                pltpu.VMEM((3 * LANES, LANES), f32), pltpu.VMEM((3, LANES, 6 * LANES), bf16),
                *extra, dma((10 + n_sems,)),
            ],
            jax.tree.map(lambda _: ANY, out_shape),
        )(order, target_dev, n_leaving.reshape(1), links, wet_blocks, fields, pool, before, after, coefs, inflow, *mats)

    sent = finish(
        True, jax.ShapeDtypeStruct((count, packed, LANES), f32), [pltpu.VMEM((blocks, packed, LANES), f32)], blocks
    )
    got = lax.all_to_all(sent, "mesh", split_axis=0, concat_axis=0, tiled=True)
    final = (jax.ShapeDtypeStruct(depth_rows.shape, f32), jax.ShapeDtypeStruct(flow_rows.shape, f32))
    whole = [pltpu.VMEM(depth_rows.shape, f32), pltpu.VMEM(flow_rows.shape, f32)]
    kept = finish(False, final, [pltpu.VMEM((2, 3 * comp, LANES), f32), *whole], 2)
    depth_new, flow_new = call(
        functools.partial(merge_kernel, t=t, blocks=blocks),
        final,
        2, 3,
        [*whole, pltpu.VMEM((blocks, packed, LANES), f32), dma((2 * blocks + 1,))],
        (ANY, ANY),
        input_output_aliases={3: 0, 4: 1},
    )(source_dev, arrives, got, *kept)
    depth_out = depth_new.reshape(members, tiles, pairs, 8, LANES).transpose(1, 3, 0, 2, 4).reshape(water_depth.shape)
    return depth_out, flow_new.transpose(0, 2, 1, 3)


def solution(mesh):
    in_specs = (
        P(("groups", "mesh"), None, None),
        P(("groups", "mesh"), None, None, None),
        P(("groups", "mesh"), None, None),
        P(("groups", "mesh"), None),
        P(("groups", "mesh"), None),
        P(("groups", "mesh"), None),
        P(("groups", "mesh"), None),
        P(("groups", "mesh")),
        P(("groups", "mesh"), None),
        P("groups"),
    )
    out_specs = (P(("groups", "mesh"), None, None), P(("groups", "mesh"), None, None, None))
    return jax.shard_map(body, mesh=mesh, in_specs=in_specs, out_specs=out_specs, check_vma=False)
```

```python
import functools
import math

import jax
import jax.numpy as jnp
import numpy as np
from jax import lax
from jax.experimental import pallas as pl
from jax.experimental.pallas import tpu as pltpu
from jax.sharding import PartitionSpec as P

time_step = 0.01
gravity = 1.0
breach_rate = 5.0
LANES = 128


def gauss_solve(matrix, right):
    dimension = matrix.shape[0]
    augmented = np.concatenate([np.array(matrix) * 1.0, np.array(right) * 1.0], axis=1)
    for pivot_col in range(dimension):
        largest = pivot_col + int(np.argmax(np.abs(augmented[pivot_col:, pivot_col])))
        swapped = augmented[[largest, pivot_col]]
        augmented[[pivot_col, largest]] = swapped
        augmented[pivot_col] = augmented[pivot_col] / augmented[pivot_col, pivot_col]
        for row_id in range(dimension):
            if row_id != pivot_col:
                augmented[row_id] = (
                    augmented[row_id] - augmented[row_id, pivot_col] * augmented[pivot_col]
                )
    return augmented[:, dimension:]


def node_tables():
    points = np.array(
        [(across / 3.0, upward / 3.0) for upward in range(4) for across in range(4 - upward)]
    )
    powers = [(power_r, power_s) for power_r in range(4) for power_s in range(4 - power_r)]
    vander = np.zeros((10, 10))
    grad_r = np.zeros((10, 10))
    grad_s = np.zeros((10, 10))
    mono_mass = np.zeros((10, 10))
    for column, (power_r, power_s) in enumerate(powers):
        vander[:, column] = points[:, 0] ** power_r * points[:, 1] ** power_s
        if power_r > 0:
            grad_r[:, column] = power_r * points[:, 0] ** (power_r - 1) * points[:, 1] ** power_s
        if power_s > 0:
            grad_s[:, column] = power_s * points[:, 0] ** power_r * points[:, 1] ** (power_s - 1)
        for second_column, (other_r, other_s) in enumerate(powers):
            mono_mass[column, second_column] = (
                math.factorial(power_r + other_r)
                * math.factorial(power_s + other_s)
                / math.factorial(power_r + other_r + power_s + other_s + 2)
            )
    inverse = gauss_solve(vander, np.eye(10))
    mass_matrix = inverse.T @ mono_mass @ inverse
    line_points = np.arange(4) / 3.0
    line_vander = line_points[:, None] ** np.arange(4)[None, :]
    hilbert = 1.0 / (np.arange(4)[:, None] + np.arange(4)[None, :] + 1.0)
    line_inverse = gauss_solve(line_vander, np.eye(4))
    edge_mass = line_inverse.T @ hilbert @ line_inverse
    face_nodes = np.array([[0, 1, 2, 3], [3, 6, 8, 9], [9, 7, 4, 0]])
    edge_embed = np.zeros((10, 12))
    for face_id in range(3):
        for node_id in range(4):
            edge_embed[face_nodes[face_id, node_id], 4 * face_id : 4 * face_id + 4] += edge_mass[
                node_id
            ]
    lifting = gauss_solve(mass_matrix, edge_embed).reshape(10, 3, 4)
    return (
        np.asarray(grad_r @ inverse, np.float32),
        np.asarray(grad_s @ inverse, np.float32),
        np.asarray(lifting, np.float32),
        face_nodes.reshape(-1),
    )


def round_up(value, step):
    return (value + step - 1) // step * step


def static_tables(members, elements):
    deriv_r, deriv_s, lifting, face_order = node_tables()
    nodes = deriv_r.shape[0]
    pairs = nodes // 2
    used = members * pairs
    comp = round_up(used, 8)
    face_nodes = face_order.reshape(3, 4)
    wide = members * 4

    def lane_of(s, n):
        return (n % 2) * comp + s * pairs + n // 2

    own = np.zeros((LANES, LANES), np.float32)
    back = np.zeros((LANES, LANES), np.float32)
    lift = np.zeros((2 * comp, LANES), np.float32)
    along = np.zeros((2, 2 * comp, LANES), np.float32)
    for s in range(members):
        for f in range(3):
            for k in range(4):
                n = int(face_nodes[f, k])
                own[lane_of(s, n), f * wide + s * 4 + k] = 1.0
                back[lane_of(s, n), f * wide + s * 4 + 3 - k] = 1.0
        for n in range(nodes):
            for f in range(3):
                for k in range(4):
                    lift[lane_of(s, n), f * wide + s * 4 + k] = lifting[n, f, k]
            for m in range(nodes):
                along[0, lane_of(s, n), lane_of(s, m)] = -deriv_r[n, m]
                along[1, lane_of(s, n), lane_of(s, m)] = -deriv_s[n, m]
            along[0, lane_of(s, n), 2 * comp + s] = breach_rate
    spread = np.zeros((16, 8 * LANES), np.float32)
    for q in range(4):
        for f in range(3):
            spread[3 * q + f, q * LANES + f * wide : q * LANES + (f + 1) * wide] = 1.0
        spread[12 + q, (4 + q) * LANES : (5 + q) * LANES] = 1.0
    return dict(
        own=own, back=back, lift=lift, along=along, spread=spread,
        comp=comp, pairs=pairs, used=used, wide=wide, nodes=nodes, members=members,
    )


def high_low(matrix):
    high = matrix.astype(jnp.bfloat16)
    low = (matrix - high.astype(np.float32)).astype(jnp.bfloat16)
    return high, low


def mm(a, b, dims=((1,), (0,))):
    return lax.dot_general(a, b, (dims, ((), ())), preferred_element_type=jnp.float32)


def split(x):
    high = x.astype(jnp.bfloat16)
    return high, (x - high.astype(jnp.float32)).astype(jnp.bfloat16)


def swap_halves(x):
    return pltpu.roll(x, LANES // 2, 1)


def turn(x, eye):
    return mm(eye[...], jnp.concatenate(split(x), axis=1), ((1,), (1,)))


def turn_pair(fields, first, second, eye, turned, halves, comp):
    lower = lax.broadcasted_iota(jnp.int32, (comp, LANES), 1) < LANES // 2
    for c in range(3):
        a = fields[first, c * comp : (c + 1) * comp]
        b = fields[second, c * comp : (c + 1) * comp]
        even = jnp.where(lower, a, swap_halves(b))
        odd = jnp.where(lower, swap_halves(a), b)
        fill = jnp.full((LANES - 2 * comp, LANES), 1.0 if c == 0 else 0.0, jnp.float32)
        flat = turn(jnp.concatenate([even, odd, fill], axis=0), eye)
        if turned is not None:
            turned[c] = flat
        high, low = split(flat)
        halves[c * LANES : (c + 1) * LANES, :LANES] = high
        halves[c * LANES : (c + 1) * LANES, LANES:] = low


def place_face(pieces, c, wide, lane):
    moved = [pltpu.roll(p, ((i - c) * wide) % LANES, 1) if i != c else p for i, p in enumerate(pieces)]
    return jnp.where(lane < wide, moved[0], jnp.where(lane < 2 * wide, moved[1], moved[2]))


def root(x):
    return x * lax.rsqrt(x)


def start_all(copies):
    for copy in copies:
        copy.start()
    return copies


def wait_all(copies):
    for copy in copies:
        copy.wait()


def prepare_kernel(
    rim, depth_in, flow_in, back_in, eye_in, fields_out, pool_out, head, tail,
    depth, flow, back, eye, fields, pool, halves, sems, *, t, blocks, elements,
):
    comp, pairs, members, wide = t["comp"], t["pairs"], t["members"], t["wide"]
    tiles = blocks // 8
    steps = blocks // 2
    group = 2 * 3 * elements
    first = start_all(
        [
            pltpu.make_async_copy(depth_in, depth, sems.at[0]), pltpu.make_async_copy(back_in, back, sems.at[1]),
            pltpu.make_async_copy(eye_in, eye, sems.at[2]),
        ]
    )

    def part(tile):
        rows = pl.ds(8 * tile, 8)
        return pltpu.make_async_copy(flow_in.at[rows], flow.at[rows], sems.at[3 + tile])

    def outward(i):
        rows, lines = pl.ds(2 * i, 2), pl.ds(group * i, group)
        return [
            pltpu.make_async_copy(fields.at[rows], fields_out.at[rows], sems.at[3 + tiles + i]),
            pltpu.make_async_copy(pool.at[lines], pool_out.at[lines], sems.at[3 + tiles + steps + i]),
        ]

    start_all([part(tile) for tile in range(tiles)])
    wait_all(first)

    def build(i):
        for u in range(2):
            b = 2 * i + u
            tile, sub = b // 8, b % 8
            for c in range(3):
                end = comp * (c + 1)
                fields[b, end - 8 : end] = jnp.full((8, LANES), 1.0 if c == 0 else 0.0, jnp.float32)
            for s in range(members):
                start = (s * tiles + tile) * pairs * 8 + sub
                fields[b, s * pairs : (s + 1) * pairs] = depth[pl.ds(start, pairs, stride=8), :]
                for j in range(pairs):
                    two = flow[b, s, :, j * LANES : (j + 1) * LANES]
                    row = s * pairs + j
                    fields[b, comp + row : comp + row + 1] = two[0:1]
                    fields[b, 2 * comp + row : 2 * comp + row + 1] = two[1:2]

    def faces_of(i):
        turn_pair(fields, 2 * i, 2 * i + 1, eye, None, halves, comp)
        rows = mm(halves[...], back[...])
        lane = lax.broadcasted_iota(jnp.int32, (LANES, LANES), 1)
        pieces = [rows[c * LANES : (c + 1) * LANES] for c in range(3)]
        for f in range(3):
            face = place_face(pieces, f, wide, lane)
            for u in range(2):
                at = ((2 * i + u) * 3 + f) * elements
                pool[pl.ds(at, elements), :] = face[u * elements : (u + 1) * elements]

    part(0).wait()
    build(0)

    def one(i, carry):
        @pl.when(i % 4 == 0)
        def _():
            part(i // 4).wait()

        faces_of(i - 1)
        build(i)
        start_all(outward(i - 1))
        return carry

    lax.fori_loop(1, steps, one, 0)
    faces_of(steps - 1)
    start_all(outward(steps - 1))
    width = head.shape[0]

    def pick(i, carry):
        for u in range(16):
            r = i * 16 + u
            head[pl.ds(r, 1), :] = pool[pl.ds(rim[r], 1), :]
            tail[pl.ds(r, 1), :] = pool[pl.ds(rim[width + r], 1), :]
        return carry

    lax.fori_loop(0, width // 16, pick, 0)

    def drain(i, carry):
        wait_all(outward(i))
        return carry

    lax.fori_loop(0, steps, drain, 0)


def finish_kernel(
    order, place, count, wet,
    links, fields_in, pool_in, before_in, after_in, coefs_in, inflow_in, own_in, spread_in, matrix_in, low_in, eye_in,
    *rest, t, blocks, elements, leaving,
):
    outs, scratch = (rest[:1], rest[1:]) if leaving else (rest[:2], rest[2:])
    fields, pool, coefs, inflow, own, spread, matrix, low, eye, turned, halves, traces, factors, outer, pieces, near, *scratch = scratch
    staged, sems = scratch[0], scratch[-1]
    comp, pairs, members, wide, used = t["comp"], t["pairs"], t["members"], t["wide"], t["used"]
    faces = blocks * 3 * elements
    width = before_in.shape[0]
    loads = [
        (fields_in, fields), (pool_in, pool.at[pl.ds(0, faces)]), (before_in, pool.at[pl.ds(faces, width)]),
        (after_in, pool.at[pl.ds(faces + width, width)]), (coefs_in, coefs), (inflow_in, inflow), (own_in, own),
        (spread_in, spread), (matrix_in, matrix), (low_in, low),
        (eye_in, eye),
    ]
    begin = 0 if leaving else count[0]
    end = count[0] if leaving else blocks
    n_loads = len(loads) + 2

    def indices(i):
        at = (begin + 2 * i, jnp.minimum(begin + 2 * i + 1, end - 1))
        return [
            pltpu.make_async_copy(links.at[order[at[u]]], near.at[u], sems.at[len(loads) + u]) for u in range(2)
        ]

    steps = (end - begin + 1) // 2

    @pl.when(steps > 0)
    def _():
        start_all(indices(0))

    wait_all(start_all([pltpu.make_async_copy(a, b, sems.at[i]) for i, (a, b) in enumerate(loads)]))
    step = 16
    chunks = [slice(i * step, (i + 1) * step) for i in range(LANES // step)]

    def one(i, carry):
        at = (begin + 2 * i, jnp.minimum(begin + 2 * i + 1, end - 1))
        both = (order[at[0]], order[at[1]])

        wait_all(indices(i))
        for u in range(2):
            for f in range(3):
                for e in range(elements):
                    v = near[u, f * elements + e]
                    row = f * LANES + u * elements + e
                    outer[row : row + 1, :] = pool[pl.ds(v, 1), :]

        @pl.when(i + 1 < steps)
        def _():
            start_all(indices(i + 1))

        turn_pair(fields, both[0], both[1], eye, turned, halves, comp)
        inner = mm(halves[...], own[...])
        for c in range(3):
            traces[c] = inner[c * LANES : (c + 1) * LANES]
        lower = lax.broadcasted_iota(jnp.int32, (16, LANES), 1) < elements
        values = jnp.where(lower, coefs[both[0]], coefs[both[1]])
        rough = values.astype(jnp.bfloat16).astype(jnp.float32)
        stacked = jnp.concatenate([rough, values - rough], axis=0).astype(jnp.bfloat16)
        stacked = mm(eye[:, :LANES], stacked, ((1,), (1,))).astype(jnp.bfloat16)
        factors[...] = mm(stacked, spread[...])

        lane = lax.broadcasted_iota(jnp.int32, (step, LANES), 1)
        for rows in chunks:
            n_x, n_y, scale, wall, rx, sx, ry, sy = (
                factors[rows, q * LANES : (q + 1) * LANES] for q in range(8)
            )
            height, flow_x, flow_y = (turned[c, rows] for c in range(3))
            pressure = 0.5 * gravity * height * height
            inverse = 1.0 / height
            speed_x = flow_x * inverse
            speed_y = flow_y * inverse
            cross = flow_y * speed_x
            flux_f = (flow_x, flow_x * speed_x + pressure, cross)
            flux_g = (flow_y, cross, flow_y * speed_y + pressure)
            add = inflow[pl.ds(both[0] if rows.start < elements else both[1], 1), :]
            for c in range(3):
                along_r = rx * flux_f[c] + ry * flux_g[c]
                along_s = sx * flux_f[c] + sy * flux_g[c]
                along_r = jnp.where(lane < 2 * comp, along_r, add if c == 0 else 0.0)
                pieces[c, rows, 0:LANES], pieces[c, rows, LANES : 2 * LANES] = split(along_r)
                pieces[c, rows, 2 * LANES : 3 * LANES], pieces[c, rows, 3 * LANES : 4 * LANES] = split(along_s)

            live = lane < 3 * wide
            theirs = [outer[f * LANES + rows.start : f * LANES + rows.stop] for f in range(3)]
            height = jnp.where(live, traces[0, rows], 1.0)
            flow_x, flow_y = traces[1, rows], traces[2, rows]
            is_wall = wall > 0.5
            through = flow_x * n_x + flow_y * n_y
            height_o = jnp.where(live, jnp.where(is_wall, height, place_face(theirs, 0, wide, lane)), 1.0)
            flow_xo = jnp.where(is_wall, flow_x - 2.0 * through * n_x, place_face(theirs, 1, wide, lane))
            flow_yo = jnp.where(is_wall, flow_y - 2.0 * through * n_y, place_face(theirs, 2, wide, lane))
            through_o = flow_xo * n_x + flow_yo * n_y
            speed = through / height
            speed_o = through_o / height_o
            fast = jnp.maximum(
                jnp.abs(speed) + root(gravity * height), jnp.abs(speed_o) + root(gravity * height_o)
            )
            push = 0.5 * gravity * (height * height - height_o * height_o)
            half = 0.5 * scale
            jumps = (
                half * (through - through_o + fast * (height_o - height)),
                half * (flow_x * speed - flow_xo * speed_o + push * n_x + fast * (flow_xo - flow_x)),
                half * (flow_y * speed - flow_yo * speed_o + push * n_y + fast * (flow_yo - flow_y)),
            )
            for c in range(3):
                jump = jnp.where(live, jumps[c], 0.0)
                pieces[c, rows, 4 * LANES : 5 * LANES], pieces[c, rows, 5 * LANES : 6 * LANES] = split(jump)

        rates = [time_step * wet[b].astype(jnp.float32) for b in both]
        last = ((1,), (1,))
        narrow = lax.broadcasted_iota(jnp.int32, (comp, LANES), 1) < elements
        for c in range(3):
            tall = mm(matrix[...], pieces[c], last) + mm(low[...], pieces[c, :, 4 * LANES : 5 * LANES], last)
            even, odd = tall[:comp], tall[comp:]
            gains = (jnp.where(narrow, even, swap_halves(odd)), jnp.where(narrow, swap_halves(even), odd))
            for u in range(2):
                done = fields[both[u], c * comp : (c + 1) * comp] + rates[u] * gains[u]
                if leaving:
                    staged[at[u], c * used : (c + 1) * used] = done[:used]
                else:
                    staged[u, c * comp : (c + 1) * comp] = done

        if leaving:
            for u in range(2):

                @pl.when(begin + 2 * i + u < end)
                def _():
                    pltpu.make_async_copy(
                        staged.at[at[u]], outs[0].at[place[both[u]]], sems.at[n_loads + at[u]]
                    ).start()
        else:
            for u in range(2):
                write_block(both[u], staged.at[u], comp, scratch[1], scratch[2], t, blocks)
        return carry

    lax.fori_loop(0, steps, one, 0)
    if leaving:

        def finish(i, carry):
            pltpu.make_async_copy(staged.at[i], outs[0].at[place[order[i]]], sems.at[n_loads + i]).wait()
            return carry

        lax.fori_loop(0, end, finish, 0)
    else:
        wait_all(
            start_all([pltpu.make_async_copy(scratch[1 + i], outs[i], sems.at[n_loads + i]) for i in range(2)])
        )


def write_block(b, rows, step, depth, flow, t, blocks):
    pairs, members = t["pairs"], t["members"]
    tile, sub = b // 8, b % 8
    for s in range(members):
        start = (s * (blocks // 8) + tile) * pairs * 8 + sub
        depth[pl.ds(start, pairs, stride=8), :] = rows[s * pairs : (s + 1) * pairs]
        for j in range(pairs):
            row = s * pairs + j
            flow[b, s, 0:1, j * LANES : (j + 1) * LANES] = rows[step + row : step + row + 1]
            flow[b, s, 1:2, j * LANES : (j + 1) * LANES] = rows[2 * step + row : 2 * step + row + 1]


def merge_kernel(source, arrives, got, depth_in, flow_in, depth_out, flow_out, depth, flow, came, sems, *, t, blocks):
    def arrival(b):
        return pltpu.make_async_copy(got.at[source[b]], came.at[b], sems.at[b])

    def leave(b):
        return pltpu.make_async_copy(flow.at[b], flow_out.at[b], sems.at[blocks + b])

    whole = pltpu.make_async_copy(depth_in, depth, sems.at[2 * blocks])
    whole.start()

    def each(act):
        def one(b, carry):
            @pl.when(arrives[b] == 1)
            def _():
                act(b)

            return carry

        lax.fori_loop(0, blocks, one, 0)

    each(lambda b: arrival(b).start())
    whole.wait()

    def put(b):
        arrival(b).wait()
        write_block(b, came.at[b], t["used"], depth, flow, t, blocks)
        leave(b).start()

    each(put)
    back = pltpu.make_async_copy(depth, depth_out, sems.at[2 * blocks])
    back.start()
    each(lambda b: leave(b).wait())
    back.wait()


SMEM = pl.BlockSpec(memory_space=pltpu.SMEM)
HBM = pl.BlockSpec(memory_space=pltpu.HBM)
VMEM = pl.BlockSpec(memory_space=pltpu.VMEM)


def call(kernel, out_shape, n_smem, n_args, scratch, out_specs, **keys):
    return pl.pallas_call(
        kernel,
        out_shape=out_shape,
        in_specs=[SMEM] * n_smem + [HBM] * n_args,
        out_specs=out_specs,
        scratch_shapes=scratch,
        compiler_params=pltpu.CompilerParams(vmem_limit_bytes=64 << 20),
        **keys,
    )


def body(
    water_depth, momentum, metric, face_scale, face_angle, face_map, rim_faces, wet_blocks, breach, block_plan
):
    blocks, members, node_cells = water_depth.shape
    elements = metric.shape[2]
    t = static_tables(members, elements)
    comp, pairs, used = t["comp"], t["pairs"], t["used"]
    f32, bf16 = jnp.float32, jnp.bfloat16
    tiles = blocks // 8
    depth_rows = water_depth.reshape(tiles, 8, members, pairs, LANES).transpose(2, 0, 3, 1, 4).reshape(-1, LANES)
    flow_rows = momentum.transpose(0, 2, 1, 3)
    links = face_map.reshape(-1)
    faces = links.shape[0]
    rim_list = rim_faces.reshape(-1)
    width = rim_list.shape[0] // 2
    dma = pltpu.SemaphoreType.DMA

    back = jnp.asarray(np.tile(t["back"], (2, 1)), bf16)
    eye = jnp.asarray(np.tile(np.eye(LANES), (1, 2)), bf16)
    fields, pool, head, tail = call(
        functools.partial(prepare_kernel, t=t, blocks=blocks, elements=elements),
        (
            jax.ShapeDtypeStruct((blocks, 3 * comp, LANES), f32),
            jax.ShapeDtypeStruct((faces, LANES), f32),
            jax.ShapeDtypeStruct((width, LANES), f32),
            jax.ShapeDtypeStruct((width, LANES), f32),
        ),
        1, 4,
        [
            pltpu.VMEM(depth_rows.shape, f32), pltpu.VMEM(flow_rows.shape, f32), pltpu.VMEM(back.shape, bf16),
            pltpu.VMEM(eye.shape, bf16),
            pltpu.VMEM((blocks, 3 * comp, LANES), f32), pltpu.VMEM((faces, LANES), f32),
            pltpu.VMEM((3 * LANES, 2 * LANES), bf16), dma((3 + tiles + blocks,)),
        ],
        (HBM, HBM, VMEM, VMEM),
    )(rim_list, depth_rows, flow_rows, back, eye)

    count = lax.axis_size("mesh")
    before = lax.ppermute(tail, "mesh", [(i, i + 1) for i in range(count - 1)])
    after = lax.ppermute(head, "mesh", [(i + 1, i) for i in range(count - 1)])

    own_index = lax.axis_index("mesh")
    all_slots = block_plan.shape[0]
    local_ids = jnp.arange(blocks, dtype=jnp.int32)
    slot_ids = own_index * blocks + local_ids
    targets = lax.dynamic_slice_in_dim(block_plan, own_index * blocks, blocks)
    target_dev = targets // blocks
    leaves = (target_dev != own_index).astype(jnp.int32)
    every_slot = jnp.arange(all_slots, dtype=jnp.int32)
    source = jnp.sum(jnp.where(block_plan[None, :] == slot_ids[:, None], every_slot[None, :], 0), axis=1)
    source_dev = source // blocks
    arrives = (source_dev != own_index).astype(jnp.int32)
    n_leaving = jnp.sum(leaves)
    earlier = local_ids[None, :] < local_ids[:, None]
    rank_leave = jnp.sum(jnp.where(earlier, leaves[None, :], 0), axis=1)
    rank = jnp.where(leaves == 1, rank_leave, n_leaving + local_ids - rank_leave)
    order = jnp.sum(jnp.where(rank[None, :] == local_ids[:, None], local_ids[None, :], 0), axis=1)

    walls = (links == jnp.arange(faces, dtype=jnp.int32)).astype(f32).reshape(blocks, 3, elements)
    angles = face_angle.reshape(blocks, 3, elements)
    coefs = jnp.concatenate(
        [jnp.cos(angles), jnp.sin(angles), face_scale.reshape(blocks, 3, elements), walls, metric], axis=1
    )
    coefs = jnp.concatenate([coefs, coefs], axis=2)
    inflow = jnp.pad(breach.astype(f32), ((0, 0), (2 * comp, LANES - 2 * comp - members)))
    lift_h, lift_l = high_low(t["lift"])
    matrix = np.concatenate(
        [t["along"][0], t["along"][0], t["along"][1], t["along"][1], lift_h.astype(np.float32), lift_h.astype(np.float32)],
        axis=1,
    )
    mats = [
        jnp.asarray(np.tile(t["own"], (2, 1)), bf16), jnp.asarray(np.tile(t["spread"], (2, 1)), bf16),
        jnp.asarray(matrix, bf16), jnp.asarray(lift_l), eye,
    ]
    packed = round_up(3 * used, 8)

    def finish(leaving, out_shape, extra, n_sems):
        return call(
            functools.partial(finish_kernel, t=t, blocks=blocks, elements=elements, leaving=leaving),
            out_shape,
            4, 12,
            [
                pltpu.VMEM((blocks, 3 * comp, LANES), f32), pltpu.VMEM((faces + 2 * width, LANES), f32),
                pltpu.VMEM(coefs.shape, f32), pltpu.VMEM(inflow.shape, f32),
                *[pltpu.VMEM(m.shape, bf16) for m in mats],
                pltpu.VMEM((3, LANES, LANES), f32), pltpu.VMEM((3 * LANES, 2 * LANES), bf16),
                pltpu.VMEM((3, LANES, LANES), f32), pltpu.VMEM((LANES, 8 * LANES), f32),
                pltpu.VMEM((3 * LANES, LANES), f32), pltpu.VMEM((3, LANES, 6 * LANES), bf16),
                pltpu.SMEM((2, face_map.shape[1]), jnp.int32),
                *extra, dma((13 + n_sems,)),
            ],
            jax.tree.map(lambda _: HBM, out_shape),
        )(order, target_dev, n_leaving.reshape(1), wet_blocks, face_map, fields, pool, before, after, coefs, inflow, *mats)

    sent = finish(
        True, jax.ShapeDtypeStruct((count, packed, LANES), f32), [pltpu.VMEM((blocks, packed, LANES), f32)], blocks
    )
    got = lax.all_to_all(sent, "mesh", split_axis=0, concat_axis=0, tiled=True)
    final = (jax.ShapeDtypeStruct(depth_rows.shape, f32), jax.ShapeDtypeStruct(flow_rows.shape, f32))
    whole = [pltpu.VMEM(depth_rows.shape, f32), pltpu.VMEM(flow_rows.shape, f32)]
    kept = finish(False, final, [pltpu.VMEM((2, 3 * comp, LANES), f32), *whole], 2)
    depth_new, flow_new = call(
        functools.partial(merge_kernel, t=t, blocks=blocks),
        final,
        2, 3,
        [*whole, pltpu.VMEM((blocks, packed, LANES), f32), dma((2 * blocks + 1,))],
        (HBM, HBM),
        input_output_aliases={3: 0, 4: 1},
    )(source_dev, arrives, got, *kept)
    depth_out = depth_new.reshape(members, tiles, pairs, 8, LANES).transpose(1, 3, 0, 2, 4).reshape(water_depth.shape)
    return depth_out, flow_new.transpose(0, 2, 1, 3)


def solution(mesh):
    in_specs = (
        P(("groups", "mesh"), None, None),
        P(("groups", "mesh"), None, None, None),
        P(("groups", "mesh"), None, None),
        P(("groups", "mesh"), None),
        P(("groups", "mesh"), None),
        P(("groups", "mesh"), None),
        P(("groups", "mesh"), None),
        P(("groups", "mesh")),
        P(("groups", "mesh"), None),
        P("groups"),
    )
    out_specs = (P(("groups", "mesh"), None, None), P(("groups", "mesh"), None, None, None))
    return jax.shard_map(body, mesh=mesh, in_specs=in_specs, out_specs=out_specs, check_vma=False)
```

```python
import functools
import math

import jax
import jax.numpy as jnp
import numpy as np
from jax import lax
from jax.experimental import pallas as pl
from jax.experimental.pallas import tpu as pltpu
from jax.sharding import PartitionSpec as P

time_step = 0.01
gravity = 1.0
breach_rate = 5.0
LANES = 128


def gauss_solve(matrix, right):
    dimension = matrix.shape[0]
    augmented = np.concatenate([np.array(matrix) * 1.0, np.array(right) * 1.0], axis=1)
    for pivot_col in range(dimension):
        largest = pivot_col + int(np.argmax(np.abs(augmented[pivot_col:, pivot_col])))
        swapped = augmented[[largest, pivot_col]]
        augmented[[pivot_col, largest]] = swapped
        augmented[pivot_col] = augmented[pivot_col] / augmented[pivot_col, pivot_col]
        for row_id in range(dimension):
            if row_id != pivot_col:
                augmented[row_id] = (
                    augmented[row_id] - augmented[row_id, pivot_col] * augmented[pivot_col]
                )
    return augmented[:, dimension:]


def node_tables():
    points = np.array(
        [(across / 3.0, upward / 3.0) for upward in range(4) for across in range(4 - upward)]
    )
    powers = [(power_r, power_s) for power_r in range(4) for power_s in range(4 - power_r)]
    vander = np.zeros((10, 10))
    grad_r = np.zeros((10, 10))
    grad_s = np.zeros((10, 10))
    mono_mass = np.zeros((10, 10))
    for column, (power_r, power_s) in enumerate(powers):
        vander[:, column] = points[:, 0] ** power_r * points[:, 1] ** power_s
        if power_r > 0:
            grad_r[:, column] = power_r * points[:, 0] ** (power_r - 1) * points[:, 1] ** power_s
        if power_s > 0:
            grad_s[:, column] = power_s * points[:, 0] ** power_r * points[:, 1] ** (power_s - 1)
        for second_column, (other_r, other_s) in enumerate(powers):
            mono_mass[column, second_column] = (
                math.factorial(power_r + other_r)
                * math.factorial(power_s + other_s)
                / math.factorial(power_r + other_r + power_s + other_s + 2)
            )
    inverse = gauss_solve(vander, np.eye(10))
    mass_matrix = inverse.T @ mono_mass @ inverse
    line_points = np.arange(4) / 3.0
    line_vander = line_points[:, None] ** np.arange(4)[None, :]
    hilbert = 1.0 / (np.arange(4)[:, None] + np.arange(4)[None, :] + 1.0)
    line_inverse = gauss_solve(line_vander, np.eye(4))
    edge_mass = line_inverse.T @ hilbert @ line_inverse
    face_nodes = np.array([[0, 1, 2, 3], [3, 6, 8, 9], [9, 7, 4, 0]])
    edge_embed = np.zeros((10, 12))
    for face_id in range(3):
        for node_id in range(4):
            edge_embed[face_nodes[face_id, node_id], 4 * face_id : 4 * face_id + 4] += edge_mass[
                node_id
            ]
    lifting = gauss_solve(mass_matrix, edge_embed).reshape(10, 3, 4)
    return (
        np.asarray(grad_r @ inverse, np.float32),
        np.asarray(grad_s @ inverse, np.float32),
        np.asarray(lifting, np.float32),
        face_nodes.reshape(-1),
    )


def round_up(value, step):
    return (value + step - 1) // step * step


def static_tables(members, elements):
    deriv_r, deriv_s, lifting, face_order = node_tables()
    nodes = deriv_r.shape[0]
    pairs = nodes // 2
    used = members * pairs
    comp = round_up(used, 8)
    face_nodes = face_order.reshape(3, 4)
    wide = members * 4

    def lane_of(s, n):
        return (n % 2) * comp + s * pairs + n // 2

    own = np.zeros((LANES, LANES), np.float32)
    back = np.zeros((LANES, LANES), np.float32)
    lift = np.zeros((2 * comp, LANES), np.float32)
    along = np.zeros((2, 2 * comp, LANES), np.float32)
    for s in range(members):
        for f in range(3):
            for k in range(4):
                n = int(face_nodes[f, k])
                own[lane_of(s, n), f * wide + s * 4 + k] = 1.0
                back[lane_of(s, n), f * wide + s * 4 + 3 - k] = 1.0
        for n in range(nodes):
            for f in range(3):
                for k in range(4):
                    lift[lane_of(s, n), f * wide + s * 4 + k] = lifting[n, f, k]
            for m in range(nodes):
                along[0, lane_of(s, n), lane_of(s, m)] = -deriv_r[n, m]
                along[1, lane_of(s, n), lane_of(s, m)] = -deriv_s[n, m]
            along[0, lane_of(s, n), 2 * comp + s] = breach_rate
    spread = np.zeros((16, 8 * LANES), np.float32)
    for q in range(4):
        for f in range(3):
            spread[3 * q + f, q * LANES + f * wide : q * LANES + (f + 1) * wide] = 1.0
        spread[12 + q, (4 + q) * LANES : (5 + q) * LANES] = 1.0
    return dict(
        own=own, back=back, lift=lift, along=along, spread=spread,
        comp=comp, pairs=pairs, used=used, wide=wide, nodes=nodes, members=members,
    )


def high_low(matrix):
    high = matrix.astype(jnp.bfloat16)
    low = (matrix - high.astype(np.float32)).astype(jnp.bfloat16)
    return high, low


def mm(a, b, dims=((1,), (0,))):
    return lax.dot_general(a, b, (dims, ((), ())), preferred_element_type=jnp.float32)


def split(x):
    high = x.astype(jnp.bfloat16)
    return high, (x - high.astype(jnp.float32)).astype(jnp.bfloat16)


def swap_halves(x):
    return pltpu.roll(x, LANES // 2, 1)


def turn(x, eye):
    return mm(eye[...], jnp.concatenate(split(x), axis=1), ((1,), (1,)))


def turn_pair(fields, first, second, eye, turned, halves, comp):
    lower = lax.broadcasted_iota(jnp.int32, (comp, LANES), 1) < LANES // 2
    for c in range(3):
        a = fields[first, c * comp : (c + 1) * comp]
        b = fields[second, c * comp : (c + 1) * comp]
        even = jnp.where(lower, a, swap_halves(b))
        odd = jnp.where(lower, swap_halves(a), b)
        fill = jnp.full((LANES - 2 * comp, LANES), 1.0 if c == 0 else 0.0, jnp.float32)
        flat = turn(jnp.concatenate([even, odd, fill], axis=0), eye)
        if turned is not None:
            turned[c] = flat
        high, low = split(flat)
        halves[c * LANES : (c + 1) * LANES, :LANES] = high
        halves[c * LANES : (c + 1) * LANES, LANES:] = low


def place_face(pieces, c, wide, lane):
    moved = [pltpu.roll(p, ((i - c) * wide) % LANES, 1) if i != c else p for i, p in enumerate(pieces)]
    return jnp.where(lane < wide, moved[0], jnp.where(lane < 2 * wide, moved[1], moved[2]))


def root(x):
    return x * lax.rsqrt(x)


def start_all(copies):
    for copy in copies:
        copy.start()
    return copies


def wait_all(copies):
    for copy in copies:
        copy.wait()


def prepare_kernel(
    rim_in, depth_in, flow_in, back_in, eye_in, fields_out, pool_out, head, tail,
    rim, depth, flow, back, eye, fields, pool, halves, sems, *, t, blocks, elements,
):
    comp, pairs, members, wide = t["comp"], t["pairs"], t["members"], t["wide"]
    tiles = blocks // 8
    steps = blocks // 2
    group = 2 * 3 * elements
    first = start_all(
        [
            pltpu.make_async_copy(depth_in, depth, sems.at[0]), pltpu.make_async_copy(back_in, back, sems.at[1]),
            pltpu.make_async_copy(eye_in, eye, sems.at[2]),
            pltpu.make_async_copy(rim_in, rim, sems.at[3 + tiles + 2 * steps]),
        ]
    )

    def part(tile):
        rows = pl.ds(8 * tile, 8)
        return pltpu.make_async_copy(flow_in.at[rows], flow.at[rows], sems.at[3 + tile])

    def outward(i):
        rows, lines = pl.ds(2 * i, 2), pl.ds(group * i, group)
        return [
            pltpu.make_async_copy(fields.at[rows], fields_out.at[rows], sems.at[3 + tiles + i]),
            pltpu.make_async_copy(pool.at[lines], pool_out.at[lines], sems.at[3 + tiles + steps + i]),
        ]

    start_all([part(tile) for tile in range(tiles)])
    wait_all(first)

    def build(i):
        for u in range(2):
            b = 2 * i + u
            tile, sub = b // 8, b % 8
            for c in range(3):
                end = comp * (c + 1)
                fields[b, end - 8 : end] = jnp.full((8, LANES), 1.0 if c == 0 else 0.0, jnp.float32)
            for s in range(members):
                start = (s * tiles + tile) * pairs * 8 + sub
                fields[b, s * pairs : (s + 1) * pairs] = depth[pl.ds(start, pairs, stride=8), :]
                for j in range(pairs):
                    two = flow[b, s, :, j * LANES : (j + 1) * LANES]
                    row = s * pairs + j
                    fields[b, comp + row : comp + row + 1] = two[0:1]
                    fields[b, 2 * comp + row : 2 * comp + row + 1] = two[1:2]

    def turn_of(i):
        turn_pair(fields, 2 * i, 2 * i + 1, eye, None, halves, comp)

    def faces_of(i):
        rows = mm(halves[...], back[...])
        lane = lax.broadcasted_iota(jnp.int32, (LANES, LANES), 1)
        pieces = [rows[c * LANES : (c + 1) * LANES] for c in range(3)]
        for f in range(3):
            face = place_face(pieces, f, wide, lane)
            for u in range(2):
                at = ((2 * i + u) * 3 + f) * elements
                pool[pl.ds(at, elements), :] = face[u * elements : (u + 1) * elements]

    part(0).wait()
    build(0)
    turn_of(0)
    build(1)

    def one(i, carry):
        @pl.when(i % 4 == 0)
        def _():
            part(i // 4).wait()

        faces_of(i - 2)
        turn_of(i - 1)
        build(i)
        start_all(outward(i - 2))
        return carry

    lax.fori_loop(2, steps, one, 0)
    faces_of(steps - 2)
    turn_of(steps - 1)
    start_all(outward(steps - 2))
    faces_of(steps - 1)
    start_all(outward(steps - 1))
    width = head.shape[0]

    def pick(i, carry):
        for u in range(16):
            r = i * 16 + u
            head[pl.ds(r, 1), :] = pool[pl.ds(rim[0, r], 1), :]
            tail[pl.ds(r, 1), :] = pool[pl.ds(rim[0, width + r], 1), :]
        return carry

    lax.fori_loop(0, width // 16, pick, 0)

    def drain(i, carry):
        wait_all(outward(i))
        return carry

    lax.fori_loop(0, steps, drain, 0)


def scan_moves(plan, base, order, place, blocks):
    def one(i, carry):
        leaving, staying = carry
        slot = plan[base + i]
        away = jnp.logical_or(slot < base, slot >= base + blocks).astype(jnp.int32)
        order[jnp.where(away == 1, leaving, blocks - 1 - staying)] = i
        place[i] = lax.div(slot, jnp.int32(blocks))
        return leaving + away, staying + 1 - away

    return lax.fori_loop(0, blocks, one, (jnp.int32(0), jnp.int32(0)))[0]


def scan_origins(plan, own, origin, blocks, devices):
    def device(d, carry):
        mark = jnp.where(d == own, -1, d)
        for i in range(blocks):
            slot = plan[d * blocks + i] - own * blocks
            origin[jnp.where(jnp.logical_and(slot >= 0, slot < blocks), slot, blocks)] = mark
        return carry

    lax.fori_loop(0, devices, device, 0)


def face_rows(angle, scale, links, metric, coefs, blocks, elements):
    shape = (blocks, 3 * elements)
    own = lax.broadcasted_iota(jnp.int32, shape, 0) * (3 * elements) + lax.broadcasted_iota(jnp.int32, shape, 1)
    wall = jnp.where(links[...] == own, 1.0, 0.0)
    lower = lax.broadcasted_iota(jnp.int32, (blocks, LANES), 1) < elements
    for q, value in enumerate((jnp.cos(angle[...]), jnp.sin(angle[...]), scale[...], wall)):
        two = value[:, :LANES]
        swapped = swap_halves(two)
        third = value[:, LANES:]
        faces = (
            jnp.where(lower, two, swapped), jnp.where(lower, swapped, two), jnp.concatenate([third, third], axis=1)
        )
        for f in range(3):
            coefs[pl.ds(3 * q + f, blocks, stride=16), :] = faces[f]
    for b in range(blocks):
        factors = metric[b]
        coefs[b * 16 + 12 : b * 16 + 16] = jnp.concatenate([factors, factors], axis=1)


def finish_kernel(
    plan_in, wet_in, breach_in, links_in, angle_in, scale_in, metric_in,
    fields_in, pool_in, before_in, after_in, own_in, spread_in, matrix_in, low_in, eye_in,
    *rest, t, blocks, elements, leaving, devices,
):
    outs, scratch = (rest[:1], rest[1:]) if leaving else (rest[:3], rest[3:])
    plan, wet, breach, links, angle, scale, metric, fields, pool, own, spread, matrix, low, eye, *scratch = scratch
    order, place, coefs, turned, halves, traces, factors, outer, pieces, near, *scratch = scratch
    staged, sems = scratch[0], scratch[-1]
    comp, pairs, members, wide, used = t["comp"], t["pairs"], t["members"], t["wide"], t["used"]
    faces = blocks * 3 * elements
    width = before_in.shape[0]
    loads = [
        (plan_in, plan), (angle_in, angle), (scale_in, scale), (links_in, links), (metric_in, metric),
        (wet_in, wet), (breach_in, breach), (eye_in, eye), (own_in, own), (fields_in, fields),
        (pool_in, pool.at[pl.ds(0, faces)]), (before_in, pool.at[pl.ds(faces, width)]),
        (after_in, pool.at[pl.ds(faces + width, width)]), (spread_in, spread), (matrix_in, matrix), (low_in, low),
    ]
    n_loads = len(loads) + 2
    loads = start_all([pltpu.make_async_copy(a, b, sems.at[i]) for i, (a, b) in enumerate(loads)])
    index = lax.axis_index("mesh")
    loads[0].wait()
    n_leaving = scan_moves(plan, index * blocks, order, place, blocks)
    begin = 0 if leaving else n_leaving
    end = n_leaving if leaving else blocks

    def indices(i):
        at = (begin + 2 * i, jnp.minimum(begin + 2 * i + 1, end - 1))
        return [
            pltpu.make_async_copy(links_in.at[order[at[u]]], near.at[u], sems.at[n_loads - 2 + u]) for u in range(2)
        ]

    steps = (end - begin + 1) // 2

    @pl.when(steps > 0)
    def _():
        start_all(indices(0))

    wait_all(loads[1:5])
    face_rows(angle, scale, links, metric, coefs, blocks, elements)
    if not leaving:
        scan_origins(plan, index, scratch[3], blocks, devices)
    wait_all(loads[5:])
    step = 16
    chunks = [slice(i * step, (i + 1) * step) for i in range(LANES // step)]

    def one(i, carry):
        at = (begin + 2 * i, jnp.minimum(begin + 2 * i + 1, end - 1))
        both = (order[at[0]], order[at[1]])

        wait_all(indices(i))
        for u in range(2):
            for f in range(3):
                for e in range(elements):
                    v = near[u, f * elements + e]
                    row = f * LANES + u * elements + e
                    outer[row : row + 1, :] = pool[pl.ds(v, 1), :]

        @pl.when(i + 1 < steps)
        def _():
            start_all(indices(i + 1))

        turn_pair(fields, both[0], both[1], eye, turned, halves, comp)
        inner = mm(halves[...], own[...])
        for c in range(3):
            traces[c] = inner[c * LANES : (c + 1) * LANES]
        lower = lax.broadcasted_iota(jnp.int32, (16, LANES), 1) < elements
        values = jnp.where(lower, coefs[pl.ds(both[0] * 16, 16), :], coefs[pl.ds(both[1] * 16, 16), :])
        rough = values.astype(jnp.bfloat16).astype(jnp.float32)
        stacked = jnp.concatenate([rough, values - rough], axis=0).astype(jnp.bfloat16)
        stacked = mm(eye[:, :LANES], stacked, ((1,), (1,))).astype(jnp.bfloat16)
        factors[...] = mm(stacked, spread[...])

        lane = lax.broadcasted_iota(jnp.int32, (step, LANES), 1)
        inflow = []
        for b in both:
            row = jnp.zeros((1, LANES), jnp.float32)
            for s in range(members):
                level = breach[s, b].astype(jnp.float32)
                row = jnp.where(lax.broadcasted_iota(jnp.int32, (1, LANES), 1) == 2 * comp + s, level, row)
            inflow.append(row)
        for rows in chunks:
            n_x, n_y, scale, wall, rx, sx, ry, sy = (
                factors[rows, q * LANES : (q + 1) * LANES] for q in range(8)
            )
            height, flow_x, flow_y = (turned[c, rows] for c in range(3))
            pressure = 0.5 * gravity * height * height
            inverse = 1.0 / height
            speed_x = flow_x * inverse
            speed_y = flow_y * inverse
            cross = flow_y * speed_x
            flux_f = (flow_x, flow_x * speed_x + pressure, cross)
            flux_g = (flow_y, cross, flow_y * speed_y + pressure)
            add = inflow[rows.start // elements]
            for c in range(3):
                along_r = rx * flux_f[c] + ry * flux_g[c]
                along_s = sx * flux_f[c] + sy * flux_g[c]
                along_r = jnp.where(lane < 2 * comp, along_r, add if c == 0 else 0.0)
                pieces[c, rows, 0:LANES], pieces[c, rows, LANES : 2 * LANES] = split(along_r)
                pieces[c, rows, 2 * LANES : 3 * LANES], pieces[c, rows, 3 * LANES : 4 * LANES] = split(along_s)

            live = lane < 3 * wide
            theirs = [outer[f * LANES + rows.start : f * LANES + rows.stop] for f in range(3)]
            height = jnp.where(live, traces[0, rows], 1.0)
            flow_x, flow_y = traces[1, rows], traces[2, rows]
            is_wall = wall > 0.5
            through = flow_x * n_x + flow_y * n_y
            height_o = jnp.where(live, jnp.where(is_wall, height, place_face(theirs, 0, wide, lane)), 1.0)
            flow_xo = jnp.where(is_wall, flow_x - 2.0 * through * n_x, place_face(theirs, 1, wide, lane))
            flow_yo = jnp.where(is_wall, flow_y - 2.0 * through * n_y, place_face(theirs, 2, wide, lane))
            through_o = flow_xo * n_x + flow_yo * n_y
            speed = through / height
            speed_o = through_o / height_o
            fast = jnp.maximum(
                jnp.abs(speed) + root(gravity * height), jnp.abs(speed_o) + root(gravity * height_o)
            )
            push = 0.5 * gravity * (height * height - height_o * height_o)
            half = 0.5 * scale
            jumps = (
                half * (through - through_o + fast * (height_o - height)),
                half * (flow_x * speed - flow_xo * speed_o + push * n_x + fast * (flow_xo - flow_x)),
                half * (flow_y * speed - flow_yo * speed_o + push * n_y + fast * (flow_yo - flow_y)),
            )
            for c in range(3):
                jump = jnp.where(live, jumps[c], 0.0)
                pieces[c, rows, 4 * LANES : 5 * LANES], pieces[c, rows, 5 * LANES : 6 * LANES] = split(jump)

        rates = [time_step * wet[b].astype(jnp.float32) for b in both]
        last = ((1,), (1,))
        narrow = lax.broadcasted_iota(jnp.int32, (comp, LANES), 1) < elements
        for c in range(3):
            tall = mm(matrix[...], pieces[c], last) + mm(low[...], pieces[c, :, 4 * LANES : 5 * LANES], last)
            even, odd = tall[:comp], tall[comp:]
            gains = (jnp.where(narrow, even, swap_halves(odd)), jnp.where(narrow, swap_halves(even), odd))
            for u in range(2):
                done = fields[both[u], c * comp : (c + 1) * comp] + rates[u] * gains[u]
                if leaving:
                    staged[at[u], c * used : (c + 1) * used] = done[:used]
                else:
                    staged[u, c * comp : (c + 1) * comp] = done

        if leaving:
            for u in range(2):

                @pl.when(begin + 2 * i + u < end)
                def _():
                    pltpu.make_async_copy(
                        staged.at[at[u]], outs[0].at[place[both[u]]], sems.at[n_loads + at[u]]
                    ).start()
        else:
            for u in range(2):
                write_block(both[u], staged.at[u], comp, scratch[1], scratch[2], t, blocks)
        return carry

    lax.fori_loop(0, steps, one, 0)
    if leaving:

        def finish(i, carry):
            pltpu.make_async_copy(staged.at[i], outs[0].at[place[order[i]]], sems.at[n_loads + i]).wait()
            return carry

        lax.fori_loop(0, end, finish, 0)
    else:
        wait_all(
            start_all(
                [
                    pltpu.make_async_copy(a, outs[i], sems.at[n_loads + i])
                    for i, a in enumerate((scratch[1], scratch[2], scratch[3].at[pl.ds(0, outs[2].shape[0])]))
                ]
            )
        )


def write_block(b, rows, step, depth, flow, t, blocks):
    pairs, members = t["pairs"], t["members"]
    tile, sub = b // 8, b % 8
    for s in range(members):
        start = (s * (blocks // 8) + tile) * pairs * 8 + sub
        depth[pl.ds(start, pairs, stride=8), :] = rows[s * pairs : (s + 1) * pairs]
        for j in range(pairs):
            row = s * pairs + j
            flow[b, s, 0:1, j * LANES : (j + 1) * LANES] = rows[step + row : step + row + 1]
            flow[b, s, 1:2, j * LANES : (j + 1) * LANES] = rows[2 * step + row : 2 * step + row + 1]


def merge_kernel(
    origin_in, got, depth_in, flow_in, depth_out, flow_out, origin, depth, flow, came, sems, *, t, blocks
):
    def arrival(b):
        return pltpu.make_async_copy(got.at[origin[b]], came.at[b], sems.at[b])

    def leave(b):
        return pltpu.make_async_copy(flow.at[b], flow_out.at[b], sems.at[blocks + b])

    whole = pltpu.make_async_copy(depth_in, depth, sems.at[2 * blocks])
    first = pltpu.make_async_copy(origin_in, origin, sems.at[2 * blocks + 1])
    first.start()
    whole.start()
    first.wait()

    def each(act):
        def one(b, carry):
            @pl.when(origin[b] >= 0)
            def _():
                act(b)

            return carry

        lax.fori_loop(0, blocks, one, 0)

    each(lambda b: arrival(b).start())
    whole.wait()

    def put(b):
        arrival(b).wait()
        write_block(b, came.at[b], t["used"], depth, flow, t, blocks)
        leave(b).start()

    each(put)
    back = pltpu.make_async_copy(depth, depth_out, sems.at[2 * blocks])
    back.start()
    each(lambda b: leave(b).wait())
    back.wait()


SMEM = pl.BlockSpec(memory_space=pltpu.SMEM)
HBM = pl.BlockSpec(memory_space=pltpu.HBM)
VMEM = pl.BlockSpec(memory_space=pltpu.VMEM)


def call(kernel, out_shape, n_smem, n_args, scratch, out_specs, **keys):
    return pl.pallas_call(
        kernel,
        out_shape=out_shape,
        in_specs=[SMEM] * n_smem + [HBM] * n_args,
        out_specs=out_specs,
        scratch_shapes=scratch,
        compiler_params=pltpu.CompilerParams(vmem_limit_bytes=64 << 20),
        **keys,
    )


def body(
    water_depth, momentum, metric, face_scale, face_angle, face_map, rim_faces, wet_blocks, breach, block_plan
):
    blocks, members, node_cells = water_depth.shape
    elements = metric.shape[2]
    t = static_tables(members, elements)
    comp, pairs, used = t["comp"], t["pairs"], t["used"]
    f32, bf16 = jnp.float32, jnp.bfloat16
    tiles = blocks // 8
    depth_rows = water_depth.reshape(tiles, 8, members, pairs, LANES).transpose(2, 0, 3, 1, 4).reshape(-1, LANES)
    flow_rows = momentum.transpose(0, 2, 1, 3)
    faces = face_map.size
    width = rim_faces.shape[1] // 2
    dma = pltpu.SemaphoreType.DMA

    back = jnp.asarray(np.tile(t["back"], (2, 1)), bf16)
    eye = jnp.asarray(np.tile(np.eye(LANES), (1, 2)), bf16)
    fields, pool, head, tail = call(
        functools.partial(prepare_kernel, t=t, blocks=blocks, elements=elements),
        (
            jax.ShapeDtypeStruct((blocks, 3 * comp, LANES), f32),
            jax.ShapeDtypeStruct((faces, LANES), f32),
            jax.ShapeDtypeStruct((width, LANES), f32),
            jax.ShapeDtypeStruct((width, LANES), f32),
        ),
        0, 5,
        [
            pltpu.SMEM(rim_faces.shape, jnp.int32), pltpu.VMEM(depth_rows.shape, f32), pltpu.VMEM(flow_rows.shape, f32), pltpu.VMEM(back.shape, bf16),
            pltpu.VMEM(eye.shape, bf16),
            pltpu.VMEM((blocks, 3 * comp, LANES), f32), pltpu.VMEM((faces, LANES), f32),
            pltpu.VMEM((3 * LANES, 2 * LANES), bf16), dma((4 + tiles + blocks,)),
        ],
        (HBM, HBM, VMEM, VMEM),
    )(rim_faces, depth_rows, flow_rows, back, eye)

    count = lax.axis_size("mesh")
    before = lax.ppermute(tail, "mesh", [(i, i + 1) for i in range(count - 1)])
    after = lax.ppermute(head, "mesh", [(i + 1, i) for i in range(count - 1)])

    lift_h, lift_l = high_low(t["lift"])
    matrix = np.concatenate(
        [t["along"][0], t["along"][0], t["along"][1], t["along"][1], lift_h.astype(np.float32), lift_h.astype(np.float32)],
        axis=1,
    )
    mats = [
        jnp.asarray(np.tile(t["own"], (2, 1)), bf16), jnp.asarray(np.tile(t["spread"], (2, 1)), bf16),
        jnp.asarray(matrix, bf16), jnp.asarray(lift_l), eye,
    ]
    packed = round_up(3 * used, 8)

    def finish(leaving, out_shape, extra, n_sems):
        return call(
            functools.partial(
                finish_kernel, t=t, blocks=blocks, elements=elements, leaving=leaving, devices=count
            ),
            out_shape,
            0, 16,
            [
                pltpu.SMEM(block_plan.shape, jnp.int32), pltpu.SMEM(wet_blocks.shape, jnp.int32),
                pltpu.SMEM((members, blocks), jnp.int32), pltpu.VMEM(face_map.shape, jnp.int32),
                pltpu.VMEM(face_angle.shape, f32), pltpu.VMEM(face_scale.shape, f32), pltpu.VMEM(metric.shape, f32),
                pltpu.VMEM((blocks, 3 * comp, LANES), f32), pltpu.VMEM((faces + 2 * width, LANES), f32),
                *[pltpu.VMEM(m.shape, bf16) for m in mats],
                pltpu.SMEM((blocks,), jnp.int32), pltpu.SMEM((blocks,), jnp.int32),
                pltpu.VMEM((blocks * 16, LANES), f32),
                pltpu.VMEM((3, LANES, LANES), f32), pltpu.VMEM((3 * LANES, 2 * LANES), bf16),
                pltpu.VMEM((3, LANES, LANES), f32), pltpu.VMEM((LANES, 8 * LANES), f32),
                pltpu.VMEM((3 * LANES, LANES), f32), pltpu.VMEM((3, LANES, 6 * LANES), bf16),
                pltpu.SMEM((2, face_map.shape[1]), jnp.int32),
                *extra, dma((18 + n_sems,)),
            ],
            jax.tree.map(lambda _: HBM, out_shape),
        )(
            block_plan, wet_blocks, breach.T, face_map, face_angle, face_scale, metric, fields, pool, before, after,
            *mats,
        )

    sent = finish(
        True, jax.ShapeDtypeStruct((count, packed, LANES), f32), [pltpu.VMEM((blocks, packed, LANES), f32)], blocks
    )
    got = lax.all_to_all(sent, "mesh", split_axis=0, concat_axis=0, tiled=True)
    final = (jax.ShapeDtypeStruct(depth_rows.shape, f32), jax.ShapeDtypeStruct(flow_rows.shape, f32))
    whole = [pltpu.VMEM(depth_rows.shape, f32), pltpu.VMEM(flow_rows.shape, f32)]
    slots = LANES
    depth_kept, flow_kept, origin = finish(
        False, (*final, jax.ShapeDtypeStruct((slots,), jnp.int32)),
        [pltpu.VMEM((2, 3 * comp, LANES), f32), *whole, pltpu.SMEM((slots,), jnp.int32)], 3,
    )
    depth_new, flow_new = call(
        functools.partial(merge_kernel, t=t, blocks=blocks),
        final,
        0, 4,
        [pltpu.SMEM((slots,), jnp.int32), *whole, pltpu.VMEM((blocks, packed, LANES), f32), dma((2 * blocks + 2,))],
        (HBM, HBM),
        input_output_aliases={2: 0, 3: 1},
    )(origin, got, depth_kept, flow_kept)
    depth_out = depth_new.reshape(members, tiles, pairs, 8, LANES).transpose(1, 3, 0, 2, 4).reshape(water_depth.shape)
    return depth_out, flow_new.transpose(0, 2, 1, 3)


def solution(mesh):
    in_specs = (
        P(("groups", "mesh"), None, None),
        P(("groups", "mesh"), None, None, None),
        P(("groups", "mesh"), None, None),
        P(("groups", "mesh"), None),
        P(("groups", "mesh"), None),
        P(("groups", "mesh"), None),
        P(("groups", "mesh"), None),
        P(("groups", "mesh")),
        P(("groups", "mesh"), None),
        P("groups"),
    )
    out_specs = (P(("groups", "mesh"), None, None), P(("groups", "mesh"), None, None, None))
    return jax.shard_map(body, mesh=mesh, in_specs=in_specs, out_specs=out_specs, check_vma=False)
```

```python
import functools
import math

import jax
import jax.numpy as jnp
import numpy as np
from jax import lax
from jax.experimental import pallas as pl
from jax.experimental.pallas import tpu as pltpu
from jax.sharding import PartitionSpec as P

time_step = 0.01
gravity = 1.0
breach_rate = 5.0
LANES = 128


def gauss_solve(matrix, right):
    dimension = matrix.shape[0]
    augmented = np.concatenate([np.array(matrix) * 1.0, np.array(right) * 1.0], axis=1)
    for pivot_col in range(dimension):
        largest = pivot_col + int(np.argmax(np.abs(augmented[pivot_col:, pivot_col])))
        swapped = augmented[[largest, pivot_col]]
        augmented[[pivot_col, largest]] = swapped
        augmented[pivot_col] = augmented[pivot_col] / augmented[pivot_col, pivot_col]
        for row_id in range(dimension):
            if row_id != pivot_col:
                augmented[row_id] = (
                    augmented[row_id] - augmented[row_id, pivot_col] * augmented[pivot_col]
                )
    return augmented[:, dimension:]


def node_tables():
    points = np.array(
        [(across / 3.0, upward / 3.0) for upward in range(4) for across in range(4 - upward)]
    )
    powers = [(power_r, power_s) for power_r in range(4) for power_s in range(4 - power_r)]
    vander = np.zeros((10, 10))
    grad_r = np.zeros((10, 10))
    grad_s = np.zeros((10, 10))
    mono_mass = np.zeros((10, 10))
    for column, (power_r, power_s) in enumerate(powers):
        vander[:, column] = points[:, 0] ** power_r * points[:, 1] ** power_s
        if power_r > 0:
            grad_r[:, column] = power_r * points[:, 0] ** (power_r - 1) * points[:, 1] ** power_s
        if power_s > 0:
            grad_s[:, column] = power_s * points[:, 0] ** power_r * points[:, 1] ** (power_s - 1)
        for second_column, (other_r, other_s) in enumerate(powers):
            mono_mass[column, second_column] = (
                math.factorial(power_r + other_r)
                * math.factorial(power_s + other_s)
                / math.factorial(power_r + other_r + power_s + other_s + 2)
            )
    inverse = gauss_solve(vander, np.eye(10))
    mass_matrix = inverse.T @ mono_mass @ inverse
    line_points = np.arange(4) / 3.0
    line_vander = line_points[:, None] ** np.arange(4)[None, :]
    hilbert = 1.0 / (np.arange(4)[:, None] + np.arange(4)[None, :] + 1.0)
    line_inverse = gauss_solve(line_vander, np.eye(4))
    edge_mass = line_inverse.T @ hilbert @ line_inverse
    face_nodes = np.array([[0, 1, 2, 3], [3, 6, 8, 9], [9, 7, 4, 0]])
    edge_embed = np.zeros((10, 12))
    for face_id in range(3):
        for node_id in range(4):
            edge_embed[face_nodes[face_id, node_id], 4 * face_id : 4 * face_id + 4] += edge_mass[
                node_id
            ]
    lifting = gauss_solve(mass_matrix, edge_embed).reshape(10, 3, 4)
    return (
        np.asarray(grad_r @ inverse, np.float32),
        np.asarray(grad_s @ inverse, np.float32),
        np.asarray(lifting, np.float32),
        face_nodes.reshape(-1),
    )


def round_up(value, step):
    return (value + step - 1) // step * step


def static_tables(members, elements):
    deriv_r, deriv_s, lifting, face_order = node_tables()
    nodes = deriv_r.shape[0]
    pairs = nodes // 2
    used = members * pairs
    comp = round_up(used, 8)
    face_nodes = face_order.reshape(3, 4)
    wide = members * 4

    def lane_of(s, n):
        return (n % 2) * comp + s * pairs + n // 2

    own = np.zeros((LANES, LANES), np.float32)
    own[2 * comp, 3 * wide :] = 1.0
    back = np.zeros((LANES, LANES), np.float32)
    lift = np.zeros((2 * comp, LANES), np.float32)
    along = np.zeros((2, 2 * comp, LANES), np.float32)
    for s in range(members):
        for f in range(3):
            for k in range(4):
                n = int(face_nodes[f, k])
                own[lane_of(s, n), f * wide + s * 4 + k] = 1.0
                back[lane_of(s, n), f * wide + s * 4 + 3 - k] = 1.0
        for n in range(nodes):
            for f in range(3):
                for k in range(4):
                    lift[lane_of(s, n), f * wide + s * 4 + k] = lifting[n, f, k]
            for m in range(nodes):
                along[0, lane_of(s, n), lane_of(s, m)] = -deriv_r[n, m]
                along[1, lane_of(s, n), lane_of(s, m)] = -deriv_s[n, m]
            along[0, lane_of(s, n), 2 * comp + s] = breach_rate
    spread = np.zeros((16, 8 * LANES), np.float32)
    for q in range(4):
        for f in range(3):
            spread[3 * q + f, q * LANES + f * wide : q * LANES + (f + 1) * wide] = 1.0
        spread[12 + q, (4 + q) * LANES : (4 + q) * LANES + 2 * comp] = 1.0
    return dict(
        own=own, back=back, lift=lift, along=along, spread=spread,
        comp=comp, pairs=pairs, used=used, wide=wide, nodes=nodes, members=members,
    )


def high_low(matrix):
    high = matrix.astype(jnp.bfloat16)
    low = (matrix - high.astype(np.float32)).astype(jnp.bfloat16)
    return high, low


def mm(a, b, dims=((1,), (0,))):
    return lax.dot_general(a, b, (dims, ((), ())), preferred_element_type=jnp.float32)


def split(x):
    high = x.astype(jnp.bfloat16)
    return high, (x - high.astype(jnp.float32)).astype(jnp.bfloat16)


def swap_halves(x):
    return pltpu.roll(x, LANES // 2, 1)


def turn(x, eye):
    return mm(eye[...], jnp.concatenate(split(x), axis=1), ((1,), (1,)))


def turn_pair(fields, first, second, eye, turned, halves, comp):
    lower = lax.broadcasted_iota(jnp.int32, (comp, LANES), 1) < LANES // 2
    for c in range(3):
        a = fields[first, c * comp : (c + 1) * comp]
        b = fields[second, c * comp : (c + 1) * comp]
        even = jnp.where(lower, a, swap_halves(b))
        odd = jnp.where(lower, swap_halves(a), b)
        fill = jnp.full((LANES - 2 * comp, LANES), 1.0 if c == 0 else 0.0, jnp.float32)
        flat = turn(jnp.concatenate([even, odd, fill], axis=0), eye)
        if turned is not None:
            turned[c] = flat
        high, low = split(flat)
        halves[c * LANES : (c + 1) * LANES, :LANES] = high
        halves[c * LANES : (c + 1) * LANES, LANES:] = low


def place_face(pieces, c, wide, lane):
    moved = [pltpu.roll(p, ((i - c) * wide) % LANES, 1) if i != c else p for i, p in enumerate(pieces)]
    return jnp.where(lane < wide, moved[0], jnp.where(lane < 2 * wide, moved[1], moved[2]))


def root(x):
    return x * lax.rsqrt(x)


def start_all(copies):
    for copy in copies:
        copy.start()
    return copies


def wait_all(copies):
    for copy in copies:
        copy.wait()


def prepare_kernel(
    rim_in, depth_in, flow_in, back_in, eye_in, fields_out, pool_out, head, tail,
    rim, depth, flow, back, eye, fields, pool, halves, sems, *, t, blocks, elements,
):
    comp, pairs, members, wide = t["comp"], t["pairs"], t["members"], t["wide"]
    tiles = blocks // 8
    steps = blocks // 2
    group = 2 * 3 * elements
    first = start_all(
        [
            pltpu.make_async_copy(depth_in, depth, sems.at[0]), pltpu.make_async_copy(back_in, back, sems.at[1]),
            pltpu.make_async_copy(eye_in, eye, sems.at[2]),
            pltpu.make_async_copy(rim_in, rim, sems.at[3 + tiles + 2 * steps]),
        ]
    )

    def part(tile):
        rows = pl.ds(8 * tile, 8)
        return pltpu.make_async_copy(flow_in.at[rows], flow.at[rows], sems.at[3 + tile])

    def outward(i):
        rows, lines = pl.ds(2 * i, 2), pl.ds(group * i, group)
        return [
            pltpu.make_async_copy(fields.at[rows], fields_out.at[rows], sems.at[3 + tiles + i]),
            pltpu.make_async_copy(pool.at[lines], pool_out.at[lines], sems.at[3 + tiles + steps + i]),
        ]

    start_all([part(tile) for tile in range(tiles)])
    wait_all(first)

    def build(i):
        for u in range(2):
            b = 2 * i + u
            tile, sub = b // 8, b % 8
            for c in range(3):
                end = comp * (c + 1)
                fields[b, end - 8 : end] = jnp.full((8, LANES), 1.0 if c == 0 else 0.0, jnp.float32)
            for s in range(members):
                start = (s * tiles + tile) * pairs * 8 + sub
                fields[b, s * pairs : (s + 1) * pairs] = depth[pl.ds(start, pairs, stride=8), :]
                for j in range(pairs):
                    two = flow[b, s, :, j * LANES : (j + 1) * LANES]
                    row = s * pairs + j
                    fields[b, comp + row : comp + row + 1] = two[0:1]
                    fields[b, 2 * comp + row : 2 * comp + row + 1] = two[1:2]

    def turn_of(i):
        turn_pair(fields, 2 * i, 2 * i + 1, eye, None, halves, comp)

    def faces_of(i):
        rows = mm(halves[...], back[...])
        lane = lax.broadcasted_iota(jnp.int32, (LANES, LANES), 1)
        pieces = [rows[c * LANES : (c + 1) * LANES] for c in range(3)]
        for f in range(3):
            face = place_face(pieces, f, wide, lane)
            for u in range(2):
                at = ((2 * i + u) * 3 + f) * elements
                pool[pl.ds(at, elements), :] = face[u * elements : (u + 1) * elements]

    part(0).wait()
    build(0)
    turn_of(0)
    build(1)

    def one(i, carry):
        @pl.when(i % 4 == 0)
        def _():
            part(i // 4).wait()

        faces_of(i - 2)
        turn_of(i - 1)
        build(i)
        start_all(outward(i - 2))
        return carry

    lax.fori_loop(2, steps, one, 0)
    faces_of(steps - 2)
    turn_of(steps - 1)
    start_all(outward(steps - 2))
    faces_of(steps - 1)
    start_all(outward(steps - 1))
    width = head.shape[0]

    def pick(i, carry):
        for u in range(16):
            r = i * 16 + u
            head[pl.ds(r, 1), :] = pool[pl.ds(rim[0, r], 1), :]
            tail[pl.ds(r, 1), :] = pool[pl.ds(rim[0, width + r], 1), :]
        return carry

    lax.fori_loop(0, width // 16, pick, 0)

    def drain(i, carry):
        wait_all(outward(i))
        return carry

    lax.fori_loop(0, steps, drain, 0)


def scan_moves(plan, base, order, place, blocks):
    def one(i, carry):
        leaving, staying = carry
        slot = plan[base + i]
        away = jnp.logical_or(slot < base, slot >= base + blocks).astype(jnp.int32)
        order[jnp.where(away == 1, leaving, blocks - 1 - staying)] = i
        place[i] = lax.div(slot, jnp.int32(blocks))
        return leaving + away, staying + 1 - away

    return lax.fori_loop(0, blocks, one, (jnp.int32(0), jnp.int32(0)))[0]


def scan_origins(plan, own, origin, blocks, devices):
    def device(d, carry):
        mark = jnp.where(d == own, -1, d)
        for i in range(blocks):
            slot = plan[d * blocks + i] - own * blocks
            origin[jnp.where(jnp.logical_and(slot >= 0, slot < blocks), slot, blocks)] = mark
        return carry

    lax.fori_loop(0, devices, device, 0)


def face_rows(angle, scale, links, metric, coefs, blocks, elements):
    shape = (blocks, 3 * elements)
    own = lax.broadcasted_iota(jnp.int32, shape, 0) * (3 * elements) + lax.broadcasted_iota(jnp.int32, shape, 1)
    free = jnp.where(links[...] == own, 0.0, 1.0)
    lower = lax.broadcasted_iota(jnp.int32, (blocks, LANES), 1) < elements
    for q, value in enumerate((jnp.cos(angle[...]), jnp.sin(angle[...]), scale[...], free)):
        two = value[:, :LANES]
        swapped = swap_halves(two)
        third = value[:, LANES:]
        faces = (
            jnp.where(lower, two, swapped), jnp.where(lower, swapped, two), jnp.concatenate([third, third], axis=1)
        )
        for f in range(3):
            coefs[pl.ds(3 * q + f, blocks, stride=16), :] = faces[f]
    for b in range(blocks):
        factors = metric[b]
        coefs[b * 16 + 12 : b * 16 + 16] = jnp.concatenate([factors, factors], axis=1)


def spread_pair(coefs, both, eye, spread, factors, elements):
    lower = lax.broadcasted_iota(jnp.int32, (16, LANES), 1) < elements
    values = jnp.where(lower, coefs[pl.ds(both[0] * 16, 16), :], coefs[pl.ds(both[1] * 16, 16), :])
    rough = values.astype(jnp.bfloat16).astype(jnp.float32)
    stacked = jnp.concatenate([rough, values - rough], axis=0).astype(jnp.bfloat16)
    stacked = mm(eye[:, :LANES], stacked, ((1,), (1,))).astype(jnp.bfloat16)
    factors[...] = mm(stacked, spread[...])


def inflow_rows(breach, both, t):
    rows = []
    for b in both:
        row = jnp.zeros((1, LANES), jnp.float32)
        for s in range(t["members"]):
            level = breach[s, b].astype(jnp.float32)
            row = jnp.where(lax.broadcasted_iota(jnp.int32, (1, LANES), 1) == 2 * t["comp"] + s, level, row)
        rows.append(row)
    return rows


def volume_rows(rows, turned, factors, first, inflow, pieces):
    rx, sx, ry, sy = (factors[rows, q * LANES : (q + 1) * LANES] for q in range(first, first + 4))
    height, flow_x, flow_y = (turned[c, rows] for c in range(3))
    pressure = 0.5 * gravity * height * height
    inverse = 1.0 / height
    speed_x = flow_x * inverse
    speed_y = flow_y * inverse
    cross = flow_y * speed_x
    flux_f = (flow_x, flow_x * speed_x + pressure, cross)
    flux_g = (flow_y, cross, flow_y * speed_y + pressure)
    for c in range(3):
        along_r = rx * flux_f[c] + ry * flux_g[c]
        along_s = sx * flux_f[c] + sy * flux_g[c]
        if c == 0:
            along_r = along_r + inflow
        pieces[c, rows, 0:LANES], pieces[c, rows, LANES : 2 * LANES] = split(along_r)
        pieces[c, rows, 2 * LANES : 3 * LANES], pieces[c, rows, 3 * LANES : 4 * LANES] = split(along_s)


def flux_rows(rows, traces, outer, factors, pieces, first, wide):
    lane = lax.broadcasted_iota(jnp.int32, (rows.stop - rows.start, LANES), 1)
    n_x, n_y, scale, free = (factors[rows, q * LANES : (q + 1) * LANES] for q in range(4))
    theirs = [outer[f * LANES + rows.start : f * LANES + rows.stop] for f in range(3)]
    height, flow_x, flow_y = (traces[c, rows] for c in range(3))
    is_wall = free < 0.5
    through = flow_x * n_x + flow_y * n_y
    twice = through + through
    height_o = jnp.where(is_wall, height, place_face(theirs, 0, wide, lane))
    flow_xo = jnp.where(is_wall, flow_x - twice * n_x, place_face(theirs, 1, wide, lane))
    flow_yo = jnp.where(is_wall, flow_y - twice * n_y, place_face(theirs, 2, wide, lane))
    speed = through / height
    speed_o = (flow_xo * n_x + flow_yo * n_y) / height_o
    fast = jnp.maximum(
        jnp.abs(speed) + root(gravity * height), jnp.abs(speed_o) + root(gravity * height_o)
    )
    ours, others = speed - fast, speed_o - fast
    half = 0.5 * scale
    push = 0.5 * gravity * (height * height - height_o * height_o)
    jumps = (
        half * (height * ours - height_o * others),
        half * (flow_x * ours - flow_xo * others + push * n_x),
        half * (flow_y * ours - flow_yo * others + push * n_y),
    )
    for c in range(3):
        pieces[c, rows, first : first + LANES], pieces[c, rows, first + LANES : first + 2 * LANES] = split(jumps[c])


def lift_mm(lift, low, pieces, c, first):
    last = ((1,), (1,))
    return mm(lift, pieces[c, :, : first + 2 * LANES], last) + mm(low[...], pieces[c, :, first : first + LANES], last)


def pair_gains(tall, comp, elements):
    narrow = lax.broadcasted_iota(jnp.int32, (comp, LANES), 1) < elements
    even, odd = tall[:comp], tall[comp:]
    return jnp.where(narrow, even, swap_halves(odd)), jnp.where(narrow, swap_halves(even), odd)


def gather_pair(near, pool, outer, elements):
    for u in range(2):
        for f in range(3):
            for e in range(elements):
                row = f * LANES + u * elements + e
                outer[row : row + 1, :] = pool[pl.ds(near[u, f * elements + e], 1), :]


def row_chunks(step):
    return [slice(i * step, (i + 1) * step) for i in range(LANES // step)]


def volume_kernel(
    plan_in, wet_in, breach_in, links_in, angle_in, scale_in, metric_in, fields_in, own_in, spread_in, matrix_in,
    eye_in, base_out, traces_out, coefs_out, near_out, facts_out,
    plan, wet, breach, links, angle, scale, metric, own, spread, matrix, eye,
    order, facts, coefs, fields, turned, halves, traces, factors, pieces, base, sems, *, t, blocks, elements,
):
    comp = t["comp"]
    loads = [
        (plan_in, plan), (angle_in, angle), (scale_in, scale), (links_in, links), (metric_in, metric),
        (wet_in, wet), (breach_in, breach), (eye_in, eye), (own_in, own), (spread_in, spread), (matrix_in, matrix),
    ]
    n = len(loads)
    loads = start_all([pltpu.make_async_copy(a, b, sems.at[i]) for i, (a, b) in enumerate(loads)])
    index = lax.axis_index("mesh")
    loads[0].wait()
    loads[5].wait()
    end = scan_moves(plan, index * blocks, order, facts, blocks)

    def fetch(p):
        return pltpu.make_async_copy(fields_in.at[order[p]], fields.at[p], sems.at[n + p])

    def relay(p):
        return pltpu.make_async_copy(
            links_in.at[order[jnp.minimum(p, end - 1)]], near_out.at[p], sems.at[n + blocks + p]
        )

    def keep(p):
        return pltpu.make_async_copy(base.at[p], base_out.at[p], sems.at[n + 2 * blocks + p])

    def hold(i):
        return pltpu.make_async_copy(traces.at[i], traces_out.at[i], sems.at[n + 3 * blocks + i])

    def each(stop, act):
        def one(p, carry):
            act(p)
            return carry

        lax.fori_loop(0, stop, one, 0)

    steps = (end + 1) // 2
    each(end, lambda p: fetch(p).start())
    each(2 * steps, lambda p: relay(p).start())
    wait_all(loads[1:5])
    face_rows(angle, scale, links, metric, coefs, blocks, elements)

    def describe(p):
        facts[2 * blocks + p] = wet[order[p]]
        facts[3 * blocks + p] = facts[order[p]]

    facts[4 * blocks] = end
    each(end, describe)
    extra = start_all(
        [
            pltpu.make_async_copy(facts, facts_out, sems.at[n + 4 * blocks]),
        ]
    )
    wait_all(loads[6:])

    def one(i, carry):
        at = (2 * i, jnp.minimum(2 * i + 1, end - 1))
        both = (order[at[0]], order[at[1]])
        fetch(at[0]).wait()

        @pl.when(2 * i + 1 < end)
        def _():
            fetch(at[1]).wait()

        turn_pair(fields, at[0], at[1], eye, turned, halves, comp)
        inner = mm(halves[...], own[...])
        for c in range(3):
            traces[i, c] = inner[c * LANES : (c + 1) * LANES]
        lower = lax.broadcasted_iota(jnp.int32, (16, LANES), 1) < elements
        values = jnp.where(lower, coefs[pl.ds(both[0] * 16, 16), :], coefs[pl.ds(both[1] * 16, 16), :])
        coefs_pair = pl.ds(blocks * 16 + i * 16, 16)
        coefs[coefs_pair, :] = values
        spread_pair(coefs, both, eye, spread, factors, elements)
        inflow = inflow_rows(breach, both, t)
        for rows in row_chunks(16):
            volume_rows(rows, turned, factors, 0, inflow[rows.start // elements], pieces)
        for c in range(3):
            gains = pair_gains(mm(matrix[...], pieces[c], ((1,), (1,))), comp, elements)
            for u in range(2):
                rate = time_step * wet[both[u]].astype(jnp.float32)
                span = slice(c * comp, (c + 1) * comp)
                base[at[u], span] = fields[at[u], span] + rate * gains[u]
        hold(i).start()
        keep(at[0]).start()

        @pl.when(2 * i + 1 < end)
        def _():
            keep(at[1]).start()

        return carry

    lax.fori_loop(0, steps, one, 0)
    spare = pltpu.make_async_copy(
        coefs.at[pl.ds(blocks * 16, blocks * 8)], coefs_out, sems.at[n + 4 * blocks + 1]
    )
    spare.start()

    each(end, lambda p: keep(p).wait())
    each(2 * steps, lambda p: relay(p).wait())
    each(steps, lambda i: hold(i).wait())
    wait_all(extra)
    spare.wait()


def face_kernel(
    facts_in, near_in, pool_in, before_in, after_in, base_in, traces_in, coefs_in, spread_in, matrix_in, low_in, eye_in,
    sent, facts, near, pool, base, traces, coefs, spread, matrix, low, eye, factors, outer, pieces, staged, sems,
    *, t, blocks, elements,
):
    comp, wide, used = t["comp"], t["wide"], t["used"]
    faces = blocks * 3 * elements
    width = before_in.shape[0]
    loads = [
        (facts_in, facts), (near_in.at[pl.ds(0, 2)], near), (coefs_in, coefs), (eye_in, eye), (spread_in, spread),
        (pool_in, pool.at[pl.ds(0, faces)]), (before_in, pool.at[pl.ds(faces, width)]),
        (after_in, pool.at[pl.ds(faces + width, width)]), (matrix_in, matrix), (low_in, low),
    ]
    n = len(loads)
    loads = start_all([pltpu.make_async_copy(a, b, sems.at[i]) for i, (a, b) in enumerate(loads)])
    loads[0].wait()
    end = facts[4 * blocks]
    steps = (end + 1) // 2

    def indices(i):
        return pltpu.make_async_copy(near_in.at[pl.ds(2 * i, 2)], near, sems.at[1])

    def get_base(p):
        return pltpu.make_async_copy(base_in.at[p], base.at[p], sems.at[n + p])

    def get_traces(i):
        return pltpu.make_async_copy(traces_in.at[i], traces.at[i], sems.at[n + blocks + i])

    def send(p):
        return pltpu.make_async_copy(
            staged.at[p], sent.at[facts[3 * blocks + p]], sems.at[n + 2 * blocks + p]
        )

    def each(stop, act):
        def one(p, carry):
            act(p)
            return carry

        lax.fori_loop(0, stop, one, 0)

    each(steps, lambda i: get_traces(i).start())
    each(end, lambda p: get_base(p).start())
    wait_all(loads[1:])

    def one(i, carry):
        at = (2 * i, jnp.minimum(2 * i + 1, end - 1))

        @pl.when(i > 0)
        def _():
            indices(i).wait()

        get_traces(i).wait()
        get_base(at[0]).wait()

        @pl.when(2 * i + 1 < end)
        def _():
            get_base(at[1]).wait()

        gather_pair(near, pool, outer, elements)

        @pl.when(i + 1 < steps)
        def _():
            indices(i + 1).start()

        spread_pair(coefs, (i, i), eye, spread, factors, elements)
        for rows in row_chunks(16):
            flux_rows(rows, traces.at[i], outer, factors, pieces, 0, wide)
        for c in range(3):
            gains = pair_gains(lift_mm(matrix[...], low, pieces, c, 0), comp, elements)
            for u in range(2):
                rate = time_step * facts[2 * blocks + at[u]].astype(jnp.float32)
                done = base[at[u], c * comp : (c + 1) * comp] + rate * gains[u]
                staged[at[u], c * used : (c + 1) * used] = done[:used]
        send(at[0]).start()

        @pl.when(2 * i + 1 < end)
        def _():
            send(at[1]).start()

        return carry

    lax.fori_loop(0, steps, one, 0)
    each(end, lambda p: send(p).wait())


def finish_kernel(
    plan_in, wet_in, breach_in, links_in, angle_in, scale_in, metric_in,
    fields_in, pool_in, before_in, after_in, own_in, spread_in, matrix_in, low_in, eye_in,
    depth_out, flow_out, origin_out,
    plan, wet, breach, links, angle, scale, metric, fields, pool, own, spread, matrix, low, eye,
    order, place, coefs, turned, halves, traces, factors, outer, pieces, near, staged, depth, flow, origin, sems,
    *, t, blocks, elements, devices,
):
    comp, wide = t["comp"], t["wide"]
    faces = blocks * 3 * elements
    width = before_in.shape[0]
    loads = [
        (plan_in, plan), (angle_in, angle), (scale_in, scale), (links_in, links), (metric_in, metric),
        (wet_in, wet), (breach_in, breach), (eye_in, eye), (own_in, own), (fields_in, fields),
        (pool_in, pool.at[pl.ds(0, faces)]), (before_in, pool.at[pl.ds(faces, width)]),
        (after_in, pool.at[pl.ds(faces + width, width)]), (spread_in, spread), (matrix_in, matrix), (low_in, low),
    ]
    n = len(loads)
    loads = start_all([pltpu.make_async_copy(a, b, sems.at[i]) for i, (a, b) in enumerate(loads)])
    index = lax.axis_index("mesh")
    loads[0].wait()
    begin = scan_moves(plan, index * blocks, order, place, blocks)
    end = blocks

    def indices(i):
        at = (begin + 2 * i, jnp.minimum(begin + 2 * i + 1, end - 1))
        return [pltpu.make_async_copy(links_in.at[order[at[u]]], near.at[u], sems.at[n + u]) for u in range(2)]

    steps = (end - begin + 1) // 2

    @pl.when(steps > 0)
    def _():
        start_all(indices(0))

    wait_all(loads[1:5])
    face_rows(angle, scale, links, metric, coefs, blocks, elements)
    scan_origins(plan, index, origin, blocks, devices)
    wait_all(loads[5:])

    def one(i, carry):
        both = (order[begin + 2 * i], order[jnp.minimum(begin + 2 * i + 1, end - 1)])
        wait_all(indices(i))
        gather_pair(near, pool, outer, elements)

        @pl.when(i + 1 < steps)
        def _():
            start_all(indices(i + 1))

        turn_pair(fields, both[0], both[1], eye, turned, halves, comp)
        inner = mm(halves[...], own[...])
        for c in range(3):
            traces[c] = inner[c * LANES : (c + 1) * LANES]
        spread_pair(coefs, both, eye, spread, factors, elements)
        inflow = inflow_rows(breach, both, t)
        for rows in row_chunks(16):
            volume_rows(rows, turned, factors, 4, inflow[rows.start // elements], pieces)
            flux_rows(rows, traces, outer, factors, pieces, 4 * LANES, wide)
        for c in range(3):
            gains = pair_gains(lift_mm(matrix[...], low, pieces, c, 4 * LANES), comp, elements)
            for u in range(2):
                span = slice(c * comp, (c + 1) * comp)
                rate = time_step * wet[both[u]].astype(jnp.float32)
                staged[u, span] = fields[both[u], span] + rate * gains[u]
        for u in range(2):
            write_block(both[u], staged.at[u], comp, depth, flow, t, blocks)
        return carry

    lax.fori_loop(0, steps, one, 0)
    kept = ((depth, depth_out), (flow, flow_out), (origin.at[pl.ds(0, origin_out.shape[0])], origin_out))
    wait_all(start_all([pltpu.make_async_copy(a, b, sems.at[n + i]) for i, (a, b) in enumerate(kept)]))


def write_block(b, rows, step, depth, flow, t, blocks):
    pairs, members = t["pairs"], t["members"]
    tile, sub = b // 8, b % 8
    for s in range(members):
        start = (s * (blocks // 8) + tile) * pairs * 8 + sub
        depth[pl.ds(start, pairs, stride=8), :] = rows[s * pairs : (s + 1) * pairs]
        for j in range(pairs):
            row = s * pairs + j
            flow[b, s, 0:1, j * LANES : (j + 1) * LANES] = rows[step + row : step + row + 1]
            flow[b, s, 1:2, j * LANES : (j + 1) * LANES] = rows[2 * step + row : 2 * step + row + 1]


def merge_kernel(
    origin_in, got, depth_in, flow_in, depth_out, flow_out, origin, depth, flow, came, sems, *, t, blocks
):
    def arrival(b):
        return pltpu.make_async_copy(got.at[origin[b]], came.at[b], sems.at[b])

    def leave(b):
        return pltpu.make_async_copy(flow.at[b], flow_out.at[b], sems.at[blocks + b])

    whole = pltpu.make_async_copy(depth_in, depth, sems.at[2 * blocks])
    first = pltpu.make_async_copy(origin_in, origin, sems.at[2 * blocks + 1])
    first.start()
    whole.start()
    first.wait()

    def each(act):
        def one(b, carry):
            @pl.when(origin[b] >= 0)
            def _():
                act(b)

            return carry

        lax.fori_loop(0, blocks, one, 0)

    each(lambda b: arrival(b).start())
    whole.wait()

    def put(b):
        arrival(b).wait()
        write_block(b, came.at[b], t["used"], depth, flow, t, blocks)
        leave(b).start()

    each(put)
    back = pltpu.make_async_copy(depth, depth_out, sems.at[2 * blocks])
    back.start()
    each(lambda b: leave(b).wait())
    back.wait()


SMEM = pl.BlockSpec(memory_space=pltpu.SMEM)
HBM = pl.BlockSpec(memory_space=pltpu.HBM)
VMEM = pl.BlockSpec(memory_space=pltpu.VMEM)


def call(kernel, out_shape, n_smem, n_args, scratch, out_specs, **keys):
    return pl.pallas_call(
        kernel,
        out_shape=out_shape,
        in_specs=[SMEM] * n_smem + [HBM] * n_args,
        out_specs=out_specs,
        scratch_shapes=scratch,
        compiler_params=pltpu.CompilerParams(vmem_limit_bytes=64 << 20),
        **keys,
    )


def body(
    water_depth, momentum, metric, face_scale, face_angle, face_map, rim_faces, wet_blocks, breach, block_plan
):
    blocks, members, node_cells = water_depth.shape
    elements = metric.shape[2]
    t = static_tables(members, elements)
    comp, pairs, used = t["comp"], t["pairs"], t["used"]
    f32, bf16 = jnp.float32, jnp.bfloat16
    tiles = blocks // 8
    depth_rows = water_depth.reshape(tiles, 8, members, pairs, LANES).transpose(2, 0, 3, 1, 4).reshape(-1, LANES)
    flow_rows = momentum.transpose(0, 2, 1, 3)
    faces = face_map.size
    width = rim_faces.shape[1] // 2
    dma = pltpu.SemaphoreType.DMA

    back = jnp.asarray(np.tile(t["back"], (2, 1)), bf16)
    eye = jnp.asarray(np.tile(np.eye(LANES), (1, 2)), bf16)
    fields, pool, head, tail = call(
        functools.partial(prepare_kernel, t=t, blocks=blocks, elements=elements),
        (
            jax.ShapeDtypeStruct((blocks, 3 * comp, LANES), f32),
            jax.ShapeDtypeStruct((faces, LANES), f32),
            jax.ShapeDtypeStruct((width, LANES), f32),
            jax.ShapeDtypeStruct((width, LANES), f32),
        ),
        0, 5,
        [
            pltpu.SMEM(rim_faces.shape, jnp.int32), pltpu.VMEM(depth_rows.shape, f32), pltpu.VMEM(flow_rows.shape, f32), pltpu.VMEM(back.shape, bf16),
            pltpu.VMEM(eye.shape, bf16),
            pltpu.VMEM((blocks, 3 * comp, LANES), f32), pltpu.VMEM((faces, LANES), f32),
            pltpu.VMEM((3 * LANES, 2 * LANES), bf16), dma((4 + tiles + blocks,)),
        ],
        (HBM, HBM, VMEM, VMEM),
    )(rim_faces, depth_rows, flow_rows, back, eye)

    count = lax.axis_size("mesh")
    before = lax.ppermute(tail, "mesh", [(i, i + 1) for i in range(count - 1)])
    after = lax.ppermute(head, "mesh", [(i + 1, i) for i in range(count - 1)])

    lift_h, lift_l = high_low(t["lift"])
    matrix = np.concatenate(
        [t["along"][0], t["along"][0], t["along"][1], t["along"][1], lift_h.astype(np.float32), lift_h.astype(np.float32)],
        axis=1,
    )
    mats = [
        jnp.asarray(np.tile(t["own"], (2, 1)), bf16), jnp.asarray(np.tile(t["spread"], (2, 1)), bf16),
        jnp.asarray(matrix, bf16), jnp.asarray(lift_l), eye,
    ]
    packed = round_up(3 * used, 8)

    own_mat, spread_mat, full_mat, low_mat = mats[:4]
    face_cols, volume_cols = spread_mat[:, : 4 * LANES], spread_mat[:, 4 * LANES :]
    volume_mat, lift_mat = full_mat[:, : 4 * LANES], full_mat[:, 4 * LANES :]
    i32 = jnp.int32
    tables = [
        pltpu.SMEM(block_plan.shape, i32), pltpu.SMEM(wet_blocks.shape, i32), pltpu.SMEM((members, blocks), i32),
        pltpu.VMEM(face_map.shape, i32), pltpu.VMEM(face_angle.shape, f32), pltpu.VMEM(face_scale.shape, f32),
        pltpu.VMEM(metric.shape, f32),
    ]
    rows_of = (3 * comp, LANES)
    base, traces, coefs, near, facts = call(
        functools.partial(volume_kernel, t=t, blocks=blocks, elements=elements),
        (
            jax.ShapeDtypeStruct((blocks, *rows_of), f32),
            jax.ShapeDtypeStruct((blocks // 2, 3, LANES, LANES), f32),
            jax.ShapeDtypeStruct((blocks * 8, LANES), f32),
            jax.ShapeDtypeStruct(face_map.shape, i32),
            jax.ShapeDtypeStruct((LANES,), i32),
        ),
        0, 12,
        [
            *tables, pltpu.VMEM(own_mat.shape, bf16), pltpu.VMEM(volume_cols.shape, bf16),
            pltpu.VMEM(volume_mat.shape, bf16), pltpu.VMEM(eye.shape, bf16),
            pltpu.SMEM((blocks,), i32), pltpu.SMEM((LANES,), i32), pltpu.VMEM((blocks * 24, LANES), f32),
            pltpu.VMEM((blocks, *rows_of), f32), pltpu.VMEM((3, LANES, LANES), f32),
            pltpu.VMEM((3 * LANES, 2 * LANES), bf16), pltpu.VMEM((blocks // 2, 3, LANES, LANES), f32),
            pltpu.VMEM((LANES, 4 * LANES), f32), pltpu.VMEM((3, LANES, 4 * LANES), bf16),
            pltpu.VMEM((blocks, *rows_of), f32), dma((11 + 5 * blocks,)),
        ],
        (HBM,) * 5,
    )(
        block_plan, wet_blocks, breach.T, face_map, face_angle, face_scale, metric, fields,
        own_mat, volume_cols, volume_mat, eye,
    )
    sent = call(
        functools.partial(face_kernel, t=t, blocks=blocks, elements=elements),
        jax.ShapeDtypeStruct((count, packed, LANES), f32),
        0, 12,
        [
            pltpu.SMEM((LANES,), i32), pltpu.SMEM((2, face_map.shape[1]), i32),
            pltpu.VMEM((faces + 2 * width, LANES), f32), pltpu.VMEM((blocks, *rows_of), f32),
            pltpu.VMEM((blocks // 2, 3, LANES, LANES), f32), pltpu.VMEM((blocks * 8, LANES), f32),
            pltpu.VMEM(face_cols.shape, bf16), pltpu.VMEM(lift_mat.shape, bf16), pltpu.VMEM(low_mat.shape, bf16),
            pltpu.VMEM(eye.shape, bf16), pltpu.VMEM((LANES, 4 * LANES), f32), pltpu.VMEM((3 * LANES, LANES), f32),
            pltpu.VMEM((3, LANES, 2 * LANES), bf16), pltpu.VMEM((blocks, packed, LANES), f32),
            dma((10 + 3 * blocks,)),
        ],
        HBM,
    )(facts, near, pool, before, after, base, traces, coefs, face_cols, lift_mat, low_mat, eye)
    got = lax.all_to_all(sent, "mesh", split_axis=0, concat_axis=0, tiled=True)
    final = (jax.ShapeDtypeStruct(depth_rows.shape, f32), jax.ShapeDtypeStruct(flow_rows.shape, f32))
    whole = [pltpu.VMEM(depth_rows.shape, f32), pltpu.VMEM(flow_rows.shape, f32)]
    slots = LANES
    depth_kept, flow_kept, origin = call(
        functools.partial(finish_kernel, t=t, blocks=blocks, elements=elements, devices=count),
        (*final, jax.ShapeDtypeStruct((slots,), i32)),
        0, 16,
        [
            *tables, pltpu.VMEM((blocks, *rows_of), f32), pltpu.VMEM((faces + 2 * width, LANES), f32),
            *[pltpu.VMEM(m.shape, bf16) for m in mats],
            pltpu.SMEM((blocks,), i32), pltpu.SMEM((blocks,), i32),
            pltpu.VMEM((blocks * 16, LANES), f32),
            pltpu.VMEM((3, LANES, LANES), f32), pltpu.VMEM((3 * LANES, 2 * LANES), bf16),
            pltpu.VMEM((3, LANES, LANES), f32), pltpu.VMEM((LANES, 8 * LANES), f32),
            pltpu.VMEM((3 * LANES, LANES), f32), pltpu.VMEM((3, LANES, 6 * LANES), bf16),
            pltpu.SMEM((2, face_map.shape[1]), i32),
            pltpu.VMEM((2, *rows_of), f32), *whole, pltpu.SMEM((slots,), i32), dma((19,)),
        ],
        (HBM,) * 3,
    )(
        block_plan, wet_blocks, breach.T, face_map, face_angle, face_scale, metric, fields, pool, before, after,
        *mats,
    )
    depth_new, flow_new = call(
        functools.partial(merge_kernel, t=t, blocks=blocks),
        final,
        0, 4,
        [pltpu.SMEM((slots,), jnp.int32), *whole, pltpu.VMEM((blocks, packed, LANES), f32), dma((2 * blocks + 2,))],
        (HBM, HBM),
        input_output_aliases={2: 0, 3: 1},
    )(origin, got, depth_kept, flow_kept)
    depth_out = depth_new.reshape(members, tiles, pairs, 8, LANES).transpose(1, 3, 0, 2, 4).reshape(water_depth.shape)
    return depth_out, flow_new.transpose(0, 2, 1, 3)


def solution(mesh):
    in_specs = (
        P(("groups", "mesh"), None, None),
        P(("groups", "mesh"), None, None, None),
        P(("groups", "mesh"), None, None),
        P(("groups", "mesh"), None),
        P(("groups", "mesh"), None),
        P(("groups", "mesh"), None),
        P(("groups", "mesh"), None),
        P(("groups", "mesh")),
        P(("groups", "mesh"), None),
        P("groups"),
    )
    out_specs = (P(("groups", "mesh"), None, None), P(("groups", "mesh"), None, None, None))
    return jax.shard_map(body, mesh=mesh, in_specs=in_specs, out_specs=out_specs, check_vma=False)
```

```python
import functools
import math

import jax
import jax.numpy as jnp
import numpy as np
from jax import lax
from jax.experimental import pallas as pl
from jax.experimental.pallas import tpu as pltpu
from jax.sharding import PartitionSpec as P

time_step = 0.01
gravity = 1.0
breach_rate = 5.0
LANES = 128


def gauss_solve(matrix, right):
    dimension = matrix.shape[0]
    augmented = np.concatenate([np.array(matrix) * 1.0, np.array(right) * 1.0], axis=1)
    for pivot_col in range(dimension):
        largest = pivot_col + int(np.argmax(np.abs(augmented[pivot_col:, pivot_col])))
        swapped = augmented[[largest, pivot_col]]
        augmented[[pivot_col, largest]] = swapped
        augmented[pivot_col] = augmented[pivot_col] / augmented[pivot_col, pivot_col]
        for row_id in range(dimension):
            if row_id != pivot_col:
                augmented[row_id] = (
                    augmented[row_id] - augmented[row_id, pivot_col] * augmented[pivot_col]
                )
    return augmented[:, dimension:]


def node_tables():
    points = np.array(
        [(across / 3.0, upward / 3.0) for upward in range(4) for across in range(4 - upward)]
    )
    powers = [(power_r, power_s) for power_r in range(4) for power_s in range(4 - power_r)]
    vander = np.zeros((10, 10))
    grad_r = np.zeros((10, 10))
    grad_s = np.zeros((10, 10))
    mono_mass = np.zeros((10, 10))
    for column, (power_r, power_s) in enumerate(powers):
        vander[:, column] = points[:, 0] ** power_r * points[:, 1] ** power_s
        if power_r > 0:
            grad_r[:, column] = power_r * points[:, 0] ** (power_r - 1) * points[:, 1] ** power_s
        if power_s > 0:
            grad_s[:, column] = power_s * points[:, 0] ** power_r * points[:, 1] ** (power_s - 1)
        for second_column, (other_r, other_s) in enumerate(powers):
            mono_mass[column, second_column] = (
                math.factorial(power_r + other_r)
                * math.factorial(power_s + other_s)
                / math.factorial(power_r + other_r + power_s + other_s + 2)
            )
    inverse = gauss_solve(vander, np.eye(10))
    mass_matrix = inverse.T @ mono_mass @ inverse
    line_points = np.arange(4) / 3.0
    line_vander = line_points[:, None] ** np.arange(4)[None, :]
    hilbert = 1.0 / (np.arange(4)[:, None] + np.arange(4)[None, :] + 1.0)
    line_inverse = gauss_solve(line_vander, np.eye(4))
    edge_mass = line_inverse.T @ hilbert @ line_inverse
    face_nodes = np.array([[0, 1, 2, 3], [3, 6, 8, 9], [9, 7, 4, 0]])
    edge_embed = np.zeros((10, 12))
    for face_id in range(3):
        for node_id in range(4):
            edge_embed[face_nodes[face_id, node_id], 4 * face_id : 4 * face_id + 4] += edge_mass[
                node_id
            ]
    lifting = gauss_solve(mass_matrix, edge_embed).reshape(10, 3, 4)
    return (
        np.asarray(grad_r @ inverse, np.float32),
        np.asarray(grad_s @ inverse, np.float32),
        np.asarray(lifting, np.float32),
        face_nodes.reshape(-1),
    )


def round_up(value, step):
    return (value + step - 1) // step * step


def static_tables(members, elements):
    deriv_r, deriv_s, lifting, face_order = node_tables()
    nodes = deriv_r.shape[0]
    pairs = nodes // 2
    used = members * pairs
    comp = round_up(used, 8)
    face_nodes = face_order.reshape(3, 4)
    wide = members * 4

    def lane_of(s, n):
        return (n % 2) * comp + s * pairs + n // 2

    own = np.zeros((LANES, LANES), np.float32)
    own[2 * comp, 3 * wide :] = 1.0
    back = np.zeros((LANES, LANES), np.float32)
    lift = np.zeros((2 * comp, LANES), np.float32)
    along = np.zeros((2, 2 * comp, LANES), np.float32)
    for s in range(members):
        for f in range(3):
            for k in range(4):
                n = int(face_nodes[f, k])
                own[lane_of(s, n), f * wide + s * 4 + k] = 1.0
                back[lane_of(s, n), f * wide + s * 4 + 3 - k] = 1.0
        for n in range(nodes):
            for f in range(3):
                for k in range(4):
                    lift[lane_of(s, n), f * wide + s * 4 + k] = lifting[n, f, k]
            for m in range(nodes):
                along[0, lane_of(s, n), lane_of(s, m)] = -deriv_r[n, m]
                along[1, lane_of(s, n), lane_of(s, m)] = -deriv_s[n, m]
            along[0, lane_of(s, n), 2 * comp + s] = breach_rate
    spread = np.zeros((16, 8 * LANES), np.float32)
    for q in range(4):
        for f in range(3):
            spread[3 * q + f, q * LANES + f * wide : q * LANES + (f + 1) * wide] = 1.0
        spread[12 + q, (4 + q) * LANES : (4 + q) * LANES + 2 * comp] = 1.0
    return dict(
        own=own, back=back, lift=lift, along=along, spread=spread,
        comp=comp, pairs=pairs, used=used, wide=wide, nodes=nodes, members=members,
    )


def high_low(matrix):
    high = matrix.astype(jnp.bfloat16)
    low = (matrix - high.astype(np.float32)).astype(jnp.bfloat16)
    return high, low


def mm(a, b, dims=((1,), (0,))):
    return lax.dot_general(a, b, (dims, ((), ())), preferred_element_type=jnp.float32)


def split(x):
    high = x.astype(jnp.bfloat16)
    return high, (x - high.astype(jnp.float32)).astype(jnp.bfloat16)


def swap_halves(x):
    return pltpu.roll(x, LANES // 2, 1)


def turn(x, eye):
    return mm(eye[...], jnp.concatenate(split(x), axis=1), ((1,), (1,)))


def turn_pair(fields, first, second, eye, turned, halves, comp):
    lower = lax.broadcasted_iota(jnp.int32, (comp, LANES), 1) < LANES // 2
    for c in range(3):
        a = fields[first, c * comp : (c + 1) * comp]
        b = fields[second, c * comp : (c + 1) * comp]
        even = jnp.where(lower, a, swap_halves(b))
        odd = jnp.where(lower, swap_halves(a), b)
        fill = jnp.full((LANES - 2 * comp, LANES), 1.0 if c == 0 else 0.0, jnp.float32)
        flat = turn(jnp.concatenate([even, odd, fill], axis=0), eye)
        if turned is not None:
            turned[c] = flat
        high, low = split(flat)
        halves[c * LANES : (c + 1) * LANES, :LANES] = high
        halves[c * LANES : (c + 1) * LANES, LANES:] = low


def place_face(pieces, c, wide, lane):
    moved = [pltpu.roll(p, ((i - c) * wide) % LANES, 1) if i != c else p for i, p in enumerate(pieces)]
    return jnp.where(lane < wide, moved[0], jnp.where(lane < 2 * wide, moved[1], moved[2]))


def root(x):
    return x * lax.rsqrt(x)


def start_all(copies):
    for copy in copies:
        copy.start()
    return copies


def wait_all(copies):
    for copy in copies:
        copy.wait()


def prepare_kernel(
    rim_in, depth_in, flow_in, back_in, eye_in, fields_out, pool_out, head, tail,
    rim, depth, flow, back, eye, fields, pool, halves, sems, *, t, blocks, elements,
):
    comp, pairs, members, wide = t["comp"], t["pairs"], t["members"], t["wide"]
    tiles = blocks // 8
    steps = blocks // 2
    group = 2 * 3 * elements
    first = start_all(
        [
            pltpu.make_async_copy(depth_in, depth, sems.at[0]), pltpu.make_async_copy(back_in, back, sems.at[1]),
            pltpu.make_async_copy(eye_in, eye, sems.at[2]),
            pltpu.make_async_copy(rim_in, rim, sems.at[3 + tiles + 2 * steps]),
        ]
    )

    def part(tile):
        rows = pl.ds(8 * tile, 8)
        return pltpu.make_async_copy(flow_in.at[rows], flow.at[rows], sems.at[3 + tile])

    def outward(i):
        rows, lines = pl.ds(2 * i, 2), pl.ds(group * i, group)
        return [
            pltpu.make_async_copy(fields.at[rows], fields_out.at[rows], sems.at[3 + tiles + i]),
            pltpu.make_async_copy(pool.at[lines], pool_out.at[lines], sems.at[3 + tiles + steps + i]),
        ]

    start_all([part(tile) for tile in range(tiles)])
    wait_all(first)

    def build(i):
        for u in range(2):
            b = 2 * i + u
            tile, sub = b // 8, b % 8
            for c in range(3):
                end = comp * (c + 1)
                fields[b, end - 8 : end] = jnp.full((8, LANES), 1.0 if c == 0 else 0.0, jnp.float32)
            for s in range(members):
                start = (s * tiles + tile) * pairs * 8 + sub
                fields[b, s * pairs : (s + 1) * pairs] = depth[pl.ds(start, pairs, stride=8), :]
                for j in range(pairs):
                    two = flow[b, s, :, j * LANES : (j + 1) * LANES]
                    row = s * pairs + j
                    fields[b, comp + row : comp + row + 1] = two[0:1]
                    fields[b, 2 * comp + row : 2 * comp + row + 1] = two[1:2]

    def turn_of(i):
        turn_pair(fields, 2 * i, 2 * i + 1, eye, None, halves, comp)

    def faces_of(i):
        rows = mm(halves[...], back[...])
        lane = lax.broadcasted_iota(jnp.int32, (LANES, LANES), 1)
        pieces = [rows[c * LANES : (c + 1) * LANES] for c in range(3)]
        for f in range(3):
            face = place_face(pieces, f, wide, lane)
            for u in range(2):
                at = ((2 * i + u) * 3 + f) * elements
                pool[pl.ds(at, elements), :] = face[u * elements : (u + 1) * elements]

    part(0).wait()
    build(0)
    turn_of(0)
    build(1)

    def one(i, carry):
        @pl.when(i % 4 == 0)
        def _():
            part(i // 4).wait()

        faces_of(i - 2)
        turn_of(i - 1)
        build(i)
        start_all(outward(i - 2))
        return carry

    lax.fori_loop(2, steps, one, 0)
    faces_of(steps - 2)
    turn_of(steps - 1)
    start_all(outward(steps - 2))
    faces_of(steps - 1)
    start_all(outward(steps - 1))
    width = head.shape[0]

    def pick(i, carry):
        for u in range(16):
            r = i * 16 + u
            head[pl.ds(r, 1), :] = pool[pl.ds(rim[0, r], 1), :]
            tail[pl.ds(r, 1), :] = pool[pl.ds(rim[0, width + r], 1), :]
        return carry

    lax.fori_loop(0, width // 16, pick, 0)

    def drain(i, carry):
        wait_all(outward(i))
        return carry

    lax.fori_loop(0, steps, drain, 0)


def scan_moves(plan, base, order, place, blocks):
    def one(i, carry):
        leaving, staying = carry
        slot = plan[base + i]
        away = jnp.logical_or(slot < base, slot >= base + blocks).astype(jnp.int32)
        order[jnp.where(away == 1, leaving, blocks - 1 - staying)] = i
        place[i] = lax.div(slot, jnp.int32(blocks))
        return leaving + away, staying + 1 - away

    return lax.fori_loop(0, blocks, one, (jnp.int32(0), jnp.int32(0)))[0]


def scan_origins(plan, own, origin, blocks, devices):
    def device(d, carry):
        mark = jnp.where(d == own, -1, d)
        for i in range(blocks):
            slot = plan[d * blocks + i] - own * blocks
            origin[jnp.where(jnp.logical_and(slot >= 0, slot < blocks), slot, blocks)] = mark
        return carry

    lax.fori_loop(0, devices, device, 0)


def face_rows(angle, scale, links, metric, coefs, blocks, elements):
    shape = (blocks, 3 * elements)
    own = lax.broadcasted_iota(jnp.int32, shape, 0) * (3 * elements) + lax.broadcasted_iota(jnp.int32, shape, 1)
    free = jnp.where(links[...] == own, 0.0, 1.0)
    lower = lax.broadcasted_iota(jnp.int32, (blocks, LANES), 1) < elements
    for q, value in enumerate((jnp.cos(angle[...]), jnp.sin(angle[...]), scale[...], free)):
        two = value[:, :LANES]
        swapped = swap_halves(two)
        third = value[:, LANES:]
        faces = (
            jnp.where(lower, two, swapped), jnp.where(lower, swapped, two), jnp.concatenate([third, third], axis=1)
        )
        for f in range(3):
            coefs[pl.ds(3 * q + f, blocks, stride=16), :] = faces[f]
    for b in range(blocks):
        factors = metric[b]
        coefs[b * 16 + 12 : b * 16 + 16] = jnp.concatenate([factors, factors], axis=1)


def spread_pair(coefs, both, eye, spread, factors, elements):
    lower = lax.broadcasted_iota(jnp.int32, (16, LANES), 1) < elements
    values = jnp.where(lower, coefs[pl.ds(both[0] * 16, 16), :], coefs[pl.ds(both[1] * 16, 16), :])
    rough = values.astype(jnp.bfloat16).astype(jnp.float32)
    stacked = jnp.concatenate([rough, values - rough], axis=0).astype(jnp.bfloat16)
    stacked = mm(eye[:, :LANES], stacked, ((1,), (1,))).astype(jnp.bfloat16)
    factors[...] = mm(stacked, spread[...])


def inflow_rows(breach, both, t):
    rows = []
    for b in both:
        row = jnp.zeros((1, LANES), jnp.float32)
        for s in range(t["members"]):
            level = breach[s, b].astype(jnp.float32)
            row = jnp.where(lax.broadcasted_iota(jnp.int32, (1, LANES), 1) == 2 * t["comp"] + s, level, row)
        rows.append(row)
    return rows


def volume_rows(rows, turned, factors, first, inflow, pieces):
    rx, sx, ry, sy = (factors[rows, q * LANES : (q + 1) * LANES] for q in range(first, first + 4))
    height, flow_x, flow_y = (turned[c, rows] for c in range(3))
    pressure = 0.5 * gravity * height * height
    inverse = 1.0 / height
    speed_x = flow_x * inverse
    speed_y = flow_y * inverse
    cross = flow_y * speed_x
    flux_f = (flow_x, flow_x * speed_x + pressure, cross)
    flux_g = (flow_y, cross, flow_y * speed_y + pressure)
    for c in range(3):
        along_r = rx * flux_f[c] + ry * flux_g[c]
        along_s = sx * flux_f[c] + sy * flux_g[c]
        if c == 0:
            along_r = along_r + inflow
        pieces[c, rows, 0:LANES], pieces[c, rows, LANES : 2 * LANES] = split(along_r)
        pieces[c, rows, 2 * LANES : 3 * LANES], pieces[c, rows, 3 * LANES : 4 * LANES] = split(along_s)


def flux_rows(rows, traces, outer, factors, pieces, first, wide):
    lane = lax.broadcasted_iota(jnp.int32, (rows.stop - rows.start, LANES), 1)
    n_x, n_y, scale, free = (factors[rows, q * LANES : (q + 1) * LANES] for q in range(4))
    theirs = [outer[f * LANES + rows.start : f * LANES + rows.stop] for f in range(3)]
    height, flow_x, flow_y = (traces[c, rows] for c in range(3))
    is_wall = free < 0.5
    through = flow_x * n_x + flow_y * n_y
    twice = through + through
    height_o = jnp.where(is_wall, height, place_face(theirs, 0, wide, lane))
    flow_xo = jnp.where(is_wall, flow_x - twice * n_x, place_face(theirs, 1, wide, lane))
    flow_yo = jnp.where(is_wall, flow_y - twice * n_y, place_face(theirs, 2, wide, lane))
    speed = through / height
    speed_o = (flow_xo * n_x + flow_yo * n_y) / height_o
    fast = jnp.maximum(
        jnp.abs(speed) + root(gravity * height), jnp.abs(speed_o) + root(gravity * height_o)
    )
    ours, others = speed - fast, speed_o - fast
    half = 0.5 * scale
    push = 0.5 * gravity * (height * height - height_o * height_o)
    jumps = (
        half * (height * ours - height_o * others),
        half * (flow_x * ours - flow_xo * others + push * n_x),
        half * (flow_y * ours - flow_yo * others + push * n_y),
    )
    for c in range(3):
        pieces[c, rows, first : first + LANES], pieces[c, rows, first + LANES : first + 2 * LANES] = split(jumps[c])


def lift_mm(lift, low, pieces, c, first):
    last = ((1,), (1,))
    return mm(lift, pieces[c, :, : first + 2 * LANES], last) + mm(low[...], pieces[c, :, first : first + LANES], last)


def pair_gains(tall, comp, elements):
    narrow = lax.broadcasted_iota(jnp.int32, (comp, LANES), 1) < elements
    even, odd = tall[:comp], tall[comp:]
    return jnp.where(narrow, even, swap_halves(odd)), jnp.where(narrow, swap_halves(even), odd)


def row_chunks(step):
    return [slice(i * step, (i + 1) * step) for i in range(LANES // step)]


RING = 8


def finish_kernel(
    plan_in, wet_in, breach_in, links_in, angle_in, scale_in, metric_in,
    fields_in, pool_in, before_in, after_in, own_in, spread_in, matrix_in, low_in, eye_in,
    *rest, t, blocks, elements, devices, leaving,
):
    outs, scratch = (rest[:1], rest[1:]) if leaving else (rest[:3], rest[3:])
    plan, wet, breach, links, angle, scale, metric, fields, pool, own, spread, matrix, low, eye, *scratch = scratch
    order, place, coefs, turned, halves, traces, factors, outer, pieces, near, sems, staged, *scratch = scratch
    comp, wide, used = t["comp"], t["wide"], t["used"]
    faces = blocks * 3 * elements
    width = before_in.shape[0]
    loads = [
        (plan_in, plan), (angle_in, angle), (scale_in, scale), (links_in, links), (metric_in, metric),
        (wet_in, wet), (breach_in, breach), (eye_in, eye), (own_in, own), (fields_in, fields),
        (pool_in, pool.at[pl.ds(0, faces)]), (before_in, pool.at[pl.ds(faces, width)]),
        (after_in, pool.at[pl.ds(faces + width, width)]), (spread_in, spread), (matrix_in, matrix), (low_in, low),
    ]
    n = len(loads)
    loads = start_all([pltpu.make_async_copy(a, b, sems.at[i]) for i, (a, b) in enumerate(loads)])
    index = lax.axis_index("mesh")
    loads[0].wait()
    n_leaving = scan_moves(plan, index * blocks, order, place, blocks)
    begin = 0 if leaving else n_leaving
    end = n_leaving if leaving else blocks
    steps = (end - begin + 3) // 4

    def at(i, u):
        return jnp.minimum(begin + 4 * i + u, end - 1)

    def indices(i):
        return [pltpu.make_async_copy(links_in.at[order[at(i, u)]], near.at[u], sems.at[n + u]) for u in range(4)]

    def send(p):
        return pltpu.make_async_copy(staged.at[p], outs[0].at[place[order[p]]], sems.at[n + 4 + p % RING])

    @pl.when(steps > 0)
    def _():
        start_all(indices(0))

    wait_all(loads[1:5])
    face_rows(angle, scale, links, metric, coefs, blocks, elements)
    if not leaving:
        scan_origins(plan, index, scratch[2], blocks, devices)
    wait_all(loads[5:])
    chunks = row_chunks(16)
    rows_to_pick = [
        (u, f, e) for u in range(2) for f in range(3) for e in range(elements)
    ]

    def pick(w, some):
        for u, f, e in some:
            row = f * LANES + u * elements + e
            outer[w, row : row + 1, :] = pool[pl.ds(near[2 * w + u, f * elements + e], 1), :]

    def one(i, carry):
        both = [[order[at(i, 2 * w + u)] for u in range(2)] for w in range(2)]
        inflow = [None, None]

        def lay_out(w):
            turn_pair(fields, both[w][0], both[w][1], eye, turned.at[w], halves.at[w], comp)
            inner = mm(halves[w], own[...])
            for c in range(3):
                traces[w, c] = inner[c * LANES : (c + 1) * LANES]
            spread_pair(coefs, both[w], eye, spread, factors.at[w], elements)
            inflow[w] = inflow_rows(breach, both[w], t)

        def fluxes(w, rows):
            volume_rows(rows, turned.at[w], factors.at[w], 4, inflow[w][rows.start // elements], pieces.at[w])
            flux_rows(rows, traces.at[w], outer.at[w], factors.at[w], pieces.at[w], 4 * LANES, wide)

        def combine(w, c):
            gains = pair_gains(lift_mm(matrix[...], low, pieces.at[w], c, 4 * LANES), comp, elements)
            for u in range(2):
                b = both[w][u]
                rate = time_step * wet[b].astype(jnp.float32)
                done = fields[b, c * comp : (c + 1) * comp] + rate * gains[u]
                if leaving:
                    staged[at(i, 2 * w + u), c * used : (c + 1) * used] = done[:used]
                else:
                    staged[2 * w + u, c * comp : (c + 1) * comp] = done

        def hand_over(w):
            for u in range(2):
                if leaving:
                    p = 4 * i + 2 * w + u

                    @pl.when(p < end)
                    def _():
                        @pl.when(p >= RING)
                        def _():
                            send(p - RING).wait()

                        send(p).start()
                else:
                    write_block(both[w][u], staged.at[2 * w + u], comp, scratch[0], scratch[1], t, blocks)

        wait_all(indices(i))
        pick(0, rows_to_pick)
        lay_out(0)
        share = len(rows_to_pick) // len(chunks)
        for k, rows in enumerate(chunks):
            fluxes(0, rows)
            pick(1, rows_to_pick[k * share : (k + 1) * share])
            if k == 1:
                lay_out(1)
        for k, rows in enumerate(chunks):
            if k < 3:
                combine(0, k)
            fluxes(1, rows)
        for c in range(3):
            combine(1, c)

        @pl.when(i + 1 < steps)
        def _():
            start_all(indices(i + 1))

        hand_over(0)
        hand_over(1)
        return carry

    lax.fori_loop(0, steps, one, 0)
    if leaving:

        def drain(p, carry):
            send(p).wait()
            return carry

        lax.fori_loop(jnp.maximum(end - RING, 0), end, drain, 0)
    else:
        kept = ((scratch[0], outs[0]), (scratch[1], outs[1]), (scratch[2].at[pl.ds(0, outs[2].shape[0])], outs[2]))
        wait_all(start_all([pltpu.make_async_copy(a, b, sems.at[n + 4 + i]) for i, (a, b) in enumerate(kept)]))


def write_block(b, rows, step, depth, flow, t, blocks):
    pairs, members = t["pairs"], t["members"]
    tile, sub = b // 8, b % 8
    for s in range(members):
        start = (s * (blocks // 8) + tile) * pairs * 8 + sub
        depth[pl.ds(start, pairs, stride=8), :] = rows[s * pairs : (s + 1) * pairs]
        for j in range(pairs):
            row = s * pairs + j
            flow[b, s, 0:1, j * LANES : (j + 1) * LANES] = rows[step + row : step + row + 1]
            flow[b, s, 1:2, j * LANES : (j + 1) * LANES] = rows[2 * step + row : 2 * step + row + 1]


def merge_kernel(
    origin_in, got_in, depth_in, flow_in, depth_out, flow_out, origin, depth, flow, got, sems, *, t, blocks
):
    def leave(b, k):
        return pltpu.make_async_copy(flow.at[b], flow_out.at[b], sems.at[3 + k % RING])

    loads = start_all(
        [
            pltpu.make_async_copy(a, b, sems.at[i])
            for i, (a, b) in enumerate(((origin_in, origin), (got_in, got), (depth_in, depth)))
        ]
    )
    wait_all(loads)

    def put(b, k):
        came = origin[b] >= 0

        @pl.when(came)
        def _():
            write_block(b, got.at[origin[b]], t["used"], depth, flow, t, blocks)

            @pl.when(k >= RING)
            def _():
                leave(b, k).wait()

            leave(b, k).start()

        return k + came.astype(jnp.int32)

    arrivals = lax.fori_loop(0, blocks, put, jnp.int32(0))
    back = pltpu.make_async_copy(depth, depth_out, sems.at[2])
    back.start()

    def drain(k, carry):
        leave(0, k).wait()
        return carry

    lax.fori_loop(jnp.maximum(arrivals - RING, 0), arrivals, drain, 0)
    back.wait()


SMEM = pl.BlockSpec(memory_space=pltpu.SMEM)
HBM = pl.BlockSpec(memory_space=pltpu.HBM)
VMEM = pl.BlockSpec(memory_space=pltpu.VMEM)


def call(kernel, out_shape, n_smem, n_args, scratch, out_specs, **keys):
    return pl.pallas_call(
        kernel,
        out_shape=out_shape,
        in_specs=[SMEM] * n_smem + [HBM] * n_args,
        out_specs=out_specs,
        scratch_shapes=scratch,
        compiler_params=pltpu.CompilerParams(vmem_limit_bytes=64 << 20),
        **keys,
    )


def body(
    water_depth, momentum, metric, face_scale, face_angle, face_map, rim_faces, wet_blocks, breach, block_plan
):
    blocks, members, node_cells = water_depth.shape
    elements = metric.shape[2]
    t = static_tables(members, elements)
    comp, pairs, used = t["comp"], t["pairs"], t["used"]
    f32, bf16 = jnp.float32, jnp.bfloat16
    tiles = blocks // 8
    depth_rows = water_depth.reshape(tiles, 8, members, pairs, LANES).transpose(2, 0, 3, 1, 4).reshape(-1, LANES)
    flow_rows = momentum.transpose(0, 2, 1, 3)
    faces = face_map.size
    width = rim_faces.shape[1] // 2
    dma = pltpu.SemaphoreType.DMA

    back = jnp.asarray(np.tile(t["back"], (2, 1)), bf16)
    eye = jnp.asarray(np.tile(np.eye(LANES), (1, 2)), bf16)
    fields, pool, head, tail = call(
        functools.partial(prepare_kernel, t=t, blocks=blocks, elements=elements),
        (
            jax.ShapeDtypeStruct((blocks, 3 * comp, LANES), f32),
            jax.ShapeDtypeStruct((faces, LANES), f32),
            jax.ShapeDtypeStruct((width, LANES), f32),
            jax.ShapeDtypeStruct((width, LANES), f32),
        ),
        0, 5,
        [
            pltpu.SMEM(rim_faces.shape, jnp.int32), pltpu.VMEM(depth_rows.shape, f32), pltpu.VMEM(flow_rows.shape, f32), pltpu.VMEM(back.shape, bf16),
            pltpu.VMEM(eye.shape, bf16),
            pltpu.VMEM((blocks, 3 * comp, LANES), f32), pltpu.VMEM((faces, LANES), f32),
            pltpu.VMEM((3 * LANES, 2 * LANES), bf16), dma((4 + tiles + blocks,)),
        ],
        (HBM, HBM, VMEM, VMEM),
    )(rim_faces, depth_rows, flow_rows, back, eye)

    count = lax.axis_size("mesh")
    before = lax.ppermute(tail, "mesh", [(i, i + 1) for i in range(count - 1)])
    after = lax.ppermute(head, "mesh", [(i + 1, i) for i in range(count - 1)])

    lift_h, lift_l = high_low(t["lift"])
    matrix = np.concatenate(
        [t["along"][0], t["along"][0], t["along"][1], t["along"][1], lift_h.astype(np.float32), lift_h.astype(np.float32)],
        axis=1,
    )
    mats = [
        jnp.asarray(np.tile(t["own"], (2, 1)), bf16), jnp.asarray(np.tile(t["spread"], (2, 1)), bf16),
        jnp.asarray(matrix, bf16), jnp.asarray(lift_l), eye,
    ]
    packed = round_up(3 * used, 8)

    i32 = jnp.int32
    rows_of = (3 * comp, LANES)

    def finish(leaving, out_shape, extra):
        return call(
            functools.partial(
                finish_kernel, t=t, blocks=blocks, elements=elements, devices=count, leaving=leaving
            ),
            out_shape,
            0, 16,
            [
                pltpu.SMEM(block_plan.shape, i32), pltpu.SMEM(wet_blocks.shape, i32),
                pltpu.SMEM((members, blocks), i32), pltpu.VMEM(face_map.shape, i32),
                pltpu.VMEM(face_angle.shape, f32), pltpu.VMEM(face_scale.shape, f32), pltpu.VMEM(metric.shape, f32),
                pltpu.VMEM((blocks, *rows_of), f32), pltpu.VMEM((faces + 2 * width, LANES), f32),
                *[pltpu.VMEM(m.shape, bf16) for m in mats],
                pltpu.SMEM((blocks,), i32), pltpu.SMEM((blocks,), i32), pltpu.VMEM((blocks * 16, LANES), f32),
                pltpu.VMEM((2, 3, LANES, LANES), f32), pltpu.VMEM((2, 3 * LANES, 2 * LANES), bf16),
                pltpu.VMEM((2, 3, LANES, LANES), f32), pltpu.VMEM((2, LANES, 8 * LANES), f32),
                pltpu.VMEM((2, 3 * LANES, LANES), f32), pltpu.VMEM((2, 3, LANES, 6 * LANES), bf16),
                pltpu.SMEM((4, face_map.shape[1]), i32), dma((20 + RING,)), *extra,
            ],
            jax.tree.map(lambda _: HBM, out_shape),
        )(
            block_plan, wet_blocks, breach.T, face_map, face_angle, face_scale, metric, fields, pool, before, after,
            *mats,
        )

    sent = finish(True, jax.ShapeDtypeStruct((count, packed, LANES), f32), [pltpu.VMEM((blocks, packed, LANES), f32)])
    got = lax.all_to_all(sent, "mesh", split_axis=0, concat_axis=0, tiled=True)
    final = (jax.ShapeDtypeStruct(depth_rows.shape, f32), jax.ShapeDtypeStruct(flow_rows.shape, f32))
    whole = [pltpu.VMEM(depth_rows.shape, f32), pltpu.VMEM(flow_rows.shape, f32)]
    depth_kept, flow_kept, origin = finish(
        False, (*final, jax.ShapeDtypeStruct((LANES,), i32)),
        [pltpu.VMEM((4, *rows_of), f32), *whole, pltpu.SMEM((LANES,), i32)],
    )
    depth_new, flow_new = call(
        functools.partial(merge_kernel, t=t, blocks=blocks),
        final,
        0, 4,
        [pltpu.SMEM((LANES,), i32), *whole, pltpu.VMEM((count, packed, LANES), f32), dma((3 + RING,))],
        (HBM, HBM),
        input_output_aliases={2: 0, 3: 1},
    )(origin, got, depth_kept, flow_kept)
    depth_out = depth_new.reshape(members, tiles, pairs, 8, LANES).transpose(1, 3, 0, 2, 4).reshape(water_depth.shape)
    return depth_out, flow_new.transpose(0, 2, 1, 3)


def solution(mesh):
    in_specs = (
        P(("groups", "mesh"), None, None),
        P(("groups", "mesh"), None, None, None),
        P(("groups", "mesh"), None, None),
        P(("groups", "mesh"), None),
        P(("groups", "mesh"), None),
        P(("groups", "mesh"), None),
        P(("groups", "mesh"), None),
        P(("groups", "mesh")),
        P(("groups", "mesh"), None),
        P("groups"),
    )
    out_specs = (P(("groups", "mesh"), None, None), P(("groups", "mesh"), None, None, None))
    return jax.shard_map(body, mesh=mesh, in_specs=in_specs, out_specs=out_specs, check_vma=False)
```

```python
import functools
import math

import jax
import jax.numpy as jnp
import numpy as np
from jax import lax
from jax.experimental import pallas as pl
from jax.experimental.pallas import tpu as pltpu
from jax.sharding import PartitionSpec as P

time_step = 0.01
gravity = 1.0
breach_rate = 5.0
LANES = 128


def gauss_solve(matrix, right):
    dimension = matrix.shape[0]
    augmented = np.concatenate([np.array(matrix) * 1.0, np.array(right) * 1.0], axis=1)
    for pivot_col in range(dimension):
        largest = pivot_col + int(np.argmax(np.abs(augmented[pivot_col:, pivot_col])))
        swapped = augmented[[largest, pivot_col]]
        augmented[[pivot_col, largest]] = swapped
        augmented[pivot_col] = augmented[pivot_col] / augmented[pivot_col, pivot_col]
        for row_id in range(dimension):
            if row_id != pivot_col:
                augmented[row_id] = (
                    augmented[row_id] - augmented[row_id, pivot_col] * augmented[pivot_col]
                )
    return augmented[:, dimension:]


def node_tables():
    points = np.array(
        [(across / 3.0, upward / 3.0) for upward in range(4) for across in range(4 - upward)]
    )
    powers = [(power_r, power_s) for power_r in range(4) for power_s in range(4 - power_r)]
    vander = np.zeros((10, 10))
    grad_r = np.zeros((10, 10))
    grad_s = np.zeros((10, 10))
    mono_mass = np.zeros((10, 10))
    for column, (power_r, power_s) in enumerate(powers):
        vander[:, column] = points[:, 0] ** power_r * points[:, 1] ** power_s
        if power_r > 0:
            grad_r[:, column] = power_r * points[:, 0] ** (power_r - 1) * points[:, 1] ** power_s
        if power_s > 0:
            grad_s[:, column] = power_s * points[:, 0] ** power_r * points[:, 1] ** (power_s - 1)
        for second_column, (other_r, other_s) in enumerate(powers):
            mono_mass[column, second_column] = (
                math.factorial(power_r + other_r)
                * math.factorial(power_s + other_s)
                / math.factorial(power_r + other_r + power_s + other_s + 2)
            )
    inverse = gauss_solve(vander, np.eye(10))
    mass_matrix = inverse.T @ mono_mass @ inverse
    line_points = np.arange(4) / 3.0
    line_vander = line_points[:, None] ** np.arange(4)[None, :]
    hilbert = 1.0 / (np.arange(4)[:, None] + np.arange(4)[None, :] + 1.0)
    line_inverse = gauss_solve(line_vander, np.eye(4))
    edge_mass = line_inverse.T @ hilbert @ line_inverse
    face_nodes = np.array([[0, 1, 2, 3], [3, 6, 8, 9], [9, 7, 4, 0]])
    edge_embed = np.zeros((10, 12))
    for face_id in range(3):
        for node_id in range(4):
            edge_embed[face_nodes[face_id, node_id], 4 * face_id : 4 * face_id + 4] += edge_mass[
                node_id
            ]
    lifting = gauss_solve(mass_matrix, edge_embed).reshape(10, 3, 4)
    return (
        np.asarray(grad_r @ inverse, np.float32),
        np.asarray(grad_s @ inverse, np.float32),
        np.asarray(lifting, np.float32),
        face_nodes.reshape(-1),
    )


def round_up(value, step):
    return (value + step - 1) // step * step


def static_tables(members, elements):
    deriv_r, deriv_s, lifting, face_order = node_tables()
    nodes = deriv_r.shape[0]
    pairs = nodes // 2
    used = members * pairs
    comp = round_up(used, 8)
    face_nodes = face_order.reshape(3, 4)
    wide = members * 4

    def lane_of(s, n):
        return (n % 2) * comp + s * pairs + n // 2

    own = np.zeros((LANES, LANES), np.float32)
    own[2 * comp, 3 * wide :] = 1.0
    back = np.zeros((LANES, LANES), np.float32)
    lift = np.zeros((2 * comp, LANES), np.float32)
    along = np.zeros((2, 2 * comp, LANES), np.float32)
    for s in range(members):
        for f in range(3):
            for k in range(4):
                n = int(face_nodes[f, k])
                own[lane_of(s, n), f * wide + s * 4 + k] = 1.0
                back[lane_of(s, n), f * wide + s * 4 + 3 - k] = 1.0
        for n in range(nodes):
            for f in range(3):
                for k in range(4):
                    lift[lane_of(s, n), f * wide + s * 4 + k] = lifting[n, f, k]
            for m in range(nodes):
                along[0, lane_of(s, n), lane_of(s, m)] = -deriv_r[n, m]
                along[1, lane_of(s, n), lane_of(s, m)] = -deriv_s[n, m]
            along[0, lane_of(s, n), 2 * comp + s] = breach_rate
    spread = np.zeros((16, 8 * LANES), np.float32)
    for q in range(4):
        for f in range(3):
            spread[3 * q + f, q * LANES + f * wide : q * LANES + (f + 1) * wide] = 1.0
        spread[12 + q, (4 + q) * LANES : (4 + q) * LANES + 2 * comp] = 1.0
    return dict(
        own=own, back=back, lift=lift, along=along, spread=spread,
        comp=comp, pairs=pairs, used=used, wide=wide, nodes=nodes, members=members,
    )


def high_low(matrix):
    high = matrix.astype(jnp.bfloat16)
    low = (matrix - high.astype(np.float32)).astype(jnp.bfloat16)
    return high, low


def mm(a, b, dims=((1,), (0,))):
    return lax.dot_general(a, b, (dims, ((), ())), preferred_element_type=jnp.float32)


def split(x):
    high = x.astype(jnp.bfloat16)
    return high, (x - high.astype(jnp.float32)).astype(jnp.bfloat16)


def swap_halves(x):
    return pltpu.roll(x, LANES // 2, 1)


def turn(x, eye):
    return mm(eye[...], jnp.concatenate(split(x), axis=1), ((1,), (1,)))


def turn_rows(first, second, c, eye, turned, halves, comp):
    lower = lax.broadcasted_iota(jnp.int32, (comp, LANES), 1) < LANES // 2
    even = jnp.where(lower, first, swap_halves(second))
    odd = jnp.where(lower, swap_halves(first), second)
    fill = jnp.full((LANES - 2 * comp, LANES), 1.0 if c == 0 else 0.0, jnp.float32)
    flat = turn(jnp.concatenate([even, odd, fill], axis=0), eye)
    if turned is not None:
        turned[c] = flat
    high, low = split(flat)
    halves[c * LANES : (c + 1) * LANES, :LANES] = high
    halves[c * LANES : (c + 1) * LANES, LANES:] = low


def rows_of(fields, block, c, comp):
    if c == 0:
        return fields[block, :comp]
    return fields[block, pl.ds(comp + c - 1, comp, stride=2), :]


def weave(*lists):
    count = max(len(steps) for steps in lists)
    for i in range(count):
        for steps in lists:
            for step in steps[len(steps) * i // count : len(steps) * (i + 1) // count]:
                step()


def place_face(pieces, c, wide, lane):
    moved = [pltpu.roll(p, ((i - c) * wide) % LANES, 1) if i != c else p for i, p in enumerate(pieces)]
    return jnp.where(lane < wide, moved[0], jnp.where(lane < 2 * wide, moved[1], moved[2]))


def root(x):
    return x * lax.rsqrt(x)


def start_all(copies):
    for copy in copies:
        copy.start()
    return copies


def wait_all(copies):
    for copy in copies:
        copy.wait()


def prepare_kernel(
    rim_in, depth_in, flow_in, back_in, eye_in, fields_out, pool_out, partner, across,
    rim, depth, flow, back, eye, fields, pool, halves, sems, *, t, blocks, elements,
):
    comp, pairs, members, wide = t["comp"], t["pairs"], t["members"], t["wide"]
    odd = lax.axis_index("mesh") % 2
    tiles = blocks // 8
    steps = blocks // 2
    group = 8 * 3 * elements
    first = start_all(
        [
            pltpu.make_async_copy(depth_in, depth, sems.at[0]), pltpu.make_async_copy(back_in, back, sems.at[1]),
            pltpu.make_async_copy(eye_in, eye, sems.at[2]), pltpu.make_async_copy(rim_in, rim, sems.at[3]),
        ]
    )

    def part(tile):
        rows = pl.ds(8 * tile, 8)
        return pltpu.make_async_copy(flow_in.at[rows], flow.at[rows], sems.at[4 + tile])

    def field_part(i, slot):
        return pltpu.make_async_copy(
            fields.at[slot], fields_out.at[pl.ds(2 * i, 2)], sems.at[4 + 2 * tiles + slot]
        )

    def pool_part(tile):
        lines = pl.ds(group * tile, group)
        return pltpu.make_async_copy(pool.at[lines], pool_out.at[lines], sems.at[4 + tiles + tile])

    start_all([part(tile) for tile in range(tiles)])
    for slot in range(2):
        for u in range(2):
            fields[slot, u, comp - 8 : comp] = jnp.full((8, LANES), 1.0, jnp.float32)
            fields[slot, u, 3 * comp - 16 : 3 * comp] = jnp.zeros((16, LANES), jnp.float32)
    wait_all(first)

    def build(i, slot):
        def scenario(u, s):
            b = 2 * i + u
            tile, sub = b // 8, b % 8
            start = (s * tiles + tile) * pairs * 8 + sub
            fields[slot, u, s * pairs : (s + 1) * pairs] = depth[pl.ds(start, pairs, stride=8), :]
            for j in range(pairs):
                row = comp + 2 * (s * pairs + j)
                fields[slot, u, row : row + 2] = flow[b, s, :, j * LANES : (j + 1) * LANES]

        return [functools.partial(scenario, u, s) for u in range(2) for s in range(members)]

    def turn_of(slot):
        def component(c):
            pair = fields.at[slot]
            turn_rows(rows_of(pair, 0, c, comp), rows_of(pair, 1, c, comp), c, eye, None, halves.at[slot], comp)

        return [functools.partial(component, c) for c in range(3)]

    def faces_of(i, slot):
        lane = lax.broadcasted_iota(jnp.int32, (LANES, LANES), 1)
        pieces = []

        def multiply():
            rows = mm(halves[slot], back[...])
            pieces.extend(rows[c * LANES : (c + 1) * LANES] for c in range(3))

        def face(f, u):
            span = slice(u * elements, (u + 1) * elements)
            at = ((2 * i + u) * 3 + f) * elements
            pool[pl.ds(at, elements), :] = place_face([p[span] for p in pieces], f, wide, lane[span])

        return [multiply] + [functools.partial(face, f, u) for u in range(2) for f in range(3)]

    part(0).wait()
    weave(build(0, 0))
    field_part(0, 0).start()
    weave(build(1, 1), turn_of(0))
    field_part(1, 1).start()

    def one(h, carry):
        i = 2 * h

        @pl.when(h % 2 == 0)
        def _():
            part(h // 2).wait()

        for slot in range(2):
            field_part(i - 2 + slot, slot).wait()
            weave(build(i + slot, slot), turn_of(1 - slot), faces_of(i - 2 + slot, slot))
            field_part(i + slot, slot).start()

        @pl.when(h % 2 == 0)
        def _():
            pool_part(h // 2 - 1).start()

        return carry

    lax.fori_loop(1, steps // 2, one, 0)
    weave(turn_of(1), faces_of(steps - 2, 0))
    weave(faces_of(steps - 1, 1))
    pool_part(tiles - 1).start()
    width = partner.shape[0]
    near, far = (1 - odd) * width, odd * width

    def pick(i, carry):
        for u in range(32):
            r = i * 32 + u
            partner[pl.ds(r, 1), :] = pool[pl.ds(rim[0, near + r], 1), :]
            across[pl.ds(r, 1), :] = pool[pl.ds(rim[0, far + r], 1), :]
        return carry

    lax.fori_loop(0, width // 32, pick, 0)
    for slot in range(2):
        field_part(steps - 2 + slot, slot).wait()
    for tile in range(tiles):
        pool_part(tile).wait()


def scan_moves(plan, base, order, place, blocks):
    def one(i, carry):
        leaving, staying = carry
        slot = plan[base + i]
        away = jnp.logical_or(slot < base, slot >= base + blocks).astype(jnp.int32)
        order[jnp.where(away == 1, leaving, blocks - 1 - staying)] = i
        place[i] = lax.div(slot, jnp.int32(blocks))
        return leaving + away, staying + 1 - away

    return lax.fori_loop(0, blocks, one, (jnp.int32(0), jnp.int32(0)))[0]


def scan_origins(plan, own, origin, blocks, devices):
    def device(d, carry):
        mark = jnp.where(d == own, -1, d)
        for i in range(blocks):
            slot = plan[d * blocks + i] - own * blocks
            origin[jnp.where(jnp.logical_and(slot >= 0, slot < blocks), slot, blocks)] = mark
        return carry

    lax.fori_loop(0, devices, device, 0)


def face_rows(angle, scale, links, metric, coefs, blocks, elements):
    shape = (blocks, 3 * elements)
    own = lax.broadcasted_iota(jnp.int32, shape, 0) * (3 * elements) + lax.broadcasted_iota(jnp.int32, shape, 1)
    free = jnp.where(links[...] == own, 0.0, 1.0)
    lower = lax.broadcasted_iota(jnp.int32, (blocks, LANES), 1) < elements
    for q, value in enumerate((jnp.cos(angle[...]), jnp.sin(angle[...]), scale[...], free)):
        two = value[:, :LANES]
        swapped = swap_halves(two)
        third = value[:, LANES:]
        faces = (
            jnp.where(lower, two, swapped), jnp.where(lower, swapped, two), jnp.concatenate([third, third], axis=1)
        )
        for f in range(3):
            coefs[pl.ds(3 * q + f, blocks, stride=16), :] = faces[f]
    for b in range(blocks):
        factors = metric[b]
        coefs[b * 16 + 12 : b * 16 + 16] = jnp.concatenate([factors, factors], axis=1)


def spread_pair(coefs, both, eye, spread, factors, elements):
    lower = lax.broadcasted_iota(jnp.int32, (16, LANES), 1) < elements
    values = jnp.where(lower, coefs[pl.ds(both[0] * 16, 16), :], coefs[pl.ds(both[1] * 16, 16), :])
    rough = values.astype(jnp.bfloat16).astype(jnp.float32)
    stacked = jnp.concatenate([rough, values - rough], axis=0).astype(jnp.bfloat16)
    stacked = mm(eye[:, :LANES], stacked, ((1,), (1,))).astype(jnp.bfloat16)
    factors[...] = mm(stacked, spread[...])


def inflow_rows(breach, both, t):
    rows = []
    for b in both:
        row = jnp.zeros((1, LANES), jnp.float32)
        for s in range(t["members"]):
            level = breach[s, b].astype(jnp.float32)
            row = jnp.where(lax.broadcasted_iota(jnp.int32, (1, LANES), 1) == 2 * t["comp"] + s, level, row)
        rows.append(row)
    return rows


def volume_rows(rows, turned, factors, first, inflow, pieces):
    rx, sx, ry, sy = (factors[rows, q * LANES : (q + 1) * LANES] for q in range(first, first + 4))
    height, flow_x, flow_y = (turned[c, rows] for c in range(3))
    pressure = 0.5 * gravity * height * height
    inverse = 1.0 / height
    speed_x = flow_x * inverse
    speed_y = flow_y * inverse
    cross = flow_y * speed_x
    flux_f = (flow_x, flow_x * speed_x + pressure, cross)
    flux_g = (flow_y, cross, flow_y * speed_y + pressure)
    for c in range(3):
        along_r = rx * flux_f[c] + ry * flux_g[c]
        along_s = sx * flux_f[c] + sy * flux_g[c]
        if c == 0:
            along_r = along_r + inflow
        pieces[c, rows, 0:LANES], pieces[c, rows, LANES : 2 * LANES] = split(along_r)
        pieces[c, rows, 2 * LANES : 3 * LANES], pieces[c, rows, 3 * LANES : 4 * LANES] = split(along_s)


def flux_rows(rows, traces, outer, factors, pieces, first, wide):
    lane = lax.broadcasted_iota(jnp.int32, (rows.stop - rows.start, LANES), 1)
    n_x, n_y, scale, free = (factors[rows, q * LANES : (q + 1) * LANES] for q in range(4))
    theirs = [outer[f * LANES + rows.start : f * LANES + rows.stop] for f in range(3)]
    height, flow_x, flow_y = (traces[c, rows] for c in range(3))
    is_wall = free < 0.5
    through = flow_x * n_x + flow_y * n_y
    twice = through + through
    height_o = jnp.where(is_wall, height, place_face(theirs, 0, wide, lane))
    flow_xo = jnp.where(is_wall, flow_x - twice * n_x, place_face(theirs, 1, wide, lane))
    flow_yo = jnp.where(is_wall, flow_y - twice * n_y, place_face(theirs, 2, wide, lane))
    speed = through / height
    speed_o = (flow_xo * n_x + flow_yo * n_y) / height_o
    fast = jnp.maximum(
        jnp.abs(speed) + root(gravity * height), jnp.abs(speed_o) + root(gravity * height_o)
    )
    ours, others = speed - fast, speed_o - fast
    half = 0.5 * scale
    push = 0.5 * gravity * (height * height - height_o * height_o)
    jumps = (
        half * (height * ours - height_o * others),
        half * (flow_x * ours - flow_xo * others + push * n_x),
        half * (flow_y * ours - flow_yo * others + push * n_y),
    )
    for c in range(3):
        high, rest = split(jumps[c])
        pieces[c, rows, first : first + LANES] = high
        pieces[c, rows, first + LANES : first + 2 * LANES] = rest
        pieces[c, rows, first + 2 * LANES : first + 3 * LANES] = high


def pair_gains(tall, comp, elements):
    narrow = lax.broadcasted_iota(jnp.int32, (comp, LANES), 1) < elements
    even, odd = tall[:comp], tall[comp:]
    return jnp.where(narrow, even, swap_halves(odd)), jnp.where(narrow, swap_halves(even), odd)


def row_chunks(step):
    return [slice(i * step, (i + 1) * step) for i in range(LANES // step)]


RING = 8


def finish_kernel(
    plan_in, wet_in, breach_in, links_in, angle_in, scale_in, metric_in,
    fields_in, pool_in, partner_in, across_in, own_in, spread_in, matrix_in, eye_in,
    *rest, t, blocks, elements, devices, leaving,
):
    outs, scratch = (rest[:1], rest[1:]) if leaving else (rest[:3], rest[3:])
    plan, wet, breach, links, angle, scale, metric, fields, pool, own, spread, matrix, eye, *scratch = scratch
    order, place, coefs, turned, halves, traces, factors, outer, pieces, near, sems, staged, *scratch = scratch
    comp, wide, used = t["comp"], t["wide"], t["used"]
    faces = blocks * 3 * elements
    width = partner_in.shape[0]
    odd = lax.axis_index("mesh") % 2
    near_rows = pl.multiple_of(faces + (1 - odd) * width, 8)
    far_rows = pl.multiple_of(faces + odd * width, 8)
    loads = [
        (plan_in, plan), (angle_in, angle), (scale_in, scale), (links_in, links), (metric_in, metric),
        (wet_in, wet), (breach_in, breach), (eye_in, eye), (own_in, own), (fields_in, fields),
        (pool_in, pool.at[pl.ds(0, faces)]), (partner_in, pool.at[pl.ds(near_rows, width)]),
        (across_in, pool.at[pl.ds(far_rows, width)]), (spread_in, spread), (matrix_in, matrix),
    ]
    n = len(loads)
    loads = start_all([pltpu.make_async_copy(a, b, sems.at[i]) for i, (a, b) in enumerate(loads)])
    index = lax.axis_index("mesh")
    loads[0].wait()
    n_leaving = scan_moves(plan, index * blocks, order, place, blocks)
    begin = 0 if leaving else n_leaving
    end = n_leaving if leaving else blocks
    n_pairs = near.shape[0] // 2
    steps = (end - begin + 2 * n_pairs - 1) // (2 * n_pairs)

    def at(i, u):
        return jnp.minimum(begin + 2 * n_pairs * i + u, end - 1)

    def indices(i):
        return [
            pltpu.make_async_copy(links_in.at[order[at(i, u)]], near.at[u], sems.at[n + u])
            for u in range(2 * n_pairs)
        ]

    def send(p):
        rows = outs[0].shape[1]
        return pltpu.make_async_copy(staged.at[p, pl.ds(0, rows)], outs[0].at[place[order[p]]], sems.at[n + 2 * n_pairs + p % RING])

    @pl.when(steps > 0)
    def _():
        start_all(indices(0))

    wait_all(loads[1:5])
    face_rows(angle, scale, links, metric, coefs, blocks, elements)
    if not leaving:
        scan_origins(plan, index, scratch[2], blocks, devices)
    wait_all(loads[5:])
    chunks = row_chunks(16)
    rows_to_pick = [
        (u, f, e) for u in range(2) for f in range(3) for e in range(elements)
    ]

    def pick(w, some):
        for u, f, e in some:
            row = f * LANES + u * elements + e
            outer[w, row : row + 1, :] = pool[pl.ds(near[2 * w + u, f * elements + e], 1), :]

    def one(i, carry):
        both = [[order[at(i, 2 * w + u)] for u in range(2)] for w in range(2)]
        inflow = [None, None]

        def lay_out(w):
            for c in range(3):
                turn_rows(
                    rows_of(fields, both[w][0], c, comp), rows_of(fields, both[w][1], c, comp), c, eye,
                    turned.at[w], halves.at[w], comp,
                )
            inner = mm(halves[w], own[...])
            for c in range(3):
                traces[w, c] = inner[c * LANES : (c + 1) * LANES]
            spread_pair(coefs, both[w], eye, spread, factors.at[w], elements)
            inflow[w] = inflow_rows(breach, both[w], t)

        def fluxes(w, rows):
            volume_rows(rows, turned.at[w], factors.at[w], 4, inflow[w][rows.start // elements], pieces.at[w])
            flux_rows(rows, traces.at[w], outer.at[w], factors.at[w], pieces.at[w], 4 * LANES, wide)

        def combine(w, c):
            gains = pair_gains(mm(matrix[...], pieces[w, c], ((1,), (1,))), comp, elements)
            for u in range(2):
                b = both[w][u]
                rate = time_step * wet[b].astype(jnp.float32)
                done = rows_of(fields, b, c, comp) + rate * gains[u]
                row = at(i, 2 * w + u) if leaving else 2 * w + u
                if c == 0:
                    staged[row, :comp] = done
                else:
                    staged[row, pl.ds(used + c - 1, comp, stride=2), :] = done

        def hand_over(w):
            for u in range(2):
                if leaving:
                    p = 4 * i + 2 * w + u

                    @pl.when(p < end)
                    def _():
                        @pl.when(p >= RING)
                        def _():
                            send(p - RING).wait()

                        send(p).start()
                else:
                    write_block(both[w][u], staged.at[2 * w + u], scratch[0], scratch[1], t, blocks)

        wait_all(indices(i))
        pick(0, rows_to_pick)
        lay_out(0)
        share = len(rows_to_pick) // len(chunks)
        for k, rows in enumerate(chunks):
            fluxes(0, rows)
            pick(1, rows_to_pick[k * share : (k + 1) * share])
            if k == 1:
                lay_out(1)
        for k, rows in enumerate(chunks):
            if k < 3:
                combine(0, k)
            fluxes(1, rows)
        for c in range(3):
            combine(1, c)

        @pl.when(i + 1 < steps)
        def _():
            start_all(indices(i + 1))

        hand_over(0)
        hand_over(1)
        return carry

    lax.fori_loop(0, steps, one, 0)
    if leaving:

        def drain(p, carry):
            send(p).wait()
            return carry

        lax.fori_loop(jnp.maximum(end - RING, 0), end, drain, 0)
    else:
        kept = ((scratch[0], outs[0]), (scratch[1], outs[1]), (scratch[2].at[pl.ds(0, outs[2].shape[0])], outs[2]))
        wait_all(start_all([pltpu.make_async_copy(a, b, sems.at[n + 2 * n_pairs + i]) for i, (a, b) in enumerate(kept)]))


def write_block(b, rows, depth, flow, t, blocks):
    pairs, members, used = t["pairs"], t["members"], t["used"]
    tile, sub = b // 8, b % 8
    for s in range(members):
        start = (s * (blocks // 8) + tile) * pairs * 8 + sub
        depth[pl.ds(start, pairs, stride=8), :] = rows[s * pairs : (s + 1) * pairs]
        for j in range(pairs):
            row = used + 2 * (s * pairs + j)
            flow[b, s, :, j * LANES : (j + 1) * LANES] = rows[row : row + 2]


def merge_kernel(
    origin_in, got_in, depth_in, flow_in, depth_out, flow_out, origin, depth, flow, got, sems, *, t, blocks
):
    def leave(b, k):
        return pltpu.make_async_copy(flow.at[b], flow_out.at[b], sems.at[3 + k % RING])

    loads = start_all(
        [
            pltpu.make_async_copy(a, b, sems.at[i])
            for i, (a, b) in enumerate(((origin_in, origin), (got_in, got), (depth_in, depth)))
        ]
    )
    wait_all(loads)

    def put(b, k):
        came = origin[b] >= 0

        @pl.when(came)
        def _():
            write_block(b, got.at[origin[b]], depth, flow, t, blocks)

            @pl.when(k >= RING)
            def _():
                leave(b, k).wait()

            leave(b, k).start()

        return k + came.astype(jnp.int32)

    arrivals = lax.fori_loop(0, blocks, put, jnp.int32(0))
    back = pltpu.make_async_copy(depth, depth_out, sems.at[2])
    back.start()

    def drain(k, carry):
        leave(0, k).wait()
        return carry

    lax.fori_loop(jnp.maximum(arrivals - RING, 0), arrivals, drain, 0)
    back.wait()


SMEM = pl.BlockSpec(memory_space=pltpu.SMEM)
HBM = pl.BlockSpec(memory_space=pltpu.HBM)
VMEM = pl.BlockSpec(memory_space=pltpu.VMEM)


def call(kernel, out_shape, n_smem, n_args, scratch, out_specs, **keys):
    return pl.pallas_call(
        kernel,
        out_shape=out_shape,
        in_specs=[SMEM] * n_smem + [HBM] * n_args,
        out_specs=out_specs,
        scratch_shapes=scratch,
        compiler_params=pltpu.CompilerParams(vmem_limit_bytes=64 << 20),
        **keys,
    )


def body(
    water_depth, momentum, metric, face_scale, face_angle, face_map, rim_faces, wet_blocks, breach, block_plan
):
    blocks, members, node_cells = water_depth.shape
    elements = metric.shape[2]
    t = static_tables(members, elements)
    comp, pairs, used = t["comp"], t["pairs"], t["used"]
    f32, bf16 = jnp.float32, jnp.bfloat16
    tiles = blocks // 8
    depth_rows = water_depth.reshape(tiles, 8, members, pairs, LANES).transpose(2, 0, 3, 1, 4).reshape(-1, LANES)
    flow_rows = momentum.transpose(0, 2, 1, 3)
    faces = face_map.size
    width = rim_faces.shape[1] // 2
    dma = pltpu.SemaphoreType.DMA

    back = jnp.asarray(np.tile(t["back"], (2, 1)), bf16)
    eye = jnp.asarray(np.tile(np.eye(LANES), (1, 2)), bf16)
    fields, pool, to_partner, to_across = call(
        functools.partial(prepare_kernel, t=t, blocks=blocks, elements=elements),
        (
            jax.ShapeDtypeStruct((blocks, 3 * comp, LANES), f32),
            jax.ShapeDtypeStruct((faces, LANES), f32),
            jax.ShapeDtypeStruct((width, LANES), f32),
            jax.ShapeDtypeStruct((width, LANES), f32),
        ),
        0, 5,
        [
            pltpu.SMEM(rim_faces.shape, jnp.int32), pltpu.VMEM(depth_rows.shape, f32), pltpu.VMEM(flow_rows.shape, f32), pltpu.VMEM(back.shape, bf16),
            pltpu.VMEM(eye.shape, bf16),
            pltpu.VMEM((2, 2, 3 * comp, LANES), f32), pltpu.VMEM((faces, LANES), f32),
            pltpu.VMEM((2, 3 * LANES, 2 * LANES), bf16), dma((6 + 2 * tiles,)),
        ],
        (HBM, HBM, VMEM, VMEM),
    )(rim_faces, depth_rows, flow_rows, back, eye)

    count = lax.axis_size("mesh")
    partners = [(i, i ^ 1) for i in range(count)]
    neighbours = [(i, i + 1 if i % 2 else i - 1) for i in range(1, count - 1)]
    across = lax.ppermute(to_across, "mesh", neighbours)
    partner = lax.ppermute(to_partner, "mesh", partners)

    lift_h, lift_l = high_low(t["lift"])
    along_r, along_s = t["along"]
    matrix = np.concatenate(
        [along_r, along_r, along_s, along_s, *(np.asarray(m, np.float32) for m in (lift_h, lift_h, lift_l))], axis=1
    )
    mats = [
        jnp.asarray(np.tile(t["own"], (2, 1)), bf16), jnp.asarray(np.tile(t["spread"], (2, 1)), bf16),
        jnp.asarray(matrix, bf16), eye,
    ]
    packed = round_up(3 * used, 8)

    i32 = jnp.int32
    block_rows = (3 * comp, LANES)
    n_pairs = 2

    def finish(leaving, out_shape, extra):
        return call(
            functools.partial(
                finish_kernel, t=t, blocks=blocks, elements=elements, devices=count, leaving=leaving
            ),
            out_shape,
            0, 15,
            [
                pltpu.SMEM(block_plan.shape, i32), pltpu.SMEM(wet_blocks.shape, i32),
                pltpu.SMEM((members, blocks), i32), pltpu.VMEM(face_map.shape, i32),
                pltpu.VMEM(face_angle.shape, f32), pltpu.VMEM(face_scale.shape, f32), pltpu.VMEM(metric.shape, f32),
                pltpu.VMEM((blocks, *block_rows), f32), pltpu.VMEM((faces + 2 * width, LANES), f32),
                *[pltpu.VMEM(m.shape, bf16) for m in mats],
                pltpu.SMEM((blocks,), i32), pltpu.SMEM((blocks,), i32), pltpu.VMEM((blocks * 16, LANES), f32),
                pltpu.VMEM((2, 3, LANES, LANES), f32), pltpu.VMEM((2, 3 * LANES, 2 * LANES), bf16),
                pltpu.VMEM((2, 3, LANES, LANES), f32), pltpu.VMEM((2, LANES, 8 * LANES), f32),
                pltpu.VMEM((2, 3 * LANES, LANES), f32), pltpu.VMEM((2, 3, LANES, 7 * LANES), bf16),
                pltpu.SMEM((2 * n_pairs, face_map.shape[1]), i32), dma((16 + 2 * n_pairs + RING,)), *extra,
            ],
            jax.tree.map(lambda _: HBM, out_shape),
        )(
            block_plan, wet_blocks, breach.T, face_map, face_angle, face_scale, metric, fields, pool, partner, across,
            *mats,
        )

    sent = finish(True, jax.ShapeDtypeStruct((count, packed, LANES), f32), [pltpu.VMEM((blocks, *block_rows), f32)])
    got = lax.all_to_all(sent, "mesh", split_axis=0, concat_axis=0, tiled=True)
    final = (jax.ShapeDtypeStruct(depth_rows.shape, f32), jax.ShapeDtypeStruct(flow_rows.shape, f32))
    whole = [pltpu.VMEM(depth_rows.shape, f32), pltpu.VMEM(flow_rows.shape, f32)]
    depth_kept, flow_kept, origin = finish(
        False, (*final, jax.ShapeDtypeStruct((LANES,), i32)),
        [pltpu.VMEM((2 * n_pairs, *block_rows), f32), *whole, pltpu.SMEM((LANES,), i32)],
    )
    depth_new, flow_new = call(
        functools.partial(merge_kernel, t=t, blocks=blocks),
        final,
        0, 4,
        [pltpu.SMEM((LANES,), i32), *whole, pltpu.VMEM((count, packed, LANES), f32), dma((3 + RING,))],
        (HBM, HBM),
        input_output_aliases={2: 0, 3: 1},
    )(origin, got, depth_kept, flow_kept)
    depth_out = depth_new.reshape(members, tiles, pairs, 8, LANES).transpose(1, 3, 0, 2, 4).reshape(water_depth.shape)
    return depth_out, flow_new.transpose(0, 2, 1, 3)


def solution(mesh):
    in_specs = (
        P(("groups", "mesh"), None, None),
        P(("groups", "mesh"), None, None, None),
        P(("groups", "mesh"), None, None),
        P(("groups", "mesh"), None),
        P(("groups", "mesh"), None),
        P(("groups", "mesh"), None),
        P(("groups", "mesh"), None),
        P(("groups", "mesh")),
        P(("groups", "mesh"), None),
        P("groups"),
    )
    out_specs = (P(("groups", "mesh"), None, None), P(("groups", "mesh"), None, None, None))
    return jax.shard_map(body, mesh=mesh, in_specs=in_specs, out_specs=out_specs, check_vma=False)
```

```python
import functools
import math

import jax
import jax.numpy as jnp
import numpy as np
from jax import lax
from jax.experimental import pallas as pl
from jax.experimental.pallas import tpu as pltpu
from jax.sharding import PartitionSpec as P

time_step = 0.01
gravity = 1.0
breach_rate = 5.0
LANES = 128


def gauss_solve(matrix, right):
    dimension = matrix.shape[0]
    augmented = np.concatenate([np.array(matrix) * 1.0, np.array(right) * 1.0], axis=1)
    for pivot_col in range(dimension):
        largest = pivot_col + int(np.argmax(np.abs(augmented[pivot_col:, pivot_col])))
        swapped = augmented[[largest, pivot_col]]
        augmented[[pivot_col, largest]] = swapped
        augmented[pivot_col] = augmented[pivot_col] / augmented[pivot_col, pivot_col]
        for row_id in range(dimension):
            if row_id != pivot_col:
                augmented[row_id] = (
                    augmented[row_id] - augmented[row_id, pivot_col] * augmented[pivot_col]
                )
    return augmented[:, dimension:]


def node_tables():
    points = np.array(
        [(across / 3.0, upward / 3.0) for upward in range(4) for across in range(4 - upward)]
    )
    powers = [(power_r, power_s) for power_r in range(4) for power_s in range(4 - power_r)]
    vander = np.zeros((10, 10))
    grad_r = np.zeros((10, 10))
    grad_s = np.zeros((10, 10))
    mono_mass = np.zeros((10, 10))
    for column, (power_r, power_s) in enumerate(powers):
        vander[:, column] = points[:, 0] ** power_r * points[:, 1] ** power_s
        if power_r > 0:
            grad_r[:, column] = power_r * points[:, 0] ** (power_r - 1) * points[:, 1] ** power_s
        if power_s > 0:
            grad_s[:, column] = power_s * points[:, 0] ** power_r * points[:, 1] ** (power_s - 1)
        for second_column, (other_r, other_s) in enumerate(powers):
            mono_mass[column, second_column] = (
                math.factorial(power_r + other_r)
                * math.factorial(power_s + other_s)
                / math.factorial(power_r + other_r + power_s + other_s + 2)
            )
    inverse = gauss_solve(vander, np.eye(10))
    mass_matrix = inverse.T @ mono_mass @ inverse
    line_points = np.arange(4) / 3.0
    line_vander = line_points[:, None] ** np.arange(4)[None, :]
    hilbert = 1.0 / (np.arange(4)[:, None] + np.arange(4)[None, :] + 1.0)
    line_inverse = gauss_solve(line_vander, np.eye(4))
    edge_mass = line_inverse.T @ hilbert @ line_inverse
    face_nodes = np.array([[0, 1, 2, 3], [3, 6, 8, 9], [9, 7, 4, 0]])
    edge_embed = np.zeros((10, 12))
    for face_id in range(3):
        for node_id in range(4):
            edge_embed[face_nodes[face_id, node_id], 4 * face_id : 4 * face_id + 4] += edge_mass[
                node_id
            ]
    lifting = gauss_solve(mass_matrix, edge_embed).reshape(10, 3, 4)
    return (
        np.asarray(grad_r @ inverse, np.float32),
        np.asarray(grad_s @ inverse, np.float32),
        np.asarray(lifting, np.float32),
        face_nodes.reshape(-1),
    )


def round_up(value, step):
    return (value + step - 1) // step * step


def static_tables(members, elements):
    deriv_r, deriv_s, lifting, face_order = node_tables()
    nodes = deriv_r.shape[0]
    pairs = nodes // 2
    used = members * pairs
    comp = round_up(used, 8)
    face_nodes = face_order.reshape(3, 4)
    wide = members * 4

    def lane_of(s, n):
        return (n % 2) * comp + s * pairs + n // 2

    own = np.zeros((LANES, LANES), np.float32)
    own[2 * comp, 3 * wide :] = 1.0
    back = np.zeros((LANES, LANES), np.float32)
    lift = np.zeros((2 * comp, LANES), np.float32)
    along = np.zeros((2, 2 * comp, LANES), np.float32)
    for s in range(members):
        for f in range(3):
            for k in range(4):
                n = int(face_nodes[f, k])
                own[lane_of(s, n), f * wide + s * 4 + k] = 1.0
                back[lane_of(s, n), f * wide + s * 4 + 3 - k] = 1.0
        for n in range(nodes):
            for f in range(3):
                for k in range(4):
                    lift[lane_of(s, n), f * wide + s * 4 + k] = lifting[n, f, k]
            for m in range(nodes):
                along[0, lane_of(s, n), lane_of(s, m)] = -deriv_r[n, m]
                along[1, lane_of(s, n), lane_of(s, m)] = -deriv_s[n, m]
            along[0, lane_of(s, n), 2 * comp + s] = breach_rate
    spread = np.zeros((16, 8 * LANES), np.float32)
    for q in range(4):
        for f in range(3):
            spread[3 * q + f, q * LANES + f * wide : q * LANES + (f + 1) * wide] = 1.0
        spread[12 + q, (4 + q) * LANES : (4 + q) * LANES + 2 * comp] = 1.0
    return dict(
        own=own, back=back, lift=lift, along=along, spread=spread,
        comp=comp, pairs=pairs, used=used, wide=wide, nodes=nodes, members=members,
    )


def high_low(matrix):
    high = matrix.astype(jnp.bfloat16)
    low = (matrix - high.astype(np.float32)).astype(jnp.bfloat16)
    return high, low


def mm(a, b, dims=((1,), (0,))):
    return lax.dot_general(a, b, (dims, ((), ())), preferred_element_type=jnp.float32)


def split(x):
    high = x.astype(jnp.bfloat16)
    return high, (x - high.astype(jnp.float32)).astype(jnp.bfloat16)


def swap_halves(x):
    return pltpu.roll(x, LANES // 2, 1)


def turn(x, eye):
    return mm(eye[...], jnp.concatenate(split(x), axis=1), ((1,), (1,)))


def turn_rows(first, second, c, eye, turned, halves, comp):
    lower = lax.broadcasted_iota(jnp.int32, (comp, LANES), 1) < LANES // 2
    even = jnp.where(lower, first, swap_halves(second))
    odd = jnp.where(lower, swap_halves(first), second)
    fill = jnp.full((LANES - 2 * comp, LANES), 1.0 if c == 0 else 0.0, jnp.float32)
    flat = turn(jnp.concatenate([even, odd, fill], axis=0), eye)
    if turned is not None:
        turned[c] = flat
    high, low = split(flat)
    halves[c * LANES : (c + 1) * LANES, :LANES] = high
    halves[c * LANES : (c + 1) * LANES, LANES:] = low


def rows_of(fields, block, c, comp):
    if c == 0:
        return fields[block, :comp]
    return fields[block, pl.ds(comp + c - 1, comp, stride=2), :]


def place_face(pieces, c, wide, lane):
    moved = [pltpu.roll(p, ((i - c) * wide) % LANES, 1) if i != c else p for i, p in enumerate(pieces)]
    return jnp.where(lane < wide, moved[0], jnp.where(lane < 2 * wide, moved[1], moved[2]))


def root(x):
    return x * lax.rsqrt(x)


def start_all(copies):
    for copy in copies:
        copy.start()
    return copies


def wait_all(copies):
    for copy in copies:
        copy.wait()


def prepare_kernel(
    rim_in, depth_in, flow_in, back_in, eye_in, fields_out, pool_out, across, partner,
    rim, depth, flow, back, eye, fields, pool, halves, sems, *, t, blocks, elements,
):
    comp, pairs, members, wide = t["comp"], t["pairs"], t["members"], t["wide"]
    odd = lax.axis_index("mesh") % 2
    tiles = blocks // 8
    steps = blocks // 2
    group = 2 * 3 * elements
    first = start_all(
        [
            pltpu.make_async_copy(depth_in, depth, sems.at[0]), pltpu.make_async_copy(back_in, back, sems.at[1]),
            pltpu.make_async_copy(eye_in, eye, sems.at[2]), pltpu.make_async_copy(rim_in, rim, sems.at[3]),
        ]
    )

    def part(tile):
        rows = pl.ds(8 * tile, 8)
        return pltpu.make_async_copy(flow_in.at[rows], flow.at[rows], sems.at[4 + tile])

    def field_part(tile):
        rows = pl.ds(8 * tile, 8)
        return pltpu.make_async_copy(fields.at[rows], fields_out.at[rows], sems.at[4 + tiles + tile])

    def pool_part(i):
        lines = pl.ds(group * i, group)
        return pltpu.make_async_copy(pool.at[lines], pool_out.at[lines], sems.at[4 + 2 * tiles + i])

    start_all([part(tile) for tile in range(tiles)])
    wait_all(first)

    def build(i):
        for u in range(2):
            b = 2 * i + u
            tile, sub = b // 8, b % 8
            fields[b, comp - 8 : comp] = jnp.full((8, LANES), 1.0, jnp.float32)
            fields[b, 3 * comp - 16 : 3 * comp] = jnp.zeros((16, LANES), jnp.float32)
            for s in range(members):
                start = (s * tiles + tile) * pairs * 8 + sub
                fields[b, s * pairs : (s + 1) * pairs] = depth[pl.ds(start, pairs, stride=8), :]
                for j in range(pairs):
                    row = comp + 2 * (s * pairs + j)
                    fields[b, row : row + 2] = flow[b, s, :, j * LANES : (j + 1) * LANES]

    def turn_of(i):
        for c in range(3):
            turn_rows(
                rows_of(fields, 2 * i, c, comp), rows_of(fields, 2 * i + 1, c, comp), c, eye, None, halves, comp
            )

    def faces_of(i):
        rows = mm(halves[...], back[...])
        lane = lax.broadcasted_iota(jnp.int32, (LANES, LANES), 1)
        pieces = [rows[c * LANES : (c + 1) * LANES] for c in range(3)]
        for f in range(3):
            face = place_face(pieces, f, wide, lane)
            for u in range(2):
                at = ((2 * i + u) * 3 + f) * elements
                pool[pl.ds(at, elements), :] = face[u * elements : (u + 1) * elements]

    part(0).wait()
    build(0)
    turn_of(0)
    build(1)

    def one(i, carry):
        @pl.when(i % 4 == 0)
        def _():
            part(i // 4).wait()

        faces_of(i - 2)
        turn_of(i - 1)
        build(i)
        pool_part(i - 2).start()

        @pl.when(i % 4 == 3)
        def _():
            field_part(i // 4).start()

        return carry

    lax.fori_loop(2, steps, one, 0)
    faces_of(steps - 2)
    turn_of(steps - 1)
    pool_part(steps - 2).start()
    faces_of(steps - 1)
    pool_part(steps - 1).start()
    width = partner.shape[0]
    near, far = (1 - odd) * width, odd * width

    def pick(i, carry):
        for u in range(32):
            r = i * 32 + u
            partner[pl.ds(r, 1), :] = pool[pl.ds(rim[0, near + r], 1), :]
            across[pl.ds(r, 1), :] = pool[pl.ds(rim[0, far + r], 1), :]
        return carry

    lax.fori_loop(0, width // 32, pick, 0)
    for tile in range(tiles):
        field_part(tile).wait()
    for i in range(steps):
        pool_part(i).wait()


def scan_moves(plan, base, order, place, blocks):
    def one(i, carry):
        leaving, staying = carry
        slot = plan[base + i]
        away = jnp.logical_or(slot < base, slot >= base + blocks).astype(jnp.int32)
        order[jnp.where(away == 1, leaving, blocks - 1 - staying)] = i
        place[i] = lax.div(slot, jnp.int32(blocks))
        return leaving + away, staying + 1 - away

    return lax.fori_loop(0, blocks, one, (jnp.int32(0), jnp.int32(0)))[0]


def scan_origins(plan, own, origin, blocks, devices):
    def device(d, carry):
        mark = jnp.where(d == own, -1, d)
        for i in range(blocks):
            slot = plan[d * blocks + i] - own * blocks
            origin[jnp.where(jnp.logical_and(slot >= 0, slot < blocks), slot, blocks)] = mark
        return carry

    lax.fori_loop(0, devices, device, 0)


def face_rows(angle, scale, links, metric, coefs, blocks, elements):
    shape = (blocks, 3 * elements)
    own = lax.broadcasted_iota(jnp.int32, shape, 0) * (3 * elements) + lax.broadcasted_iota(jnp.int32, shape, 1)
    free = jnp.where(links[...] == own, 0.0, 1.0)
    lower = lax.broadcasted_iota(jnp.int32, (blocks, LANES), 1) < elements
    for q, value in enumerate((jnp.cos(angle[...]), jnp.sin(angle[...]), scale[...], free)):
        two = value[:, :LANES]
        swapped = swap_halves(two)
        third = value[:, LANES:]
        faces = (
            jnp.where(lower, two, swapped), jnp.where(lower, swapped, two), jnp.concatenate([third, third], axis=1)
        )
        for f in range(3):
            coefs[pl.ds(3 * q + f, blocks, stride=16), :] = faces[f]
    for b in range(blocks):
        factors = metric[b]
        coefs[b * 16 + 12 : b * 16 + 16] = jnp.concatenate([factors, factors], axis=1)


def spread_pair(coefs, both, eye, spread, factors, elements):
    lower = lax.broadcasted_iota(jnp.int32, (16, LANES), 1) < elements
    values = jnp.where(lower, coefs[pl.ds(both[0] * 16, 16), :], coefs[pl.ds(both[1] * 16, 16), :])
    rough = values.astype(jnp.bfloat16).astype(jnp.float32)
    stacked = jnp.concatenate([rough, values - rough], axis=0).astype(jnp.bfloat16)
    stacked = mm(eye[:, :LANES], stacked, ((1,), (1,))).astype(jnp.bfloat16)
    factors[...] = mm(stacked, spread[...])


def inflow_rows(breach, both, t):
    rows = []
    for b in both:
        row = jnp.zeros((1, LANES), jnp.float32)
        for s in range(t["members"]):
            level = breach[s, b].astype(jnp.float32)
            row = jnp.where(lax.broadcasted_iota(jnp.int32, (1, LANES), 1) == 2 * t["comp"] + s, level, row)
        rows.append(row)
    return rows


def volume_rows(rows, turned, factors, first, inflow, pieces):
    rx, sx, ry, sy = (factors[rows, q * LANES : (q + 1) * LANES] for q in range(first, first + 4))
    height, flow_x, flow_y = (turned[c, rows] for c in range(3))
    pressure = 0.5 * gravity * height * height
    inverse = 1.0 / height
    speed_x = flow_x * inverse
    speed_y = flow_y * inverse
    cross = flow_y * speed_x
    flux_f = (flow_x, flow_x * speed_x + pressure, cross)
    flux_g = (flow_y, cross, flow_y * speed_y + pressure)
    for c in range(3):
        along_r = rx * flux_f[c] + ry * flux_g[c]
        along_s = sx * flux_f[c] + sy * flux_g[c]
        if c == 0:
            along_r = along_r + inflow
        pieces[c, rows, 0:LANES], pieces[c, rows, LANES : 2 * LANES] = split(along_r)
        pieces[c, rows, 2 * LANES : 3 * LANES], pieces[c, rows, 3 * LANES : 4 * LANES] = split(along_s)


def flux_rows(rows, traces, outer, factors, pieces, first, wide):
    lane = lax.broadcasted_iota(jnp.int32, (rows.stop - rows.start, LANES), 1)
    n_x, n_y, scale, free = (factors[rows, q * LANES : (q + 1) * LANES] for q in range(4))
    theirs = [outer[f * LANES + rows.start : f * LANES + rows.stop] for f in range(3)]
    height, flow_x, flow_y = (traces[c, rows] for c in range(3))
    is_wall = free < 0.5
    through = flow_x * n_x + flow_y * n_y
    twice = through + through
    height_o = jnp.where(is_wall, height, place_face(theirs, 0, wide, lane))
    flow_xo = jnp.where(is_wall, flow_x - twice * n_x, place_face(theirs, 1, wide, lane))
    flow_yo = jnp.where(is_wall, flow_y - twice * n_y, place_face(theirs, 2, wide, lane))
    speed = through / height
    speed_o = (flow_xo * n_x + flow_yo * n_y) / height_o
    fast = jnp.maximum(
        jnp.abs(speed) + root(gravity * height), jnp.abs(speed_o) + root(gravity * height_o)
    )
    ours, others = speed - fast, speed_o - fast
    half = 0.5 * scale
    push = 0.5 * gravity * (height * height - height_o * height_o)
    jumps = (
        half * (height * ours - height_o * others),
        half * (flow_x * ours - flow_xo * others + push * n_x),
        half * (flow_y * ours - flow_yo * others + push * n_y),
    )
    for c in range(3):
        high, rest = split(jumps[c])
        pieces[c, rows, first : first + LANES] = high
        pieces[c, rows, first + LANES : first + 2 * LANES] = rest
        pieces[c, rows, first + 2 * LANES : first + 3 * LANES] = high


def pair_gains(tall, comp, elements):
    narrow = lax.broadcasted_iota(jnp.int32, (comp, LANES), 1) < elements
    even, odd = tall[:comp], tall[comp:]
    return jnp.where(narrow, even, swap_halves(odd)), jnp.where(narrow, swap_halves(even), odd)


def row_chunks(step):
    return [slice(i * step, (i + 1) * step) for i in range(LANES // step)]


RING = 8


def finish_kernel(
    plan_in, wet_in, breach_in, links_in, angle_in, scale_in, metric_in,
    fields_in, pool_in, partner_in, across_in, own_in, spread_in, matrix_in, eye_in,
    *rest, t, blocks, elements, devices, leaving,
):
    outs, scratch = (rest[:1], rest[1:]) if leaving else (rest[:3], rest[3:])
    plan, wet, breach, links, angle, scale, metric, fields, pool, own, spread, matrix, eye, *scratch = scratch
    order, place, coefs, turned, halves, traces, factors, outer, pieces, near, sems, staged, *scratch = scratch
    comp, wide, used = t["comp"], t["wide"], t["used"]
    faces = blocks * 3 * elements
    width = partner_in.shape[0]
    odd = lax.axis_index("mesh") % 2
    near_rows = pl.multiple_of(faces + (1 - odd) * width, 8)
    far_rows = pl.multiple_of(faces + odd * width, 8)
    loads = [
        (plan_in, plan), (angle_in, angle), (scale_in, scale), (links_in, links), (metric_in, metric),
        (fields_in, fields), (wet_in, wet), (breach_in, breach), (eye_in, eye), (own_in, own),
        (spread_in, spread), (matrix_in, matrix), (pool_in, pool.at[pl.ds(0, faces)]),
        (partner_in, pool.at[pl.ds(near_rows, width)]), (across_in, pool.at[pl.ds(far_rows, width)]),
    ]
    n = len(loads)
    loads = start_all([pltpu.make_async_copy(a, b, sems.at[i]) for i, (a, b) in enumerate(loads)])
    index = lax.axis_index("mesh")
    loads[0].wait()
    n_leaving = scan_moves(plan, index * blocks, order, place, blocks)
    begin = 0 if leaving else n_leaving
    end = n_leaving if leaving else blocks
    n_pairs = near.shape[0] // 2
    steps = (end - begin + 2 * n_pairs - 1) // (2 * n_pairs)

    def at(i, u):
        return jnp.maximum(jnp.minimum(begin + 2 * n_pairs * i + u, end - 1), 0)

    def indices(i):
        return [
            pltpu.make_async_copy(links_in.at[order[at(i, u)]], near.at[u], sems.at[n + u])
            for u in range(2 * n_pairs)
        ]

    def send(p):
        rows = outs[0].shape[1]
        return pltpu.make_async_copy(staged.at[p, pl.ds(0, rows)], outs[0].at[place[order[p]]], sems.at[n + 2 * n_pairs + p % RING])

    @pl.when(steps > 0)
    def _():
        start_all(indices(0))

    wait_all(loads[1:5])
    face_rows(angle, scale, links, metric, coefs, blocks, elements)
    if not leaving:
        scan_origins(plan, index, scratch[2], blocks, devices)
    wait_all(loads[5:-3])
    chunks = row_chunks(16)

    def pick(w, rows):
        for f in range(3):
            for line in range(rows.start, rows.stop):
                v = near[2 * w + line // elements, f * elements + line % elements]
                outer[w, f * LANES + line : f * LANES + line + 1, :] = pool[pl.ds(v, 1), :]

    def pair_of(i, w):
        return [order[at(i, 2 * w + u)] for u in range(2)]

    def lay_out(w, pair):
        for c in range(3):
            turn_rows(
                rows_of(fields, pair[0], c, comp), rows_of(fields, pair[1], c, comp), c, eye,
                turned.at[w], halves.at[w], comp,
            )
        inner = mm(halves[w], own[...])
        for c in range(3):
            traces[w, c] = inner[c * LANES : (c + 1) * LANES]
        spread_pair(coefs, pair, eye, spread, factors.at[w], elements)

    def one(i, carry):
        both = [pair_of(i, w) for w in range(2)]
        inflow = [inflow_rows(breach, pair, t) for pair in both]

        def fluxes(w, rows):
            volume_rows(rows, turned.at[w], factors.at[w], 4, inflow[w][rows.start // elements], pieces.at[w])
            flux_rows(rows, traces.at[w], outer.at[w], factors.at[w], pieces.at[w], 4 * LANES, wide)

        def combine(w, c):
            gains = pair_gains(mm(matrix[...], pieces[w, c], ((1,), (1,))), comp, elements)
            for u in range(2):
                b = both[w][u]
                rate = time_step * wet[b].astype(jnp.float32)
                done = rows_of(fields, b, c, comp) + rate * gains[u]
                row = at(i, 2 * w + u) if leaving else 2 * w + u
                if c == 0:
                    staged[row, :comp] = done
                else:
                    staged[row, pl.ds(used + c - 1, comp, stride=2), :] = done

        def hand_over(w):
            for u in range(2):
                if leaving:
                    p = 4 * i + 2 * w + u

                    @pl.when(p < end)
                    def _():
                        @pl.when(p >= RING)
                        def _():
                            send(p - RING).wait()

                        send(p).start()
                else:
                    write_depth(both[w][u], staged.at[2 * w + u], scratch[0], t, blocks)
                    write_flow(both[w][u], staged.at[2 * w + u], scratch[1], t)

        wait_all(indices(i))
        for rows in chunks:
            pick(0, rows)
        lay_out(1, both[1])
        for rows in chunks:
            fluxes(0, rows)
            pick(1, rows)
        for k, rows in enumerate(chunks):
            if k < 3:
                combine(0, k)
            fluxes(1, rows)
        for c in range(3):
            combine(1, c)

        @pl.when(i + 1 < steps)
        def _():
            start_all(indices(i + 1))
            lay_out(0, pair_of(i + 1, 0))

        hand_over(0)
        hand_over(1)
        return carry

    lay_out(0, pair_of(0, 0))
    wait_all(loads[-3:])
    lax.fori_loop(0, steps, one, 0)
    if leaving:

        def drain(p, carry):
            send(p).wait()
            return carry

        lax.fori_loop(jnp.maximum(end - RING, 0), end, drain, 0)
    else:
        kept = ((scratch[0], outs[0]), (scratch[1], outs[1]), (scratch[2].at[pl.ds(0, outs[2].shape[0])], outs[2]))
        wait_all(start_all([pltpu.make_async_copy(a, b, sems.at[n + 2 * n_pairs + i]) for i, (a, b) in enumerate(kept)]))


def write_depth(b, rows, depth, t, blocks):
    pairs, members = t["pairs"], t["members"]
    tile, sub = b // 8, b % 8
    for s in range(members):
        start = (s * (blocks // 8) + tile) * pairs * 8 + sub
        depth[pl.ds(start, pairs, stride=8), :] = rows[s * pairs : (s + 1) * pairs]


def write_flow(b, rows, flow, t):
    pairs, members, used = t["pairs"], t["members"], t["used"]
    for s in range(members):
        for j in range(pairs):
            row = used + 2 * (s * pairs + j)
            flow[b, s, :, j * LANES : (j + 1) * LANES] = rows[row : row + 2]


def merge_kernel(
    origin_in, got_in, depth_in, flow_in, depth_out, flow_out, origin, depth, flow, got, sems, *, t, blocks
):
    def leave(b, k):
        return pltpu.make_async_copy(flow.at[b], flow_out.at[b], sems.at[3 + k % RING])

    loads = start_all(
        [
            pltpu.make_async_copy(a, b, sems.at[i])
            for i, (a, b) in enumerate(((origin_in, origin), (got_in, got), (depth_in, depth)))
        ]
    )
    wait_all(loads)

    def put_depth(b, carry):
        @pl.when(origin[b] >= 0)
        def _():
            write_depth(b, got.at[origin[b]], depth, t, blocks)

        return carry

    lax.fori_loop(0, blocks, put_depth, 0)
    back = pltpu.make_async_copy(depth, depth_out, sems.at[2])
    back.start()

    def put(b, k):
        came = origin[b] >= 0

        @pl.when(came)
        def _():
            write_flow(b, got.at[origin[b]], flow, t)

            @pl.when(k >= RING)
            def _():
                leave(b, k).wait()

            leave(b, k).start()

        return k + came.astype(jnp.int32)

    arrivals = lax.fori_loop(0, blocks, put, jnp.int32(0))

    def drain(k, carry):
        leave(0, k).wait()
        return carry

    lax.fori_loop(jnp.maximum(arrivals - RING, 0), arrivals, drain, 0)
    back.wait()


SMEM = pl.BlockSpec(memory_space=pltpu.SMEM)
HBM = pl.BlockSpec(memory_space=pltpu.HBM)
VMEM = pl.BlockSpec(memory_space=pltpu.VMEM)


def call(kernel, out_shape, n_smem, n_args, scratch, out_specs, **keys):
    return pl.pallas_call(
        kernel,
        out_shape=out_shape,
        in_specs=[SMEM] * n_smem + [HBM] * n_args,
        out_specs=out_specs,
        scratch_shapes=scratch,
        compiler_params=pltpu.CompilerParams(vmem_limit_bytes=64 << 20),
        **keys,
    )


def body(
    water_depth, momentum, metric, face_scale, face_angle, face_map, rim_faces, wet_blocks, breach, block_plan
):
    blocks, members, node_cells = water_depth.shape
    elements = metric.shape[2]
    t = static_tables(members, elements)
    comp, pairs, used = t["comp"], t["pairs"], t["used"]
    f32, bf16 = jnp.float32, jnp.bfloat16
    tiles = blocks // 8
    depth_rows = water_depth.reshape(tiles, 8, members, pairs, LANES).transpose(2, 0, 3, 1, 4).reshape(-1, LANES)
    flow_rows = momentum.transpose(0, 2, 1, 3)
    faces = face_map.size
    width = rim_faces.shape[1] // 2
    dma = pltpu.SemaphoreType.DMA

    back = jnp.asarray(np.tile(t["back"], (2, 1)), bf16)
    eye = jnp.asarray(np.tile(np.eye(LANES), (1, 2)), bf16)
    fields, pool, to_across, to_partner = call(
        functools.partial(prepare_kernel, t=t, blocks=blocks, elements=elements),
        (
            jax.ShapeDtypeStruct((blocks, 3 * comp, LANES), f32),
            jax.ShapeDtypeStruct((faces, LANES), f32),
            jax.ShapeDtypeStruct((width, LANES), f32),
            jax.ShapeDtypeStruct((width, LANES), f32),
        ),
        0, 5,
        [
            pltpu.SMEM(rim_faces.shape, jnp.int32), pltpu.VMEM(depth_rows.shape, f32), pltpu.VMEM(flow_rows.shape, f32), pltpu.VMEM(back.shape, bf16),
            pltpu.VMEM(eye.shape, bf16),
            pltpu.VMEM((blocks, 3 * comp, LANES), f32), pltpu.VMEM((faces, LANES), f32),
            pltpu.VMEM((3 * LANES, 2 * LANES), bf16), dma((4 + 2 * tiles + blocks // 2,)),
        ],
        (HBM, HBM, VMEM, VMEM),
    )(rim_faces, depth_rows, flow_rows, back, eye)

    count = lax.axis_size("mesh")
    partners = [(i, i ^ 1) for i in range(count)]
    neighbours = [(i, i + 1 if i % 2 else i - 1) for i in range(1, count - 1)]
    partner = lax.ppermute(to_partner, "mesh", partners)
    across = lax.ppermute(to_across, "mesh", neighbours)

    lift_h, lift_l = high_low(t["lift"])
    along_r, along_s = t["along"]
    matrix = np.concatenate(
        [along_r, along_r, along_s, along_s, *(np.asarray(m, np.float32) for m in (lift_h, lift_h, lift_l))], axis=1
    )
    mats = [
        jnp.asarray(np.tile(t["own"], (2, 1)), bf16), jnp.asarray(np.tile(t["spread"], (2, 1)), bf16),
        jnp.asarray(matrix, bf16), eye,
    ]
    packed = round_up(3 * used, 8)

    i32 = jnp.int32
    block_rows = (3 * comp, LANES)
    n_pairs = 2

    def finish(leaving, out_shape, extra):
        return call(
            functools.partial(
                finish_kernel, t=t, blocks=blocks, elements=elements, devices=count, leaving=leaving
            ),
            out_shape,
            0, 15,
            [
                pltpu.SMEM(block_plan.shape, i32), pltpu.SMEM(wet_blocks.shape, i32),
                pltpu.SMEM((members, blocks), i32), pltpu.VMEM(face_map.shape, i32),
                pltpu.VMEM(face_angle.shape, f32), pltpu.VMEM(face_scale.shape, f32), pltpu.VMEM(metric.shape, f32),
                pltpu.VMEM((blocks, *block_rows), f32), pltpu.VMEM((faces + 2 * width, LANES), f32),
                *[pltpu.VMEM(m.shape, bf16) for m in mats],
                pltpu.SMEM((blocks,), i32), pltpu.SMEM((blocks,), i32), pltpu.VMEM((blocks * 16, LANES), f32),
                pltpu.VMEM((2, 3, LANES, LANES), f32), pltpu.VMEM((2, 3 * LANES, 2 * LANES), bf16),
                pltpu.VMEM((2, 3, LANES, LANES), f32), pltpu.VMEM((2, LANES, 8 * LANES), f32),
                pltpu.VMEM((2, 3 * LANES, LANES), f32), pltpu.VMEM((2, 3, LANES, 7 * LANES), bf16),
                pltpu.SMEM((2 * n_pairs, face_map.shape[1]), i32), dma((16 + 2 * n_pairs + RING,)), *extra,
            ],
            jax.tree.map(lambda _: HBM, out_shape),
        )(
            block_plan, wet_blocks, breach.T, face_map, face_angle, face_scale, metric, fields, pool, partner, across,
            *mats,
        )

    sent = finish(True, jax.ShapeDtypeStruct((count, packed, LANES), f32), [pltpu.VMEM((blocks, *block_rows), f32)])
    got = lax.all_to_all(sent, "mesh", split_axis=0, concat_axis=0, tiled=True)
    final = (jax.ShapeDtypeStruct(depth_rows.shape, f32), jax.ShapeDtypeStruct(flow_rows.shape, f32))
    whole = [pltpu.VMEM(depth_rows.shape, f32), pltpu.VMEM(flow_rows.shape, f32)]
    depth_kept, flow_kept, origin = finish(
        False, (*final, jax.ShapeDtypeStruct((LANES,), i32)),
        [pltpu.VMEM((2 * n_pairs, *block_rows), f32), *whole, pltpu.SMEM((LANES,), i32)],
    )
    depth_new, flow_new = call(
        functools.partial(merge_kernel, t=t, blocks=blocks),
        final,
        0, 4,
        [pltpu.SMEM((LANES,), i32), *whole, pltpu.VMEM((count, packed, LANES), f32), dma((3 + RING,))],
        (HBM, HBM),
        input_output_aliases={2: 0, 3: 1},
    )(origin, got, depth_kept, flow_kept)
    depth_out = depth_new.reshape(members, tiles, pairs, 8, LANES).transpose(1, 3, 0, 2, 4).reshape(water_depth.shape)
    return depth_out, flow_new.transpose(0, 2, 1, 3)


def solution(mesh):
    in_specs = (
        P(("groups", "mesh"), None, None),
        P(("groups", "mesh"), None, None, None),
        P(("groups", "mesh"), None, None),
        P(("groups", "mesh"), None),
        P(("groups", "mesh"), None),
        P(("groups", "mesh"), None),
        P(("groups", "mesh"), None),
        P(("groups", "mesh")),
        P(("groups", "mesh"), None),
        P("groups"),
    )
    out_specs = (P(("groups", "mesh"), None, None), P(("groups", "mesh"), None, None, None))
    return jax.shard_map(body, mesh=mesh, in_specs=in_specs, out_specs=out_specs, check_vma=False)
```

```python
import functools
import math

import jax
import jax.numpy as jnp
import numpy as np
from jax import lax
from jax.experimental import pallas as pl
from jax.experimental.pallas import tpu as pltpu
from jax.sharding import PartitionSpec as P

time_step = 0.01
gravity = 1.0
breach_rate = 5.0
LANES = 128


def gauss_solve(matrix, right):
    dimension = matrix.shape[0]
    augmented = np.concatenate([np.array(matrix) * 1.0, np.array(right) * 1.0], axis=1)
    for pivot_col in range(dimension):
        largest = pivot_col + int(np.argmax(np.abs(augmented[pivot_col:, pivot_col])))
        swapped = augmented[[largest, pivot_col]]
        augmented[[pivot_col, largest]] = swapped
        augmented[pivot_col] = augmented[pivot_col] / augmented[pivot_col, pivot_col]
        for row_id in range(dimension):
            if row_id != pivot_col:
                augmented[row_id] = (
                    augmented[row_id] - augmented[row_id, pivot_col] * augmented[pivot_col]
                )
    return augmented[:, dimension:]


def node_tables():
    points = np.array(
        [(across / 3.0, upward / 3.0) for upward in range(4) for across in range(4 - upward)]
    )
    powers = [(power_r, power_s) for power_r in range(4) for power_s in range(4 - power_r)]
    vander = np.zeros((10, 10))
    grad_r = np.zeros((10, 10))
    grad_s = np.zeros((10, 10))
    mono_mass = np.zeros((10, 10))
    for column, (power_r, power_s) in enumerate(powers):
        vander[:, column] = points[:, 0] ** power_r * points[:, 1] ** power_s
        if power_r > 0:
            grad_r[:, column] = power_r * points[:, 0] ** (power_r - 1) * points[:, 1] ** power_s
        if power_s > 0:
            grad_s[:, column] = power_s * points[:, 0] ** power_r * points[:, 1] ** (power_s - 1)
        for second_column, (other_r, other_s) in enumerate(powers):
            mono_mass[column, second_column] = (
                math.factorial(power_r + other_r)
                * math.factorial(power_s + other_s)
                / math.factorial(power_r + other_r + power_s + other_s + 2)
            )
    inverse = gauss_solve(vander, np.eye(10))
    mass_matrix = inverse.T @ mono_mass @ inverse
    line_points = np.arange(4) / 3.0
    line_vander = line_points[:, None] ** np.arange(4)[None, :]
    hilbert = 1.0 / (np.arange(4)[:, None] + np.arange(4)[None, :] + 1.0)
    line_inverse = gauss_solve(line_vander, np.eye(4))
    edge_mass = line_inverse.T @ hilbert @ line_inverse
    face_nodes = np.array([[0, 1, 2, 3], [3, 6, 8, 9], [9, 7, 4, 0]])
    edge_embed = np.zeros((10, 12))
    for face_id in range(3):
        for node_id in range(4):
            edge_embed[face_nodes[face_id, node_id], 4 * face_id : 4 * face_id + 4] += edge_mass[
                node_id
            ]
    lifting = gauss_solve(mass_matrix, edge_embed).reshape(10, 3, 4)
    return (
        np.asarray(grad_r @ inverse, np.float32),
        np.asarray(grad_s @ inverse, np.float32),
        np.asarray(lifting, np.float32),
        face_nodes.reshape(-1),
    )


def round_up(value, step):
    return (value + step - 1) // step * step


def static_tables(members, elements):
    deriv_r, deriv_s, lifting, face_order = node_tables()
    nodes = deriv_r.shape[0]
    pairs = nodes // 2
    used = members * pairs
    comp = round_up(used, 8)
    face_nodes = face_order.reshape(3, 4)
    wide = members * 4

    def lane_of(s, n):
        return (n % 2) * comp + s * pairs + n // 2

    own = np.zeros((LANES, LANES), np.float32)
    own[2 * comp, 3 * wide :] = 1.0
    back = np.zeros((LANES, LANES), np.float32)
    lift = np.zeros((2 * comp, LANES), np.float32)
    along = np.zeros((2, 2 * comp, LANES), np.float32)
    for s in range(members):
        for f in range(3):
            for k in range(4):
                n = int(face_nodes[f, k])
                own[lane_of(s, n), f * wide + s * 4 + k] = 1.0
                back[lane_of(s, n), f * wide + s * 4 + 3 - k] = 1.0
        for n in range(nodes):
            for f in range(3):
                for k in range(4):
                    lift[lane_of(s, n), f * wide + s * 4 + k] = lifting[n, f, k]
            for m in range(nodes):
                along[0, lane_of(s, n), lane_of(s, m)] = -deriv_r[n, m]
                along[1, lane_of(s, n), lane_of(s, m)] = -deriv_s[n, m]
            along[0, lane_of(s, n), 2 * comp + s] = breach_rate
    spread = np.zeros((16, 8 * LANES), np.float32)
    for q in range(4):
        for f in range(3):
            spread[3 * q + f, q * LANES + f * wide : q * LANES + (f + 1) * wide] = 1.0
        spread[12 + q, (4 + q) * LANES : (4 + q) * LANES + 2 * comp] = 1.0
    return dict(
        own=own, back=back, lift=lift, along=along, spread=spread,
        comp=comp, pairs=pairs, used=used, wide=wide, nodes=nodes, members=members,
    )


def high_low(matrix):
    high = matrix.astype(jnp.bfloat16)
    low = (matrix - high.astype(np.float32)).astype(jnp.bfloat16)
    return high, low


def mm(a, b, dims=((1,), (0,))):
    return lax.dot_general(a, b, (dims, ((), ())), preferred_element_type=jnp.float32)


def split(x):
    high = x.astype(jnp.bfloat16)
    return high, (x - high.astype(jnp.float32)).astype(jnp.bfloat16)


def swap_halves(x):
    return pltpu.roll(x, LANES // 2, 1)


def turn(x, eye):
    return mm(eye[...], jnp.concatenate(split(x), axis=1), ((1,), (1,)))


def turn_rows(first, second, c, eye, turned, halves, comp):
    lower = lax.broadcasted_iota(jnp.int32, (comp, LANES), 1) < LANES // 2
    even = jnp.where(lower, first, swap_halves(second))
    odd = jnp.where(lower, swap_halves(first), second)
    fill = jnp.full((LANES - 2 * comp, LANES), 1.0 if c == 0 else 0.0, jnp.float32)
    flat = turn(jnp.concatenate([even, odd, fill], axis=0), eye)
    if turned is not None:
        turned[c] = flat
    high, low = split(flat)
    halves[c * LANES : (c + 1) * LANES, :LANES] = high
    halves[c * LANES : (c + 1) * LANES, LANES:] = low


def rows_of(fields, block, c, comp):
    if c == 0:
        return fields[block, :comp]
    return fields[block, pl.ds(comp + c - 1, comp, stride=2), :]


def place_face(pieces, c, wide, lane):
    moved = [pltpu.roll(p, ((i - c) * wide) % LANES, 1) if i != c else p for i, p in enumerate(pieces)]
    return jnp.where(lane < wide, moved[0], jnp.where(lane < 2 * wide, moved[1], moved[2]))


def root(x):
    return x * lax.rsqrt(x)


def start_all(copies):
    for copy in copies:
        copy.start()
    return copies


def wait_all(copies):
    for copy in copies:
        copy.wait()


def prepare_kernel(
    rim_in, depth_in, flow_in, back_in, eye_in, fields_out, pool_out, across, partner,
    rim, depth, flow, back, eye, fields, pool, halves, sems, *, t, blocks, elements,
):
    comp, pairs, members, wide = t["comp"], t["pairs"], t["members"], t["wide"]
    odd = lax.axis_index("mesh") % 2
    tiles = blocks // 8
    steps = blocks // 2
    group = 2 * 3 * elements
    first = start_all(
        [
            pltpu.make_async_copy(depth_in, depth, sems.at[0]), pltpu.make_async_copy(back_in, back, sems.at[1]),
            pltpu.make_async_copy(eye_in, eye, sems.at[2]), pltpu.make_async_copy(rim_in, rim, sems.at[3]),
        ]
    )

    def part(tile):
        rows = pl.ds(8 * tile, 8)
        return pltpu.make_async_copy(flow_in.at[rows], flow.at[rows], sems.at[4 + tile])

    def field_part(tile):
        rows = pl.ds(8 * tile, 8)
        return pltpu.make_async_copy(fields.at[rows], fields_out.at[rows], sems.at[4 + tiles + tile])

    def pool_part(i):
        lines = pl.ds(group * i, group)
        return pltpu.make_async_copy(pool.at[lines], pool_out.at[lines], sems.at[4 + 2 * tiles + i])

    start_all([part(tile) for tile in range(tiles)])
    wait_all(first)

    def build(i):
        for u in range(2):
            b = 2 * i + u
            tile, sub = b // 8, b % 8
            fields[b, comp - 8 : comp] = jnp.full((8, LANES), 1.0, jnp.float32)
            fields[b, 3 * comp - 16 : 3 * comp] = jnp.zeros((16, LANES), jnp.float32)
            for s in range(members):
                start = (s * tiles + tile) * pairs * 8 + sub
                fields[b, s * pairs : (s + 1) * pairs] = depth[pl.ds(start, pairs, stride=8), :]
                for j in range(pairs):
                    row = comp + 2 * (s * pairs + j)
                    fields[b, row : row + 2] = flow[b, s, :, j * LANES : (j + 1) * LANES]

    def turn_of(i):
        for c in range(3):
            turn_rows(
                rows_of(fields, 2 * i, c, comp), rows_of(fields, 2 * i + 1, c, comp), c, eye, None, halves, comp
            )

    def faces_of(i):
        rows = mm(halves[...], back[...])
        lane = lax.broadcasted_iota(jnp.int32, (LANES, LANES), 1)
        pieces = [rows[c * LANES : (c + 1) * LANES] for c in range(3)]
        for f in range(3):
            face = place_face(pieces, f, wide, lane)
            for u in range(2):
                at = ((2 * i + u) * 3 + f) * elements
                pool[pl.ds(at, elements), :] = face[u * elements : (u + 1) * elements]

    part(0).wait()
    build(0)
    turn_of(0)
    build(1)

    def one(i, carry):
        @pl.when(i % 4 == 0)
        def _():
            part(i // 4).wait()

        faces_of(i - 2)
        turn_of(i - 1)
        build(i)
        pool_part(i - 2).start()

        @pl.when(i % 4 == 3)
        def _():
            field_part(i // 4).start()

        return carry

    lax.fori_loop(2, steps, one, 0)
    faces_of(steps - 2)
    turn_of(steps - 1)
    pool_part(steps - 2).start()
    faces_of(steps - 1)
    pool_part(steps - 1).start()
    width = partner.shape[0]
    near, far = (1 - odd) * width, odd * width

    def pick(i, carry):
        for u in range(32):
            r = i * 32 + u
            partner[pl.ds(r, 1), :] = pool[pl.ds(rim[0, near + r], 1), :]
            across[pl.ds(r, 1), :] = pool[pl.ds(rim[0, far + r], 1), :]
        return carry

    lax.fori_loop(0, width // 32, pick, 0)
    for tile in range(tiles):
        field_part(tile).wait()
    for i in range(steps):
        pool_part(i).wait()


def scan_moves(plan, base, order, place, blocks):
    def one(i, carry):
        leaving, staying = carry
        slot = plan[base + i]
        away = jnp.logical_or(slot < base, slot >= base + blocks).astype(jnp.int32)
        order[jnp.where(away == 1, leaving, blocks - 1 - staying)] = i
        place[i] = lax.div(slot, jnp.int32(blocks))
        return leaving + away, staying + 1 - away

    return lax.fori_loop(0, blocks, one, (jnp.int32(0), jnp.int32(0)))[0]


def scan_origins(plan, own, origin, blocks, devices):
    def device(d, carry):
        mark = jnp.where(d == own, -1, d)
        for i in range(blocks):
            slot = plan[d * blocks + i] - own * blocks
            origin[jnp.where(jnp.logical_and(slot >= 0, slot < blocks), slot, blocks)] = mark
        return carry

    lax.fori_loop(0, devices, device, 0)


def face_rows(angle, scale, links, metric, coefs, blocks, elements):
    shape = (blocks, 3 * elements)
    own = lax.broadcasted_iota(jnp.int32, shape, 0) * (3 * elements) + lax.broadcasted_iota(jnp.int32, shape, 1)
    free = jnp.where(links[...] == own, 0.0, 1.0)
    lower = lax.broadcasted_iota(jnp.int32, (blocks, LANES), 1) < elements
    for q, value in enumerate((jnp.cos(angle[...]), jnp.sin(angle[...]), scale[...], free)):
        two = value[:, :LANES]
        swapped = swap_halves(two)
        third = value[:, LANES:]
        faces = (
            jnp.where(lower, two, swapped), jnp.where(lower, swapped, two), jnp.concatenate([third, third], axis=1)
        )
        for f in range(3):
            coefs[pl.ds(3 * q + f, blocks, stride=16), :] = faces[f]
    for b in range(blocks):
        factors = metric[b]
        coefs[b * 16 + 12 : b * 16 + 16] = jnp.concatenate([factors, factors], axis=1)


def spread_pair(coefs, both, eye, spread, factors, elements):
    lower = lax.broadcasted_iota(jnp.int32, (16, LANES), 1) < elements
    values = jnp.where(lower, coefs[pl.ds(both[0] * 16, 16), :], coefs[pl.ds(both[1] * 16, 16), :])
    rough = values.astype(jnp.bfloat16).astype(jnp.float32)
    stacked = jnp.concatenate([rough, values - rough], axis=0).astype(jnp.bfloat16)
    stacked = mm(eye[:, :LANES], stacked, ((1,), (1,))).astype(jnp.bfloat16)
    factors[...] = mm(stacked, spread[...])


def inflow_rows(breach, both, t):
    rows = []
    for b in both:
        row = jnp.zeros((1, LANES), jnp.float32)
        for s in range(t["members"]):
            level = breach[s, b].astype(jnp.float32)
            row = jnp.where(lax.broadcasted_iota(jnp.int32, (1, LANES), 1) == 2 * t["comp"] + s, level, row)
        rows.append(row)
    return rows


def volume_rows(rows, turned, factors, first, inflow, pieces):
    rx, sx, ry, sy = (factors[rows, q * LANES : (q + 1) * LANES] for q in range(first, first + 4))
    height, flow_x, flow_y = (turned[c, rows] for c in range(3))
    pressure = 0.5 * gravity * height * height
    inverse = 1.0 / height
    speed_x = flow_x * inverse
    speed_y = flow_y * inverse
    cross = flow_y * speed_x
    flux_f = (flow_x, flow_x * speed_x + pressure, cross)
    flux_g = (flow_y, cross, flow_y * speed_y + pressure)
    for c in range(3):
        along_r = rx * flux_f[c] + ry * flux_g[c]
        along_s = sx * flux_f[c] + sy * flux_g[c]
        if c == 0:
            along_r = along_r + inflow
        pieces[c, rows, 0:LANES], pieces[c, rows, LANES : 2 * LANES] = split(along_r)
        pieces[c, rows, 2 * LANES : 3 * LANES], pieces[c, rows, 3 * LANES : 4 * LANES] = split(along_s)


def flux_rows(rows, traces, outer, factors, pieces, first, wide):
    lane = lax.broadcasted_iota(jnp.int32, (rows.stop - rows.start, LANES), 1)
    n_x, n_y, scale, free = (factors[rows, q * LANES : (q + 1) * LANES] for q in range(4))
    theirs = [outer[f * LANES + rows.start : f * LANES + rows.stop] for f in range(3)]
    height, flow_x, flow_y = (traces[c, rows] for c in range(3))
    is_wall = free < 0.5
    through = flow_x * n_x + flow_y * n_y
    twice = through + through
    height_o = jnp.where(is_wall, height, place_face(theirs, 0, wide, lane))
    flow_xo = jnp.where(is_wall, flow_x - twice * n_x, place_face(theirs, 1, wide, lane))
    flow_yo = jnp.where(is_wall, flow_y - twice * n_y, place_face(theirs, 2, wide, lane))
    speed = through / height
    speed_o = (flow_xo * n_x + flow_yo * n_y) / height_o
    fast = jnp.maximum(
        jnp.abs(speed) + root(gravity * height), jnp.abs(speed_o) + root(gravity * height_o)
    )
    ours, others = speed - fast, speed_o - fast
    half = 0.5 * scale
    push = 0.5 * gravity * (height * height - height_o * height_o)
    jumps = (
        half * (height * ours - height_o * others),
        half * (flow_x * ours - flow_xo * others + push * n_x),
        half * (flow_y * ours - flow_yo * others + push * n_y),
    )
    for c in range(3):
        high, rest = split(jumps[c])
        pieces[c, rows, first : first + LANES] = high
        pieces[c, rows, first + LANES : first + 2 * LANES] = rest
        pieces[c, rows, first + 2 * LANES : first + 3 * LANES] = high


def pair_gains(tall, comp, elements):
    narrow = lax.broadcasted_iota(jnp.int32, (comp, LANES), 1) < elements
    even, odd = tall[:comp], tall[comp:]
    return jnp.where(narrow, even, swap_halves(odd)), jnp.where(narrow, swap_halves(even), odd)


def row_chunks(step):
    return [slice(i * step, (i + 1) * step) for i in range(LANES // step)]


RING = 8


def finish_kernel(
    plan_in, wet_in, breach_in, links_in, angle_in, scale_in, metric_in,
    fields_in, pool_in, partner_in, across_in, own_in, spread_in, matrix_in, eye_in,
    *rest, t, blocks, elements, devices, leaving,
):
    outs, scratch = (rest[:1], rest[1:]) if leaving else (rest[:3], rest[3:])
    plan, wet, breach, links, angle, scale, metric, fields, pool, own, spread, matrix, eye, *scratch = scratch
    order, place, coefs, turned, halves, traces, factors, outer, pieces, near, sems, staged, *scratch = scratch
    comp, wide, used = t["comp"], t["wide"], t["used"]
    faces = blocks * 3 * elements
    width = partner_in.shape[0]
    odd = lax.axis_index("mesh") % 2
    near_rows = pl.multiple_of(faces + (1 - odd) * width, 8)
    far_rows = pl.multiple_of(faces + odd * width, 8)
    loads = [
        (plan_in, plan), (angle_in, angle), (scale_in, scale), (links_in, links), (metric_in, metric),
        (fields_in, fields), (wet_in, wet), (breach_in, breach), (eye_in, eye), (own_in, own),
        (spread_in, spread), (matrix_in, matrix), (pool_in, pool.at[pl.ds(0, faces)]),
        (partner_in, pool.at[pl.ds(near_rows, width)]), (across_in, pool.at[pl.ds(far_rows, width)]),
    ]
    n = len(loads)
    loads = start_all([pltpu.make_async_copy(a, b, sems.at[i]) for i, (a, b) in enumerate(loads)])
    index = lax.axis_index("mesh")
    loads[0].wait()
    n_leaving = scan_moves(plan, index * blocks, order, place, blocks)
    begin = 0 if leaving else n_leaving
    end = n_leaving if leaving else blocks
    n_pairs = near.shape[0] // 2
    steps = (end - begin + 2 * n_pairs - 1) // (2 * n_pairs)

    def at(i, u):
        return jnp.maximum(jnp.minimum(begin + 2 * n_pairs * i + u, end - 1), 0)

    def indices(i):
        return [
            pltpu.make_async_copy(links_in.at[order[at(i, u)]], near.at[u], sems.at[n + u])
            for u in range(2 * n_pairs)
        ]

    def send(p):
        rows = outs[0].shape[1]
        return pltpu.make_async_copy(staged.at[p, pl.ds(0, rows)], outs[0].at[place[order[p]]], sems.at[n + 2 * n_pairs + p % RING])

    @pl.when(steps > 0)
    def _():
        start_all(indices(0))

    wait_all(loads[1:5])
    face_rows(angle, scale, links, metric, coefs, blocks, elements)
    if not leaving:
        scan_origins(plan, index, scratch[2], blocks, devices)
    wait_all(loads[5:-3])
    chunks = row_chunks(16)

    def pick(w, rows):
        for f in range(3):
            for line in range(rows.start, rows.stop):
                v = near[2 * w + line // elements, f * elements + line % elements]
                outer[w, f * LANES + line : f * LANES + line + 1, :] = pool[pl.ds(v, 1), :]

    def pair_of(i, w):
        return [order[at(i, 2 * w + u)] for u in range(2)]

    def lay_out(w, pair):
        for c in range(3):
            turn_rows(
                rows_of(fields, pair[0], c, comp), rows_of(fields, pair[1], c, comp), c, eye,
                turned.at[w], halves.at[w], comp,
            )
        inner = mm(halves[w], own[...])
        for c in range(3):
            traces[w, c] = inner[c * LANES : (c + 1) * LANES]
        spread_pair(coefs, pair, eye, spread, factors.at[w], elements)

    def one(i, carry):
        both = [pair_of(i, w) for w in range(2)]
        inflow = [inflow_rows(breach, pair, t) for pair in both]

        def fluxes(w, rows):
            volume_rows(rows, turned.at[w], factors.at[w], 4, inflow[w][rows.start // elements], pieces.at[w])
            flux_rows(rows, traces.at[w], outer.at[w], factors.at[w], pieces.at[w], 4 * LANES, wide)

        def combine(w, c):
            gains = pair_gains(mm(matrix[...], pieces[w, c], ((1,), (1,))), comp, elements)
            for u in range(2):
                b = both[w][u]
                rate = time_step * wet[b].astype(jnp.float32)
                done = rows_of(fields, b, c, comp) + rate * gains[u]
                row = at(i, 2 * w + u) if leaving else 2 * w + u
                if c == 0:
                    staged[row, :comp] = done
                else:
                    staged[row, pl.ds(used + c - 1, comp, stride=2), :] = done

        def hand_over(w):
            for u in range(2):
                if leaving:
                    p = 4 * i + 2 * w + u

                    @pl.when(p < end)
                    def _():
                        @pl.when(p >= RING)
                        def _():
                            send(p - RING).wait()

                        send(p).start()
                else:
                    write_depth(both[w][u], staged.at[2 * w + u], scratch[0], t, blocks)
                    write_flow(both[w][u], staged.at[2 * w + u], scratch[1], t)

        wait_all(indices(i))
        for rows in chunks:
            pick(0, rows)
        lay_out(1, both[1])
        for rows in chunks:
            fluxes(0, rows)
            pick(1, rows)
        for k, rows in enumerate(chunks):
            if k < 3:
                combine(0, k)
            fluxes(1, rows)
        for c in range(3):
            combine(1, c)

        @pl.when(i + 1 < steps)
        def _():
            start_all(indices(i + 1))
            lay_out(0, pair_of(i + 1, 0))

        hand_over(0)
        hand_over(1)
        return carry

    lay_out(0, pair_of(0, 0))
    wait_all(loads[-3:])
    lax.fori_loop(0, steps, one, 0)
    if leaving:

        def drain(p, carry):
            send(p).wait()
            return carry

        lax.fori_loop(jnp.maximum(end - RING, 0), end, drain, 0)
    else:
        kept = ((scratch[0], outs[0]), (scratch[1], outs[1]), (scratch[2].at[pl.ds(0, outs[2].shape[0])], outs[2]))
        wait_all(start_all([pltpu.make_async_copy(a, b, sems.at[n + 2 * n_pairs + i]) for i, (a, b) in enumerate(kept)]))


def write_depth(b, rows, depth, t, blocks):
    pairs, members = t["pairs"], t["members"]
    tile, sub = b // 8, b % 8
    for s in range(members):
        start = (s * (blocks // 8) + tile) * pairs * 8 + sub
        depth[pl.ds(start, pairs, stride=8), :] = rows[s * pairs : (s + 1) * pairs]


def write_flow(b, rows, flow, t):
    pairs, members, used = t["pairs"], t["members"], t["used"]
    for s in range(members):
        for j in range(pairs):
            row = used + 2 * (s * pairs + j)
            flow[b, s, :, j * LANES : (j + 1) * LANES] = rows[row : row + 2]


def merge_kernel(
    origin_in, got_in, depth_in, flow_in, depth_out, flow_out, origin, depth, flow, got, sems, *, t, blocks
):
    pairs, members = t["pairs"], t["members"]
    loads = start_all(
        [
            pltpu.make_async_copy(a, b, sems.at[i])
            for i, (a, b) in enumerate(((origin_in, origin), (got_in, got)))
        ]
    )
    wait_all(loads)

    def flow_part(b, k):
        return pltpu.make_async_copy(flow.at[b], flow_out.at[b], sems.at[2 + k % RING])

    def depth_part(b, k):
        return pltpu.make_async_copy(
            depth.at[b], depth_out.at[:, b // 8, :, b % 8], sems.at[2 + RING + k % RING]
        )

    def settle(k):
        flow_part(0, k).wait()
        depth_part(0, k).wait()

    def put(b, k):
        came = origin[b] >= 0

        @pl.when(came)
        def _():
            @pl.when(k >= RING)
            def _():
                settle(k)

            for s in range(members):
                depth[b, s] = got[origin[b], s * pairs : (s + 1) * pairs]
            depth_part(b, k).start()
            write_flow(b, got.at[origin[b]], flow, t)
            flow_part(b, k).start()

        return k + came.astype(jnp.int32)

    arrivals = lax.fori_loop(0, blocks, put, jnp.int32(0))

    def drain(k, carry):
        settle(k)
        return carry

    lax.fori_loop(jnp.maximum(arrivals - RING, 0), arrivals, drain, 0)


SMEM = pl.BlockSpec(memory_space=pltpu.SMEM)
HBM = pl.BlockSpec(memory_space=pltpu.HBM)
VMEM = pl.BlockSpec(memory_space=pltpu.VMEM)


def call(kernel, out_shape, n_smem, n_args, scratch, out_specs, **keys):
    return pl.pallas_call(
        kernel,
        out_shape=out_shape,
        in_specs=[SMEM] * n_smem + [HBM] * n_args,
        out_specs=out_specs,
        scratch_shapes=scratch,
        compiler_params=pltpu.CompilerParams(vmem_limit_bytes=64 << 20),
        **keys,
    )


def body(
    water_depth, momentum, metric, face_scale, face_angle, face_map, rim_faces, wet_blocks, breach, block_plan
):
    blocks, members, node_cells = water_depth.shape
    elements = metric.shape[2]
    t = static_tables(members, elements)
    comp, pairs, used = t["comp"], t["pairs"], t["used"]
    f32, bf16 = jnp.float32, jnp.bfloat16
    tiles = blocks // 8
    depth_rows = water_depth.reshape(tiles, 8, members, pairs, LANES).transpose(2, 0, 3, 1, 4).reshape(-1, LANES)
    flow_rows = momentum.transpose(0, 2, 1, 3)
    faces = face_map.size
    width = rim_faces.shape[1] // 2
    dma = pltpu.SemaphoreType.DMA

    back = jnp.asarray(np.tile(t["back"], (2, 1)), bf16)
    eye = jnp.asarray(np.tile(np.eye(LANES), (1, 2)), bf16)
    fields, pool, to_across, to_partner = call(
        functools.partial(prepare_kernel, t=t, blocks=blocks, elements=elements),
        (
            jax.ShapeDtypeStruct((blocks, 3 * comp, LANES), f32),
            jax.ShapeDtypeStruct((faces, LANES), f32),
            jax.ShapeDtypeStruct((width, LANES), f32),
            jax.ShapeDtypeStruct((width, LANES), f32),
        ),
        0, 5,
        [
            pltpu.SMEM(rim_faces.shape, jnp.int32), pltpu.VMEM(depth_rows.shape, f32), pltpu.VMEM(flow_rows.shape, f32), pltpu.VMEM(back.shape, bf16),
            pltpu.VMEM(eye.shape, bf16),
            pltpu.VMEM((blocks, 3 * comp, LANES), f32), pltpu.VMEM((faces, LANES), f32),
            pltpu.VMEM((3 * LANES, 2 * LANES), bf16), dma((4 + 2 * tiles + blocks // 2,)),
        ],
        (HBM, HBM, VMEM, VMEM),
    )(rim_faces, depth_rows, flow_rows, back, eye)

    count = lax.axis_size("mesh")
    partners = [(i, i ^ 1) for i in range(count)]
    neighbours = [(i, i + 1 if i % 2 else i - 1) for i in range(1, count - 1)]
    partner = lax.ppermute(to_partner, "mesh", partners)
    across = lax.ppermute(to_across, "mesh", neighbours)

    lift_h, lift_l = high_low(t["lift"])
    along_r, along_s = t["along"]
    matrix = np.concatenate(
        [along_r, along_r, along_s, along_s, *(np.asarray(m, np.float32) for m in (lift_h, lift_h, lift_l))], axis=1
    )
    mats = [
        jnp.asarray(np.tile(t["own"], (2, 1)), bf16), jnp.asarray(np.tile(t["spread"], (2, 1)), bf16),
        jnp.asarray(matrix, bf16), eye,
    ]
    packed = round_up(3 * used, 8)

    i32 = jnp.int32
    block_rows = (3 * comp, LANES)
    n_pairs = 2

    def finish(leaving, out_shape, extra):
        return call(
            functools.partial(
                finish_kernel, t=t, blocks=blocks, elements=elements, devices=count, leaving=leaving
            ),
            out_shape,
            0, 15,
            [
                pltpu.SMEM(block_plan.shape, i32), pltpu.SMEM(wet_blocks.shape, i32),
                pltpu.SMEM((members, blocks), i32), pltpu.VMEM(face_map.shape, i32),
                pltpu.VMEM(face_angle.shape, f32), pltpu.VMEM(face_scale.shape, f32), pltpu.VMEM(metric.shape, f32),
                pltpu.VMEM((blocks, *block_rows), f32), pltpu.VMEM((faces + 2 * width, LANES), f32),
                *[pltpu.VMEM(m.shape, bf16) for m in mats],
                pltpu.SMEM((blocks,), i32), pltpu.SMEM((blocks,), i32), pltpu.VMEM((blocks * 16, LANES), f32),
                pltpu.VMEM((2, 3, LANES, LANES), f32), pltpu.VMEM((2, 3 * LANES, 2 * LANES), bf16),
                pltpu.VMEM((2, 3, LANES, LANES), f32), pltpu.VMEM((2, LANES, 8 * LANES), f32),
                pltpu.VMEM((2, 3 * LANES, LANES), f32), pltpu.VMEM((2, 3, LANES, 7 * LANES), bf16),
                pltpu.SMEM((2 * n_pairs, face_map.shape[1]), i32), dma((16 + 2 * n_pairs + RING,)), *extra,
            ],
            jax.tree.map(lambda _: HBM, out_shape),
        )(
            block_plan, wet_blocks, breach.T, face_map, face_angle, face_scale, metric, fields, pool, partner, across,
            *mats,
        )

    sent = finish(True, jax.ShapeDtypeStruct((count, packed, LANES), f32), [pltpu.VMEM((blocks, *block_rows), f32)])
    got = lax.all_to_all(sent, "mesh", split_axis=0, concat_axis=0, tiled=True)
    final = (jax.ShapeDtypeStruct(depth_rows.shape, f32), jax.ShapeDtypeStruct(flow_rows.shape, f32))
    whole = [pltpu.VMEM(depth_rows.shape, f32), pltpu.VMEM(flow_rows.shape, f32)]
    depth_kept, flow_kept, origin = finish(
        False, (*final, jax.ShapeDtypeStruct((LANES,), i32)),
        [pltpu.VMEM((2 * n_pairs, *block_rows), f32), *whole, pltpu.SMEM((LANES,), i32)],
    )
    tall = (members, tiles, pairs, 8, LANES)
    depth_new, flow_new = call(
        functools.partial(merge_kernel, t=t, blocks=blocks),
        (jax.ShapeDtypeStruct(tall, f32), final[1]),
        0, 4,
        [
            pltpu.SMEM((LANES,), i32), pltpu.VMEM((blocks, members, pairs, LANES), f32), whole[1],
            pltpu.VMEM((count, packed, LANES), f32), dma((2 + 2 * RING,)),
        ],
        (HBM, HBM),
        input_output_aliases={2: 0, 3: 1},
    )(origin, got, depth_kept.reshape(tall), flow_kept)
    depth_out = depth_new.reshape(members, tiles, pairs, 8, LANES).transpose(1, 3, 0, 2, 4).reshape(water_depth.shape)
    return depth_out, flow_new.transpose(0, 2, 1, 3)


def solution(mesh):
    in_specs = (
        P(("groups", "mesh"), None, None),
        P(("groups", "mesh"), None, None, None),
        P(("groups", "mesh"), None, None),
        P(("groups", "mesh"), None),
        P(("groups", "mesh"), None),
        P(("groups", "mesh"), None),
        P(("groups", "mesh"), None),
        P(("groups", "mesh")),
        P(("groups", "mesh"), None),
        P("groups"),
    )
    out_specs = (P(("groups", "mesh"), None, None), P(("groups", "mesh"), None, None, None))
    return jax.shard_map(body, mesh=mesh, in_specs=in_specs, out_specs=out_specs, check_vma=False)
```

```python
import functools
import math

import jax
import jax.numpy as jnp
import numpy as np
from jax import lax
from jax.experimental import pallas as pl
from jax.experimental.pallas import tpu as pltpu
from jax.sharding import PartitionSpec as P


time_step = 0.01
gravity = 1.0
breach_rate = 5.0
LANES = 128


def gauss_solve(matrix, right):
    dimension = matrix.shape[0]
    augmented = np.concatenate([np.array(matrix) * 1.0, np.array(right) * 1.0], axis=1)
    for pivot_col in range(dimension):
        largest = pivot_col + int(np.argmax(np.abs(augmented[pivot_col:, pivot_col])))
        swapped = augmented[[largest, pivot_col]]
        augmented[[pivot_col, largest]] = swapped
        augmented[pivot_col] = augmented[pivot_col] / augmented[pivot_col, pivot_col]
        for row_id in range(dimension):
            if row_id != pivot_col:
                augmented[row_id] = (
                    augmented[row_id] - augmented[row_id, pivot_col] * augmented[pivot_col]
                )
    return augmented[:, dimension:]


def node_tables():
    points = np.array(
        [(across / 3.0, upward / 3.0) for upward in range(4) for across in range(4 - upward)]
    )
    powers = [(power_r, power_s) for power_r in range(4) for power_s in range(4 - power_r)]
    vander = np.zeros((10, 10))
    grad_r = np.zeros((10, 10))
    grad_s = np.zeros((10, 10))
    mono_mass = np.zeros((10, 10))
    for column, (power_r, power_s) in enumerate(powers):
        vander[:, column] = points[:, 0] ** power_r * points[:, 1] ** power_s
        if power_r > 0:
            grad_r[:, column] = power_r * points[:, 0] ** (power_r - 1) * points[:, 1] ** power_s
        if power_s > 0:
            grad_s[:, column] = power_s * points[:, 0] ** power_r * points[:, 1] ** (power_s - 1)
        for second_column, (other_r, other_s) in enumerate(powers):
            mono_mass[column, second_column] = (
                math.factorial(power_r + other_r)
                * math.factorial(power_s + other_s)
                / math.factorial(power_r + other_r + power_s + other_s + 2)
            )
    inverse = gauss_solve(vander, np.eye(10))
    mass_matrix = inverse.T @ mono_mass @ inverse
    line_points = np.arange(4) / 3.0
    line_vander = line_points[:, None] ** np.arange(4)[None, :]
    hilbert = 1.0 / (np.arange(4)[:, None] + np.arange(4)[None, :] + 1.0)
    line_inverse = gauss_solve(line_vander, np.eye(4))
    edge_mass = line_inverse.T @ hilbert @ line_inverse
    face_nodes = np.array([[0, 1, 2, 3], [3, 6, 8, 9], [9, 7, 4, 0]])
    edge_embed = np.zeros((10, 12))
    for face_id in range(3):
        for node_id in range(4):
            edge_embed[face_nodes[face_id, node_id], 4 * face_id : 4 * face_id + 4] += edge_mass[
                node_id
            ]
    lifting = gauss_solve(mass_matrix, edge_embed).reshape(10, 3, 4)
    return (
        np.asarray(grad_r @ inverse, np.float32),
        np.asarray(grad_s @ inverse, np.float32),
        np.asarray(lifting, np.float32),
        face_nodes.reshape(-1),
    )


def round_up(value, step):
    return (value + step - 1) // step * step


def static_tables(members):
    deriv_r, deriv_s, lifting, face_order = node_tables()
    nodes = deriv_r.shape[0]
    pairs = nodes // 2
    used = members * pairs
    comp = round_up(used, 8)
    face_nodes = face_order.reshape(3, 4)
    wide = members * 4

    def lane_of(s, n):
        return (n % 2) * comp + s * pairs + n // 2

    own = np.zeros((LANES, LANES), np.float32)
    own[2 * comp, 3 * wide :] = 1.0
    back = np.zeros((LANES, LANES), np.float32)
    lift = np.zeros((2 * comp, LANES), np.float32)
    along = np.zeros((2, 2 * comp, LANES), np.float32)
    for s in range(members):
        for f in range(3):
            for k in range(4):
                n = int(face_nodes[f, k])
                own[lane_of(s, n), f * wide + s * 4 + k] = 1.0
                back[lane_of(s, n), f * wide + s * 4 + 3 - k] = 1.0
        for n in range(nodes):
            for f in range(3):
                for k in range(4):
                    lift[lane_of(s, n), f * wide + s * 4 + k] = lifting[n, f, k]
            for m in range(nodes):
                along[0, lane_of(s, n), lane_of(s, m)] = -deriv_r[n, m]
                along[1, lane_of(s, n), lane_of(s, m)] = -deriv_s[n, m]
            along[0, lane_of(s, n), 2 * comp + s] = breach_rate
    spread = np.zeros((16, 8 * LANES), np.float32)
    for q in range(4):
        for f in range(3):
            spread[3 * q + f, q * LANES + f * wide : q * LANES + (f + 1) * wide] = 1.0
        spread[12 + q, (4 + q) * LANES : (4 + q) * LANES + 2 * comp] = 1.0
    return dict(
        own=own, back=back, lift=lift, along=along, spread=spread,
        comp=comp, pairs=pairs, used=used, wide=wide, nodes=nodes, members=members,
    )


def high_low(matrix):
    high = matrix.astype(jnp.bfloat16)
    low = (matrix - high.astype(np.float32)).astype(jnp.bfloat16)
    return high, low


def mm(a, b, dims=((1,), (0,))):
    return lax.dot_general(a, b, (dims, ((), ())), preferred_element_type=jnp.float32)


def split(x):
    high = x.astype(jnp.bfloat16)
    return high, (x - high.astype(jnp.float32)).astype(jnp.bfloat16)


def swap_halves(x):
    return pltpu.roll(x, LANES // 2, 1)


def turn(x, eye):
    return mm(eye[...], jnp.concatenate(split(x), axis=1), ((1,), (1,)))


def turn_rows(first, second, c, eye, turned, halves, comp):
    lower = lax.broadcasted_iota(jnp.int32, (comp, LANES), 1) < LANES // 2
    even = jnp.where(lower, first, swap_halves(second))
    odd = jnp.where(lower, swap_halves(first), second)
    fill = jnp.full((LANES - 2 * comp, LANES), 1.0 if c == 0 else 0.0, jnp.float32)
    flat = turn(jnp.concatenate([even, odd, fill], axis=0), eye)
    if turned is not None:
        turned[c] = flat
    high, low = split(flat)
    halves[c * LANES : (c + 1) * LANES, :LANES] = high
    halves[c * LANES : (c + 1) * LANES, LANES:] = low


def rows_of(fields, block, c, comp):
    if c == 0:
        return fields[block, :comp]
    return fields[block, pl.ds(comp + c - 1, comp, stride=2), :]


def place_face(pieces, c, wide, lane):
    moved = [pltpu.roll(p, ((i - c) * wide) % LANES, 1) if i != c else p for i, p in enumerate(pieces)]
    return jnp.where(lane < wide, moved[0], jnp.where(lane < 2 * wide, moved[1], moved[2]))


def root(x):
    return x * lax.rsqrt(x)


def start_all(copies):
    for copy in copies:
        copy.start()
    return copies


def wait_all(copies):
    for copy in copies:
        copy.wait()


def prepare_kernel(
    rim_in, depth_in, flow_in, back_in, eye_in, fields_out, pool_out, across, partner,
    rim, depth, flow, back, eye, fields, pool, halves, sems, *, t, blocks, elements,
):
    comp, pairs, members, wide = t["comp"], t["pairs"], t["members"], t["wide"]
    odd = lax.axis_index("mesh") % 2
    tiles = blocks // 8
    steps = blocks // 2
    group = 2 * 3 * elements
    first = start_all(
        [
            pltpu.make_async_copy(depth_in, depth, sems.at[0]), pltpu.make_async_copy(back_in, back, sems.at[1]),
            pltpu.make_async_copy(eye_in, eye, sems.at[2]), pltpu.make_async_copy(rim_in, rim, sems.at[3]),
        ]
    )

    def part(tile):
        rows = pl.ds(8 * tile, 8)
        return pltpu.make_async_copy(flow_in.at[rows], flow.at[rows], sems.at[4 + tile])

    def field_part(tile):
        rows = pl.ds(8 * tile, 8)
        return pltpu.make_async_copy(fields.at[rows], fields_out.at[rows], sems.at[4 + tiles + tile])

    def pool_part(i):
        lines = pl.ds(group * i, group)
        return pltpu.make_async_copy(pool.at[lines], pool_out.at[lines], sems.at[4 + 2 * tiles + i])

    start_all([part(tile) for tile in range(tiles)])
    wait_all(first)

    def build(i):
        for u in range(2):
            b = 2 * i + u
            tile, sub = b // 8, b % 8
            fields[b, comp - 8 : comp] = jnp.full((8, LANES), 1.0, jnp.float32)
            fields[b, 3 * comp - 16 : 3 * comp] = jnp.zeros((16, LANES), jnp.float32)
            for s in range(members):
                start = (s * tiles + tile) * pairs * 8 + sub
                fields[b, s * pairs : (s + 1) * pairs] = depth[pl.ds(start, pairs, stride=8), :]
                for j in range(pairs):
                    row = comp + 2 * (s * pairs + j)
                    fields[b, row : row + 2] = flow[b, s, :, j * LANES : (j + 1) * LANES]

    def turn_of(i):
        for c in range(3):
            turn_rows(
                rows_of(fields, 2 * i, c, comp), rows_of(fields, 2 * i + 1, c, comp), c, eye, None, halves, comp
            )

    def faces_of(i):
        rows = mm(halves[...], back[...])
        lane = lax.broadcasted_iota(jnp.int32, (LANES, LANES), 1)
        pieces = [rows[c * LANES : (c + 1) * LANES] for c in range(3)]
        for f in range(3):
            face = place_face(pieces, f, wide, lane)
            for u in range(2):
                at = ((2 * i + u) * 3 + f) * elements
                pool[pl.ds(at, elements), :] = face[u * elements : (u + 1) * elements]

    part(0).wait()
    build(0)
    turn_of(0)
    build(1)

    def one(i, carry):
        @pl.when(i % 4 == 0)
        def _():
            part(i // 4).wait()

        faces_of(i - 2)
        turn_of(i - 1)
        build(i)
        pool_part(i - 2).start()

        @pl.when(i % 4 == 3)
        def _():
            field_part(i // 4).start()

        return carry

    lax.fori_loop(2, steps, one, 0)
    faces_of(steps - 2)
    turn_of(steps - 1)
    pool_part(steps - 2).start()
    faces_of(steps - 1)
    pool_part(steps - 1).start()
    width = partner.shape[0]
    near, far = (1 - odd) * width, odd * width

    def pick(i, carry):
        for u in range(32):
            r = i * 32 + u
            partner[pl.ds(r, 1), :] = pool[pl.ds(rim[0, near + r], 1), :]
            across[pl.ds(r, 1), :] = pool[pl.ds(rim[0, far + r], 1), :]
        return carry

    lax.fori_loop(0, width // 32, pick, 0)
    for tile in range(tiles):
        field_part(tile).wait()
    for i in range(steps):
        pool_part(i).wait()


def scan_moves(plan, base, order, place, blocks):
    def one(i, carry):
        leaving, staying = carry
        slot = plan[base + i]
        away = jnp.logical_or(slot < base, slot >= base + blocks).astype(jnp.int32)
        order[jnp.where(away == 1, leaving, blocks - 1 - staying)] = i
        place[i] = lax.div(slot, jnp.int32(blocks))
        return leaving + away, staying + 1 - away

    return lax.fori_loop(0, blocks, one, (jnp.int32(0), jnp.int32(0)))[0]


def scan_origins(plan, own, origin, blocks, devices):
    def device(d, carry):
        mark = jnp.where(d == own, -1, d)
        for i in range(blocks):
            slot = plan[d * blocks + i] - own * blocks
            origin[jnp.where(jnp.logical_and(slot >= 0, slot < blocks), slot, blocks)] = mark
        return carry

    lax.fori_loop(0, devices, device, 0)


def face_rows(angle, scale, links, metric, coefs, blocks, elements):
    shape = (blocks, 3 * elements)
    own = lax.broadcasted_iota(jnp.int32, shape, 0) * (3 * elements) + lax.broadcasted_iota(jnp.int32, shape, 1)
    free = jnp.where(links[...] == own, 0.0, 1.0)
    lower = lax.broadcasted_iota(jnp.int32, (blocks, LANES), 1) < elements
    for q, value in enumerate((jnp.cos(angle[...]), jnp.sin(angle[...]), scale[...], free)):
        two = value[:, :LANES]
        swapped = swap_halves(two)
        third = value[:, LANES:]
        faces = (
            jnp.where(lower, two, swapped), jnp.where(lower, swapped, two), jnp.concatenate([third, third], axis=1)
        )
        for f in range(3):
            coefs[pl.ds(3 * q + f, blocks, stride=16), :] = faces[f]
    for b in range(blocks):
        factors = metric[b]
        coefs[b * 16 + 12 : b * 16 + 16] = jnp.concatenate([factors, factors], axis=1)


def spread_pair(coefs, both, eye, spread, factors, elements):
    lower = lax.broadcasted_iota(jnp.int32, (16, LANES), 1) < elements
    values = jnp.where(lower, coefs[pl.ds(both[0] * 16, 16), :], coefs[pl.ds(both[1] * 16, 16), :])
    rough = values.astype(jnp.bfloat16).astype(jnp.float32)
    stacked = jnp.concatenate([rough, values - rough], axis=0).astype(jnp.bfloat16)
    stacked = mm(eye[:, :LANES], stacked, ((1,), (1,))).astype(jnp.bfloat16)
    factors[...] = mm(stacked, spread[...])


def inflow_rows(breach, both, t):
    rows = []
    for b in both:
        row = jnp.zeros((1, LANES), jnp.float32)
        for s in range(t["members"]):
            level = breach[s, b].astype(jnp.float32)
            row = jnp.where(lax.broadcasted_iota(jnp.int32, (1, LANES), 1) == 2 * t["comp"] + s, level, row)
        rows.append(row)
    return rows


def volume_rows(rows, turned, factors, first, inflow, pieces):
    rx, sx, ry, sy = (factors[rows, q * LANES : (q + 1) * LANES] for q in range(first, first + 4))
    height, flow_x, flow_y = (turned[c, rows] for c in range(3))
    pressure = 0.5 * gravity * height * height
    inverse = 1.0 / height
    speed_x = flow_x * inverse
    speed_y = flow_y * inverse
    cross = flow_y * speed_x
    flux_f = (flow_x, flow_x * speed_x + pressure, cross)
    flux_g = (flow_y, cross, flow_y * speed_y + pressure)
    for c in range(3):
        along_r = rx * flux_f[c] + ry * flux_g[c]
        along_s = sx * flux_f[c] + sy * flux_g[c]
        if c == 0:
            along_r = along_r + inflow
        pieces[c, rows, 0:LANES], pieces[c, rows, LANES : 2 * LANES] = split(along_r)
        pieces[c, rows, 2 * LANES : 3 * LANES], pieces[c, rows, 3 * LANES : 4 * LANES] = split(along_s)


def flux_rows(rows, traces, outer, factors, pieces, first, wide):
    lane = lax.broadcasted_iota(jnp.int32, (rows.stop - rows.start, LANES), 1)
    n_x, n_y, scale, free = (factors[rows, q * LANES : (q + 1) * LANES] for q in range(4))
    theirs = [outer[f * LANES + rows.start : f * LANES + rows.stop] for f in range(3)]
    height, flow_x, flow_y = (traces[c, rows] for c in range(3))
    is_wall = free < 0.5
    through = flow_x * n_x + flow_y * n_y
    twice = through + through
    height_o = jnp.where(is_wall, height, place_face(theirs, 0, wide, lane))
    flow_xo = jnp.where(is_wall, flow_x - twice * n_x, place_face(theirs, 1, wide, lane))
    flow_yo = jnp.where(is_wall, flow_y - twice * n_y, place_face(theirs, 2, wide, lane))
    speed = through / height
    speed_o = (flow_xo * n_x + flow_yo * n_y) / height_o
    fast = jnp.maximum(
        jnp.abs(speed) + root(gravity * height), jnp.abs(speed_o) + root(gravity * height_o)
    )
    ours, others = speed - fast, speed_o - fast
    half = 0.5 * scale
    push = 0.5 * gravity * (height * height - height_o * height_o)
    jumps = (
        half * (height * ours - height_o * others),
        half * (flow_x * ours - flow_xo * others + push * n_x),
        half * (flow_y * ours - flow_yo * others + push * n_y),
    )
    for c in range(3):
        high, rest = split(jumps[c])
        pieces[c, rows, first : first + LANES] = high
        pieces[c, rows, first + LANES : first + 2 * LANES] = rest
        pieces[c, rows, first + 2 * LANES : first + 3 * LANES] = high


def pair_gains(tall, comp, elements):
    narrow = lax.broadcasted_iota(jnp.int32, (comp, LANES), 1) < elements
    even, odd = tall[:comp], tall[comp:]
    return jnp.where(narrow, even, swap_halves(odd)), jnp.where(narrow, swap_halves(even), odd)


def row_chunks(step):
    return [slice(i * step, (i + 1) * step) for i in range(LANES // step)]


RING = 8


def finish_kernel(
    plan_in, wet_in, breach_in, links_in, angle_in, scale_in, metric_in,
    fields_in, pool_in, partner_in, across_in, own_in, spread_in, matrix_in, eye_in,
    *rest, t, blocks, elements, devices, leaving,
):
    outs, scratch = (rest[:1], rest[1:]) if leaving else (rest[:3], rest[3:])
    plan, wet, breach, links, angle, scale, metric, fields, pool, own, spread, matrix, eye, *scratch = scratch
    order, place, coefs, turned, halves, traces, factors, outer, pieces, near, sems, staged, *scratch = scratch
    comp, wide, used = t["comp"], t["wide"], t["used"]
    faces = blocks * 3 * elements
    width = partner_in.shape[0]
    odd = lax.axis_index("mesh") % 2
    near_rows = pl.multiple_of(faces + (1 - odd) * width, 8)
    far_rows = pl.multiple_of(faces + odd * width, 8)
    loads = [
        (plan_in, plan), (angle_in, angle), (scale_in, scale), (links_in, links), (metric_in, metric),
        (fields_in, fields), (wet_in, wet), (breach_in, breach), (eye_in, eye), (own_in, own),
        (spread_in, spread), (matrix_in, matrix), (pool_in, pool.at[pl.ds(0, faces)]),
        (partner_in, pool.at[pl.ds(near_rows, width)]), (across_in, pool.at[pl.ds(far_rows, width)]),
    ]
    n = len(loads)
    loads = start_all([pltpu.make_async_copy(a, b, sems.at[i]) for i, (a, b) in enumerate(loads)])
    index = lax.axis_index("mesh")
    loads[0].wait()
    n_leaving = scan_moves(plan, index * blocks, order, place, blocks)
    begin = 0 if leaving else n_leaving
    end = n_leaving if leaving else blocks
    n_pairs = near.shape[0] // 2
    steps = (end - begin + 2 * n_pairs - 1) // (2 * n_pairs)

    def at(i, u):
        return jnp.maximum(jnp.minimum(begin + 2 * n_pairs * i + u, end - 1), 0)

    def indices(i):
        return [
            pltpu.make_async_copy(links_in.at[order[at(i, u)]], near.at[u], sems.at[n + u])
            for u in range(2 * n_pairs)
        ]

    def send(p):
        rows = outs[0].shape[1]
        return pltpu.make_async_copy(staged.at[p, pl.ds(0, rows)], outs[0].at[place[order[p]]], sems.at[n + 2 * n_pairs + p % RING])

    @pl.when(steps > 0)
    def _():
        start_all(indices(0))

    wait_all(loads[1:5])
    face_rows(angle, scale, links, metric, coefs, blocks, elements)
    if not leaving:
        scan_origins(plan, index, scratch[2], blocks, devices)
    wait_all(loads[5:-3])
    chunks = row_chunks(16)

    def pick(w, rows):
        for f in range(3):
            for line in range(rows.start, rows.stop):
                v = near[2 * w + line // elements, f * elements + line % elements]
                outer[w, f * LANES + line : f * LANES + line + 1, :] = pool[pl.ds(v, 1), :]

    def pair_of(i, w):
        return [order[at(i, 2 * w + u)] for u in range(2)]

    def lay_out(w, pair):
        for c in range(3):
            turn_rows(
                rows_of(fields, pair[0], c, comp), rows_of(fields, pair[1], c, comp), c, eye,
                turned.at[w], halves.at[w], comp,
            )
        inner = mm(halves[w], own[...])
        for c in range(3):
            traces[w, c] = inner[c * LANES : (c + 1) * LANES]
        spread_pair(coefs, pair, eye, spread, factors.at[w], elements)

    def one(i, carry):
        both = [pair_of(i, w) for w in range(2)]
        inflow = [inflow_rows(breach, pair, t) for pair in both]

        def fluxes(w, rows):
            volume_rows(rows, turned.at[w], factors.at[w], 4, inflow[w][rows.start // elements], pieces.at[w])
            flux_rows(rows, traces.at[w], outer.at[w], factors.at[w], pieces.at[w], 4 * LANES, wide)

        def combine(w, c):
            gains = pair_gains(mm(matrix[...], pieces[w, c], ((1,), (1,))), comp, elements)
            for u in range(2):
                b = both[w][u]
                rate = time_step * wet[b].astype(jnp.float32)
                done = rows_of(fields, b, c, comp) + rate * gains[u]
                row = at(i, 2 * w + u) if leaving else 2 * w + u
                if c == 0:
                    staged[row, :comp] = done
                else:
                    staged[row, pl.ds(used + c - 1, comp, stride=2), :] = done

        def hand_over(w):
            for u in range(2):
                if leaving:
                    p = 4 * i + 2 * w + u

                    @pl.when(p < end)
                    def _():
                        @pl.when(p >= RING)
                        def _():
                            send(p - RING).wait()

                        send(p).start()
                else:
                    write_depth(both[w][u], staged.at[2 * w + u], scratch[0], t, blocks)
                    write_flow(both[w][u], staged.at[2 * w + u], scratch[1], t)

        wait_all(indices(i))
        for rows in chunks:
            pick(0, rows)
        lay_out(1, both[1])
        for rows in chunks:
            fluxes(0, rows)
            pick(1, rows)
        for k, rows in enumerate(chunks):
            if k < 3:
                combine(0, k)
            fluxes(1, rows)
        for c in range(3):
            combine(1, c)

        @pl.when(i + 1 < steps)
        def _():
            start_all(indices(i + 1))
            lay_out(0, pair_of(i + 1, 0))

        hand_over(0)
        hand_over(1)
        return carry

    lay_out(0, pair_of(0, 0))
    wait_all(loads[-3:])
    lax.fori_loop(0, steps, one, 0)
    if leaving:

        def drain(p, carry):
            send(p).wait()
            return carry

        lax.fori_loop(jnp.maximum(end - RING, 0), end, drain, 0)
    else:
        kept = ((scratch[0], outs[0]), (scratch[1], outs[1]), (scratch[2].at[pl.ds(0, outs[2].shape[0])], outs[2]))
        wait_all(start_all([pltpu.make_async_copy(a, b, sems.at[n + 2 * n_pairs + i]) for i, (a, b) in enumerate(kept)]))


def write_depth(b, rows, depth, t, blocks):
    pairs, members = t["pairs"], t["members"]
    tile, sub = b // 8, b % 8
    for s in range(members):
        start = (s * (blocks // 8) + tile) * pairs * 8 + sub
        depth[pl.ds(start, pairs, stride=8), :] = rows[s * pairs : (s + 1) * pairs]


def write_flow(b, rows, flow, t):
    pairs, members, used = t["pairs"], t["members"], t["used"]
    for s in range(members):
        for j in range(pairs):
            row = used + 2 * (s * pairs + j)
            flow[b, s, :, j * LANES : (j + 1) * LANES] = rows[row : row + 2]


def merge_kernel(
    origin_in, got_in, depth_in, flow_in, depth_out, flow_out, origin, depth, flow, got, sems, *, t, blocks
):
    pairs, members = t["pairs"], t["members"]
    loads = start_all(
        [
            pltpu.make_async_copy(a, b, sems.at[i])
            for i, (a, b) in enumerate(((origin_in, origin), (got_in, got)))
        ]
    )
    wait_all(loads)

    def flow_part(b, k):
        return pltpu.make_async_copy(flow.at[b], flow_out.at[b], sems.at[2 + k % RING])

    def depth_part(b, k):
        return pltpu.make_async_copy(
            depth.at[b], depth_out.at[:, b // 8, :, b % 8], sems.at[2 + RING + k % RING]
        )

    def settle(k):
        flow_part(0, k).wait()
        depth_part(0, k).wait()

    def put(b, k):
        came = origin[b] >= 0

        @pl.when(came)
        def _():
            @pl.when(k >= RING)
            def _():
                settle(k)

            for s in range(members):
                depth[b, s] = got[origin[b], s * pairs : (s + 1) * pairs]
            depth_part(b, k).start()
            write_flow(b, got.at[origin[b]], flow, t)
            flow_part(b, k).start()

        return k + came.astype(jnp.int32)

    arrivals = lax.fori_loop(0, blocks, put, jnp.int32(0))

    def drain(k, carry):
        settle(k)
        return carry

    lax.fori_loop(jnp.maximum(arrivals - RING, 0), arrivals, drain, 0)


SMEM = pl.BlockSpec(memory_space=pltpu.SMEM)
HBM = pl.BlockSpec(memory_space=pltpu.HBM)
VMEM = pl.BlockSpec(memory_space=pltpu.VMEM)


def call(kernel, out_shape, n_smem, n_args, scratch, out_specs, **keys):
    return pl.pallas_call(
        kernel,
        out_shape=out_shape,
        in_specs=[SMEM] * n_smem + [HBM] * n_args,
        out_specs=out_specs,
        scratch_shapes=scratch,
        compiler_params=pltpu.CompilerParams(vmem_limit_bytes=64 << 20),
        **keys,
    )


def body(
    water_depth, momentum, metric, face_scale, face_angle, face_map, rim_faces, wet_blocks, breach, block_plan
):
    blocks, members, _ = water_depth.shape
    elements = metric.shape[2]
    t = static_tables(members)
    comp, pairs, used = t["comp"], t["pairs"], t["used"]
    f32, bf16 = jnp.float32, jnp.bfloat16
    tiles = blocks // 8
    depth_rows = water_depth.reshape(tiles, 8, members, pairs, LANES).transpose(2, 0, 3, 1, 4).reshape(-1, LANES)
    flow_rows = momentum.transpose(0, 2, 1, 3)
    faces = face_map.size
    width = rim_faces.shape[1] // 2
    dma = pltpu.SemaphoreType.DMA

    back = jnp.asarray(np.tile(t["back"], (2, 1)), bf16)
    eye = jnp.asarray(np.tile(np.eye(LANES), (1, 2)), bf16)
    fields, pool, to_across, to_partner = call(
        functools.partial(prepare_kernel, t=t, blocks=blocks, elements=elements),
        (
            jax.ShapeDtypeStruct((blocks, 3 * comp, LANES), f32),
            jax.ShapeDtypeStruct((faces, LANES), f32),
            jax.ShapeDtypeStruct((width, LANES), f32),
            jax.ShapeDtypeStruct((width, LANES), f32),
        ),
        0, 5,
        [
            pltpu.SMEM(rim_faces.shape, jnp.int32), pltpu.VMEM(depth_rows.shape, f32), pltpu.VMEM(flow_rows.shape, f32), pltpu.VMEM(back.shape, bf16),
            pltpu.VMEM(eye.shape, bf16),
            pltpu.VMEM((blocks, 3 * comp, LANES), f32), pltpu.VMEM((faces, LANES), f32),
            pltpu.VMEM((3 * LANES, 2 * LANES), bf16), dma((4 + 2 * tiles + blocks // 2,)),
        ],
        (HBM, HBM, VMEM, VMEM),
    )(rim_faces, depth_rows, flow_rows, back, eye)

    count = lax.axis_size("mesh")
    partners = [(i, i ^ 1) for i in range(count)]
    neighbours = [(i, i + 1 if i % 2 else i - 1) for i in range(1, count - 1)]
    across = lax.ppermute(to_across, "mesh", neighbours)
    partner = lax.ppermute(to_partner, "mesh", partners)

    lift_h, lift_l = high_low(t["lift"])
    along_r, along_s = t["along"]
    matrix = np.concatenate(
        [along_r, along_r, along_s, along_s, *(np.asarray(m, np.float32) for m in (lift_h, lift_h, lift_l))], axis=1
    )
    mats = [
        jnp.asarray(np.tile(t["own"], (2, 1)), bf16), jnp.asarray(np.tile(t["spread"], (2, 1)), bf16),
        jnp.asarray(matrix, bf16), eye,
    ]
    packed = round_up(3 * used, 8)

    i32 = jnp.int32
    block_rows = (3 * comp, LANES)
    n_pairs = 2

    def finish(leaving, out_shape, extra):
        return call(
            functools.partial(
                finish_kernel, t=t, blocks=blocks, elements=elements, devices=count, leaving=leaving
            ),
            out_shape,
            0, 15,
            [
                pltpu.SMEM(block_plan.shape, i32), pltpu.SMEM(wet_blocks.shape, i32),
                pltpu.SMEM((members, blocks), i32), pltpu.VMEM(face_map.shape, i32),
                pltpu.VMEM(face_angle.shape, f32), pltpu.VMEM(face_scale.shape, f32), pltpu.VMEM(metric.shape, f32),
                pltpu.VMEM((blocks, *block_rows), f32), pltpu.VMEM((faces + 2 * width, LANES), f32),
                *[pltpu.VMEM(m.shape, bf16) for m in mats],
                pltpu.SMEM((blocks,), i32), pltpu.SMEM((blocks,), i32), pltpu.VMEM((blocks * 16, LANES), f32),
                pltpu.VMEM((2, 3, LANES, LANES), f32), pltpu.VMEM((2, 3 * LANES, 2 * LANES), bf16),
                pltpu.VMEM((2, 3, LANES, LANES), f32), pltpu.VMEM((2, LANES, 8 * LANES), f32),
                pltpu.VMEM((2, 3 * LANES, LANES), f32), pltpu.VMEM((2, 3, LANES, 7 * LANES), bf16),
                pltpu.SMEM((2 * n_pairs, face_map.shape[1]), i32), dma((16 + 2 * n_pairs + RING,)), *extra,
            ],
            jax.tree.map(lambda _: HBM, out_shape),
        )(
            block_plan, wet_blocks, breach.T, face_map, face_angle, face_scale, metric, fields, pool, partner, across,
            *mats,
        )

    sent = finish(True, jax.ShapeDtypeStruct((count, packed, LANES), f32), [pltpu.VMEM((blocks, *block_rows), f32)])
    got = lax.all_to_all(sent, "mesh", split_axis=0, concat_axis=0, tiled=True)
    final = (jax.ShapeDtypeStruct(depth_rows.shape, f32), jax.ShapeDtypeStruct(flow_rows.shape, f32))
    whole = [pltpu.VMEM(depth_rows.shape, f32), pltpu.VMEM(flow_rows.shape, f32)]
    depth_kept, flow_kept, origin = finish(
        False, (*final, jax.ShapeDtypeStruct((LANES,), i32)),
        [pltpu.VMEM((2 * n_pairs, *block_rows), f32), *whole, pltpu.SMEM((LANES,), i32)],
    )
    tall = (members, tiles, pairs, 8, LANES)
    depth_new, flow_new = call(
        functools.partial(merge_kernel, t=t, blocks=blocks),
        (jax.ShapeDtypeStruct(tall, f32), final[1]),
        0, 4,
        [
            pltpu.SMEM((LANES,), i32), pltpu.VMEM((blocks, members, pairs, LANES), f32), whole[1],
            pltpu.VMEM((count, packed, LANES), f32), dma((2 + 2 * RING,)),
        ],
        (HBM, HBM),
        input_output_aliases={2: 0, 3: 1},
    )(origin, got, depth_kept.reshape(tall), flow_kept)
    depth_out = depth_new.reshape(members, tiles, pairs, 8, LANES).transpose(1, 3, 0, 2, 4).reshape(water_depth.shape)
    return depth_out, flow_new.transpose(0, 2, 1, 3)


def solution(mesh):
    in_specs = (
        P(("groups", "mesh"), None, None),
        P(("groups", "mesh"), None, None, None),
        P(("groups", "mesh"), None, None),
        P(("groups", "mesh"), None),
        P(("groups", "mesh"), None),
        P(("groups", "mesh"), None),
        P(("groups", "mesh"), None),
        P(("groups", "mesh")),
        P(("groups", "mesh"), None),
        P("groups"),
    )
    out_specs = (P(("groups", "mesh"), None, None), P(("groups", "mesh"), None, None, None))
    return jax.shard_map(body, mesh=mesh, in_specs=in_specs, out_specs=out_specs, check_vma=False)
```

```python
import functools
import math

import jax
import jax.numpy as jnp
import numpy as np
from jax import lax
from jax.experimental import pallas as pl
from jax.experimental.pallas import tpu as pltpu
from jax.sharding import PartitionSpec as P


time_step = 0.01
gravity = 1.0
breach_rate = 5.0
LANES = 128


def gauss_solve(matrix, right):
    dimension = matrix.shape[0]
    augmented = np.concatenate([np.array(matrix) * 1.0, np.array(right) * 1.0], axis=1)
    for pivot_col in range(dimension):
        largest = pivot_col + int(np.argmax(np.abs(augmented[pivot_col:, pivot_col])))
        swapped = augmented[[largest, pivot_col]]
        augmented[[pivot_col, largest]] = swapped
        augmented[pivot_col] = augmented[pivot_col] / augmented[pivot_col, pivot_col]
        for row_id in range(dimension):
            if row_id != pivot_col:
                augmented[row_id] = (
                    augmented[row_id] - augmented[row_id, pivot_col] * augmented[pivot_col]
                )
    return augmented[:, dimension:]


def node_tables():
    points = np.array(
        [(across / 3.0, upward / 3.0) for upward in range(4) for across in range(4 - upward)]
    )
    powers = [(power_r, power_s) for power_r in range(4) for power_s in range(4 - power_r)]
    vander = np.zeros((10, 10))
    grad_r = np.zeros((10, 10))
    grad_s = np.zeros((10, 10))
    mono_mass = np.zeros((10, 10))
    for column, (power_r, power_s) in enumerate(powers):
        vander[:, column] = points[:, 0] ** power_r * points[:, 1] ** power_s
        if power_r > 0:
            grad_r[:, column] = power_r * points[:, 0] ** (power_r - 1) * points[:, 1] ** power_s
        if power_s > 0:
            grad_s[:, column] = power_s * points[:, 0] ** power_r * points[:, 1] ** (power_s - 1)
        for second_column, (other_r, other_s) in enumerate(powers):
            mono_mass[column, second_column] = (
                math.factorial(power_r + other_r)
                * math.factorial(power_s + other_s)
                / math.factorial(power_r + other_r + power_s + other_s + 2)
            )
    inverse = gauss_solve(vander, np.eye(10))
    mass_matrix = inverse.T @ mono_mass @ inverse
    line_points = np.arange(4) / 3.0
    line_vander = line_points[:, None] ** np.arange(4)[None, :]
    hilbert = 1.0 / (np.arange(4)[:, None] + np.arange(4)[None, :] + 1.0)
    line_inverse = gauss_solve(line_vander, np.eye(4))
    edge_mass = line_inverse.T @ hilbert @ line_inverse
    face_nodes = np.array([[0, 1, 2, 3], [3, 6, 8, 9], [9, 7, 4, 0]])
    edge_embed = np.zeros((10, 12))
    for face_id in range(3):
        for node_id in range(4):
            edge_embed[face_nodes[face_id, node_id], 4 * face_id : 4 * face_id + 4] += edge_mass[
                node_id
            ]
    lifting = gauss_solve(mass_matrix, edge_embed).reshape(10, 3, 4)
    return (
        np.asarray(grad_r @ inverse, np.float32),
        np.asarray(grad_s @ inverse, np.float32),
        np.asarray(lifting, np.float32),
        face_nodes.reshape(-1),
    )


def round_up(value, step):
    return (value + step - 1) // step * step


def static_tables(members):
    deriv_r, deriv_s, lifting, face_order = node_tables()
    nodes = deriv_r.shape[0]
    pairs = nodes // 2
    used = members * pairs
    comp = round_up(used, 8)
    face_nodes = face_order.reshape(3, 4)
    wide = members * 4

    def lane_of(s, n):
        return (n % 2) * comp + s * pairs + n // 2

    own = np.zeros((LANES, LANES), np.float32)
    own[2 * comp, 3 * wide :] = 1.0
    back = np.zeros((LANES, LANES), np.float32)
    lift = np.zeros((2 * comp, LANES), np.float32)
    along = np.zeros((2, 2 * comp, LANES), np.float32)
    for s in range(members):
        for f in range(3):
            for k in range(4):
                n = int(face_nodes[f, k])
                own[lane_of(s, n), f * wide + s * 4 + k] = 1.0
                back[lane_of(s, n), f * wide + s * 4 + 3 - k] = 1.0
        for n in range(nodes):
            for f in range(3):
                for k in range(4):
                    lift[lane_of(s, n), f * wide + s * 4 + k] = lifting[n, f, k]
            for m in range(nodes):
                along[0, lane_of(s, n), lane_of(s, m)] = -deriv_r[n, m]
                along[1, lane_of(s, n), lane_of(s, m)] = -deriv_s[n, m]
            along[0, lane_of(s, n), 2 * comp + s] = breach_rate
    spread = np.zeros((16, 8 * LANES), np.float32)
    for q in range(4):
        for f in range(3):
            spread[3 * q + f, q * LANES + f * wide : q * LANES + (f + 1) * wide] = 1.0
        spread[12 + q, (4 + q) * LANES : (4 + q) * LANES + 2 * comp] = 1.0
    return dict(
        own=own, back=back, lift=lift, along=along, spread=spread,
        comp=comp, pairs=pairs, used=used, wide=wide, nodes=nodes, members=members,
    )


def high_low(matrix):
    high = matrix.astype(jnp.bfloat16)
    low = (matrix - high.astype(np.float32)).astype(jnp.bfloat16)
    return high, low


def mm(a, b, dims=((1,), (0,))):
    return lax.dot_general(a, b, (dims, ((), ())), preferred_element_type=jnp.float32)


def split(x):
    high = x.astype(jnp.bfloat16)
    return high, (x - high.astype(jnp.float32)).astype(jnp.bfloat16)


def swap_halves(x):
    return pltpu.roll(x, LANES // 2, 1)


def turn(x, eye):
    return mm(eye[...], jnp.concatenate(split(x), axis=1), ((1,), (1,)))


def turn_rows(first, second, c, eye, turned, halves, comp):
    lower = lax.broadcasted_iota(jnp.int32, (comp, LANES), 1) < LANES // 2
    even = jnp.where(lower, first, swap_halves(second))
    odd = jnp.where(lower, swap_halves(first), second)
    fill = jnp.full((LANES - 2 * comp, LANES), 1.0 if c == 0 else 0.0, jnp.float32)
    flat = turn(jnp.concatenate([even, odd, fill], axis=0), eye)
    if turned is not None:
        turned[c] = flat
    high, low = split(flat)
    halves[c * LANES : (c + 1) * LANES, :LANES] = high
    halves[c * LANES : (c + 1) * LANES, LANES:] = low


def rows_of(fields, block, c, comp):
    if c == 0:
        return fields[block, :comp]
    return fields[block, pl.ds(comp + c - 1, comp, stride=2), :]


def place_face(pieces, c, wide, lane):
    moved = [pltpu.roll(p, ((i - c) * wide) % LANES, 1) if i != c else p for i, p in enumerate(pieces)]
    return jnp.where(lane < wide, moved[0], jnp.where(lane < 2 * wide, moved[1], moved[2]))


def root(x):
    return x * lax.rsqrt(x)


def start_all(copies):
    for copy in copies:
        copy.start()
    return copies


def wait_all(copies):
    for copy in copies:
        copy.wait()


def prepare_kernel(
    rim_in, depth_in, flow_in, back_in, eye_in, fields_out, pool_out, across, partner,
    rim, depth, flow, back, eye, fields, pool, halves, sems, *, t, blocks, elements,
):
    comp, pairs, members, wide = t["comp"], t["pairs"], t["members"], t["wide"]
    odd = lax.axis_index("mesh") % 2
    tiles = blocks // 8
    steps = blocks // 2
    group = 2 * 3 * elements
    first = start_all(
        [
            pltpu.make_async_copy(depth_in, depth, sems.at[0]), pltpu.make_async_copy(back_in, back, sems.at[1]),
            pltpu.make_async_copy(eye_in, eye, sems.at[2]), pltpu.make_async_copy(rim_in, rim, sems.at[3]),
        ]
    )

    def part(tile):
        rows = pl.ds(8 * tile, 8)
        return pltpu.make_async_copy(flow_in.at[rows], flow.at[rows], sems.at[4 + tile])

    def field_part(tile):
        rows = pl.ds(8 * tile, 8)
        return pltpu.make_async_copy(fields.at[rows], fields_out.at[rows], sems.at[4 + tiles + tile])

    def pool_part(i):
        lines = pl.ds(group * i, group)
        return pltpu.make_async_copy(pool.at[lines], pool_out.at[lines], sems.at[4 + 2 * tiles + i])

    start_all([part(tile) for tile in range(tiles)])
    wait_all(first)

    def build(i):
        for u in range(2):
            b = 2 * i + u
            tile, sub = b // 8, b % 8
            fields[b, comp - 8 : comp] = jnp.full((8, LANES), 1.0, jnp.float32)
            fields[b, 3 * comp - 16 : 3 * comp] = jnp.zeros((16, LANES), jnp.float32)
            for s in range(members):
                start = (s * tiles + tile) * pairs * 8 + sub
                fields[b, s * pairs : (s + 1) * pairs] = depth[pl.ds(start, pairs, stride=8), :]
                for j in range(pairs):
                    row = comp + 2 * (s * pairs + j)
                    fields[b, row : row + 2] = flow[b, s, :, j * LANES : (j + 1) * LANES]

    def turn_of(i):
        for c in range(3):
            turn_rows(
                rows_of(fields, 2 * i, c, comp), rows_of(fields, 2 * i + 1, c, comp), c, eye, None, halves, comp
            )

    def faces_of(i):
        rows = mm(halves[...], back[...])
        lane = lax.broadcasted_iota(jnp.int32, (LANES, LANES), 1)
        pieces = [rows[c * LANES : (c + 1) * LANES] for c in range(3)]
        for f in range(3):
            face = place_face(pieces, f, wide, lane)
            for u in range(2):
                at = ((2 * i + u) * 3 + f) * elements
                pool[pl.ds(at, elements), :] = face[u * elements : (u + 1) * elements]

    part(0).wait()
    build(0)
    turn_of(0)
    build(1)

    def one(i, carry):
        @pl.when(i % 4 == 0)
        def _():
            part(i // 4).wait()

        faces_of(i - 2)
        turn_of(i - 1)
        build(i)
        pool_part(i - 2).start()

        @pl.when(i % 4 == 3)
        def _():
            field_part(i // 4).start()

        return carry

    lax.fori_loop(2, steps, one, 0)
    faces_of(steps - 2)
    turn_of(steps - 1)
    pool_part(steps - 2).start()
    faces_of(steps - 1)
    pool_part(steps - 1).start()
    width = partner.shape[0]
    near, far = (1 - odd) * width, odd * width

    def pick(i, carry):
        for u in range(32):
            r = i * 32 + u
            partner[pl.ds(r, 1), :] = pool[pl.ds(rim[0, near + r], 1), :]
            across[pl.ds(r, 1), :] = pool[pl.ds(rim[0, far + r], 1), :]
        return carry

    lax.fori_loop(0, width // 32, pick, 0)
    for tile in range(tiles):
        field_part(tile).wait()
    for i in range(steps):
        pool_part(i).wait()


def scan_moves(plan, base, order, place, blocks):
    def one(i, carry):
        leaving, staying = carry
        slot = plan[base + i]
        away = jnp.logical_or(slot < base, slot >= base + blocks).astype(jnp.int32)
        order[jnp.where(away == 1, leaving, blocks - 1 - staying)] = i
        place[i] = lax.div(slot, jnp.int32(blocks))
        return leaving + away, staying + 1 - away

    return lax.fori_loop(0, blocks, one, (jnp.int32(0), jnp.int32(0)))[0]


def scan_origins(plan, own, origin, blocks, devices):
    def device(d, carry):
        mark = jnp.where(d == own, -1, d)
        for i in range(blocks):
            slot = plan[d * blocks + i] - own * blocks
            origin[jnp.where(jnp.logical_and(slot >= 0, slot < blocks), slot, blocks)] = mark
        return carry

    lax.fori_loop(0, devices, device, 0)


def face_rows(angle, scale, links, metric, coefs, blocks, elements):
    shape = (blocks, 3 * elements)
    own = lax.broadcasted_iota(jnp.int32, shape, 0) * (3 * elements) + lax.broadcasted_iota(jnp.int32, shape, 1)
    free = jnp.where(links[...] == own, 0.0, 1.0)
    lower = lax.broadcasted_iota(jnp.int32, (blocks, LANES), 1) < elements
    for q, value in enumerate((jnp.cos(angle[...]), jnp.sin(angle[...]), scale[...], free)):
        two = value[:, :LANES]
        swapped = swap_halves(two)
        third = value[:, LANES:]
        faces = (
            jnp.where(lower, two, swapped), jnp.where(lower, swapped, two), jnp.concatenate([third, third], axis=1)
        )
        for f in range(3):
            coefs[pl.ds(3 * q + f, blocks, stride=16), :] = faces[f]
    for b in range(blocks):
        factors = metric[b]
        coefs[b * 16 + 12 : b * 16 + 16] = jnp.concatenate([factors, factors], axis=1)


def spread_pair(coefs, both, eye, spread, factors, elements):
    lower = lax.broadcasted_iota(jnp.int32, (16, LANES), 1) < elements
    values = jnp.where(lower, coefs[pl.ds(both[0] * 16, 16), :], coefs[pl.ds(both[1] * 16, 16), :])
    rough = values.astype(jnp.bfloat16).astype(jnp.float32)
    stacked = jnp.concatenate([rough, values - rough], axis=0).astype(jnp.bfloat16)
    stacked = mm(eye[:, :LANES], stacked, ((1,), (1,))).astype(jnp.bfloat16)
    factors[...] = mm(stacked, spread[...])


def inflow_rows(breach, both, t):
    rows = []
    for b in both:
        row = jnp.zeros((1, LANES), jnp.float32)
        for s in range(t["members"]):
            level = breach[s, b].astype(jnp.float32)
            row = jnp.where(lax.broadcasted_iota(jnp.int32, (1, LANES), 1) == 2 * t["comp"] + s, level, row)
        rows.append(row)
    return rows


def volume_rows(rows, turned, factors, first, inflow, pieces):
    rx, sx, ry, sy = (factors[rows, q * LANES : (q + 1) * LANES] for q in range(first, first + 4))
    height, flow_x, flow_y = (turned[c, rows] for c in range(3))
    pressure = 0.5 * gravity * height * height
    inverse = 1.0 / height
    speed_x = flow_x * inverse
    speed_y = flow_y * inverse
    cross = flow_y * speed_x
    flux_f = (flow_x, flow_x * speed_x + pressure, cross)
    flux_g = (flow_y, cross, flow_y * speed_y + pressure)
    for c in range(3):
        along_r = rx * flux_f[c] + ry * flux_g[c]
        along_s = sx * flux_f[c] + sy * flux_g[c]
        if c == 0:
            along_r = along_r + inflow
        pieces[c, rows, 0:LANES], pieces[c, rows, LANES : 2 * LANES] = split(along_r)
        pieces[c, rows, 2 * LANES : 3 * LANES], pieces[c, rows, 3 * LANES : 4 * LANES] = split(along_s)


def flux_rows(rows, traces, outer, factors, pieces, first, wide):
    lane = lax.broadcasted_iota(jnp.int32, (rows.stop - rows.start, LANES), 1)
    n_x, n_y, scale, free = (factors[rows, q * LANES : (q + 1) * LANES] for q in range(4))
    theirs = [outer[f * LANES + rows.start : f * LANES + rows.stop] for f in range(3)]
    height, flow_x, flow_y = (traces[c, rows] for c in range(3))
    is_wall = free < 0.5
    through = flow_x * n_x + flow_y * n_y
    twice = through + through
    height_o = jnp.where(is_wall, height, place_face(theirs, 0, wide, lane))
    flow_xo = jnp.where(is_wall, flow_x - twice * n_x, place_face(theirs, 1, wide, lane))
    flow_yo = jnp.where(is_wall, flow_y - twice * n_y, place_face(theirs, 2, wide, lane))
    speed = through / height
    speed_o = (flow_xo * n_x + flow_yo * n_y) / height_o
    fast = jnp.maximum(
        jnp.abs(speed) + root(gravity * height), jnp.abs(speed_o) + root(gravity * height_o)
    )
    ours, others = speed - fast, speed_o - fast
    half = 0.5 * scale
    push = 0.5 * gravity * (height * height - height_o * height_o)
    jumps = (
        half * (height * ours - height_o * others),
        half * (flow_x * ours - flow_xo * others + push * n_x),
        half * (flow_y * ours - flow_yo * others + push * n_y),
    )
    for c in range(3):
        high, rest = split(jumps[c])
        pieces[c, rows, first : first + LANES] = high
        pieces[c, rows, first + LANES : first + 2 * LANES] = rest
        pieces[c, rows, first + 2 * LANES : first + 3 * LANES] = high


def pair_gains(tall, comp, elements):
    narrow = lax.broadcasted_iota(jnp.int32, (comp, LANES), 1) < elements
    even, odd = tall[:comp], tall[comp:]
    return jnp.where(narrow, even, swap_halves(odd)), jnp.where(narrow, swap_halves(even), odd)


def row_chunks(step):
    return [slice(i * step, (i + 1) * step) for i in range(LANES // step)]


RING = 8


def finish_kernel(
    plan_in, wet_in, breach_in, links_in, angle_in, scale_in, metric_in,
    fields_in, pool_in, partner_in, across_in, own_in, spread_in, matrix_in, eye_in,
    *rest, t, blocks, elements, devices, leaving,
):
    outs, scratch = (rest[:1], rest[1:]) if leaving else (rest[:3], rest[3:])
    plan, wet, breach, links, angle, scale, metric, fields, pool, own, spread, matrix, eye, *scratch = scratch
    order, place, coefs, turned, halves, traces, factors, outer, pieces, near, sems, staged, *scratch = scratch
    comp, wide, used = t["comp"], t["wide"], t["used"]
    faces = blocks * 3 * elements
    width = partner_in.shape[0]
    odd = lax.axis_index("mesh") % 2
    near_rows = pl.multiple_of(faces + (1 - odd) * width, 8)
    far_rows = pl.multiple_of(faces + odd * width, 8)
    loads = [
        (plan_in, plan), (angle_in, angle), (scale_in, scale), (links_in, links), (metric_in, metric),
        (fields_in, fields), (wet_in, wet), (breach_in, breach), (eye_in, eye), (own_in, own),
        (spread_in, spread), (matrix_in, matrix), (pool_in, pool.at[pl.ds(0, faces)]),
        (partner_in, pool.at[pl.ds(near_rows, width)]), (across_in, pool.at[pl.ds(far_rows, width)]),
    ]
    n = len(loads)
    loads = start_all([pltpu.make_async_copy(a, b, sems.at[i]) for i, (a, b) in enumerate(loads)])
    index = lax.axis_index("mesh")
    loads[0].wait()
    n_leaving = scan_moves(plan, index * blocks, order, place, blocks)
    begin = 0 if leaving else n_leaving
    end = n_leaving if leaving else blocks
    n_pairs = near.shape[0] // 2
    steps = (end - begin + 2 * n_pairs - 1) // (2 * n_pairs)

    def at(i, u):
        return jnp.maximum(jnp.minimum(begin + 2 * n_pairs * i + u, end - 1), 0)

    def indices(i):
        return [
            pltpu.make_async_copy(links_in.at[order[at(i, u)]], near.at[u], sems.at[n + u])
            for u in range(2 * n_pairs)
        ]

    def send(p):
        rows = outs[0].shape[1]
        return pltpu.make_async_copy(staged.at[p, pl.ds(0, rows)], outs[0].at[place[order[p]]], sems.at[n + 2 * n_pairs + p % RING])

    @pl.when(steps > 0)
    def _():
        start_all(indices(0))

    wait_all(loads[1:5])
    face_rows(angle, scale, links, metric, coefs, blocks, elements)
    if not leaving:
        scan_origins(plan, index, scratch[2], blocks, devices)
    wait_all(loads[5:-3])
    chunks = row_chunks(16)

    def pick(w, rows):
        for f in range(3):
            for line in range(rows.start, rows.stop):
                v = near[2 * w + line // elements, f * elements + line % elements]
                outer[w % 2, f * LANES + line : f * LANES + line + 1, :] = pool[pl.ds(v, 1), :]

    def pair_of(i, w):
        return [order[at(i, 2 * w + u)] for u in range(2)]

    def lay_out(w, pair):
        for c in range(3):
            turn_rows(
                rows_of(fields, pair[0], c, comp), rows_of(fields, pair[1], c, comp), c, eye,
                turned.at[w % 2], halves.at[w % 2], comp,
            )
        inner = mm(halves[w % 2], own[...])
        for c in range(3):
            traces[w % 2, c] = inner[c * LANES : (c + 1) * LANES]
        spread_pair(coefs, pair, eye, spread, factors.at[w % 2], elements)

    def one(i, carry):
        both = [pair_of(i, w) for w in range(n_pairs)]
        inflow = [inflow_rows(breach, pair, t) for pair in both]

        def fluxes(w, rows):
            q = w % 2
            volume_rows(rows, turned.at[q], factors.at[q], 4, inflow[w][rows.start // elements], pieces.at[q])
            flux_rows(rows, traces.at[q], outer.at[q], factors.at[q], pieces.at[q], 4 * LANES, wide)

        def combine(w, c):
            gains = pair_gains(mm(matrix[...], pieces[w % 2, c], ((1,), (1,))), comp, elements)
            for u in range(2):
                b = both[w][u]
                rate = time_step * wet[b].astype(jnp.float32)
                done = rows_of(fields, b, c, comp) + rate * gains[u]
                row = at(i, 2 * w + u) if leaving else 2 * w + u
                if c == 0:
                    staged[row, :comp] = done
                else:
                    staged[row, pl.ds(used + c - 1, comp, stride=2), :] = done

        def hand_over(w):
            for u in range(2):
                if leaving:
                    p = 2 * n_pairs * i + 2 * w + u

                    @pl.when(p < end)
                    def _():
                        @pl.when(p >= RING)
                        def _():
                            send(p - RING).wait()

                        send(p).start()
                else:
                    write_depth(both[w][u], staged.at[2 * w + u], scratch[0], t, blocks)
                    write_flow(both[w][u], staged.at[2 * w + u], scratch[1], t)

        wait_all(indices(i))
        for rows in chunks:
            pick(0, rows)
        for w in range(n_pairs):
            if w + 1 < n_pairs:
                lay_out(w + 1, both[w + 1])
            for k, rows in enumerate(chunks):
                if w > 0 and k < 3:
                    combine(w - 1, k)
                fluxes(w, rows)
                if w + 1 < n_pairs:
                    pick(w + 1, rows)
        for c in range(3):
            combine(n_pairs - 1, c)

        @pl.when(i + 1 < steps)
        def _():
            start_all(indices(i + 1))
            lay_out(0, pair_of(i + 1, 0))

        for w in range(n_pairs):
            hand_over(w)
        return carry

    lay_out(0, pair_of(0, 0))
    wait_all(loads[-3:])
    lax.fori_loop(0, steps, one, 0)
    if leaving:

        def drain(p, carry):
            send(p).wait()
            return carry

        lax.fori_loop(jnp.maximum(end - RING, 0), end, drain, 0)
    else:
        kept = ((scratch[0], outs[0]), (scratch[1], outs[1]), (scratch[2].at[pl.ds(0, outs[2].shape[0])], outs[2]))
        wait_all(start_all([pltpu.make_async_copy(a, b, sems.at[n + 2 * n_pairs + i]) for i, (a, b) in enumerate(kept)]))


def write_depth(b, rows, depth, t, blocks):
    pairs, members = t["pairs"], t["members"]
    tile, sub = b // 8, b % 8
    for s in range(members):
        start = (s * (blocks // 8) + tile) * pairs * 8 + sub
        depth[pl.ds(start, pairs, stride=8), :] = rows[s * pairs : (s + 1) * pairs]


def write_flow(b, rows, flow, t):
    pairs, members, used = t["pairs"], t["members"], t["used"]
    for s in range(members):
        for j in range(pairs):
            row = used + 2 * (s * pairs + j)
            flow[b, s, :, j * LANES : (j + 1) * LANES] = rows[row : row + 2]


def merge_kernel(
    origin_in, got_in, depth_in, flow_in, depth_out, flow_out, origin, depth, flow, got, sems, *, t, blocks
):
    pairs, members = t["pairs"], t["members"]
    loads = start_all(
        [
            pltpu.make_async_copy(a, b, sems.at[i])
            for i, (a, b) in enumerate(((origin_in, origin), (got_in, got)))
        ]
    )
    wait_all(loads)

    def flow_part(b, k):
        return pltpu.make_async_copy(flow.at[b], flow_out.at[b], sems.at[2 + k % RING])

    def depth_part(b, k):
        return pltpu.make_async_copy(
            depth.at[b], depth_out.at[:, b // 8, :, b % 8], sems.at[2 + RING + k % RING]
        )

    def settle(k):
        flow_part(0, k).wait()
        depth_part(0, k).wait()

    def put(b, k):
        came = origin[b] >= 0

        @pl.when(came)
        def _():
            @pl.when(k >= RING)
            def _():
                settle(k)

            for s in range(members):
                depth[b, s] = got[origin[b], s * pairs : (s + 1) * pairs]
            depth_part(b, k).start()
            write_flow(b, got.at[origin[b]], flow, t)
            flow_part(b, k).start()

        return k + came.astype(jnp.int32)

    arrivals = lax.fori_loop(0, blocks, put, jnp.int32(0))

    def drain(k, carry):
        settle(k)
        return carry

    lax.fori_loop(jnp.maximum(arrivals - RING, 0), arrivals, drain, 0)


SMEM = pl.BlockSpec(memory_space=pltpu.SMEM)
HBM = pl.BlockSpec(memory_space=pltpu.HBM)
VMEM = pl.BlockSpec(memory_space=pltpu.VMEM)


def call(kernel, out_shape, n_smem, n_args, scratch, out_specs, **keys):
    return pl.pallas_call(
        kernel,
        out_shape=out_shape,
        in_specs=[SMEM] * n_smem + [HBM] * n_args,
        out_specs=out_specs,
        scratch_shapes=scratch,
        compiler_params=pltpu.CompilerParams(vmem_limit_bytes=64 << 20),
        **keys,
    )


def body(
    water_depth, momentum, metric, face_scale, face_angle, face_map, rim_faces, wet_blocks, breach, block_plan
):
    blocks, members, _ = water_depth.shape
    elements = metric.shape[2]
    t = static_tables(members)
    comp, pairs, used = t["comp"], t["pairs"], t["used"]
    f32, bf16 = jnp.float32, jnp.bfloat16
    tiles = blocks // 8
    depth_rows = water_depth.reshape(tiles, 8, members, pairs, LANES).transpose(2, 0, 3, 1, 4).reshape(-1, LANES)
    flow_rows = momentum.transpose(0, 2, 1, 3)
    faces = face_map.size
    width = rim_faces.shape[1] // 2
    dma = pltpu.SemaphoreType.DMA

    back = jnp.asarray(np.tile(t["back"], (2, 1)), bf16)
    eye = jnp.asarray(np.tile(np.eye(LANES), (1, 2)), bf16)
    fields, pool, to_across, to_partner = call(
        functools.partial(prepare_kernel, t=t, blocks=blocks, elements=elements),
        (
            jax.ShapeDtypeStruct((blocks, 3 * comp, LANES), f32),
            jax.ShapeDtypeStruct((faces, LANES), f32),
            jax.ShapeDtypeStruct((width, LANES), f32),
            jax.ShapeDtypeStruct((width, LANES), f32),
        ),
        0, 5,
        [
            pltpu.SMEM(rim_faces.shape, jnp.int32), pltpu.VMEM(depth_rows.shape, f32), pltpu.VMEM(flow_rows.shape, f32), pltpu.VMEM(back.shape, bf16),
            pltpu.VMEM(eye.shape, bf16),
            pltpu.VMEM((blocks, 3 * comp, LANES), f32), pltpu.VMEM((faces, LANES), f32),
            pltpu.VMEM((3 * LANES, 2 * LANES), bf16), dma((4 + 2 * tiles + blocks // 2,)),
        ],
        (HBM, HBM, VMEM, VMEM),
    )(rim_faces, depth_rows, flow_rows, back, eye)

    count = lax.axis_size("mesh")
    partners = [(i, i ^ 1) for i in range(count)]
    neighbours = [(i, i + 1 if i % 2 else i - 1) for i in range(1, count - 1)]
    across = lax.ppermute(to_across, "mesh", neighbours)
    partner = lax.ppermute(to_partner, "mesh", partners)

    lift_h, lift_l = high_low(t["lift"])
    along_r, along_s = t["along"]
    matrix = np.concatenate(
        [along_r, along_r, along_s, along_s, *(np.asarray(m, np.float32) for m in (lift_h, lift_h, lift_l))], axis=1
    )
    mats = [
        jnp.asarray(np.tile(t["own"], (2, 1)), bf16), jnp.asarray(np.tile(t["spread"], (2, 1)), bf16),
        jnp.asarray(matrix, bf16), eye,
    ]
    packed = round_up(3 * used, 8)

    i32 = jnp.int32
    block_rows = (3 * comp, LANES)

    def finish(leaving, n_pairs, out_shape, extra):
        return call(
            functools.partial(
                finish_kernel, t=t, blocks=blocks, elements=elements, devices=count, leaving=leaving
            ),
            out_shape,
            0, 15,
            [
                pltpu.SMEM(block_plan.shape, i32), pltpu.SMEM(wet_blocks.shape, i32),
                pltpu.SMEM((members, blocks), i32), pltpu.VMEM(face_map.shape, i32),
                pltpu.VMEM(face_angle.shape, f32), pltpu.VMEM(face_scale.shape, f32), pltpu.VMEM(metric.shape, f32),
                pltpu.VMEM((blocks, *block_rows), f32), pltpu.VMEM((faces + 2 * width, LANES), f32),
                *[pltpu.VMEM(m.shape, bf16) for m in mats],
                pltpu.SMEM((blocks,), i32), pltpu.SMEM((blocks,), i32), pltpu.VMEM((blocks * 16, LANES), f32),
                pltpu.VMEM((2, 3, LANES, LANES), f32), pltpu.VMEM((2, 3 * LANES, 2 * LANES), bf16),
                pltpu.VMEM((2, 3, LANES, LANES), f32), pltpu.VMEM((2, LANES, 8 * LANES), f32),
                pltpu.VMEM((2, 3 * LANES, LANES), f32), pltpu.VMEM((2, 3, LANES, 7 * LANES), bf16),
                pltpu.SMEM((2 * n_pairs, face_map.shape[1]), i32), dma((16 + 2 * n_pairs + RING,)), *extra,
            ],
            jax.tree.map(lambda _: HBM, out_shape),
        )(
            block_plan, wet_blocks, breach.T, face_map, face_angle, face_scale, metric, fields, pool, partner, across,
            *mats,
        )

    sent = finish(True, 4, jax.ShapeDtypeStruct((count, packed, LANES), f32), [pltpu.VMEM((blocks, *block_rows), f32)])
    got = lax.all_to_all(sent, "mesh", split_axis=0, concat_axis=0, tiled=True)
    final = (jax.ShapeDtypeStruct(depth_rows.shape, f32), jax.ShapeDtypeStruct(flow_rows.shape, f32))
    whole = [pltpu.VMEM(depth_rows.shape, f32), pltpu.VMEM(flow_rows.shape, f32)]
    depth_kept, flow_kept, origin = finish(
        False, 2, (*final, jax.ShapeDtypeStruct((LANES,), i32)),
        [pltpu.VMEM((4, *block_rows), f32), *whole, pltpu.SMEM((LANES,), i32)],
    )
    tall = (members, tiles, pairs, 8, LANES)
    depth_new, flow_new = call(
        functools.partial(merge_kernel, t=t, blocks=blocks),
        (jax.ShapeDtypeStruct(tall, f32), final[1]),
        0, 4,
        [
            pltpu.SMEM((LANES,), i32), pltpu.VMEM((blocks, members, pairs, LANES), f32), whole[1],
            pltpu.VMEM((count, packed, LANES), f32), dma((2 + 2 * RING,)),
        ],
        (HBM, HBM),
        input_output_aliases={2: 0, 3: 1},
    )(origin, got, depth_kept.reshape(tall), flow_kept)
    depth_out = depth_new.reshape(members, tiles, pairs, 8, LANES).transpose(1, 3, 0, 2, 4).reshape(water_depth.shape)
    return depth_out, flow_new.transpose(0, 2, 1, 3)


def solution(mesh):
    in_specs = (
        P(("groups", "mesh"), None, None),
        P(("groups", "mesh"), None, None, None),
        P(("groups", "mesh"), None, None),
        P(("groups", "mesh"), None),
        P(("groups", "mesh"), None),
        P(("groups", "mesh"), None),
        P(("groups", "mesh"), None),
        P(("groups", "mesh")),
        P(("groups", "mesh"), None),
        P("groups"),
    )
    out_specs = (P(("groups", "mesh"), None, None), P(("groups", "mesh"), None, None, None))
    return jax.shard_map(body, mesh=mesh, in_specs=in_specs, out_specs=out_specs, check_vma=False)
```

```python
import functools
import math

import jax
import jax.numpy as jnp
import numpy as np
from jax import lax
from jax.experimental import pallas as pl
from jax.experimental.pallas import tpu as pltpu
from jax.sharding import PartitionSpec as P


time_step = 0.01
gravity = 1.0
breach_rate = 5.0
LANES = 128


def gauss_solve(matrix, right):
    dimension = matrix.shape[0]
    augmented = np.concatenate([np.array(matrix) * 1.0, np.array(right) * 1.0], axis=1)
    for pivot_col in range(dimension):
        largest = pivot_col + int(np.argmax(np.abs(augmented[pivot_col:, pivot_col])))
        swapped = augmented[[largest, pivot_col]]
        augmented[[pivot_col, largest]] = swapped
        augmented[pivot_col] = augmented[pivot_col] / augmented[pivot_col, pivot_col]
        for row_id in range(dimension):
            if row_id != pivot_col:
                augmented[row_id] = (
                    augmented[row_id] - augmented[row_id, pivot_col] * augmented[pivot_col]
                )
    return augmented[:, dimension:]


def node_tables():
    points = np.array(
        [(across / 3.0, upward / 3.0) for upward in range(4) for across in range(4 - upward)]
    )
    powers = [(power_r, power_s) for power_r in range(4) for power_s in range(4 - power_r)]
    vander = np.zeros((10, 10))
    grad_r = np.zeros((10, 10))
    grad_s = np.zeros((10, 10))
    mono_mass = np.zeros((10, 10))
    for column, (power_r, power_s) in enumerate(powers):
        vander[:, column] = points[:, 0] ** power_r * points[:, 1] ** power_s
        if power_r > 0:
            grad_r[:, column] = power_r * points[:, 0] ** (power_r - 1) * points[:, 1] ** power_s
        if power_s > 0:
            grad_s[:, column] = power_s * points[:, 0] ** power_r * points[:, 1] ** (power_s - 1)
        for second_column, (other_r, other_s) in enumerate(powers):
            mono_mass[column, second_column] = (
                math.factorial(power_r + other_r)
                * math.factorial(power_s + other_s)
                / math.factorial(power_r + other_r + power_s + other_s + 2)
            )
    inverse = gauss_solve(vander, np.eye(10))
    mass_matrix = inverse.T @ mono_mass @ inverse
    line_points = np.arange(4) / 3.0
    line_vander = line_points[:, None] ** np.arange(4)[None, :]
    hilbert = 1.0 / (np.arange(4)[:, None] + np.arange(4)[None, :] + 1.0)
    line_inverse = gauss_solve(line_vander, np.eye(4))
    edge_mass = line_inverse.T @ hilbert @ line_inverse
    face_nodes = np.array([[0, 1, 2, 3], [3, 6, 8, 9], [9, 7, 4, 0]])
    edge_embed = np.zeros((10, 12))
    for face_id in range(3):
        for node_id in range(4):
            edge_embed[face_nodes[face_id, node_id], 4 * face_id : 4 * face_id + 4] += edge_mass[
                node_id
            ]
    lifting = gauss_solve(mass_matrix, edge_embed).reshape(10, 3, 4)
    return (
        np.asarray(grad_r @ inverse, np.float32),
        np.asarray(grad_s @ inverse, np.float32),
        np.asarray(lifting, np.float32),
        face_nodes.reshape(-1),
    )


def round_up(value, step):
    return (value + step - 1) // step * step


def static_tables(members):
    deriv_r, deriv_s, lifting, face_order = node_tables()
    nodes = deriv_r.shape[0]
    pairs = nodes // 2
    used = members * pairs
    comp = round_up(used, 8)
    face_nodes = face_order.reshape(3, 4)
    wide = members * 4

    def lane_of(s, n):
        return (n % 2) * comp + s * pairs + n // 2

    own = np.zeros((LANES, LANES), np.float32)
    own[2 * comp, 3 * wide :] = 1.0
    back = np.zeros((LANES, LANES), np.float32)
    lift = np.zeros((2 * comp, LANES), np.float32)
    along = np.zeros((2, 2 * comp, LANES), np.float32)
    for s in range(members):
        for f in range(3):
            for k in range(4):
                n = int(face_nodes[f, k])
                own[lane_of(s, n), f * wide + s * 4 + k] = 1.0
                back[lane_of(s, n), f * wide + s * 4 + 3 - k] = 1.0
        for n in range(nodes):
            for f in range(3):
                for k in range(4):
                    lift[lane_of(s, n), f * wide + s * 4 + k] = lifting[n, f, k]
            for m in range(nodes):
                along[0, lane_of(s, n), lane_of(s, m)] = -deriv_r[n, m]
                along[1, lane_of(s, n), lane_of(s, m)] = -deriv_s[n, m]
            along[0, lane_of(s, n), 2 * comp + s] = breach_rate
    spread = np.zeros((16, 8 * LANES), np.float32)
    for q in range(4):
        for f in range(3):
            spread[3 * q + f, q * LANES + f * wide : q * LANES + (f + 1) * wide] = 1.0
        spread[12 + q, (4 + q) * LANES : (4 + q) * LANES + 2 * comp] = 1.0
    return dict(
        own=own, back=back, lift=lift, along=along, spread=spread,
        comp=comp, pairs=pairs, used=used, wide=wide, nodes=nodes, members=members,
    )


def high_low(matrix):
    high = matrix.astype(jnp.bfloat16)
    low = (matrix - high.astype(np.float32)).astype(jnp.bfloat16)
    return high, low


def mm(a, b, dims=((1,), (0,))):
    return lax.dot_general(a, b, (dims, ((), ())), preferred_element_type=jnp.float32)


def split(x):
    high = x.astype(jnp.bfloat16)
    return high, (x - high.astype(jnp.float32)).astype(jnp.bfloat16)


def swap_halves(x):
    return pltpu.roll(x, LANES // 2, 1)


def turn(x, eye):
    return mm(eye[...], jnp.concatenate(split(x), axis=1), ((1,), (1,)))


def turn_rows(first, second, c, eye, turned, halves, comp):
    lower = lax.broadcasted_iota(jnp.int32, (comp, LANES), 1) < LANES // 2
    even = jnp.where(lower, first, swap_halves(second))
    odd = jnp.where(lower, swap_halves(first), second)
    fill = jnp.full((LANES - 2 * comp, LANES), 1.0 if c == 0 else 0.0, jnp.float32)
    flat = turn(jnp.concatenate([even, odd, fill], axis=0), eye)
    if turned is not None:
        turned[c] = flat
    high, low = split(flat)
    halves[c * LANES : (c + 1) * LANES, :LANES] = high
    halves[c * LANES : (c + 1) * LANES, LANES:] = low


def rows_of(fields, block, c, comp):
    if c == 0:
        return fields[block, :comp]
    return fields[block, pl.ds(comp + c - 1, comp, stride=2), :]


def place_face(pieces, c, wide, lane):
    moved = [pltpu.roll(p, ((i - c) * wide) % LANES, 1) if i != c else p for i, p in enumerate(pieces)]
    return jnp.where(lane < wide, moved[0], jnp.where(lane < 2 * wide, moved[1], moved[2]))


def root(x):
    return x * lax.rsqrt(x)


def start_all(copies):
    for copy in copies:
        copy.start()
    return copies


def wait_all(copies):
    for copy in copies:
        copy.wait()


def prepare_kernel(
    rim_in, depth_in, flow_in, back_in, eye_in, fields_out, pool_out, across, partner,
    rim, depth, flow, back, eye, fields, pool, halves, sems, *, t, blocks, elements,
):
    comp, pairs, members, wide = t["comp"], t["pairs"], t["members"], t["wide"]
    odd = lax.axis_index("mesh") % 2
    tiles = blocks // 8
    steps = blocks // 2
    group = 2 * 3 * elements
    first = start_all(
        [
            pltpu.make_async_copy(depth_in, depth, sems.at[0]), pltpu.make_async_copy(back_in, back, sems.at[1]),
            pltpu.make_async_copy(eye_in, eye, sems.at[2]), pltpu.make_async_copy(rim_in, rim, sems.at[3]),
        ]
    )

    def part(tile):
        rows = pl.ds(8 * tile, 8)
        return pltpu.make_async_copy(flow_in.at[rows], flow.at[rows], sems.at[4 + tile])

    def field_part(tile):
        rows = pl.ds(8 * tile, 8)
        return pltpu.make_async_copy(fields.at[rows], fields_out.at[rows], sems.at[4 + tiles + tile])

    def pool_part(i):
        lines = pl.ds(group * i, group)
        return pltpu.make_async_copy(pool.at[lines], pool_out.at[lines], sems.at[4 + 2 * tiles + i])

    start_all([part(tile) for tile in range(tiles)])
    wait_all(first)

    def build(i):
        for u in range(2):
            b = 2 * i + u
            tile, sub = b // 8, b % 8
            fields[b, comp - 8 : comp] = jnp.full((8, LANES), 1.0, jnp.float32)
            fields[b, 3 * comp - 16 : 3 * comp] = jnp.zeros((16, LANES), jnp.float32)
            for s in range(members):
                start = (s * tiles + tile) * pairs * 8 + sub
                fields[b, s * pairs : (s + 1) * pairs] = depth[pl.ds(start, pairs, stride=8), :]
                for j in range(pairs):
                    row = comp + 2 * (s * pairs + j)
                    fields[b, row : row + 2] = flow[b, s, :, j * LANES : (j + 1) * LANES]

    def turn_of(i, slot):
        for c in range(3):
            turn_rows(
                rows_of(fields, 2 * i, c, comp), rows_of(fields, 2 * i + 1, c, comp), c, eye, None,
                halves.at[slot], comp,
            )

    def faces_of(i, slot):
        rows = mm(halves[slot], back[...])
        lane = lax.broadcasted_iota(jnp.int32, (LANES, LANES), 1)
        pieces = [rows[c * LANES : (c + 1) * LANES] for c in range(3)]
        for f in range(3):
            face = place_face(pieces, f, wide, lane)
            for u in range(2):
                at = ((2 * i + u) * 3 + f) * elements
                pool[pl.ds(at, elements), :] = face[u * elements : (u + 1) * elements]

    part(0).wait()
    build(0)
    build(1)
    turn_of(0, 0)
    turn_of(1, 1)
    build(2)
    build(3)
    field_part(0).start()

    def one(h, carry):
        i = 2 * h

        @pl.when(h % 2 == 0)
        def _():
            part(h // 2).wait()

        for slot in range(2):
            faces_of(i - 4 + slot, slot)
        for slot in range(2):
            turn_of(i - 2 + slot, slot)
        for slot in range(2):
            build(i + slot)
        for slot in range(2):
            pool_part(i - 4 + slot).start()

        @pl.when(h % 2 == 1)
        def _():
            field_part(h // 2).start()

        return carry

    lax.fori_loop(2, steps // 2, one, 0)
    for slot in range(2):
        faces_of(steps - 4 + slot, slot)
    for slot in range(2):
        turn_of(steps - 2 + slot, slot)
    for slot in range(2):
        pool_part(steps - 4 + slot).start()
    for slot in range(2):
        faces_of(steps - 2 + slot, slot)
        pool_part(steps - 2 + slot).start()
    width = partner.shape[0]
    near, far = (1 - odd) * width, odd * width

    def pick(i, carry):
        for u in range(32):
            r = i * 32 + u
            partner[pl.ds(r, 1), :] = pool[pl.ds(rim[0, near + r], 1), :]
            across[pl.ds(r, 1), :] = pool[pl.ds(rim[0, far + r], 1), :]
        return carry

    lax.fori_loop(0, width // 32, pick, 0)
    for tile in range(tiles):
        field_part(tile).wait()
    for i in range(steps):
        pool_part(i).wait()


def scan_moves(plan, base, order, place, blocks):
    def one(i, carry):
        leaving, staying = carry
        slot = plan[base + i]
        away = jnp.logical_or(slot < base, slot >= base + blocks).astype(jnp.int32)
        order[jnp.where(away == 1, leaving, blocks - 1 - staying)] = i
        place[i] = lax.div(slot, jnp.int32(blocks))
        return leaving + away, staying + 1 - away

    return lax.fori_loop(0, blocks, one, (jnp.int32(0), jnp.int32(0)))[0]


def scan_origins(plan, own, origin, blocks, devices):
    def device(d, carry):
        mark = jnp.where(d == own, -1, d)
        for i in range(blocks):
            slot = plan[d * blocks + i] - own * blocks
            origin[jnp.where(jnp.logical_and(slot >= 0, slot < blocks), slot, blocks)] = mark
        return carry

    lax.fori_loop(0, devices, device, 0)


def face_rows(angle, scale, links, metric, coefs, blocks, elements):
    shape = (blocks, 3 * elements)
    own = lax.broadcasted_iota(jnp.int32, shape, 0) * (3 * elements) + lax.broadcasted_iota(jnp.int32, shape, 1)
    free = jnp.where(links[...] == own, 0.0, 1.0)
    lower = lax.broadcasted_iota(jnp.int32, (blocks, LANES), 1) < elements
    for q, value in enumerate((jnp.cos(angle[...]), jnp.sin(angle[...]), scale[...], free)):
        two = value[:, :LANES]
        swapped = swap_halves(two)
        third = value[:, LANES:]
        faces = (
            jnp.where(lower, two, swapped), jnp.where(lower, swapped, two), jnp.concatenate([third, third], axis=1)
        )
        for f in range(3):
            coefs[pl.ds(3 * q + f, blocks, stride=16), :] = faces[f]
    for b in range(blocks):
        factors = metric[b]
        coefs[b * 16 + 12 : b * 16 + 16] = jnp.concatenate([factors, factors], axis=1)


def spread_pair(coefs, both, eye, spread, factors, elements):
    lower = lax.broadcasted_iota(jnp.int32, (16, LANES), 1) < elements
    values = jnp.where(lower, coefs[pl.ds(both[0] * 16, 16), :], coefs[pl.ds(both[1] * 16, 16), :])
    rough = values.astype(jnp.bfloat16).astype(jnp.float32)
    stacked = jnp.concatenate([rough, values - rough], axis=0).astype(jnp.bfloat16)
    stacked = mm(eye[:, :LANES], stacked, ((1,), (1,))).astype(jnp.bfloat16)
    factors[...] = mm(stacked, spread[...])


def inflow_rows(breach, both, t):
    rows = []
    for b in both:
        row = jnp.zeros((1, LANES), jnp.float32)
        for s in range(t["members"]):
            level = breach[s, b].astype(jnp.float32)
            row = jnp.where(lax.broadcasted_iota(jnp.int32, (1, LANES), 1) == 2 * t["comp"] + s, level, row)
        rows.append(row)
    return rows


def volume_rows(rows, turned, factors, first, inflow, pieces):
    rx, sx, ry, sy = (factors[rows, q * LANES : (q + 1) * LANES] for q in range(first, first + 4))
    height, flow_x, flow_y = (turned[c, rows] for c in range(3))
    pressure = 0.5 * gravity * height * height
    inverse = 1.0 / height
    speed_x = flow_x * inverse
    speed_y = flow_y * inverse
    cross = flow_y * speed_x
    flux_f = (flow_x, flow_x * speed_x + pressure, cross)
    flux_g = (flow_y, cross, flow_y * speed_y + pressure)
    for c in range(3):
        along_r = rx * flux_f[c] + ry * flux_g[c]
        along_s = sx * flux_f[c] + sy * flux_g[c]
        if c == 0:
            along_r = along_r + inflow
        pieces[c, rows, 0:LANES], pieces[c, rows, LANES : 2 * LANES] = split(along_r)
        pieces[c, rows, 2 * LANES : 3 * LANES], pieces[c, rows, 3 * LANES : 4 * LANES] = split(along_s)


def flux_rows(rows, traces, outer, factors, pieces, first, wide):
    lane = lax.broadcasted_iota(jnp.int32, (rows.stop - rows.start, LANES), 1)
    n_x, n_y, scale, free = (factors[rows, q * LANES : (q + 1) * LANES] for q in range(4))
    theirs = [outer[f * LANES + rows.start : f * LANES + rows.stop] for f in range(3)]
    height, flow_x, flow_y = (traces[c, rows] for c in range(3))
    is_wall = free < 0.5
    through = flow_x * n_x + flow_y * n_y
    twice = through + through
    height_o = jnp.where(is_wall, height, place_face(theirs, 0, wide, lane))
    flow_xo = jnp.where(is_wall, flow_x - twice * n_x, place_face(theirs, 1, wide, lane))
    flow_yo = jnp.where(is_wall, flow_y - twice * n_y, place_face(theirs, 2, wide, lane))
    speed = through / height
    speed_o = (flow_xo * n_x + flow_yo * n_y) / height_o
    fast = jnp.maximum(
        jnp.abs(speed) + root(gravity * height), jnp.abs(speed_o) + root(gravity * height_o)
    )
    ours, others = speed - fast, speed_o - fast
    half = 0.5 * scale
    push = 0.5 * gravity * (height * height - height_o * height_o)
    jumps = (
        half * (height * ours - height_o * others),
        half * (flow_x * ours - flow_xo * others + push * n_x),
        half * (flow_y * ours - flow_yo * others + push * n_y),
    )
    for c in range(3):
        high, rest = split(jumps[c])
        pieces[c, rows, first : first + LANES] = high
        pieces[c, rows, first + LANES : first + 2 * LANES] = rest
        pieces[c, rows, first + 2 * LANES : first + 3 * LANES] = high


def pair_gains(tall, comp, elements):
    narrow = lax.broadcasted_iota(jnp.int32, (comp, LANES), 1) < elements
    even, odd = tall[:comp], tall[comp:]
    return jnp.where(narrow, even, swap_halves(odd)), jnp.where(narrow, swap_halves(even), odd)


def row_chunks(step):
    return [slice(i * step, (i + 1) * step) for i in range(LANES // step)]


RING = 8


def finish_kernel(
    plan_in, wet_in, breach_in, links_in, angle_in, scale_in, metric_in,
    fields_in, pool_in, partner_in, across_in, own_in, spread_in, matrix_in, eye_in,
    *rest, t, blocks, elements, devices, leaving,
):
    outs, scratch = (rest[:1], rest[1:]) if leaving else (rest[:3], rest[3:])
    plan, wet, breach, links, angle, scale, metric, fields, pool, own, spread, matrix, eye, *scratch = scratch
    order, place, coefs, turned, halves, traces, factors, outer, pieces, near, sems, staged, *scratch = scratch
    comp, wide, used = t["comp"], t["wide"], t["used"]
    faces = blocks * 3 * elements
    width = partner_in.shape[0]
    odd = lax.axis_index("mesh") % 2
    near_rows = pl.multiple_of(faces + (1 - odd) * width, 8)
    far_rows = pl.multiple_of(faces + odd * width, 8)
    loads = [
        (plan_in, plan), (angle_in, angle), (scale_in, scale), (links_in, links), (metric_in, metric),
        (fields_in, fields), (wet_in, wet), (breach_in, breach), (eye_in, eye), (own_in, own),
        (spread_in, spread), (matrix_in, matrix), (pool_in, pool.at[pl.ds(0, faces)]),
        (partner_in, pool.at[pl.ds(near_rows, width)]), (across_in, pool.at[pl.ds(far_rows, width)]),
    ]
    n = len(loads)
    loads = start_all([pltpu.make_async_copy(a, b, sems.at[i]) for i, (a, b) in enumerate(loads)])
    index = lax.axis_index("mesh")
    loads[0].wait()
    n_leaving = scan_moves(plan, index * blocks, order, place, blocks)
    begin = 0 if leaving else n_leaving
    end = n_leaving if leaving else blocks
    n_pairs = near.shape[0] // 2
    steps = (end - begin + 2 * n_pairs - 1) // (2 * n_pairs)

    def at(i, u):
        return jnp.maximum(jnp.minimum(begin + 2 * n_pairs * i + u, end - 1), 0)

    def indices(i):
        return [
            pltpu.make_async_copy(links_in.at[order[at(i, u)]], near.at[u], sems.at[n + u])
            for u in range(2 * n_pairs)
        ]

    def send(p):
        rows = outs[0].shape[1]
        return pltpu.make_async_copy(staged.at[p, pl.ds(0, rows)], outs[0].at[place[order[p]]], sems.at[n + 2 * n_pairs + p % RING])

    @pl.when(steps > 0)
    def _():
        start_all(indices(0))

    wait_all(loads[1:5])
    face_rows(angle, scale, links, metric, coefs, blocks, elements)
    if not leaving:
        scan_origins(plan, index, scratch[2], blocks, devices)
    wait_all(loads[5:-3])
    chunks = row_chunks(16)

    def pick(w, rows):
        for f in range(3):
            for line in range(rows.start, rows.stop):
                v = near[2 * w + line // elements, f * elements + line % elements]
                outer[w % 2, f * LANES + line : f * LANES + line + 1, :] = pool[pl.ds(v, 1), :]

    def pair_of(i, w):
        return [order[at(i, 2 * w + u)] for u in range(2)]

    def lay_out(w, pair):
        for c in range(3):
            turn_rows(
                rows_of(fields, pair[0], c, comp), rows_of(fields, pair[1], c, comp), c, eye,
                turned.at[w % 2], halves.at[w % 2], comp,
            )
        inner = mm(halves[w % 2], own[...])
        for c in range(3):
            traces[w % 2, c] = inner[c * LANES : (c + 1) * LANES]
        spread_pair(coefs, pair, eye, spread, factors.at[w % 2], elements)

    def one(i, carry):
        both = [pair_of(i, w) for w in range(n_pairs)]
        inflow = [inflow_rows(breach, pair, t) for pair in both]

        def fluxes(w, rows):
            q = w % 2
            volume_rows(rows, turned.at[q], factors.at[q], 4, inflow[w][rows.start // elements], pieces.at[q])
            flux_rows(rows, traces.at[q], outer.at[q], factors.at[q], pieces.at[q], 4 * LANES, wide)

        def combine(w, c):
            gains = pair_gains(mm(matrix[...], pieces[w % 2, c], ((1,), (1,))), comp, elements)
            for u in range(2):
                b = both[w][u]
                rate = time_step * wet[b].astype(jnp.float32)
                done = rows_of(fields, b, c, comp) + rate * gains[u]
                row = at(i, 2 * w + u) if leaving else 2 * w + u
                if c == 0:
                    staged[row, :comp] = done
                else:
                    staged[row, pl.ds(used + c - 1, comp, stride=2), :] = done

        def hand_over(w):
            for u in range(2):
                if leaving:
                    p = 2 * n_pairs * i + 2 * w + u

                    @pl.when(p < end)
                    def _():
                        @pl.when(p >= RING)
                        def _():
                            send(p - RING).wait()

                        send(p).start()
                else:
                    write_depth(both[w][u], staged.at[2 * w + u], scratch[0], t, blocks)
                    write_flow(both[w][u], staged.at[2 * w + u], scratch[1], t)

        wait_all(indices(i))
        for rows in chunks:
            pick(0, rows)
        for w in range(n_pairs):
            if w + 1 < n_pairs:
                lay_out(w + 1, both[w + 1])
            for k, rows in enumerate(chunks):
                if w > 0 and k < 3:
                    combine(w - 1, k)
                fluxes(w, rows)
                if w + 1 < n_pairs:
                    pick(w + 1, rows)
        for c in range(3):
            combine(n_pairs - 1, c)

        @pl.when(i + 1 < steps)
        def _():
            start_all(indices(i + 1))
            lay_out(0, pair_of(i + 1, 0))

        for w in range(n_pairs):
            hand_over(w)
        return carry

    lay_out(0, pair_of(0, 0))
    wait_all(loads[-3:])
    lax.fori_loop(0, steps, one, 0)
    if leaving:

        def drain(p, carry):
            send(p).wait()
            return carry

        lax.fori_loop(jnp.maximum(end - RING, 0), end, drain, 0)
    else:
        kept = ((scratch[0], outs[0]), (scratch[1], outs[1]), (scratch[2].at[pl.ds(0, outs[2].shape[0])], outs[2]))
        wait_all(start_all([pltpu.make_async_copy(a, b, sems.at[n + 2 * n_pairs + i]) for i, (a, b) in enumerate(kept)]))


def write_depth(b, rows, depth, t, blocks):
    pairs, members = t["pairs"], t["members"]
    tile, sub = b // 8, b % 8
    for s in range(members):
        start = (s * (blocks // 8) + tile) * pairs * 8 + sub
        depth[pl.ds(start, pairs, stride=8), :] = rows[s * pairs : (s + 1) * pairs]


def write_flow(b, rows, flow, t):
    pairs, members, used = t["pairs"], t["members"], t["used"]
    for s in range(members):
        for j in range(pairs):
            row = used + 2 * (s * pairs + j)
            flow[b, s, :, j * LANES : (j + 1) * LANES] = rows[row : row + 2]


def merge_kernel(
    origin_in, got_in, depth_in, flow_in, depth_out, flow_out, origin, depth, flow, got, sems, *, t, blocks
):
    pairs, members = t["pairs"], t["members"]
    loads = start_all(
        [
            pltpu.make_async_copy(a, b, sems.at[i])
            for i, (a, b) in enumerate(((origin_in, origin), (got_in, got)))
        ]
    )
    wait_all(loads)

    def flow_part(b, k):
        return pltpu.make_async_copy(flow.at[b], flow_out.at[b], sems.at[2 + k % RING])

    def depth_part(b, k):
        return pltpu.make_async_copy(
            depth.at[b], depth_out.at[:, b // 8, :, b % 8], sems.at[2 + RING + k % RING]
        )

    def settle(k):
        flow_part(0, k).wait()
        depth_part(0, k).wait()

    def put(b, k):
        came = origin[b] >= 0

        @pl.when(came)
        def _():
            @pl.when(k >= RING)
            def _():
                settle(k)

            for s in range(members):
                depth[b, s] = got[origin[b], s * pairs : (s + 1) * pairs]
            depth_part(b, k).start()
            write_flow(b, got.at[origin[b]], flow, t)
            flow_part(b, k).start()

        return k + came.astype(jnp.int32)

    arrivals = lax.fori_loop(0, blocks, put, jnp.int32(0))

    def drain(k, carry):
        settle(k)
        return carry

    lax.fori_loop(jnp.maximum(arrivals - RING, 0), arrivals, drain, 0)


SMEM = pl.BlockSpec(memory_space=pltpu.SMEM)
HBM = pl.BlockSpec(memory_space=pltpu.HBM)
VMEM = pl.BlockSpec(memory_space=pltpu.VMEM)


def call(kernel, out_shape, n_smem, n_args, scratch, out_specs, **keys):
    return pl.pallas_call(
        kernel,
        out_shape=out_shape,
        in_specs=[SMEM] * n_smem + [HBM] * n_args,
        out_specs=out_specs,
        scratch_shapes=scratch,
        compiler_params=pltpu.CompilerParams(vmem_limit_bytes=64 << 20),
        **keys,
    )


def body(
    water_depth, momentum, metric, face_scale, face_angle, face_map, rim_faces, wet_blocks, breach, block_plan
):
    blocks, members, _ = water_depth.shape
    elements = metric.shape[2]
    t = static_tables(members)
    comp, pairs, used = t["comp"], t["pairs"], t["used"]
    f32, bf16 = jnp.float32, jnp.bfloat16
    tiles = blocks // 8
    depth_rows = water_depth.reshape(tiles, 8, members, pairs, LANES).transpose(2, 0, 3, 1, 4).reshape(-1, LANES)
    flow_rows = momentum.transpose(0, 2, 1, 3)
    faces = face_map.size
    width = rim_faces.shape[1] // 2
    dma = pltpu.SemaphoreType.DMA

    back = jnp.asarray(np.tile(t["back"], (2, 1)), bf16)
    eye = jnp.asarray(np.tile(np.eye(LANES), (1, 2)), bf16)
    fields, pool, to_across, to_partner = call(
        functools.partial(prepare_kernel, t=t, blocks=blocks, elements=elements),
        (
            jax.ShapeDtypeStruct((blocks, 3 * comp, LANES), f32),
            jax.ShapeDtypeStruct((faces, LANES), f32),
            jax.ShapeDtypeStruct((width, LANES), f32),
            jax.ShapeDtypeStruct((width, LANES), f32),
        ),
        0, 5,
        [
            pltpu.SMEM(rim_faces.shape, jnp.int32), pltpu.VMEM(depth_rows.shape, f32), pltpu.VMEM(flow_rows.shape, f32), pltpu.VMEM(back.shape, bf16),
            pltpu.VMEM(eye.shape, bf16),
            pltpu.VMEM((blocks, 3 * comp, LANES), f32), pltpu.VMEM((faces, LANES), f32),
            pltpu.VMEM((2, 3 * LANES, 2 * LANES), bf16), dma((4 + 2 * tiles + blocks // 2,)),
        ],
        (HBM, HBM, VMEM, VMEM),
    )(rim_faces, depth_rows, flow_rows, back, eye)

    count = lax.axis_size("mesh")
    partners = [(i, i ^ 1) for i in range(count)]
    neighbours = [(i, i + 1 if i % 2 else i - 1) for i in range(1, count - 1)]
    across = lax.ppermute(to_across, "mesh", neighbours)
    partner = lax.ppermute(to_partner, "mesh", partners)

    lift_h, lift_l = high_low(t["lift"])
    along_r, along_s = t["along"]
    matrix = np.concatenate(
        [along_r, along_r, along_s, along_s, *(np.asarray(m, np.float32) for m in (lift_h, lift_h, lift_l))], axis=1
    )
    mats = [
        jnp.asarray(np.tile(t["own"], (2, 1)), bf16), jnp.asarray(np.tile(t["spread"], (2, 1)), bf16),
        jnp.asarray(matrix, bf16), eye,
    ]
    packed = round_up(3 * used, 8)

    i32 = jnp.int32
    block_rows = (3 * comp, LANES)

    def finish(leaving, n_pairs, out_shape, extra):
        return call(
            functools.partial(
                finish_kernel, t=t, blocks=blocks, elements=elements, devices=count, leaving=leaving
            ),
            out_shape,
            0, 15,
            [
                pltpu.SMEM(block_plan.shape, i32), pltpu.SMEM(wet_blocks.shape, i32),
                pltpu.SMEM((members, blocks), i32), pltpu.VMEM(face_map.shape, i32),
                pltpu.VMEM(face_angle.shape, f32), pltpu.VMEM(face_scale.shape, f32), pltpu.VMEM(metric.shape, f32),
                pltpu.VMEM((blocks, *block_rows), f32), pltpu.VMEM((faces + 2 * width, LANES), f32),
                *[pltpu.VMEM(m.shape, bf16) for m in mats],
                pltpu.SMEM((blocks,), i32), pltpu.SMEM((blocks,), i32), pltpu.VMEM((blocks * 16, LANES), f32),
                pltpu.VMEM((2, 3, LANES, LANES), f32), pltpu.VMEM((2, 3 * LANES, 2 * LANES), bf16),
                pltpu.VMEM((2, 3, LANES, LANES), f32), pltpu.VMEM((2, LANES, 8 * LANES), f32),
                pltpu.VMEM((2, 3 * LANES, LANES), f32), pltpu.VMEM((2, 3, LANES, 7 * LANES), bf16),
                pltpu.SMEM((2 * n_pairs, face_map.shape[1]), i32), dma((16 + 2 * n_pairs + RING,)), *extra,
            ],
            jax.tree.map(lambda _: HBM, out_shape),
        )(
            block_plan, wet_blocks, breach.T, face_map, face_angle, face_scale, metric, fields, pool, partner, across,
            *mats,
        )

    sent = finish(True, 4, jax.ShapeDtypeStruct((count, packed, LANES), f32), [pltpu.VMEM((blocks, *block_rows), f32)])
    got = lax.all_to_all(sent, "mesh", split_axis=0, concat_axis=0, tiled=True)
    final = (jax.ShapeDtypeStruct(depth_rows.shape, f32), jax.ShapeDtypeStruct(flow_rows.shape, f32))
    whole = [pltpu.VMEM(depth_rows.shape, f32), pltpu.VMEM(flow_rows.shape, f32)]
    depth_kept, flow_kept, origin = finish(
        False, 2, (*final, jax.ShapeDtypeStruct((LANES,), i32)),
        [pltpu.VMEM((4, *block_rows), f32), *whole, pltpu.SMEM((LANES,), i32)],
    )
    tall = (members, tiles, pairs, 8, LANES)
    depth_new, flow_new = call(
        functools.partial(merge_kernel, t=t, blocks=blocks),
        (jax.ShapeDtypeStruct(tall, f32), final[1]),
        0, 4,
        [
            pltpu.SMEM((LANES,), i32), pltpu.VMEM((blocks, members, pairs, LANES), f32), whole[1],
            pltpu.VMEM((count, packed, LANES), f32), dma((2 + 2 * RING,)),
        ],
        (HBM, HBM),
        input_output_aliases={2: 0, 3: 1},
    )(origin, got, depth_kept.reshape(tall), flow_kept)
    depth_out = depth_new.reshape(members, tiles, pairs, 8, LANES).transpose(1, 3, 0, 2, 4).reshape(water_depth.shape)
    return depth_out, flow_new.transpose(0, 2, 1, 3)


def solution(mesh):
    in_specs = (
        P(("groups", "mesh"), None, None),
        P(("groups", "mesh"), None, None, None),
        P(("groups", "mesh"), None, None),
        P(("groups", "mesh"), None),
        P(("groups", "mesh"), None),
        P(("groups", "mesh"), None),
        P(("groups", "mesh"), None),
        P(("groups", "mesh")),
        P(("groups", "mesh"), None),
        P("groups"),
    )
    out_specs = (P(("groups", "mesh"), None, None), P(("groups", "mesh"), None, None, None))
    return jax.shard_map(body, mesh=mesh, in_specs=in_specs, out_specs=out_specs, check_vma=False)
```

```python
import functools
import math

import jax
import jax.numpy as jnp
import numpy as np
from jax import lax
from jax.experimental import pallas as pl
from jax.experimental.pallas import tpu as pltpu
from jax.sharding import PartitionSpec as P


time_step = 0.01
gravity = 1.0
breach_rate = 5.0
LANES = 128


def gauss_solve(matrix, right):
    dimension = matrix.shape[0]
    augmented = np.concatenate([np.array(matrix) * 1.0, np.array(right) * 1.0], axis=1)
    for pivot_col in range(dimension):
        largest = pivot_col + int(np.argmax(np.abs(augmented[pivot_col:, pivot_col])))
        swapped = augmented[[largest, pivot_col]]
        augmented[[pivot_col, largest]] = swapped
        augmented[pivot_col] = augmented[pivot_col] / augmented[pivot_col, pivot_col]
        for row_id in range(dimension):
            if row_id != pivot_col:
                augmented[row_id] = (
                    augmented[row_id] - augmented[row_id, pivot_col] * augmented[pivot_col]
                )
    return augmented[:, dimension:]


def node_tables():
    points = np.array(
        [(across / 3.0, upward / 3.0) for upward in range(4) for across in range(4 - upward)]
    )
    powers = [(power_r, power_s) for power_r in range(4) for power_s in range(4 - power_r)]
    vander = np.zeros((10, 10))
    grad_r = np.zeros((10, 10))
    grad_s = np.zeros((10, 10))
    mono_mass = np.zeros((10, 10))
    for column, (power_r, power_s) in enumerate(powers):
        vander[:, column] = points[:, 0] ** power_r * points[:, 1] ** power_s
        if power_r > 0:
            grad_r[:, column] = power_r * points[:, 0] ** (power_r - 1) * points[:, 1] ** power_s
        if power_s > 0:
            grad_s[:, column] = power_s * points[:, 0] ** power_r * points[:, 1] ** (power_s - 1)
        for second_column, (other_r, other_s) in enumerate(powers):
            mono_mass[column, second_column] = (
                math.factorial(power_r + other_r)
                * math.factorial(power_s + other_s)
                / math.factorial(power_r + other_r + power_s + other_s + 2)
            )
    inverse = gauss_solve(vander, np.eye(10))
    mass_matrix = inverse.T @ mono_mass @ inverse
    line_points = np.arange(4) / 3.0
    line_vander = line_points[:, None] ** np.arange(4)[None, :]
    hilbert = 1.0 / (np.arange(4)[:, None] + np.arange(4)[None, :] + 1.0)
    line_inverse = gauss_solve(line_vander, np.eye(4))
    edge_mass = line_inverse.T @ hilbert @ line_inverse
    face_nodes = np.array([[0, 1, 2, 3], [3, 6, 8, 9], [9, 7, 4, 0]])
    edge_embed = np.zeros((10, 12))
    for face_id in range(3):
        for node_id in range(4):
            edge_embed[face_nodes[face_id, node_id], 4 * face_id : 4 * face_id + 4] += edge_mass[
                node_id
            ]
    lifting = gauss_solve(mass_matrix, edge_embed).reshape(10, 3, 4)
    return (
        np.asarray(grad_r @ inverse, np.float32),
        np.asarray(grad_s @ inverse, np.float32),
        np.asarray(lifting, np.float32),
        face_nodes.reshape(-1),
    )


def round_up(value, step):
    return (value + step - 1) // step * step


def static_tables(members):
    deriv_r, deriv_s, lifting, face_order = node_tables()
    nodes = deriv_r.shape[0]
    pairs = nodes // 2
    used = members * pairs
    comp = round_up(used, 8)
    face_nodes = face_order.reshape(3, 4)
    wide = members * 4

    def lane_of(s, n):
        return (n % 2) * comp + s * pairs + n // 2

    own = np.zeros((LANES, LANES), np.float32)
    own[2 * comp, 3 * wide :] = 1.0
    back = np.zeros((LANES, LANES), np.float32)
    lift = np.zeros((2 * comp, LANES), np.float32)
    along = np.zeros((2, 2 * comp, LANES), np.float32)
    for s in range(members):
        for f in range(3):
            for k in range(4):
                n = int(face_nodes[f, k])
                own[lane_of(s, n), f * wide + s * 4 + k] = 1.0
                back[lane_of(s, n), f * wide + s * 4 + 3 - k] = 1.0
        for n in range(nodes):
            for f in range(3):
                for k in range(4):
                    lift[lane_of(s, n), f * wide + s * 4 + k] = lifting[n, f, k]
            for m in range(nodes):
                along[0, lane_of(s, n), lane_of(s, m)] = -deriv_r[n, m]
                along[1, lane_of(s, n), lane_of(s, m)] = -deriv_s[n, m]
            along[0, lane_of(s, n), 2 * comp + s] = breach_rate
    spread = np.zeros((16, 8 * LANES), np.float32)
    for q in range(4):
        for f in range(3):
            spread[3 * q + f, q * LANES + f * wide : q * LANES + (f + 1) * wide] = 1.0
        spread[12 + q, (4 + q) * LANES : (4 + q) * LANES + 2 * comp] = 1.0
    return dict(
        own=own, back=back, lift=lift, along=along, spread=spread,
        comp=comp, pairs=pairs, used=used, wide=wide, nodes=nodes, members=members,
    )


def high_low(matrix):
    high = matrix.astype(jnp.bfloat16)
    low = (matrix - high.astype(np.float32)).astype(jnp.bfloat16)
    return high, low


def mm(a, b, dims=((1,), (0,))):
    return lax.dot_general(a, b, (dims, ((), ())), preferred_element_type=jnp.float32)


def split(x):
    high = x.astype(jnp.bfloat16)
    return high, (x - high.astype(jnp.float32)).astype(jnp.bfloat16)


def swap_halves(x):
    return pltpu.roll(x, LANES // 2, 1)


def turn(x, eye):
    return mm(eye[...], jnp.concatenate(split(x), axis=1), ((1,), (1,)))


def turn_rows(first, second, c, eye, turned, halves, comp):
    lower = lax.broadcasted_iota(jnp.int32, (comp, LANES), 1) < LANES // 2
    even = jnp.where(lower, first, swap_halves(second))
    odd = jnp.where(lower, swap_halves(first), second)
    fill = jnp.full((LANES - 2 * comp, LANES), 1.0 if c == 0 else 0.0, jnp.float32)
    flat = turn(jnp.concatenate([even, odd, fill], axis=0), eye)
    if turned is not None:
        turned[c] = flat
    high, low = split(flat)
    halves[c * LANES : (c + 1) * LANES, :LANES] = high
    halves[c * LANES : (c + 1) * LANES, LANES:] = low


def rows_of(fields, block, c, comp):
    if c == 0:
        return fields[block, :comp]
    return fields[block, pl.ds(comp + c - 1, comp, stride=2), :]


def place_face(pieces, c, wide, lane):
    moved = [pltpu.roll(p, ((i - c) * wide) % LANES, 1) if i != c else p for i, p in enumerate(pieces)]
    return jnp.where(lane < wide, moved[0], jnp.where(lane < 2 * wide, moved[1], moved[2]))


def root(x):
    return x * lax.rsqrt(x)


def start_all(copies):
    for copy in copies:
        copy.start()
    return copies


def wait_all(copies):
    for copy in copies:
        copy.wait()


def prepare_kernel(
    rim_in, depth_in, flow_in, back_in, eye_in, fields_out, pool_out, across, partner,
    rim, depth, flow, back, eye, fields, pool, halves, sems, *, t, blocks, elements,
):
    comp, pairs, members, wide = t["comp"], t["pairs"], t["members"], t["wide"]
    odd = lax.axis_index("mesh") % 2
    tiles = blocks // 8
    steps = blocks // 2
    group = 2 * 3 * elements
    first = start_all(
        [
            pltpu.make_async_copy(depth_in, depth, sems.at[0]), pltpu.make_async_copy(back_in, back, sems.at[1]),
            pltpu.make_async_copy(eye_in, eye, sems.at[2]), pltpu.make_async_copy(rim_in, rim, sems.at[3]),
        ]
    )

    def part(tile):
        rows = pl.ds(8 * tile, 8)
        return pltpu.make_async_copy(flow_in.at[rows], flow.at[rows], sems.at[4 + tile])

    def field_part(tile):
        rows = pl.ds(8 * tile, 8)
        return pltpu.make_async_copy(fields.at[rows], fields_out.at[rows], sems.at[4 + tiles + tile])

    def pool_part(i):
        lines = pl.ds(group * i, group)
        return pltpu.make_async_copy(pool.at[lines], pool_out.at[lines], sems.at[4 + 2 * tiles + i])

    start_all([part(tile) for tile in range(tiles)])
    wait_all(first)

    def build(i):
        for u in range(2):
            b = 2 * i + u
            tile, sub = b // 8, b % 8
            fields[b, comp - 8 : comp] = jnp.full((8, LANES), 1.0, jnp.float32)
            fields[b, 3 * comp - 16 : 3 * comp] = jnp.zeros((16, LANES), jnp.float32)
            for s in range(members):
                start = (s * tiles + tile) * pairs * 8 + sub
                fields[b, s * pairs : (s + 1) * pairs] = depth[pl.ds(start, pairs, stride=8), :]
                for j in range(pairs):
                    row = comp + 2 * (s * pairs + j)
                    fields[b, row : row + 2] = flow[b, s, :, j * LANES : (j + 1) * LANES]

    def turn_of(i, slot):
        for c in range(3):
            turn_rows(
                rows_of(fields, 2 * i, c, comp), rows_of(fields, 2 * i + 1, c, comp), c, eye, None,
                halves.at[slot], comp,
            )

    def faces_of(i, slot):
        rows = mm(halves[slot], back[...])
        lane = lax.broadcasted_iota(jnp.int32, (LANES, LANES), 1)
        pieces = [rows[c * LANES : (c + 1) * LANES] for c in range(3)]
        for f in range(3):
            face = place_face(pieces, f, wide, lane)
            for u in range(2):
                at = ((2 * i + u) * 3 + f) * elements
                pool[pl.ds(at, elements), :] = face[u * elements : (u + 1) * elements]

    part(0).wait()
    build(0)
    build(1)
    turn_of(0, 0)
    turn_of(1, 1)
    build(2)
    build(3)
    field_part(0).start()

    def one(h, carry):
        i = 2 * h

        @pl.when(h % 2 == 0)
        def _():
            part(h // 2).wait()

        for slot in range(2):
            faces_of(i - 4 + slot, slot)
        for slot in range(2):
            turn_of(i - 2 + slot, slot)
        for slot in range(2):
            build(i + slot)
        for slot in range(2):
            pool_part(i - 4 + slot).start()

        @pl.when(h % 2 == 1)
        def _():
            field_part(h // 2).start()

        return carry

    lax.fori_loop(2, steps // 2, one, 0)
    for slot in range(2):
        faces_of(steps - 4 + slot, slot)
    for slot in range(2):
        turn_of(steps - 2 + slot, slot)
    for slot in range(2):
        pool_part(steps - 4 + slot).start()
    for slot in range(2):
        faces_of(steps - 2 + slot, slot)
        pool_part(steps - 2 + slot).start()
    width = partner.shape[0]
    near, far = (1 - odd) * width, odd * width

    def pick(i, carry):
        for u in range(32):
            r = i * 32 + u
            partner[pl.ds(r, 1), :] = pool[pl.ds(rim[0, near + r], 1), :]
            across[pl.ds(r, 1), :] = pool[pl.ds(rim[0, far + r], 1), :]
        return carry

    lax.fori_loop(0, width // 32, pick, 0)
    for tile in range(tiles):
        field_part(tile).wait()
    for i in range(steps):
        pool_part(i).wait()


def scan_moves(plan, base, order, place, blocks):
    def one(i, carry):
        leaving, staying = carry
        slot = plan[base + i]
        away = jnp.logical_or(slot < base, slot >= base + blocks).astype(jnp.int32)
        order[jnp.where(away == 1, leaving, blocks - 1 - staying)] = i
        place[i] = lax.div(slot, jnp.int32(blocks))
        return leaving + away, staying + 1 - away

    return lax.fori_loop(0, blocks, one, (jnp.int32(0), jnp.int32(0)))[0]


def scan_origins(plan, own, origin, blocks, devices):
    def device(d, carry):
        mark = jnp.where(d == own, -1, d)
        for i in range(blocks):
            slot = plan[d * blocks + i] - own * blocks
            origin[jnp.where(jnp.logical_and(slot >= 0, slot < blocks), slot, blocks)] = mark
        return carry

    lax.fori_loop(0, devices, device, 0)


def face_rows(angle, scale, links, metric, coefs, blocks, elements):
    shape = (blocks, 3 * elements)
    own = lax.broadcasted_iota(jnp.int32, shape, 0) * (3 * elements) + lax.broadcasted_iota(jnp.int32, shape, 1)
    free = jnp.where(links[...] == own, 0.0, 1.0)
    lower = lax.broadcasted_iota(jnp.int32, (blocks, LANES), 1) < elements
    for q, value in enumerate((jnp.cos(angle[...]), jnp.sin(angle[...]), scale[...], free)):
        two = value[:, :LANES]
        swapped = swap_halves(two)
        third = value[:, LANES:]
        faces = (
            jnp.where(lower, two, swapped), jnp.where(lower, swapped, two), jnp.concatenate([third, third], axis=1)
        )
        for f in range(3):
            coefs[pl.ds(3 * q + f, blocks, stride=16), :] = faces[f]
    for b in range(blocks):
        factors = metric[b]
        coefs[b * 16 + 12 : b * 16 + 16] = jnp.concatenate([factors, factors], axis=1)


def spread_pair(coefs, both, eye, spread, factors, elements):
    lower = lax.broadcasted_iota(jnp.int32, (16, LANES), 1) < elements
    values = jnp.where(lower, coefs[pl.ds(both[0] * 16, 16), :], coefs[pl.ds(both[1] * 16, 16), :])
    rough = values.astype(jnp.bfloat16).astype(jnp.float32)
    stacked = jnp.concatenate([rough, values - rough], axis=0).astype(jnp.bfloat16)
    stacked = mm(eye[:, :LANES], stacked, ((1,), (1,))).astype(jnp.bfloat16)
    factors[...] = mm(stacked, spread[...])


def inflow_rows(breach, both, t):
    rows = []
    for b in both:
        row = jnp.zeros((1, LANES), jnp.float32)
        for s in range(t["members"]):
            level = breach[s, b].astype(jnp.float32)
            row = jnp.where(lax.broadcasted_iota(jnp.int32, (1, LANES), 1) == 2 * t["comp"] + s, level, row)
        rows.append(row)
    return rows


def volume_rows(rows, turned, factors, first, inflow, pieces):
    rx, sx, ry, sy = (factors[rows, q * LANES : (q + 1) * LANES] for q in range(first, first + 4))
    height, flow_x, flow_y = (turned[c, rows] for c in range(3))
    pressure = 0.5 * gravity * height * height
    inverse = 1.0 / height
    speed_x = flow_x * inverse
    speed_y = flow_y * inverse
    cross = flow_y * speed_x
    flux_f = (flow_x, flow_x * speed_x + pressure, cross)
    flux_g = (flow_y, cross, flow_y * speed_y + pressure)
    for c in range(3):
        along_r = rx * flux_f[c] + ry * flux_g[c]
        along_s = sx * flux_f[c] + sy * flux_g[c]
        if c == 0:
            along_r = along_r + inflow
        pieces[c, rows, 0:LANES], pieces[c, rows, LANES : 2 * LANES] = split(along_r)
        pieces[c, rows, 2 * LANES : 3 * LANES], pieces[c, rows, 3 * LANES : 4 * LANES] = split(along_s)


def flux_rows(rows, traces, outer, factors, pieces, first, wide):
    lane = lax.broadcasted_iota(jnp.int32, (rows.stop - rows.start, LANES), 1)
    n_x, n_y, scale, free = (factors[rows, q * LANES : (q + 1) * LANES] for q in range(4))
    theirs = [outer[f * LANES + rows.start : f * LANES + rows.stop] for f in range(3)]
    height, flow_x, flow_y = (traces[c, rows] for c in range(3))
    is_wall = free < 0.5
    through = flow_x * n_x + flow_y * n_y
    twice = through + through
    height_o = jnp.where(is_wall, height, place_face(theirs, 0, wide, lane))
    flow_xo = jnp.where(is_wall, flow_x - twice * n_x, place_face(theirs, 1, wide, lane))
    flow_yo = jnp.where(is_wall, flow_y - twice * n_y, place_face(theirs, 2, wide, lane))
    speed = through / height
    speed_o = (flow_xo * n_x + flow_yo * n_y) / height_o
    fast = jnp.maximum(
        jnp.abs(speed) + root(gravity * height), jnp.abs(speed_o) + root(gravity * height_o)
    )
    ours, others = speed - fast, speed_o - fast
    half = 0.5 * scale
    push = 0.5 * gravity * (height * height - height_o * height_o)
    jumps = (
        half * (height * ours - height_o * others),
        half * (flow_x * ours - flow_xo * others + push * n_x),
        half * (flow_y * ours - flow_yo * others + push * n_y),
    )
    for c in range(3):
        high, rest = split(jumps[c])
        pieces[c, rows, first : first + LANES] = high
        pieces[c, rows, first + LANES : first + 2 * LANES] = rest
        pieces[c, rows, first + 2 * LANES : first + 3 * LANES] = high


def pair_gains(tall, comp, elements):
    narrow = lax.broadcasted_iota(jnp.int32, (comp, LANES), 1) < elements
    even, odd = tall[:comp], tall[comp:]
    return jnp.where(narrow, even, swap_halves(odd)), jnp.where(narrow, swap_halves(even), odd)


def row_chunks(step):
    return [slice(i * step, (i + 1) * step) for i in range(LANES // step)]


RING = 8


def finish_kernel(
    plan_in, wet_in, breach_in, links_in, angle_in, scale_in, metric_in,
    fields_in, pool_in, partner_in, across_in, own_in, spread_in, matrix_in, eye_in,
    *rest, t, blocks, elements, devices, leaving,
):
    outs, scratch = (rest[:1], rest[1:]) if leaving else (rest[:3], rest[3:])
    plan, wet, breach, links, angle, scale, metric, fields, pool, own, spread, matrix, eye, *scratch = scratch
    order, place, coefs, turned, halves, traces, factors, outer, pieces, near, sems, staged, *scratch = scratch
    comp, wide, used = t["comp"], t["wide"], t["used"]
    faces = blocks * 3 * elements
    width = partner_in.shape[0]
    odd = lax.axis_index("mesh") % 2
    near_rows = pl.multiple_of(faces + (1 - odd) * width, 8)
    far_rows = pl.multiple_of(faces + odd * width, 8)
    loads = [
        (plan_in, plan), (angle_in, angle), (scale_in, scale), (links_in, links), (metric_in, metric),
        (fields_in, fields), (wet_in, wet), (breach_in, breach), (eye_in, eye), (own_in, own),
        (spread_in, spread), (matrix_in, matrix), (pool_in, pool.at[pl.ds(0, faces)]),
        (partner_in, pool.at[pl.ds(near_rows, width)]), (across_in, pool.at[pl.ds(far_rows, width)]),
    ]
    n = len(loads)
    loads = start_all([pltpu.make_async_copy(a, b, sems.at[i]) for i, (a, b) in enumerate(loads)])
    index = lax.axis_index("mesh")
    loads[0].wait()
    n_leaving = scan_moves(plan, index * blocks, order, place, blocks)
    begin = 0 if leaving else n_leaving
    end = n_leaving if leaving else blocks
    n_pairs = near.shape[0] // 2
    steps = (end - begin + 2 * n_pairs - 1) // (2 * n_pairs)

    def at(i, u):
        return jnp.maximum(jnp.minimum(begin + 2 * n_pairs * i + u, end - 1), 0)

    def indices(i):
        return [
            pltpu.make_async_copy(links_in.at[order[at(i, u)]], near.at[u], sems.at[n + u])
            for u in range(2 * n_pairs)
        ]

    def send(p):
        rows = outs[0].shape[1]
        return pltpu.make_async_copy(staged.at[p, pl.ds(0, rows)], outs[0].at[place[order[p]]], sems.at[n + 2 * n_pairs + p % RING])

    @pl.when(steps > 0)
    def _():
        start_all(indices(0))

    wait_all(loads[1:5])
    face_rows(angle, scale, links, metric, coefs, blocks, elements)
    if not leaving:
        scan_origins(plan, index, scratch[2], blocks, devices)
    wait_all(loads[5:-3])
    chunks = row_chunks(16)

    def pick(w, rows):
        for f in range(3):
            for line in range(rows.start, rows.stop):
                v = near[2 * w + line // elements, f * elements + line % elements]
                outer[w % 2, f * LANES + line : f * LANES + line + 1, :] = pool[pl.ds(v, 1), :]

    def pair_of(i, w):
        return [order[at(i, 2 * w + u)] for u in range(2)]

    def lay_out(w, pair):
        for c in range(3):
            turn_rows(
                rows_of(fields, pair[0], c, comp), rows_of(fields, pair[1], c, comp), c, eye,
                turned.at[w % 2], halves.at[w % 2], comp,
            )
        inner = mm(halves[w % 2], own[...])
        for c in range(3):
            traces[w % 2, c] = inner[c * LANES : (c + 1) * LANES]
        spread_pair(coefs, pair, eye, spread, factors.at[w % 2], elements)

    early = n_pairs // 2 if leaving else 0

    def one(i, carry):
        both = [pair_of(i, w) for w in range(n_pairs)]
        inflow = [inflow_rows(breach, pair, t) for pair in both]

        def fluxes(w, rows):
            q = w % 2
            volume_rows(rows, turned.at[q], factors.at[q], 4, inflow[w][rows.start // elements], pieces.at[q])
            flux_rows(rows, traces.at[q], outer.at[q], factors.at[q], pieces.at[q], 4 * LANES, wide)

        def combine(w, c):
            gains = pair_gains(mm(matrix[...], pieces[w % 2, c], ((1,), (1,))), comp, elements)
            for u in range(2):
                b = both[w][u]
                rate = time_step * wet[b].astype(jnp.float32)
                done = rows_of(fields, b, c, comp) + rate * gains[u]
                row = at(i, 2 * w + u) if leaving else 2 * w + u
                if c == 0:
                    staged[row, :comp] = done
                else:
                    staged[row, pl.ds(used + c - 1, comp, stride=2), :] = done

        def hand_over(w):
            for u in range(2):
                if leaving:
                    p = 2 * n_pairs * i + 2 * w + u

                    @pl.when(p < end)
                    def _():
                        @pl.when(p >= RING)
                        def _():
                            send(p - RING).wait()

                        send(p).start()
                else:
                    write_depth(both[w][u], staged.at[2 * w + u], scratch[0], t, blocks)
                    write_flow(both[w][u], staged.at[2 * w + u], scratch[1], t)

        wait_all(indices(i))
        for rows in chunks:
            pick(0, rows)
        for w in range(n_pairs):
            if w + 1 < n_pairs:
                lay_out(w + 1, both[w + 1])
            for k, rows in enumerate(chunks):
                if w > 0 and k < 3:
                    combine(w - 1, k)
                fluxes(w, rows)
                if w + 1 < n_pairs:
                    pick(w + 1, rows)
            if w == early:
                for v in range(early):
                    hand_over(v)
        for c in range(3):
            combine(n_pairs - 1, c)

        @pl.when(i + 1 < steps)
        def _():
            start_all(indices(i + 1))
            lay_out(0, pair_of(i + 1, 0))

        for w in range(early, n_pairs):
            hand_over(w)
        return carry

    lay_out(0, pair_of(0, 0))
    wait_all(loads[-3:])
    lax.fori_loop(0, steps, one, 0)
    if leaving:

        def drain(p, carry):
            send(p).wait()
            return carry

        lax.fori_loop(jnp.maximum(end - RING, 0), end, drain, 0)
    else:
        kept = ((scratch[0], outs[0]), (scratch[1], outs[1]), (scratch[2].at[pl.ds(0, outs[2].shape[0])], outs[2]))
        wait_all(start_all([pltpu.make_async_copy(a, b, sems.at[n + 2 * n_pairs + i]) for i, (a, b) in enumerate(kept)]))


def write_depth(b, rows, depth, t, blocks):
    pairs, members = t["pairs"], t["members"]
    tile, sub = b // 8, b % 8
    for s in range(members):
        start = (s * (blocks // 8) + tile) * pairs * 8 + sub
        depth[pl.ds(start, pairs, stride=8), :] = rows[s * pairs : (s + 1) * pairs]


def write_flow(b, rows, flow, t):
    pairs, members, used = t["pairs"], t["members"], t["used"]
    for s in range(members):
        for j in range(pairs):
            row = used + 2 * (s * pairs + j)
            flow[b, s, :, j * LANES : (j + 1) * LANES] = rows[row : row + 2]


def merge_kernel(
    origin_in, got_in, depth_in, flow_in, depth_out, flow_out, origin, depth, flow, got, sems, *, t, blocks
):
    pairs, members = t["pairs"], t["members"]
    loads = start_all(
        [
            pltpu.make_async_copy(a, b, sems.at[i])
            for i, (a, b) in enumerate(((origin_in, origin), (got_in, got)))
        ]
    )
    wait_all(loads)

    def flow_part(b, k):
        return pltpu.make_async_copy(flow.at[b], flow_out.at[b], sems.at[2 + k % RING])

    def depth_part(b, k):
        return pltpu.make_async_copy(
            depth.at[b], depth_out.at[:, b // 8, :, b % 8], sems.at[2 + RING + k % RING]
        )

    def settle(k):
        flow_part(0, k).wait()
        depth_part(0, k).wait()

    def put(b, k):
        came = origin[b] >= 0

        @pl.when(came)
        def _():
            @pl.when(k >= RING)
            def _():
                settle(k)

            for s in range(members):
                depth[b, s] = got[origin[b], s * pairs : (s + 1) * pairs]
            depth_part(b, k).start()
            write_flow(b, got.at[origin[b]], flow, t)
            flow_part(b, k).start()

        return k + came.astype(jnp.int32)

    arrivals = lax.fori_loop(0, blocks, put, jnp.int32(0))

    def drain(k, carry):
        settle(k)
        return carry

    lax.fori_loop(jnp.maximum(arrivals - RING, 0), arrivals, drain, 0)


SMEM = pl.BlockSpec(memory_space=pltpu.SMEM)
HBM = pl.BlockSpec(memory_space=pltpu.HBM)
VMEM = pl.BlockSpec(memory_space=pltpu.VMEM)


def call(kernel, out_shape, n_smem, n_args, scratch, out_specs, **keys):
    return pl.pallas_call(
        kernel,
        out_shape=out_shape,
        in_specs=[SMEM] * n_smem + [HBM] * n_args,
        out_specs=out_specs,
        scratch_shapes=scratch,
        compiler_params=pltpu.CompilerParams(vmem_limit_bytes=64 << 20),
        **keys,
    )


def body(
    water_depth, momentum, metric, face_scale, face_angle, face_map, rim_faces, wet_blocks, breach, block_plan
):
    blocks, members, _ = water_depth.shape
    elements = metric.shape[2]
    t = static_tables(members)
    comp, pairs, used = t["comp"], t["pairs"], t["used"]
    f32, bf16 = jnp.float32, jnp.bfloat16
    tiles = blocks // 8
    depth_rows = water_depth.reshape(tiles, 8, members, pairs, LANES).transpose(2, 0, 3, 1, 4).reshape(-1, LANES)
    flow_rows = momentum.transpose(0, 2, 1, 3)
    faces = face_map.size
    width = rim_faces.shape[1] // 2
    dma = pltpu.SemaphoreType.DMA

    back = jnp.asarray(np.tile(t["back"], (2, 1)), bf16)
    eye = jnp.asarray(np.tile(np.eye(LANES), (1, 2)), bf16)
    fields, pool, to_across, to_partner = call(
        functools.partial(prepare_kernel, t=t, blocks=blocks, elements=elements),
        (
            jax.ShapeDtypeStruct((blocks, 3 * comp, LANES), f32),
            jax.ShapeDtypeStruct((faces, LANES), f32),
            jax.ShapeDtypeStruct((width, LANES), f32),
            jax.ShapeDtypeStruct((width, LANES), f32),
        ),
        0, 5,
        [
            pltpu.SMEM(rim_faces.shape, jnp.int32), pltpu.VMEM(depth_rows.shape, f32), pltpu.VMEM(flow_rows.shape, f32), pltpu.VMEM(back.shape, bf16),
            pltpu.VMEM(eye.shape, bf16),
            pltpu.VMEM((blocks, 3 * comp, LANES), f32), pltpu.VMEM((faces, LANES), f32),
            pltpu.VMEM((2, 3 * LANES, 2 * LANES), bf16), dma((4 + 2 * tiles + blocks // 2,)),
        ],
        (HBM, HBM, VMEM, VMEM),
    )(rim_faces, depth_rows, flow_rows, back, eye)

    count = lax.axis_size("mesh")
    partners = [(i, i ^ 1) for i in range(count)]
    neighbours = [(i, i + 1 if i % 2 else i - 1) for i in range(1, count - 1)]
    across = lax.ppermute(to_across, "mesh", neighbours)
    partner = lax.ppermute(to_partner, "mesh", partners)

    lift_h, lift_l = high_low(t["lift"])
    along_r, along_s = t["along"]
    matrix = np.concatenate(
        [along_r, along_r, along_s, along_s, *(np.asarray(m, np.float32) for m in (lift_h, lift_h, lift_l))], axis=1
    )
    mats = [
        jnp.asarray(np.tile(t["own"], (2, 1)), bf16), jnp.asarray(np.tile(t["spread"], (2, 1)), bf16),
        jnp.asarray(matrix, bf16), eye,
    ]
    packed = round_up(3 * used, 8)

    i32 = jnp.int32
    block_rows = (3 * comp, LANES)

    def finish(leaving, n_pairs, out_shape, extra):
        return call(
            functools.partial(
                finish_kernel, t=t, blocks=blocks, elements=elements, devices=count, leaving=leaving
            ),
            out_shape,
            0, 15,
            [
                pltpu.SMEM(block_plan.shape, i32), pltpu.SMEM(wet_blocks.shape, i32),
                pltpu.SMEM((members, blocks), i32), pltpu.VMEM(face_map.shape, i32),
                pltpu.VMEM(face_angle.shape, f32), pltpu.VMEM(face_scale.shape, f32), pltpu.VMEM(metric.shape, f32),
                pltpu.VMEM((blocks, *block_rows), f32), pltpu.VMEM((faces + 2 * width, LANES), f32),
                *[pltpu.VMEM(m.shape, bf16) for m in mats],
                pltpu.SMEM((blocks,), i32), pltpu.SMEM((blocks,), i32), pltpu.VMEM((blocks * 16, LANES), f32),
                pltpu.VMEM((2, 3, LANES, LANES), f32), pltpu.VMEM((2, 3 * LANES, 2 * LANES), bf16),
                pltpu.VMEM((2, 3, LANES, LANES), f32), pltpu.VMEM((2, LANES, 8 * LANES), f32),
                pltpu.VMEM((2, 3 * LANES, LANES), f32), pltpu.VMEM((2, 3, LANES, 7 * LANES), bf16),
                pltpu.SMEM((2 * n_pairs, face_map.shape[1]), i32), dma((16 + 2 * n_pairs + RING,)), *extra,
            ],
            jax.tree.map(lambda _: HBM, out_shape),
        )(
            block_plan, wet_blocks, breach.T, face_map, face_angle, face_scale, metric, fields, pool, partner, across,
            *mats,
        )

    sent = finish(True, 4, jax.ShapeDtypeStruct((count, packed, LANES), f32), [pltpu.VMEM((blocks, *block_rows), f32)])
    got = lax.all_to_all(sent, "mesh", split_axis=0, concat_axis=0, tiled=True)
    final = (jax.ShapeDtypeStruct(depth_rows.shape, f32), jax.ShapeDtypeStruct(flow_rows.shape, f32))
    whole = [pltpu.VMEM(depth_rows.shape, f32), pltpu.VMEM(flow_rows.shape, f32)]
    depth_kept, flow_kept, origin = finish(
        False, 2, (*final, jax.ShapeDtypeStruct((LANES,), i32)),
        [pltpu.VMEM((4, *block_rows), f32), *whole, pltpu.SMEM((LANES,), i32)],
    )
    tall = (members, tiles, pairs, 8, LANES)
    depth_new, flow_new = call(
        functools.partial(merge_kernel, t=t, blocks=blocks),
        (jax.ShapeDtypeStruct(tall, f32), final[1]),
        0, 4,
        [
            pltpu.SMEM((LANES,), i32), pltpu.VMEM((blocks, members, pairs, LANES), f32), whole[1],
            pltpu.VMEM((count, packed, LANES), f32), dma((2 + 2 * RING,)),
        ],
        (HBM, HBM),
        input_output_aliases={2: 0, 3: 1},
    )(origin, got, depth_kept.reshape(tall), flow_kept)
    depth_out = depth_new.reshape(members, tiles, pairs, 8, LANES).transpose(1, 3, 0, 2, 4).reshape(water_depth.shape)
    return depth_out, flow_new.transpose(0, 2, 1, 3)


def solution(mesh):
    in_specs = (
        P(("groups", "mesh"), None, None),
        P(("groups", "mesh"), None, None, None),
        P(("groups", "mesh"), None, None),
        P(("groups", "mesh"), None),
        P(("groups", "mesh"), None),
        P(("groups", "mesh"), None),
        P(("groups", "mesh"), None),
        P(("groups", "mesh")),
        P(("groups", "mesh"), None),
        P("groups"),
    )
    out_specs = (P(("groups", "mesh"), None, None), P(("groups", "mesh"), None, None, None))
    return jax.shard_map(body, mesh=mesh, in_specs=in_specs, out_specs=out_specs, check_vma=False)
```
